32 devices in a mesh: dp: 4 (over y, core), seq: 8 (over z, x).
Axes of the slice: x: 2, y: 2, z: 4, core: 2. Of those that a mesh axis runs over, the one named last changes fastest.
Arguments:
- tokens: bfloat16 [8, 1024, 1152], P('dp', 'seq'), may hold values from -6 to 6
- teacher: bfloat16 [8, 1024, 1152], P('dp', 'seq'), may hold values from -6 to 6
- lengths: int32 [8], P('dp'), may hold values from 256 to 1024, as said below
- w_query: bfloat16 [1152, 1152], P('dp', 'seq'), may hold values from -0.1875 to 0.1875
- key_weight: bfloat16 [1152, 384], P('dp', 'seq'), may hold values from -0.1875 to 0.1875
- value_weight: bfloat16 [1152, 384], P('dp', 'seq'), may hold values from -0.1875 to 0.1875
- w_out: bfloat16 [1152, 1152], P('dp', 'seq'), may hold values from -0.5 to 0.5
- w_gate: bfloat16 [1152, 3072], P('dp', 'seq'), may hold values from -0.1875 to 0.1875
- w_up: bfloat16 [1152, 3072], P('dp', 'seq'), may hold values from -0.1875 to 0.1875
- w_down: bfloat16 [3072, 1152], P('dp', 'seq'), may hold values from -0.109375 to 0.109375
- gain_attn: bfloat16 [1152], P('seq'), may hold values from 0.5 to 1.5
- gain_ffn: bfloat16 [1152], P('seq'), may hold values from 0.5 to 1.5
Outputs:
- output: bfloat16 [8, 1024, 1152], P('dp', 'seq')
- loss: float32 [], replicated
- tokens_grad: float32 [8, 1024, 1152], P('dp', 'seq')
- grad_w_query: float32 [1152, 1152], P('dp', 'seq')
- grad_w_key: float32 [1152, 384], P('dp', 'seq')
- grad_w_value: float32 [1152, 384], P('dp', 'seq')
- grad_w_out: float32 [1152, 1152], P('dp', 'seq')
- grad_w_gate: float32 [1152, 3072], P('dp', 'seq')
- grad_w_up: float32 [1152, 3072], P('dp', 'seq')
- grad_w_down: float32 [3072, 1152], P('dp', 'seq')
- grad_gain_attn: float32 [1152], P('seq')
- grad_gain_ffn: float32 [1152], P('seq')
The draws below stay inside these ranges and needn't reach their ends.
Inputs may be any that keep to these rules, and one draw needn't show every extreme that they name: Slot s holds valid tokens at positions below lengths[s]; some slot has exactly 1024 and some exactly 256.
All inputs are finite; a program needn't handle non-finite values.
Results may differ from the reference program's by a relative error of at most 0.015.
Values may be sent and summed in bfloat16 or wider, within the bound.
A program may use at most 192 MiB of HBM per device.

```python
import math
import jax
import jax.numpy as jnp
from jax import lax

MODEL_DIMENSION = 1152
QUERY_HEADS = 18
KEY_VALUE_HEADS = 6
HEAD_DIMENSION = 64
FF = 3072
SLOT_LEN = 1024
SLOTS = 8
TOKENS = 8192


def draw_lengths(key, part):
    first_key, second_key = jax.random.split(jax.random.fold_in(key, 11))
    value_rows = jax.random.randint(first_key, (SLOTS,), SLOT_LEN // 4, SLOT_LEN + 1, dtype=jnp.int32)
    shuffled = jax.random.permutation(second_key, SLOTS)
    value_rows = value_rows.at[shuffled[0]].set(SLOT_LEN)
    return value_rows.at[shuffled[1]].set(SLOT_LEN // 4)


def level_of(key, extent, pieces, low, largest):
    gain = 1.0
    for position, blocks in pieces:
        draws = jax.random.uniform(jax.random.fold_in(jax.random.fold_in(key, 6), position), (blocks,), jnp.float32, low / len(pieces), largest / len(pieces))
        gain = gain * jnp.repeat(jnp.exp(draws), extent[position] // blocks).reshape((-1,) + (1,) * (len(extent) - 1 - position))
    return gain


def normal_values(own_key, shape, width, most, cuts=(), kind=jnp.bfloat16):
    entries = width * jax.random.normal(own_key, shape, jnp.float32)
    if cuts:
        entries = entries * level_of(own_key, shape, cuts, -0.22, 0.18)
    return jnp.clip(entries, -most, most).astype(kind)


def setup_inputs(seed: int = 0) -> dict:
    splits = jax.random.split(jax.random.key(seed), 13)
    tokens = normal_values(splits[0], (SLOTS, SLOT_LEN, MODEL_DIMENSION), 1.0, 6.0, ((0, 4), (1, 8)))
    teacher = normal_values(splits[1], (SLOTS, SLOT_LEN, MODEL_DIMENSION), 1.0, 6.0, ((0, 4), (1, 8)))
    lengths = draw_lengths(jax.random.fold_in(splits[12], 71), 0)
    w_query = normal_values(splits[3], (MODEL_DIMENSION, QUERY_HEADS * HEAD_DIMENSION), MODEL_DIMENSION ** -0.5, 0.1875, ((0, 4), (1, 8)))
    key_weight = normal_values(splits[4], (MODEL_DIMENSION, KEY_VALUE_HEADS * HEAD_DIMENSION), MODEL_DIMENSION ** -0.5, 0.1875, ((0, 4), (1, 8)))
    value_weight = normal_values(splits[5], (MODEL_DIMENSION, KEY_VALUE_HEADS * HEAD_DIMENSION), MODEL_DIMENSION ** -0.5, 0.1875, ((0, 4), (1, 8)))
    w_out = normal_values(splits[6], (QUERY_HEADS * HEAD_DIMENSION, MODEL_DIMENSION), (MODEL_DIMENSION // 8) ** -0.5, 0.5, ((0, 4), (1, 8)))
    w_gate = normal_values(splits[7], (MODEL_DIMENSION, FF), MODEL_DIMENSION ** -0.5, 0.1875, ((0, 4), (1, 8)))
    w_up = normal_values(splits[8], (MODEL_DIMENSION, FF), MODEL_DIMENSION ** -0.5, 0.1875, ((0, 4), (1, 8)))
    w_down = normal_values(splits[9], (FF, MODEL_DIMENSION), FF ** -0.5, 0.109375, ((0, 4), (1, 8)))
    gain_attn = jnp.clip(1.0 + 0.1 * jax.random.normal(splits[10], (MODEL_DIMENSION,), jnp.float32), 0.5, 1.5).astype(jnp.bfloat16)
    gain_ffn = jnp.clip(1.0 + 0.1 * jax.random.normal(splits[11], (MODEL_DIMENSION,), jnp.float32), 0.5, 1.5).astype(jnp.bfloat16)
    return dict(tokens=tokens, teacher=teacher, lengths=lengths, w_query=w_query, key_weight=key_weight, value_weight=value_weight, w_out=w_out, w_gate=w_gate, w_up=w_up, w_down=w_down, gain_attn=gain_attn, gain_ffn=gain_ffn)


norm_eps = 1e-05
rope_base = 10000.0

@jax.custom_vjp
def lower_precision(v):
    return lax.optimization_barrier(v.astype(jnp.bfloat16)).astype(jnp.float32)

@jax.custom_vjp
def lower_precision_backward(v):
    return v

def low_keep(v):
    return (lower_precision(v), None)

def low_pass(kept, grad):
    return (grad,)

def back_keep(v):
    return (v, None)

def back_low(kept, grad):
    return (lower_precision(grad),)
lower_precision.defvjp(low_keep, low_pass)
lower_precision_backward.defvjp(back_keep, back_low)

def rope_tables(positions, head_width):
    half_width = head_width // 2
    exponents = jnp.arange(half_width, dtype=jnp.float32) * (2.0 / head_width)
    angles = positions.astype(jnp.float32)[:, None] * (rope_base ** (-exponents))[None, :]
    return (jnp.cos(angles), jnp.sin(angles))

def apply_rotary(value_rows, cosine_table, sine_table):
    half_width = value_rows.shape[-1] // 2
    front_half = value_rows[..., :half_width]
    back_half = value_rows[..., half_width:]
    cos_wide = cosine_table[:, None, :]
    sin_wide = sine_table[:, None, :]
    return jnp.concatenate([front_half * cos_wide - back_half * sin_wide, front_half * sin_wide + back_half * cos_wide], axis=-1)

def matrix_product(left, right):
    return jnp.dot(left, right, precision=lax.Precision.HIGHEST, preferred_element_type=jnp.float32)

def slot_forward(params, slot_tokens, slot_length):
    w_query, key_weight, value_weight, w_out, w_gate, w_up, w_down, gain_attn, gain_ffn = params
    overall_length = slot_tokens.shape[0]
    query_group = QUERY_HEADS // KEY_VALUE_HEADS
    scale = HEAD_DIMENSION ** (-0.5)
    positions = jnp.arange(overall_length, dtype=jnp.int32)
    valid_keys = positions < slot_length
    inv_first = lax.rsqrt(lax.optimization_barrier(jnp.mean(slot_tokens * slot_tokens, axis=-1, keepdims=True)) + norm_eps)
    attention_input = lower_precision(slot_tokens * inv_first * gain_attn)
    unrotated_query = lower_precision_backward(matrix_product(attention_input, w_query)).reshape(overall_length, QUERY_HEADS, HEAD_DIMENSION)
    unrotated_key = lower_precision_backward(matrix_product(attention_input, key_weight)).reshape(overall_length, KEY_VALUE_HEADS, HEAD_DIMENSION)
    value_rows = lower_precision(lower_precision_backward(matrix_product(attention_input, value_weight))).reshape(overall_length, KEY_VALUE_HEADS, HEAD_DIMENSION)
    cosine_table, sine_table = rope_tables(positions, HEAD_DIMENSION)
    rotated_query = lower_precision(apply_rotary(unrotated_query, cosine_table, sine_table)).reshape(overall_length, KEY_VALUE_HEADS, query_group, HEAD_DIMENSION)
    key_rot = lower_precision(apply_rotary(unrotated_key, cosine_table, sine_table))
    block_length = math.gcd(overall_length, 512)
    number_of_blocks = overall_length // block_length

    def block_attention(block_inputs):
        query_blk, block_start = block_inputs
        query_pos = block_start + jnp.arange(block_length, dtype=jnp.int32)
        raw_scores = jnp.einsum('qhgd,khd->hgqk', query_blk, key_rot, precision=lax.Precision.HIGHEST)
        scores = lower_precision_backward(raw_scores * scale)
        allowed = (positions[None, :] <= query_pos[:, None]) & valid_keys[None, :]
        exp_scores = jnp.where(allowed[None, None], jnp.exp(scores), 0.0)
        denominator = lax.optimization_barrier(jnp.sum(exp_scores, axis=-1))
        numerator = lower_precision_backward(jnp.einsum('hgqk,khd->qhgd', lower_precision(exp_scores), value_rows, precision=lax.Precision.HIGHEST))
        return numerator / jnp.transpose(denominator, (2, 0, 1))[..., None]
    block_outputs = lax.map(jax.checkpoint(block_attention), (rotated_query.reshape(number_of_blocks, block_length, KEY_VALUE_HEADS, query_group, HEAD_DIMENSION), jnp.arange(number_of_blocks, dtype=jnp.int32) * block_length))
    attn_float = block_outputs.reshape(overall_length, QUERY_HEADS * HEAD_DIMENSION)
    attn_b = lower_precision(lower_precision_backward(attn_float))
    hidden = slot_tokens + lower_precision_backward(matrix_product(attn_b, w_out))
    inv_second = lax.rsqrt(lax.optimization_barrier(jnp.mean(hidden * hidden, axis=-1, keepdims=True)) + norm_eps)
    ffn_in = lower_precision(hidden * inv_second * gain_ffn)
    gate_proj = lower_precision_backward(matrix_product(ffn_in, w_gate))
    up_proj = lower_precision_backward(matrix_product(ffn_in, w_up))
    hid_b = lower_precision(jax.nn.silu(gate_proj) * up_proj)
    ffn_out = lower_precision_backward(matrix_product(hid_b, w_down))
    return jnp.where(valid_keys[:, None], hidden + ffn_out, 0.0)

def reference(tokens, teacher, lengths, w_query, key_weight, value_weight, w_out, w_gate, w_up, w_down, gain_attn, gain_ffn):
    params = tuple((weight.astype(jnp.float32) for weight in (w_query, key_weight, value_weight, w_out, w_gate, w_up, w_down, gain_attn, gain_ffn)))
    token_float = tokens.astype(jnp.float32)
    teach_float = teacher.astype(jnp.float32)

    def forward_one(slot_inputs):
        return slot_forward(params, slot_inputs[0], slot_inputs[1])
    outputs = lax.map(forward_one, (token_float, lengths))
    positions = jnp.arange(SLOT_LEN, dtype=jnp.int32)
    valid_rows = positions[None, :] < lengths[:, None]
    difference = jnp.where(valid_rows[..., None], outputs - teach_float, 0.0)
    valid_count = jnp.sum(lengths).astype(jnp.float32)
    loss = jnp.sum(difference * difference) / valid_count
    cotangent = TOKENS / valid_count * difference

    def grad_step(totals, slot_inputs):
        slot_tokens, slot_length, slot_cot = slot_inputs

        def run_slot(weights_in, tokens_in):
            return slot_forward(weights_in, tokens_in, slot_length)
        forward_out, pullback = jax.vjp(run_slot, params, slot_tokens)
        grad_params, grad_tokens = pullback(slot_cot)
        return (jax.tree.map(jnp.add, totals, grad_params), grad_tokens)
    zeros_init = tuple((jnp.zeros_like(weight) for weight in params))
    grad_totals, tokens_grad = lax.scan(grad_step, zeros_init, (token_float, lengths, cotangent))
    return (outputs.astype(jnp.bfloat16), loss, tokens_grad, grad_totals[0], grad_totals[1], grad_totals[2], grad_totals[3], grad_totals[4], grad_totals[5], grad_totals[6], grad_totals[7], grad_totals[8])
```

```python
import math

import jax
import jax.numpy as jnp
from jax import lax
from jax.experimental import pallas as pl
from jax.experimental.pallas import tpu as pltpu
from jax.sharding import PartitionSpec as P

QUERY_HEADS = 18
KEY_VALUE_HEADS = 6
HEAD_DIMENSION = 64


norm_eps = 1e-05
rope_base = 10000.0


def rope_tables(positions, head_width):
    half_width = head_width // 2
    exponents = jnp.arange(half_width, dtype=jnp.float32) * (2.0 / head_width)
    angles = positions.astype(jnp.float32)[:, None] * (rope_base ** (-exponents))[None, :]
    return (jnp.cos(angles), jnp.sin(angles))


def apply_rotary(value_rows, cosine_table, sine_table):
    half_width = value_rows.shape[-1] // 2
    front_half = value_rows[..., :half_width]
    back_half = value_rows[..., half_width:]
    cos_wide = cosine_table[:, None, :]
    sin_wide = sine_table[:, None, :]
    return jnp.concatenate(
        [
            front_half * cos_wide - back_half * sin_wide,
            front_half * sin_wide + back_half * cos_wide,
        ],
        axis=-1,
    )


def allowed_mask(query_pos, key_pos, live_len):
    causal = key_pos[None, :] <= query_pos[:, None]
    present = key_pos[None, :] < live_len[:, None]
    return (causal[None, :, :] & present[:, None, :])[:, None, None, :, :]


def over_blocks(piece_len, unit_len, step_fn, running):
    block_length = math.gcd(piece_len, unit_len * max(1, 512 // unit_len))
    number_of_blocks = piece_len // block_length

    def loop_step(block_number, state):
        return step_fn(state, block_number * block_length, block_length)

    return lax.fori_loop(0, number_of_blocks, loop_step, running)


def collect(shards):
    wide = (
        lax.all_gather(shards[0], "seq", axis=1, tiled=True),
        lax.all_gather(shards[1], "seq", axis=1, tiled=True),
        lax.all_gather(shards[2], "seq", axis=1, tiled=True),
        lax.all_gather(shards[3], "seq", axis=1, tiled=True),
        lax.all_gather(shards[4], "seq", axis=1, tiled=True),
        lax.all_gather(shards[5], "seq", axis=1, tiled=True),
        lax.all_gather(shards[6], "seq", axis=1, tiled=True),
        lax.all_gather(shards[7], "seq", axis=0, tiled=True),
        lax.all_gather(shards[8], "seq", axis=0, tiled=True),
    )
    whole = (
        lax.all_gather(wide[0], "dp", axis=0, tiled=True),
        lax.all_gather(wide[1], "dp", axis=0, tiled=True),
        lax.all_gather(wide[2], "dp", axis=0, tiled=True),
        lax.all_gather(wide[3], "dp", axis=0, tiled=True),
        lax.all_gather(wide[4], "dp", axis=0, tiled=True),
        lax.all_gather(wide[5], "dp", axis=0, tiled=True),
        lax.all_gather(wide[6], "dp", axis=0, tiled=True),
    )
    return tuple(whole) + (wide[7], wide[8])


def reduce_grads(grad_sums):
    summed = (
        lax.psum_scatter(grad_sums[0], "seq", scatter_dimension=1, tiled=True),
        lax.psum_scatter(grad_sums[1], "seq", scatter_dimension=1, tiled=True),
        lax.psum_scatter(grad_sums[2], "seq", scatter_dimension=1, tiled=True),
        lax.psum_scatter(grad_sums[3], "seq", scatter_dimension=1, tiled=True),
        lax.psum_scatter(grad_sums[4], "seq", scatter_dimension=1, tiled=True),
        lax.psum_scatter(grad_sums[5], "seq", scatter_dimension=1, tiled=True),
        lax.psum_scatter(grad_sums[6], "seq", scatter_dimension=1, tiled=True),
        lax.psum_scatter(grad_sums[7], "seq", scatter_dimension=0, tiled=True),
        lax.psum_scatter(grad_sums[8], "seq", scatter_dimension=0, tiled=True),
    )
    owned = (
        lax.psum_scatter(summed[0], "dp", scatter_dimension=0, tiled=True),
        lax.psum_scatter(summed[1], "dp", scatter_dimension=0, tiled=True),
        lax.psum_scatter(summed[2], "dp", scatter_dimension=0, tiled=True),
        lax.psum_scatter(summed[3], "dp", scatter_dimension=0, tiled=True),
        lax.psum_scatter(summed[4], "dp", scatter_dimension=0, tiled=True),
        lax.psum_scatter(summed[5], "dp", scatter_dimension=0, tiled=True),
        lax.psum_scatter(summed[6], "dp", scatter_dimension=0, tiled=True),
    )
    return (tuple(owned), summed[7], summed[8])


def forward_slot(weights, tok_part, live_len, query_pos, cosine_table, sine_table):
    (
        full_query,
        full_key,
        full_value,
        full_out,
        full_gate,
        full_up,
        full_down,
        full_gain_attn,
        full_gain_ffn,
    ) = weights
    slot_position, stretched_length, model_width = tok_part.shape
    number_of_rows = slot_position * stretched_length
    query_group = QUERY_HEADS // KEY_VALUE_HEADS
    scale = HEAD_DIMENSION ** (-0.5)
    tok_float = tok_part.astype(jnp.float32).reshape(number_of_rows, model_width)
    inv_first = lax.rsqrt(jnp.mean(tok_float * tok_float, axis=-1, keepdims=True) + norm_eps)
    normed_first = tok_float * inv_first
    attention_input = (normed_first * full_gain_attn.astype(jnp.float32)).astype(jnp.bfloat16)
    unrotated_query = jnp.dot(
        attention_input, full_query, preferred_element_type=jnp.float32
    ).reshape(slot_position, stretched_length, QUERY_HEADS, HEAD_DIMENSION)
    unrotated_key = jnp.dot(attention_input, full_key, preferred_element_type=jnp.float32).reshape(
        slot_position, stretched_length, KEY_VALUE_HEADS, HEAD_DIMENSION
    )
    value_block = (
        jnp.dot(attention_input, full_value, preferred_element_type=jnp.float32)
        .astype(jnp.bfloat16)
        .reshape(slot_position, stretched_length, KEY_VALUE_HEADS * HEAD_DIMENSION)
    )
    query_b = (
        apply_rotary(unrotated_query, cosine_table, sine_table)
        .astype(jnp.bfloat16)
        .reshape(slot_position, stretched_length, KEY_VALUE_HEADS, query_group, HEAD_DIMENSION)
    )
    key_block = (
        apply_rotary(unrotated_key, cosine_table, sine_table)
        .astype(jnp.bfloat16)
        .reshape(slot_position, stretched_length, KEY_VALUE_HEADS * HEAD_DIMENSION)
    )
    empty_denominator = jnp.zeros(
        (slot_position, KEY_VALUE_HEADS, query_group, stretched_length), jnp.float32
    )
    empty_numerator = jnp.zeros(
        (slot_position, KEY_VALUE_HEADS, query_group, stretched_length, HEAD_DIMENSION), jnp.float32
    )
    key_piece = lax.all_gather(key_block, "seq", axis=1, tiled=True)
    value_piece = lax.all_gather(value_block, "seq", axis=1, tiled=True)

    def one_block(partial_value, offset, block_length):
        denominator, numerator = partial_value
        key_blk = lax.dynamic_slice_in_dim(key_piece, offset, block_length, 1).reshape(
            slot_position, block_length, KEY_VALUE_HEADS, HEAD_DIMENSION
        )
        value_blk = lax.dynamic_slice_in_dim(value_piece, offset, block_length, 1).reshape(
            slot_position, block_length, KEY_VALUE_HEADS, HEAD_DIMENSION
        )
        allowed = allowed_mask(
            query_pos, offset + jnp.arange(block_length, dtype=jnp.int32), live_len
        )
        scores = (
            jnp.einsum("schgd,snhd->shgcn", query_b, key_blk, preferred_element_type=jnp.float32)
            * scale
        )
        exp_scores = jnp.where(allowed, jnp.exp(scores), 0.0)
        denominator = denominator + jnp.sum(exp_scores, axis=-1)
        numerator = numerator + jnp.einsum(
            "shgcn,snhd->shgcd",
            exp_scores.astype(jnp.bfloat16),
            value_blk,
            preferred_element_type=jnp.float32,
        )
        return (denominator, numerator)

    denominator, numerator = over_blocks(
        key_piece.shape[1], stretched_length, one_block, (empty_denominator, empty_numerator)
    )
    attn_float = jnp.transpose(numerator / denominator[..., None], (0, 3, 1, 2, 4)).reshape(
        number_of_rows, QUERY_HEADS * HEAD_DIMENSION
    )
    attn_b = attn_float.astype(jnp.bfloat16)
    hidden = tok_float + jnp.dot(attn_b, full_out, preferred_element_type=jnp.float32)
    inv_second = lax.rsqrt(jnp.mean(hidden * hidden, axis=-1, keepdims=True) + norm_eps)
    normed_second = hidden * inv_second
    ffn_in = (normed_second * full_gain_ffn.astype(jnp.float32)).astype(jnp.bfloat16)
    gate_proj = jnp.dot(ffn_in, full_gate, preferred_element_type=jnp.float32)
    up_proj = jnp.dot(ffn_in, full_up, preferred_element_type=jnp.float32)
    hid_b = (jax.nn.silu(gate_proj) * up_proj).astype(jnp.bfloat16)
    valid_rows = (query_pos[None, :] < live_len[:, None]).reshape(number_of_rows, 1)
    out_float = jnp.where(
        valid_rows, hidden + jnp.dot(hid_b, full_down, preferred_element_type=jnp.float32), 0.0
    )
    saved = (
        attention_input,
        inv_first,
        normed_first,
        query_b,
        key_block,
        value_block,
        attn_float,
        attn_b,
        denominator,
        normed_second,
        inv_second,
        ffn_in,
        gate_proj,
        up_proj,
        hid_b,
    )
    return (out_float, valid_rows, saved)


def backward_slot(weights, saved, cotangent, live_len, query_pos, cosine_table, sine_table):
    (
        full_query,
        full_key,
        full_value,
        full_out,
        full_gate,
        full_up,
        full_down,
        full_gain_attn,
        full_gain_ffn,
    ) = weights
    (
        attention_input,
        inv_first,
        normed_first,
        query_b,
        key_block,
        value_block,
        attn_float,
        attn_b,
        denominator,
        normed_second,
        inv_second,
        ffn_in,
        gate_proj,
        up_proj,
        hid_b,
    ) = saved
    slot_position = query_b.shape[0]
    stretched_length = query_b.shape[1]
    number_of_rows = slot_position * stretched_length
    query_group = QUERY_HEADS // KEY_VALUE_HEADS
    scale = HEAD_DIMENSION ** (-0.5)
    cot_b = cotangent.astype(jnp.bfloat16)
    grad_down = jnp.einsum("rf,rd->fd", hid_b, cot_b, preferred_element_type=jnp.float32)
    grad_hid = jnp.einsum("rd,fd->rf", cot_b, full_down, preferred_element_type=jnp.float32)
    sigmoid_gate = jax.nn.sigmoid(gate_proj)
    grad_gate_b = (
        grad_hid * up_proj * sigmoid_gate * (1.0 + gate_proj * (1.0 - sigmoid_gate))
    ).astype(jnp.bfloat16)
    grad_up_b = (grad_hid * gate_proj * sigmoid_gate).astype(jnp.bfloat16)
    grad_gate = jnp.einsum("rd,rf->df", ffn_in, grad_gate_b, preferred_element_type=jnp.float32)
    grad_up = jnp.einsum("rd,rf->df", ffn_in, grad_up_b, preferred_element_type=jnp.float32)
    grad_ffn_in = jnp.einsum(
        "rf,df->rd", grad_gate_b, full_gate, preferred_element_type=jnp.float32
    ) + jnp.einsum("rf,df->rd", grad_up_b, full_up, preferred_element_type=jnp.float32)
    grad_gain_ffn = jnp.sum(grad_ffn_in * normed_second, axis=0)
    grad_normed = grad_ffn_in * full_gain_ffn.astype(jnp.float32)
    grad_hidden = cotangent + inv_second * (
        grad_normed - normed_second * jnp.mean(grad_normed * normed_second, axis=-1, keepdims=True)
    )
    grad_proj_b = grad_hidden.astype(jnp.bfloat16)
    grad_out = jnp.einsum("rq,rd->qd", attn_b, grad_proj_b, preferred_element_type=jnp.float32)
    grad_attn_b = jnp.einsum(
        "rd,qd->rq", grad_proj_b, full_out, preferred_element_type=jnp.float32
    ).astype(jnp.bfloat16)
    den_rows = jnp.transpose(denominator, (0, 3, 1, 2)).reshape(number_of_rows, QUERY_HEADS)
    grad_heads_float = grad_attn_b.astype(jnp.float32).reshape(
        number_of_rows, QUERY_HEADS, HEAD_DIMENSION
    )
    softmax_ratio = (
        jnp.sum(
            grad_heads_float * attn_float.reshape(number_of_rows, QUERY_HEADS, HEAD_DIMENSION),
            axis=-1,
        )
        / den_rows
    ).reshape(slot_position, stretched_length, QUERY_HEADS)
    scaled_gradient = (
        (grad_heads_float / den_rows[..., None])
        .astype(jnp.bfloat16)
        .reshape(slot_position, stretched_length, QUERY_HEADS * HEAD_DIMENSION)
    )
    ratio_all = lax.all_gather(softmax_ratio, "seq", axis=1, tiled=True)
    head_gradient = scaled_gradient.reshape(
        slot_position, stretched_length, KEY_VALUE_HEADS, query_group, HEAD_DIMENSION
    )
    local_softmax_ratio = jnp.transpose(
        softmax_ratio.reshape(slot_position, stretched_length, KEY_VALUE_HEADS, query_group),
        (0, 2, 3, 1),
    )[..., None]
    empty_query = jnp.zeros(
        (slot_position, KEY_VALUE_HEADS, query_group, stretched_length, HEAD_DIMENSION), jnp.float32
    )
    key_piece = lax.all_gather(key_block, "seq", axis=1, tiled=True)
    value_piece = lax.all_gather(value_block, "seq", axis=1, tiled=True)

    def one_block(partial_value, offset, block_length):
        key_blk = lax.dynamic_slice_in_dim(key_piece, offset, block_length, 1).reshape(
            slot_position, block_length, KEY_VALUE_HEADS, HEAD_DIMENSION
        )
        value_blk = lax.dynamic_slice_in_dim(value_piece, offset, block_length, 1).reshape(
            slot_position, block_length, KEY_VALUE_HEADS, HEAD_DIMENSION
        )
        allowed = allowed_mask(
            query_pos, offset + jnp.arange(block_length, dtype=jnp.int32), live_len
        )
        scores = (
            jnp.einsum("schgd,snhd->shgcn", query_b, key_blk, preferred_element_type=jnp.float32)
            * scale
        )
        exp_scores = jnp.where(allowed, jnp.exp(scores), 0.0)
        grad_prob = jnp.einsum(
            "schgd,snhd->shgcn", head_gradient, value_blk, preferred_element_type=jnp.float32
        )
        grad_score = (exp_scores * (grad_prob - local_softmax_ratio)).astype(jnp.bfloat16)
        return (
            partial_value
            + jnp.einsum(
                "shgcn,snhd->shgcd", grad_score, key_blk, preferred_element_type=jnp.float32
            )
            * scale
        )

    grad_query = over_blocks(key_piece.shape[1], stretched_length, one_block, empty_query)
    query_flat = query_b.reshape(slot_position, stretched_length, QUERY_HEADS * HEAD_DIMENSION)
    per_head_keys = key_block.reshape(
        slot_position, stretched_length, KEY_VALUE_HEADS, HEAD_DIMENSION
    )
    per_head_values = value_block.reshape(
        slot_position, stretched_length, KEY_VALUE_HEADS, HEAD_DIMENSION
    )
    empty_key_value = jnp.zeros(
        (slot_position, KEY_VALUE_HEADS, stretched_length, HEAD_DIMENSION), jnp.float32
    )
    query_piece = lax.all_gather(query_flat, "seq", axis=1, tiled=True)
    grad_piece = lax.all_gather(scaled_gradient, "seq", axis=1, tiled=True)

    def one_block(partial_value, offset, block_length):
        grad_key, value_gradient = partial_value
        query_blk = lax.dynamic_slice_in_dim(query_piece, offset, block_length, 1).reshape(
            slot_position, block_length, KEY_VALUE_HEADS, query_group, HEAD_DIMENSION
        )
        grad_blk = lax.dynamic_slice_in_dim(grad_piece, offset, block_length, 1).reshape(
            slot_position, block_length, KEY_VALUE_HEADS, query_group, HEAD_DIMENSION
        )
        ratio_blk = lax.dynamic_slice_in_dim(ratio_all, offset, block_length, 1).reshape(
            slot_position, block_length, KEY_VALUE_HEADS, query_group
        )
        ratio_blk = jnp.transpose(ratio_blk, (0, 2, 3, 1))[..., None]
        remote_pos = offset + jnp.arange(block_length, dtype=jnp.int32)
        allowed = allowed_mask(remote_pos, query_pos, live_len)
        scores = (
            jnp.einsum(
                "snhgd,schd->shgnc", query_blk, per_head_keys, preferred_element_type=jnp.float32
            )
            * scale
        )
        exp_scores = jnp.where(allowed, jnp.exp(scores), 0.0)
        value_gradient = value_gradient + jnp.einsum(
            "shgnc,snhgd->shcd",
            exp_scores.astype(jnp.bfloat16),
            grad_blk,
            preferred_element_type=jnp.float32,
        )
        grad_prob = jnp.einsum(
            "snhgd,schd->shgnc", grad_blk, per_head_values, preferred_element_type=jnp.float32
        )
        grad_score = (exp_scores * (grad_prob - ratio_blk)).astype(jnp.bfloat16)
        grad_key = (
            grad_key
            + jnp.einsum(
                "shgnc,snhgd->shcd", grad_score, query_blk, preferred_element_type=jnp.float32
            )
            * scale
        )
        return (grad_key, value_gradient)

    grad_key, value_gradient = over_blocks(
        query_piece.shape[1], stretched_length, one_block, (empty_key_value, empty_key_value)
    )
    grad_query = jnp.transpose(grad_query, (0, 3, 1, 2, 4)).reshape(
        slot_position, stretched_length, QUERY_HEADS, HEAD_DIMENSION
    )
    grad_query_b = (
        apply_rotary(grad_query, cosine_table, -sine_table)
        .astype(jnp.bfloat16)
        .reshape(number_of_rows, QUERY_HEADS * HEAD_DIMENSION)
    )
    grad_key_b = (
        apply_rotary(jnp.transpose(grad_key, (0, 2, 1, 3)), cosine_table, -sine_table)
        .astype(jnp.bfloat16)
        .reshape(number_of_rows, KEY_VALUE_HEADS * HEAD_DIMENSION)
    )
    grad_value_b = (
        jnp.transpose(value_gradient, (0, 2, 1, 3))
        .astype(jnp.bfloat16)
        .reshape(number_of_rows, KEY_VALUE_HEADS * HEAD_DIMENSION)
    )
    grad_wq = jnp.einsum(
        "rd,rq->dq", attention_input, grad_query_b, preferred_element_type=jnp.float32
    )
    grad_wk = jnp.einsum(
        "rd,rq->dq", attention_input, grad_key_b, preferred_element_type=jnp.float32
    )
    grad_wv = jnp.einsum(
        "rd,rq->dq", attention_input, grad_value_b, preferred_element_type=jnp.float32
    )
    grad_attn_in = jnp.einsum(
        "rq,dq->rd", grad_query_b, full_query, preferred_element_type=jnp.float32
    )
    grad_attn_in = grad_attn_in + jnp.einsum(
        "rq,dq->rd", grad_key_b, full_key, preferred_element_type=jnp.float32
    )
    grad_attn_in = grad_attn_in + jnp.einsum(
        "rq,dq->rd", grad_value_b, full_value, preferred_element_type=jnp.float32
    )
    grad_gain_attn = jnp.sum(grad_attn_in * normed_first, axis=0)
    grad_first = grad_attn_in * full_gain_attn.astype(jnp.float32)
    grad_tokens = grad_hidden + inv_first * (
        grad_first - normed_first * jnp.mean(grad_first * normed_first, axis=-1, keepdims=True)
    )
    return (
        (
            grad_wq,
            grad_wk,
            grad_wv,
            grad_out,
            grad_gate,
            grad_up,
            grad_down,
            grad_gain_attn,
            grad_gain_ffn,
        ),
        grad_tokens,
    )


def per_device(
    tokens,
    teacher,
    lengths,
    w_query,
    key_weight,
    value_weight,
    w_out,
    w_gate,
    w_up,
    w_down,
    gain_attn,
    gain_ffn,
):
    shards = (w_query, key_weight, value_weight, w_out, w_gate, w_up, w_down, gain_attn, gain_ffn)
    slot_count, stretched_length, model_width = tokens.shape
    total_tokens = slot_count * lax.axis_size("dp") * stretched_length * lax.axis_size("seq")
    query_pos = lax.axis_index("seq") * stretched_length + jnp.arange(
        stretched_length, dtype=jnp.int32
    )
    cosine_table, sine_table = rope_tables(query_pos, HEAD_DIMENSION)
    out_rows = []
    stored = []
    differences = []
    squares_local = jnp.zeros((), jnp.float32)
    count_local = jnp.zeros((), jnp.float32)
    for micro in range(slot_count):
        weights = collect(shards)
        live_len = lengths[micro : micro + 1]
        out_float, valid_rows, saved = forward_slot(
            weights, tokens[micro : micro + 1], live_len, query_pos, cosine_table, sine_table
        )
        teach_float = teacher[micro].astype(jnp.float32)
        difference = jnp.where(valid_rows, out_float - teach_float, 0.0)
        squares_local = squares_local + jnp.sum(difference * difference)
        count_local = count_local + jnp.sum(valid_rows.astype(jnp.float32))
        out_rows.append(out_float.astype(jnp.bfloat16).reshape(1, stretched_length, model_width))
        stored.append(saved)
        differences.append(difference)
    loss_sum, count_sum = lax.psum((squares_local, count_local), ("dp", "seq"))
    loss = loss_sum / count_sum
    factor = total_tokens / count_sum
    grad_sums = None
    token_grads = []
    for micro in range(slot_count):
        weights = collect(shards)
        grads, grad_tokens = backward_slot(
            weights,
            stored[micro],
            factor * differences[micro],
            lengths[micro : micro + 1],
            query_pos,
            cosine_table,
            sine_table,
        )
        grad_sums = grads if grad_sums is None else jax.tree.map(jnp.add, grad_sums, grads)
        token_grads.append(grad_tokens.reshape(1, stretched_length, model_width))
    owned, gain_part_attn, gain_part_ffn = reduce_grads(grad_sums)
    gain_totals = lax.psum((gain_part_attn, gain_part_ffn), "dp")
    output = jnp.concatenate(out_rows, axis=0)
    tokens_grad = jnp.concatenate(token_grads, axis=0)
    return (
        output,
        loss,
        tokens_grad,
        owned[0],
        owned[1],
        owned[2],
        owned[3],
        owned[4],
        owned[5],
        owned[6],
        gain_totals[0],
        gain_totals[1],
    )


MESH_ID = pl.DeviceIdType.MESH
VMEM_MOST = 64 * 1024 * 1024 - 128 * 1024


class Place(tuple):
    def with_line(self):
        z = self[2]
        self.line = (0,) + tuple(pick(z, v) for v in ((1, -1, -1, -1), (2, 1, 1, -2), (3, 2, -2, -3)))
        self.sign = (0,) + tuple(jnp.where(offset > 0, 1, -1) for offset in self.line[1:])
        return self


def position():
    row = lax.axis_index("dp")
    column = lax.axis_index("seq")
    return Place((lax.rem(column, 2), row // 2, column // 2, lax.rem(row, 2))).with_line()


def mesh_place(x, y, z, c):
    return (2 * y + c, 2 * z + x)


def step_to(place, axis, sign=1):
    x, y, z, c = place
    if axis == "x":
        return (1 - x, y, z, c)
    if axis == "y":
        return (x, 1 - y, z, c)
    if axis == "z":
        return (x, y, z + sign, c)
    return (x, y, z, 1 - c)


def pick(z, values):
    return sum(jnp.where(z == i, v, 0) for i, v in enumerate(values) if v)


def shifted(place, rel):
    x, y, z, c = place
    dx, dy, rank = rel
    return ((1 - x) if dx else x, (1 - y) if dy else y, z + place.line[rank], c)


def on_line(z):
    return jnp.logical_and(z >= 0, z < 4)


def greet(place, lines):
    x, y, z, c = place
    d, s = mesh_place(*place)
    barrier = pltpu.get_barrier_semaphore()

    def signal(who):
        pl.semaphore_signal(barrier, inc=1, device_id=who, device_id_type=MESH_ID)

    if lines:
        for k in range(1, 8):
            signal((d, lax.rem(s + k, 8)))
        for k in range(1, 4):
            signal((lax.rem(d + k, 4), s))
        pl.semaphore_wait(barrier, 10)
        return
    for axis in "xyc":
        signal(mesh_place(*step_to(place, axis)))
    pl.when(z < 3)(lambda: signal(mesh_place(x, y, z + 1, c)))
    pl.when(z > 0)(lambda: signal(mesh_place(x, y, z - 1, c)))
    pl.semaphore_wait(barrier, 3 + jnp.where(z > 0, 1, 0) + jnp.where(z < 3, 1, 0))


def wait_bytes(region, sem):
    pltpu.make_async_copy(region, region, sem).wait()


def spread_order(order):
    held = [((0, 0, 0), -1)]
    for level, axis in enumerate(order):
        new = []
        if axis == "z":
            new = [((rel[0], rel[1], rank), level) for rank in (1, 2, 3) for rel, _ in held]
        else:
            new = [((1, rel[1], rel[2]) if axis == "x" else (rel[0], 1, rel[2]), level) for rel, _ in held]
        held = held + new
    return held


class Spread:
    def __init__(self, place, order, own, spot, sems, job, pair=None, amount=None):
        self.place, self.order, self.own, self.spot = place, order, own, spot
        self.recv, self.send, self.recv_core, self.send_core = sems
        self.job, self.pair, self.amount = job, pair, amount
        self.pieces = spread_order(order)

    def number(self, who):
        x, y, z, _ = who
        return z * 4 + y * 2 + x

    def go(self, rel, level, target):
        who = shifted(self.place, rel)
        pltpu.make_async_remote_copy(
            src_ref=self.own if level < 0 else self.spot(who),
            dst_ref=self.spot(who),
            send_sem=self.send.at[self.job],
            recv_sem=self.recv.at[self.job, self.number(who)],
            device_id=mesh_place(*target),
            device_id_type=MESH_ID,
        ).start()

    def to_core(self, rel):
        who = shifted(self.place, rel)
        pltpu.make_async_remote_copy(
            src_ref=self.pair(who),
            dst_ref=self.pair(who),
            send_sem=self.send_core.at[self.job],
            recv_sem=self.recv_core.at[self.job],
            device_id=mesh_place(*step_to(self.place, "c")),
            device_id_type=MESH_ID,
        ).start()

    def steps(self):
        out = []
        arrived = set()
        z = self.place[2]
        for rel, level in self.pieces:

            def run(rel=rel, level=level):
                arrived.add(rel)
                who = shifted(self.place, rel)
                if level >= 0:
                    there = self.spot(who)
                    pltpu.make_async_copy(there, there, self.recv.at[self.job, self.number(who)]).wait()
                if level >= 0 and self.order[level] == "z":
                    on = z - self.place.sign[rel[2]]
                    pl.when(on_line(on))(lambda: self.go(rel, level, (self.place[0], self.place[1], on, self.place[3])))
                for axis in self.order[level + 1:]:
                    if axis == "z":
                        pl.when(z < 3)(lambda: self.go(rel, level, step_to(self.place, "z", 1)))
                        pl.when(z > 0)(lambda: self.go(rel, level, step_to(self.place, "z", -1)))
                    else:
                        self.go(rel, level, step_to(self.place, axis))
                if self.pair is not None and (1 - rel[0], rel[1], rel[2]) in arrived:
                    self.to_core(rel)

            out.append(run)
        return out

    def sent(self):
        total = [0, 0]
        for i, z in enumerate((0, 1)):
            for rel, level in self.pieces:
                if level >= 0 and self.order[level] == "z":
                    offset = (0, ((1, -1)[z]), ((2, 1)[z]), ((3, 2)[z]))[rel[2]]
                    on = z - (1 if offset > 0 else -1)
                    total[i] += 0 <= on < 4
                for axis in self.order[level + 1:]:
                    total[i] += (1, 2)[z] if axis == "z" else 1
        return total

    def wait_core(self):
        wait_bytes(self.amount(16), self.recv_core.at[self.job])

    def finish(self):
        ends, inner = self.sent()
        z = self.place[2]
        at_end = jnp.logical_or(z == 0, z == 3)
        pl.when(at_end)(lambda: wait_bytes(self.amount(ends), self.send.at[self.job]))
        pl.when(jnp.logical_not(at_end))(lambda: wait_bytes(self.amount(inner), self.send.at[self.job]))
        if self.pair is not None:
            wait_bytes(self.amount(16), self.send_core.at[self.job])


def fold_pieces(order):
    out = []
    for dx in (0, 1):
        for dy in (0, 1) if "y" in order else (0,):
            for rank in (0, 1, 2, 3):
                differs = {"x": dx, "y": dy, "z": rank}
                stage = next((i for i, axis in enumerate(order) if differs[axis]), len(order))
                out.append(((dx, dy, rank), stage))
    return sorted(out, key=lambda item: (item[1], -item[0][2], -item[0][0] - item[0][1]))


def fold_slots(order):
    base, starts = 0, []
    for level, axis in enumerate(order):
        starts.append(base)
        after = order[level + 1:]
        wide = (4 if "z" in after else 1) * (2 if "x" in after else 1) * (2 if "y" in after else 1)
        base += wide * 5 if axis == "z" else wide
    return starts, base


class Fold:
    def __init__(self, place, order, mine, arrived, sems, job, out, amount, ready=None):
        self.place, self.order, self.mine, self.arrived = place, order, mine, arrived
        self.send, self.recv = sems
        self.job, self.out, self.amount, self.ready = job, out, amount, ready
        self.pieces = fold_pieces(order)
        self.base, self.slots = fold_slots(order)

    def slot(self, level, rel, last):
        index = 0
        at_z = self.place[2] + self.place.line[rel[2]]
        for other in self.order[level + 1:]:
            size = 4 if other == "z" else 2
            index = index * size + (at_z if other == "z" else (rel[0] if other == "x" else rel[1]))
        if self.order[level] == "z":
            index = index * 5 + (4 if last is True else (at_z if last is False else jnp.where(last, 4, at_z)))
        return self.base[level] + index

    def take(self, mine, slot):
        there = self.arrived.at[slot]
        pltpu.make_async_copy(there, there, self.recv.at[self.job, slot]).wait()
        mine[...] = mine[...] + self.arrived[slot]

    def steps(self):
        out = []
        present = set()
        z = self.place[2]
        for rel, stage in self.pieces:

            def run(rel=rel, stage=stage):
                if self.ready is not None and rel[1] not in present:
                    present.add(rel[1])
                    self.ready(rel[1])
                mine = self.mine(shifted(self.place, rel))
                offset, sign = self.place.line[rel[2]], self.place.sign[rel[2]]
                for level in range(min(stage + 1, len(self.order))):
                    if self.order[level] == "z":
                        if level < stage:
                            pl.when(z > 0)(lambda: self.take(mine, self.slot(level, rel, False)))
                            pl.when(z < 3)(lambda: self.take(mine, self.slot(level, rel, True)))
                        else:
                            behind = z - sign
                            pl.when(on_line(behind))(lambda: self.take(mine, self.slot(level, rel, False)))
                    elif level < stage:
                        self.take(mine, self.slot(level, rel, False))
                if stage == len(self.order):
                    self.out(mine[...].astype(jnp.float32))
                    return
                axis = self.order[stage]
                if axis == "z":
                    target = (self.place[0], self.place[1], z + sign, self.place[3])
                else:
                    target = step_to(self.place, axis)
                slot = self.slot(stage, rel, offset == -1 if axis == "z" else False)
                pltpu.make_async_remote_copy(
                    src_ref=mine,
                    dst_ref=self.arrived.at[slot],
                    send_sem=self.send.at[self.job],
                    recv_sem=self.recv.at[self.job, slot],
                    device_id=mesh_place(*target),
                    device_id_type=MESH_ID,
                ).start()

            out.append(run)
        return out

    def finish(self):
        wait_bytes(self.amount(len(self.pieces) - 1), self.send.at[self.job])


CAT_JOBS = (("cat", 0, 96, "xzy"), ("cat", 96, 96, "yzx"), ("cat", 192, 96, "zxy"))
FFN_JOBS = (
    ("gate", 0, 144, "xzy"), ("up", 0, 96, "yzx"), ("down", 0, 384, "zxy"),
    ("gate", 144, 144, "xzy"), ("up", 96, 96, "yzx"), ("down", 384, 384, "zxy"), ("up", 192, 96, "zxy"),
)
KV_JOBS = tuple((slot, 256 * third, "xz" if (slot, third) == (1, 2) else "zx") for slot in (0, 1) for third in (0, 1, 2))
FOLD_FFN = tuple(job[:3] + (job[3][::-1],) for job in FFN_JOBS)
FOLD_CAT = tuple(job[:3] + (job[3][::-1],) for job in CAT_JOBS)
FOLD_KV = tuple((slot, row, order[::-1]) for slot, row, order in KV_JOBS)
FFN_NAMES = ("gate", "up", "down")


def job_shape(job):
    return (144, job[2]) if job[0] == "down" else (job[2], 384)


def piece_of(ref, job, paired=False):
    name, first, count, _ = job
    double = 2 if paired else 1

    def spot(who):
        x, y, z, c = who
        d, s = mesh_place(0 if paired else x, y, z, c)
        if name == "down":
            return ref.at[
                pl.ds(pl.multiple_of(s * 144, 16), 144 * double), pl.ds(pl.multiple_of(d * 768 + first, 128), count)
            ]
        return ref.at[
            pl.ds(pl.multiple_of(d * 288 + first, 8), count), pl.ds(pl.multiple_of(s * 384, 128), 384 * double)
        ]

    return spot


def region(ref, elements, rows, columns):
    units = elements // 2048
    wide = max(k for k in range(1, columns // 128 + 1) if units % k == 0 and units // k <= rows // 16)
    return ref.at[pl.ds(0, units // wide * 16), pl.ds(0, wide * 128)]


def amount_of(ref, job):
    rows, columns = job_shape(job)
    return lambda pieces: region(ref, pieces * rows * columns, 1152, 3072)


def own_part(ref, job):
    name, first, count, _ = job
    return ref.at[:, pl.ds(first, count)] if name == "down" else ref.at[pl.ds(first, count), :]


def kv_spot(ref, slot, row):
    def spot(who):
        _, s = mesh_place(*who)
        return ref.at[slot, pl.ds(row, 256), pl.ds(pl.multiple_of(s * 128, 128), 128)]

    return spot


def kv_amount(ref):
    return lambda pieces: ref.at[0, pl.ds(0, 32 * pieces), :]


def make_spreads(place, jobs, shards, wholes, sems):
    return [
        Spread(
            place, job[3], own_part(shards[job[0]], job), piece_of(wholes[job[0]], job), sems, j,
            piece_of(wholes[job[0]], job, True), amount_of(wholes[job[0]], job),
        )
        for j, job in enumerate(jobs)
    ]


def make_kv_spreads(place, own, whole, sems):
    return [
        Spread(
            place, order, own.at[pl.ds(row, 256), pl.ds(slot * 128, 128)], kv_spot(whole, slot, row),
            (sems[0], sems[1], None, None), j, None, kv_amount(whole),
        )
        for j, (slot, row, order) in enumerate(KV_JOBS)
    ]


def spread_sems(jobs):
    n = len(jobs)
    return [
        pltpu.SemaphoreType.DMA((n, 16)), pltpu.SemaphoreType.DMA((n,)),
        pltpu.SemaphoreType.DMA((n,)), pltpu.SemaphoreType.DMA((n,)),
    ]


def fold_scratch(jobs):
    n = len(jobs)
    most = max(fold_slots(job[3])[1] for job in jobs)
    scratch = [
        pltpu.SemaphoreType.DMA((n,)), pltpu.SemaphoreType.DMA((n, most)),
        pltpu.SemaphoreType.DMA((n, 2)), pltpu.SemaphoreType.DMA((n, 2)), pltpu.SemaphoreType.DMA((n, 2)),
    ]
    for job in jobs:
        rows, columns = job_shape(job)
        block = (2, 1152, columns) if job[0] == "down" else (2, rows, 3072)
        scratch += [
            pltpu.VMEM(block, jnp.bfloat16), pltpu.VMEM(block, jnp.bfloat16),
            pltpu.VMEM((fold_slots(job[3])[1], rows, columns), jnp.bfloat16),
        ]
    return scratch


class JobFold:
    def __init__(self, place, job, j, sums, owned, scratch):
        self.place, self.job, self.j, self.sums = place, job, j, sums
        send, recv, self.load_sem, self.core_send, self.core_recv = scratch[:5]
        self.acc, self.other, arrived = scratch[5 + 3 * j: 8 + 3 * j]
        name, first, count, order = job

        def mine(who):
            x, y, z, c = who
            s = 2 * z + x
            if name == "down":
                return self.acc.at[y, pl.ds(pl.multiple_of(s * 144, 16), 144), :]
            return self.acc.at[y, :, pl.ds(pl.multiple_of(s * 384, 128), 384)]

        def out(value):
            if name == "down":
                owned[:, first: first + count] = value
            else:
                owned[first: first + count, :] = value

        self.fold = Fold(place, order, mine, arrived, (send, recv), j, out, amount_of(sums, job), self.ready)

    def block(self, y, c):
        name, first, count, _ = self.job
        d = 2 * y + c
        if name == "down":
            return self.sums.at[:, pl.ds(pl.multiple_of(d * 768 + first, 128), count)]
        return self.sums.at[pl.ds(pl.multiple_of(d * 288 + first, 8), count), :]

    def local_copy(self, dy):
        x, y, z, c = self.place
        at = (1 - y) if dy else y
        return pltpu.make_async_copy(self.block(at, c), self.acc.at[at], self.load_sem.at[self.j, dy])

    def core_copy(self, dy):
        x, y, z, c = self.place
        at = (1 - y) if dy else y
        return pltpu.make_async_remote_copy(
            src_ref=self.block(at, 1 - c),
            dst_ref=self.other.at[at],
            send_sem=self.core_send.at[self.j, dy],
            recv_sem=self.core_recv.at[self.j, dy],
            device_id=mesh_place(x, y, z, 1 - c),
            device_id_type=MESH_ID,
        )

    def begin(self, dy):
        self.core_copy(dy).start()
        self.local_copy(dy).start()

    def ready(self, dy):
        y = self.place[1]
        at = (1 - y) if dy else y
        self.local_copy(dy).wait()
        self.core_copy(dy).wait_recv()

        def add(k, _):
            if self.job[0] == "down":
                part = (at, pl.ds(pl.multiple_of(k * 144, 16), 144), slice(None))
            else:
                part = (at, slice(None), pl.ds(pl.multiple_of(k * 384, 128), 384))
            self.acc[part] = self.acc[part] + self.other[part]
            return _

        lax.fori_loop(0, 8, add, 0)

    def finish(self):
        self.fold.finish()
        for dy in (0, 1):
            self.core_copy(dy).wait_send()


class Notes:
    def __init__(self, place, tile_of, own, by_seq, by_dp, sems):
        self.d, self.s = mesh_place(*place)
        self.tile_of, self.own, self.by_seq, self.by_dp = tile_of, own, by_seq, by_dp
        self.seq_send, self.seq_recv, self.dp_send, self.dp_recv = sems

    def along_seq(self, k):
        peer = lax.rem(self.s + k, 8)
        return pltpu.make_async_remote_copy(
            src_ref=self.tile_of(peer), dst_ref=self.by_seq.at[self.s], send_sem=self.seq_send.at[k],
            recv_sem=self.seq_recv.at[self.s], device_id=(self.d, peer), device_id_type=MESH_ID,
        )

    def along_dp(self, k):
        peer = lax.rem(self.d + k, 4)
        return pltpu.make_async_remote_copy(
            src_ref=self.own, dst_ref=self.by_dp.at[self.d], send_sem=self.dp_send.at[k],
            recv_sem=self.dp_recv.at[self.d], device_id=(peer, self.s), device_id_type=MESH_ID,
        )

    def wait_seq(self):
        for k in range(1, 8):
            peer = lax.rem(self.s + k, 8)
            there = self.by_seq.at[peer]
            pltpu.make_async_copy(there, there, self.seq_recv.at[peer]).wait()

    def wait_dp(self):
        for k in range(1, 4):
            peer = lax.rem(self.d + k, 4)
            there = self.by_dp.at[peer]
            pltpu.make_async_copy(there, there, self.dp_recv.at[peer]).wait()


NOTE_SEMS = [
    pltpu.SemaphoreType.DMA((8,)), pltpu.SemaphoreType.DMA((8,)),
    pltpu.SemaphoreType.DMA((4,)), pltpu.SemaphoreType.DMA((4,)),
]


FORWARD_PLAN = (
    (100, 200, 0,),
    (101, 102, 108, 204, 208, 1, 2, 8, 201, 109, 104, 202, 4, 103, 3, 110, 205, 105, 209, 10, 5, 206, 212,
        203, 9, 210, 111, 112, 106, 6, 11, 207, 107, 12,),
    (7, 211, 10400, 10100, 10200, 10300, 10600, 10000, 10500, 213, 113, 214, 114, 13, 115, 215, 14, 15,),
    (20000, 20100, 20200, 20300, 20400, 20500,),
    (20001, 20004, 20101, 20201, 20104, 20204, 10002, 10001, 20304, 20301, 20401, 20404, 20002, 20502, 10102,
        20501, 10101, 10201, 10008, 10108, 10204, 10402, 20005, 20102, 10302, 10301, 10401, 20202, 10208,
        10408, 20302, 10501, 10308, 20105, 10601, 20402, 10504, 20205, 10604, 10508, 20305, 10608, 20504,
        10010, 20405, 10004, 20503, 10202, 20006, 10104, 10009, 20003, 10310, 10110, 10304, 10209, 10003,
        10212, 10404, 20505, 20106, 10502, 20103, 10103, 10410, 10602, 10309, 20406, 20206, 10205, 10109,
        20203, 20306, 20303, 10509, 10303, 10512, 20403, 10210, 10403, 10609, 10409, 10612, 10505, 10005,
        10605, 10012, 10510, 20007, 20506, 10011, 10105, 10610, 10305, 20207, 10203, 10405, 20107, 10213,
        10112, 10206, 10312, 10111, 10412, 10311, 20307, 20507, 10513, 10506, 20407,),
    (
        (0, (10411, 10613, 10606, 10503,)),
        (1, (10013, 10006,)),
        (2, (10603, 10211, 10113,)),
        (3, (10106,)),
        (4, (10413, 10313,)),
        (5, (10306, 10406,)),
        (6, (10207, 10511, 10214,)),
        (8, (10007,)),
        (9, (10107, 10514,)),
        (10, (10607, 10507, 10307, 10114,)),
        (11, (10407, 10614, 10414,)),
    ),
    (10014, 10215, 10314, 10515, 10611, 10115, 10615, 10415, 10015, 10315,),
)
BACKWARD_PLAN = (
    (10000,),
    (
        (1, (10300, 10302,)),
        (2, (10400,)),
        (3, (10600, 10200,)),
        (7, (10401, 10100,)),
        (8, (10001,)),
        (9, (10501, 10601,)),
        (11, (10101, 10002,)),
    ),
    (20500, 20000, 20100, 20200, 20300, 20400, 20502, 20504, 20001, 20101, 20201, 20301, 20401, 20002, 20102,
        20202, 20302, 20402, 20303, 20501, 20503, 10602, 20103, 20203, 20403, 10201, 10500, 10502, 10603,
        10301, 20505, 20506, 10303, 20104, 10403, 20003, 20004, 20204, 10202, 10203, 10004, 10304, 10503,
        10504, 10003, 10604, 20404, 20304, 10204, 10102, 10005, 10305, 10405, 10605, 20005, 10306, 10007,
        10205, 10103, 10402, 10404, 10006, 10406, 10506, 10008, 10505, 20105, 10606, 10104, 20205, 20006,
        10206, 20106, 10307, 10407, 10507, 10308, 10408, 10508, 10509, 10607, 10608, 10609, 20305, 20206,
        10207, 10208, 10209, 20405, 20306, 20507, 10409, 10105, 10009, 20406, 10106, 20007, 10410, 20107,
        10107, 10108, 10010, 10309, 10110, 20207, 10510, 10210, 10109, 10411, 10610, 10310, 20407, 10012,
        20307,),
    (10312, 10412, 10311, 10111, 10011, 10013, 10413, 10511, 10211, 10611, 10313, 10112, 10113, 10014, 10512,
        10612, 10212, 10414, 10314, 10513, 10514, 10213, 10613, 10214, 10614, 10114, 10315, 10415, 10515,
        10015, 10115, 10215, 10615,),
)
LAST_PLAN = (
    (10000, 10100, 10200, 10001, 10101, 10102, 10201, 10002, 10202, 10103, 10003, 10203, 10104, 10106, 10004, 10006,),
    (10204, 10206, 10105, 10107, 10108, 10109, 10110, 10005,),
    (10007, 10008, 10009, 10010, 10205, 10207, 10208, 10209, 10111, 10011, 10112, 10012, 10113, 10210, 10211,
        10212, 10013, 10014, 10114, 10213, 10214, 10015, 10115, 10215,),
)


def dot(a, b):
    return jnp.dot(a, b, preferred_element_type=jnp.float32)


def dot_t(a, b):
    return lax.dot_general(a, b, (((1,), (1,)), ((), ())), preferred_element_type=jnp.float32)


def t_dot(a, b):
    return lax.dot_general(a, b, (((0,), (0,)), ((), ())), preferred_element_type=jnp.float32)


def repeat(count, body):
    def step(k, nothing):
        body(k)
        return nothing

    lax.fori_loop(0, count, step, 0)


def rows_at(k, size, base=0):
    return pl.ds(pl.multiple_of(base + k * size, 16), size)


def lanes_at(k, size, base=0):
    return pl.ds(pl.multiple_of(base + k * size, 128), size)


def rotate(u, cosine, sine):
    front, back = u[:32], u[32:]
    return jnp.concatenate([front * cosine - back * sine, front * sine + back * cosine], axis=0)


def probabilities(keys, query, limit, chunk):
    scores = t_dot(keys, query) * (HEAD_DIMENSION ** (-0.5))
    key_pos = chunk * 256 + lax.broadcasted_iota(jnp.int32, (256, 384), 0)
    return jnp.where(key_pos <= limit, jnp.exp(scores), 0.0)


def heads_wide(ref, group, lanes):
    return jnp.concatenate(
        [ref[pl.ds(pl.multiple_of(group * 192 + 64 * i, 64), 64), lanes] for i in range(3)], axis=1
    )


def three_wide(row):
    return jnp.concatenate([row] * 3, axis=1)


def forward_body(
    cat, note, x, cosine, sine, limit, gate, up, down,
    gate_w, up_w, down_w, wcat, notes, attn_in_t, hidden, query, keys_values, attn, denom,
    attn_in, raw, own_kv, weights, proj, seq_in, dp_in, own_sems, note_a, note_b, note_c, note_d, *sems
):
    place = position()
    d, s = mesh_place(*place)
    greet(place, True)
    shards = dict(zip(FFN_NAMES, (gate, up, down)))
    wholes = dict(zip(FFN_NAMES, (gate_w, up_w, down_w)))
    cat_spreads = make_spreads(place, CAT_JOBS, {"cat": cat}, {"cat": weights}, sems[:4])
    ffn_spreads = make_spreads(place, FFN_JOBS, shards, wholes, sems[4:8])
    kv_spreads = make_kv_spreads(place, own_kv, keys_values, sems[8:10])
    steps = [[spread.steps() for spread in family] for family in (cat_spreads, ffn_spreads, kv_spreads)]

    def run(tokens):
        for token in tokens:
            steps[token // 10000][token // 100 % 100][token % 100]()

    tiles = Notes(place, lambda peer: note, note, seq_in, dp_in, (note_a, note_b, note_c, note_d))
    run(FORWARD_PLAN[0])
    for k in range(1, 8):
        tiles.along_seq(k).start()
    for k in range(1, 4):
        tiles.along_dp(k).start()
    own = [
        pltpu.make_async_copy(
            shards[name], piece_of(wholes[name], (name, 0, 768 if name == "down" else 288, ""))(place), own_sems.at[k]
        )
        for k, name in enumerate(FFN_NAMES)
    ]
    for copy in own:
        copy.start()
    weights[rows_at(d, 288), lanes_at(s, 384)] = cat[...]
    for copy in own:
        copy.wait()
    run(FORWARD_PLAN[1])
    tiles.wait_seq()
    tiles.wait_dp()
    seq_in[s] = note[...]
    dp_in[d] = note[...]
    gains = seq_in[0]
    for k in range(1, 8):
        gains = gains + seq_in[k]
    notes[0:8, :] = gains
    notes[8:16, :] = dp_in[0] + dp_in[1] + dp_in[2] + dp_in[3]

    def norm(k):
        rows = rows_at(k, 32)
        part = x[rows, :].astype(jnp.float32)
        scale = lax.rsqrt(jnp.mean(part * part, axis=-1, keepdims=True) + norm_eps)
        attn_in[rows, :] = (part * scale * notes[0:1, :]).astype(jnp.bfloat16)

    repeat(8, norm)
    attn_in_t[...] = attn_in[...].T
    run(FORWARD_PLAN[2])
    for spread in cat_spreads:
        spread.wait_core()

    def project(b):
        block = dot(attn_in[...], weights[:, lanes_at(b, 384)][:, :256]).T
        raw[rows_at(b, 144), :] = block[:144]
        raw[rows_at(b, 48, 1152), :] = block[144:192]
        raw[rows_at(b, 48, 1536), :] = block[192:240]

    repeat(8, project)
    out_copy = pltpu.make_async_copy(weights, wcat, own_sems.at[3])
    out_copy.start()

    def turn(ref, rows_of):
        def one(h):
            ref[rows_at(h, 64), :] = rotate(raw[rows_of(h), :], cosine[...], sine[...]).astype(jnp.bfloat16)

        return one

    repeat(6, turn(own_kv, lambda h: rows_at(h, 64, 1152)))
    own_kv[384:768, :] = raw[1536:1920, :].astype(jnp.bfloat16)
    repeat(18, turn(query, lambda h: rows_at(h, 64)))
    run(FORWARD_PLAN[3])
    here = lanes_at(s, 128)
    for slot in range(2):
        keys_values[slot, :, here] = own_kv[:, slot * 128: slot * 128 + 128]
    run(FORWARD_PLAN[4])

    def attend(slot, group):
        lanes = lanes_at(slot, 128)
        bound = three_wide(limit[:, lanes])
        wide = heads_wide(query, group, lanes)

        def one_chunk(chunk, carry):
            total, numer = carry
            cols = lanes_at(chunk, 256)
            expo = probabilities(keys_values[slot, rows_at(group, 64), cols], wide, bound, chunk)
            total = total + jnp.sum(expo, axis=0, keepdims=True)
            numer = numer + dot(keys_values[slot, rows_at(group, 64, 384), cols], expo.astype(jnp.bfloat16))
            return (total, numer)

        total, numer = lax.fori_loop(
            0, 4, one_chunk, (jnp.zeros((1, 384), jnp.float32), jnp.zeros((64, 384), jnp.float32))
        )
        mean = numer / total
        for i in range(3):
            attn[pl.ds(pl.multiple_of(group * 192 + 64 * i, 64), 64), lanes] = mean[:, i * 128: i * 128 + 128]
        denom[group, 0:3, lanes] = jnp.concatenate([total[:, i * 128: i * 128 + 128] for i in range(3)], axis=0)

    def unit(k):
        attend(k // 6, lax.rem(k, 6))
        for at, tokens in FORWARD_PLAN[5]:
            pl.when(k == at)(lambda tokens=tokens: run(tokens))

    repeat(12, unit)

    def out_project(b):
        block = t_dot(attn[...].astype(jnp.bfloat16), weights[:, lanes_at(b, 384)][:, 128:]).T
        proj[rows_at(b, 144), :] = block[112:256]

    repeat(8, out_project)
    hidden[...] = x[...].astype(jnp.float32) + proj[...].T
    run(FORWARD_PLAN[6])
    for spread in cat_spreads + ffn_spreads + kv_spreads:
        spread.finish()
    for spread in ffn_spreads:
        spread.wait_core()
    for k in range(1, 8):
        tiles.along_seq(k).wait_send()
    for k in range(1, 4):
        tiles.along_dp(k).wait_send()
    out_copy.wait()


def forward_call(cat, note, x, cosine, sine, limit, gate, up, down):
    vmem, anywhere = pl.BlockSpec(memory_space=pltpu.VMEM), pl.BlockSpec(memory_space=pl.ANY)
    return pl.pallas_call(
        forward_body,
        out_shape=[jax.ShapeDtypeStruct((1152, 3072), jnp.bfloat16)] * 4
        + [
            jax.ShapeDtypeStruct((16, 1152), jnp.float32),
            jax.ShapeDtypeStruct((1152, 256), jnp.bfloat16),
            jax.ShapeDtypeStruct((256, 1152), jnp.float32),
            jax.ShapeDtypeStruct((1152, 256), jnp.bfloat16),
            jax.ShapeDtypeStruct((2, 768, 1024), jnp.bfloat16),
            jax.ShapeDtypeStruct((1152, 256), jnp.float32),
            jax.ShapeDtypeStruct((6, 8, 256), jnp.float32),
        ],
        in_specs=[vmem] * 9,
        out_specs=[anywhere] * 4 + [vmem] * 7,
        scratch_shapes=[
            pltpu.VMEM((256, 1152), jnp.bfloat16),
            pltpu.VMEM((1920, 256), jnp.float32),
            pltpu.VMEM((768, 256), jnp.bfloat16),
            pltpu.VMEM((1152, 3072), jnp.bfloat16),
            pltpu.VMEM((1152, 256), jnp.float32),
            pltpu.VMEM((8, 8, 1152), jnp.float32),
            pltpu.VMEM((4, 8, 1152), jnp.float32),
            pltpu.SemaphoreType.DMA((4,)),
        ]
        + NOTE_SEMS
        + spread_sems(CAT_JOBS)
        + spread_sems(FFN_JOBS)
        + spread_sems(KV_JOBS)[:2],
        compiler_params=pltpu.CompilerParams(
            collective_id=3, has_side_effects=True, vmem_limit_bytes=48 * 1024 * 1024
        ),
        name="attention_forward",
    )(cat, note, x, cosine, sine, limit, gate, up, down)


def backward_body(
    grad_hidden, attn_in_t, wcat, keys_values, query, attn, denom, cosine, sine, limit, grad_gate, grad_up, grad_down,
    own_gate, own_up, own_down, grad_attn_in, grad_cat,
    weights, whole_kv, part_kv, turned, total, own_kv, left, grad_t,
    load, store, kv_send, kv_recv, kv_arrived, *scratch
):
    place = position()
    greet(place, False)
    sums = dict(zip(FFN_NAMES, (grad_gate, grad_up, grad_down)))
    owned = dict(zip(FFN_NAMES, (own_gate, own_up, own_down)))
    folds = [
        JobFold(place, job, j, sums[job[0]], owned[job[0]], scratch) for j, job in enumerate(FOLD_FFN)
    ]

    def kv_fold(j, slot, row, order):
        def out(value):
            own_kv[row: row + 256, slot * 128: slot * 128 + 128] = value

        spot = kv_spot(part_kv, slot, row)
        return Fold(place, order, lambda who: spot(who), kv_arrived.at[j], (kv_send, kv_recv), j, out, kv_amount(part_kv))

    kv_folds = [kv_fold(j, *job) for j, job in enumerate(FOLD_KV)]
    steps = [[], [fold.fold.steps() for fold in folds], [fold.steps() for fold in kv_folds]]

    def run(tokens):
        for token in tokens:
            steps[token // 10000][token // 100 % 100][token % 100]()

    for dy in (1, 0):
        for fold in folds:
            fold.begin(dy)

    def block_load(b):
        return pltpu.make_async_copy(wcat.at[:, lanes_at(b, 384)], weights.at[:, lanes_at(b, 384)], load.at[b])

    repeat(8, lambda b: block_load(b).start())
    kv_in = pltpu.make_async_copy(keys_values, whole_kv, load.at[8])
    kv_in.start()
    grad_t[...] = grad_hidden[...].T.astype(jnp.bfloat16)
    total[...] = jnp.zeros_like(total)

    def out_rows(b):
        return jnp.concatenate([jnp.zeros((112, 256), jnp.bfloat16), grad_t[rows_at(b, 144), :]], axis=0)

    def out_back(b):
        block_load(b).wait()
        total[...] += dot(weights[:, lanes_at(b, 384)][:, 128:], out_rows(b))

    repeat(8, out_back)
    run(BACKWARD_PLAN[0])
    kv_in.wait()
    scale = HEAD_DIMENSION ** (-0.5)

    def attend_back(slot, group):
        lanes = lanes_at(slot, 128)
        bound = three_wide(limit[:, lanes])
        wide = heads_wide(query, group, lanes)
        grads, ratios = [], []
        for i in range(3):
            rows = pl.ds(pl.multiple_of(group * 192 + 64 * i, 64), 64)
            grad = total[rows, lanes].astype(jnp.bfloat16).astype(jnp.float32)
            bottom = denom[group, i: i + 1, lanes]
            ratios.append(jnp.sum(grad * attn[rows, lanes], axis=0, keepdims=True) / bottom)
            grads.append((grad / bottom).astype(jnp.bfloat16))
        grads, ratios = jnp.concatenate(grads, axis=1), jnp.concatenate(ratios, axis=1)

        def one_chunk(chunk, sum_query):
            cols = lanes_at(chunk, 256)
            keys = whole_kv[slot, rows_at(group, 64), cols]
            values = whole_kv[slot, rows_at(group, 64, 384), cols]
            expo = probabilities(keys, wide, bound, chunk)
            grad_prob = t_dot(values, grads)
            grad_score = (expo * (grad_prob - ratios)).astype(jnp.bfloat16)
            part_kv[slot, rows_at(group, 64), cols] = (dot_t(wide, grad_score) * scale).astype(jnp.bfloat16)
            part_kv[slot, rows_at(group, 64, 384), cols] = dot_t(grads, expo.astype(jnp.bfloat16)).astype(jnp.bfloat16)
            return sum_query + dot(keys, grad_score)

        sum_query = lax.fori_loop(0, 4, one_chunk, jnp.zeros((64, 384), jnp.float32)) * scale
        for i in range(3):
            total[pl.ds(pl.multiple_of(group * 192 + 64 * i, 64), 64), lanes] = sum_query[:, i * 128: i * 128 + 128]

    def unit(k):
        attend_back(k // 6, lax.rem(k, 6))
        for at, tokens in BACKWARD_PLAN[1]:
            pl.when(k == at)(lambda tokens=tokens: run(tokens))

    repeat(12, unit)
    run(BACKWARD_PLAN[2])

    def turn_back(ref, source, count):
        def one(h):
            rows = rows_at(h, 64)
            ref[rows, :] = rotate(source[rows, :], cosine[...], -sine[...]).astype(ref.dtype)

        repeat(count, one)

    turn_back(turned, total, 18)
    turn_back(own_kv, own_kv, 6)
    total[...] = jnp.zeros_like(total)

    def last_block(b):
        rows = jnp.concatenate(
            [
                turned[rows_at(b, 144), :],
                own_kv[rows_at(b, 48), :].astype(jnp.bfloat16),
                own_kv[rows_at(b, 48, 384), :].astype(jnp.bfloat16),
                jnp.zeros((16, 256), jnp.bfloat16),
            ],
            axis=0,
        )
        total[...] += dot(weights[:, lanes_at(b, 384)][:, :256], rows)
        slot = lax.rem(b, 2)
        out = pltpu.make_async_copy(left.at[slot], grad_cat.at[:, lanes_at(b, 384)], store.at[slot])
        pl.when(b >= 2)(lambda: out.wait())
        grad = dot_t(attn_in_t[...], rows)
        out_grad = dot_t(attn[...].astype(jnp.bfloat16), out_rows(b))
        left[slot, :, 0:128] = grad[:, :128].astype(jnp.bfloat16)
        left[slot, :, 128:256] = (grad[:, 128:] + out_grad[:, :128]).astype(jnp.bfloat16)
        left[slot, :, 256:384] = out_grad[:, 128:].astype(jnp.bfloat16)
        out.start()

    repeat(8, last_block)
    grad_attn_in[...] = total[...].T
    run(BACKWARD_PLAN[3])
    for fold in folds + kv_folds:
        fold.finish()
    for slot in range(2):
        pltpu.make_async_copy(left.at[slot], grad_cat.at[:, pl.ds((6 + slot) * 384, 384)], store.at[slot]).wait()


def backward_call(
    grad_hidden, attn_in_t, wcat, keys_values, query, attn, denom, cosine, sine, limit, grad_gate, grad_up, grad_down
):
    vmem, anywhere = pl.BlockSpec(memory_space=pltpu.VMEM), pl.BlockSpec(memory_space=pl.ANY)
    jobs = len(KV_JOBS)
    most = max(fold_slots(order)[1] for _, _, order in FOLD_KV)
    return pl.pallas_call(
        backward_body,
        out_shape=[
            jax.ShapeDtypeStruct((288, 384), jnp.float32),
            jax.ShapeDtypeStruct((288, 384), jnp.float32),
            jax.ShapeDtypeStruct((144, 768), jnp.float32),
            jax.ShapeDtypeStruct((256, 1152), jnp.float32),
            jax.ShapeDtypeStruct((1152, 3072), jnp.bfloat16),
        ],
        in_specs=[vmem, vmem, anywhere, anywhere] + [vmem] * 6 + [anywhere] * 3,
        out_specs=[vmem] * 4 + [anywhere],
        scratch_shapes=[
            pltpu.VMEM((1152, 3072), jnp.bfloat16),
            pltpu.VMEM((2, 768, 1024), jnp.bfloat16),
            pltpu.VMEM((2, 768, 1024), jnp.bfloat16),
            pltpu.VMEM((1152, 256), jnp.bfloat16),
            pltpu.VMEM((1152, 256), jnp.float32),
            pltpu.VMEM((768, 256), jnp.float32),
            pltpu.VMEM((2, 1152, 384), jnp.bfloat16),
            pltpu.VMEM((1152, 256), jnp.bfloat16),
            pltpu.SemaphoreType.DMA((9,)),
            pltpu.SemaphoreType.DMA((2,)),
            pltpu.SemaphoreType.DMA((jobs,)),
            pltpu.SemaphoreType.DMA((jobs, most)),
            pltpu.VMEM((jobs, most, 256, 128), jnp.bfloat16),
        ]
        + fold_scratch(FOLD_FFN),
        compiler_params=pltpu.CompilerParams(
            collective_id=4, has_side_effects=True, vmem_limit_bytes=VMEM_MOST
        ),
        name="attention_backward",
    )(
        grad_hidden, attn_in_t, wcat, keys_values, query, attn, denom, cosine, sine, limit,
        grad_gate, grad_up, grad_down,
    )


def last_body(cat, tiles, owned, totals, seq_in, dp_in, row_sum, note_a, note_b, note_c, note_d, *scratch):
    place = position()
    d, s = mesh_place(*place)
    greet(place, True)
    notes = Notes(place, lambda peer: tiles.at[peer], row_sum, seq_in, dp_in, (note_a, note_b, note_c, note_d))
    folds = [JobFold(place, job, j, cat, owned, scratch) for j, job in enumerate(FOLD_CAT)]
    steps = [fold.fold.steps() for fold in folds]

    def run(tokens):
        for token in tokens:
            steps[token // 100 % 100][token % 100]()

    for dy in (1, 0):
        for fold in folds:
            fold.begin(dy)
    for k in range(1, 8):
        notes.along_seq(k).start()
    run(LAST_PLAN[0])
    notes.wait_seq()
    seq_in[s] = tiles[s]
    total = seq_in[0]
    for k in range(1, 8):
        total = total + seq_in[k]
    row_sum[...] = total
    run(LAST_PLAN[1])
    for k in range(1, 4):
        notes.along_dp(k).start()
    run(LAST_PLAN[2])
    notes.wait_dp()
    dp_in[d] = row_sum[...]
    totals[...] = dp_in[0] + dp_in[1] + dp_in[2] + dp_in[3]
    for fold in folds:
        fold.finish()
    for k in range(1, 8):
        notes.along_seq(k).wait_send()
    for k in range(1, 4):
        notes.along_dp(k).wait_send()


def last_call(cat, tiles):
    vmem = pl.BlockSpec(memory_space=pltpu.VMEM)
    return pl.pallas_call(
        last_body,
        out_shape=[
            jax.ShapeDtypeStruct((288, 384), jnp.float32),
            jax.ShapeDtypeStruct((8, 256), jnp.float32),
        ],
        in_specs=[pl.BlockSpec(memory_space=pl.ANY), vmem],
        out_specs=[vmem, vmem],
        scratch_shapes=[
            pltpu.VMEM((8, 8, 256), jnp.float32), pltpu.VMEM((4, 8, 256), jnp.float32),
            pltpu.VMEM((8, 256), jnp.float32),
        ]
        + NOTE_SEMS
        + fold_scratch(FOLD_CAT),
        compiler_params=pltpu.CompilerParams(
            collective_id=2, has_side_effects=True, vmem_limit_bytes=40 * 1024 * 1024
        ),
        name="fold_attention_gradients",
    )(cat, tiles)


def per_device_fast(
    tokens, teacher, lengths, w_query, key_weight, value_weight, w_out, w_gate, w_up, w_down, gain_attn, gain_ffn
):
    slots, part, width = tokens.shape
    rows = slots * part
    total_tokens = slots * lax.axis_size("dp") * part * lax.axis_size("seq")
    positions = lax.axis_index("seq") * part + jnp.arange(part, dtype=jnp.int32)
    cosine, sine = rope_tables(positions, HEAD_DIMENSION)
    cosine_t = jnp.concatenate([cosine.T] * slots, axis=1)
    sine_t = jnp.concatenate([sine.T] * slots, axis=1)
    limit = jnp.minimum(positions[None, :], lengths[:, None] - 1).reshape(1, rows)
    note = lax.dynamic_update_slice(
        jnp.zeros((8, width), jnp.float32),
        jnp.stack([gain_attn, gain_ffn]).astype(jnp.float32),
        (0, lax.axis_index("seq") * gain_attn.shape[0]),
    )
    note = note.at[2].set(jnp.sum(lengths).astype(jnp.float32))
    x_b = tokens.reshape(rows, width)
    gate_w, up_w, down_t, cat, notes, attn_in_t, hidden, query, keys_values, attn, denom = forward_call(
        jnp.concatenate([w_query, key_weight, value_weight, w_out], axis=1),
        note, x_b, cosine_t, sine_t, limit, w_gate, w_up, w_down.T,
    )
    gain_a, gain_f = notes[0:1], notes[1:2]
    count = notes[10, 0]
    factor = total_tokens / count
    r2 = lax.rsqrt(jnp.mean(hidden * hidden, axis=-1, keepdims=True) + norm_eps)
    n2 = hidden * r2
    ffn_in = (n2 * gain_f).astype(jnp.bfloat16)
    gate = dot(ffn_in, gate_w)
    up = dot(ffn_in, up_w)
    sig = jax.nn.sigmoid(gate)
    hid = (gate * sig * up).astype(jnp.bfloat16)
    valid = (positions[None, :] < lengths[:, None]).reshape(rows, 1)
    out_f = jnp.where(valid, hidden + dot_t(hid, down_t), 0.0)
    diff = jnp.where(valid, out_f - teacher.reshape(rows, width).astype(jnp.float32), 0.0)
    squares = jnp.sum(diff * diff)
    cot = factor * diff
    cot_b = cot.astype(jnp.bfloat16)
    grad_down_t = t_dot(cot_b, hid).astype(jnp.bfloat16)
    grad_hid = dot(cot_b, down_t)
    grad_gate_b = (grad_hid * up * sig * (1.0 + gate * (1.0 - sig))).astype(jnp.bfloat16)
    grad_up_b = (grad_hid * gate * sig).astype(jnp.bfloat16)
    grad_gate_w = t_dot(ffn_in, grad_gate_b).astype(jnp.bfloat16)
    grad_up_w = t_dot(ffn_in, grad_up_b).astype(jnp.bfloat16)
    grad_ffn_in = dot_t(grad_gate_b, gate_w) + dot_t(grad_up_b, up_w)
    part_gain_f = jnp.sum(grad_ffn_in * n2, axis=0)
    gn = grad_ffn_in * gain_f
    grad_hidden = cot + r2 * (gn - n2 * jnp.mean(gn * n2, axis=-1, keepdims=True))
    own_gate, own_up, own_down_t, grad_attn_in, grad_cat = backward_call(
        grad_hidden, attn_in_t, cat, keys_values, query, attn, denom, cosine_t, sine_t, limit,
        grad_gate_w, grad_up_w, grad_down_t,
    )
    x = x_b.astype(jnp.float32)
    r1 = lax.rsqrt(jnp.mean(x * x, axis=-1, keepdims=True) + norm_eps)
    n1 = x * r1
    part_gain_a = jnp.sum(grad_attn_in * n1, axis=0)
    tiles = jnp.zeros((8, 8, 256), jnp.float32)
    tiles = tiles.at[:, 0, :144].set(part_gain_a.reshape(8, 144)).at[:, 1, :144].set(part_gain_f.reshape(8, 144))
    tiles = tiles.at[:, 2, 0].set(squares)
    own_cat, totals = last_call(grad_cat, tiles)
    ga = grad_attn_in * gain_a
    grad_tokens = grad_hidden + r1 * (ga - n1 * jnp.mean(ga * n1, axis=-1, keepdims=True))
    return (
        out_f.astype(jnp.bfloat16).reshape(tokens.shape),
        totals[2, 0] / count,
        grad_tokens.reshape(tokens.shape),
        own_cat[:, :144],
        own_cat[:, 144:192],
        own_cat[:, 192:240],
        own_cat[:, 240:],
        own_gate,
        own_up,
        own_down_t.T,
        totals[0, :144],
        totals[1, :144],
    )


def solution(mesh):
    placed = (
        P("dp", "seq", None),
        P("dp", "seq", None),
        P("dp"),
        P("dp", "seq"),
        P("dp", "seq"),
        P("dp", "seq"),
        P("dp", "seq"),
        P("dp", "seq"),
        P("dp", "seq"),
        P("dp", "seq"),
        P("seq"),
        P("seq"),
    )
    fits = mesh.shape["dp"] == 4 and mesh.shape["seq"] == 8
    return jax.shard_map(
        per_device_fast if fits else per_device,
        mesh=mesh,
        in_specs=placed,
        out_specs=(
            P("dp", "seq", None),
            P(),
            P("dp", "seq", None),
            P("dp", "seq"),
            P("dp", "seq"),
            P("dp", "seq"),
            P("dp", "seq"),
            P("dp", "seq"),
            P("dp", "seq"),
            P("dp", "seq"),
            P("seq"),
            P("seq"),
        ),
        check_vma=False,
    )
```

```python
import math

import jax
import jax.numpy as jnp
from jax import lax
from jax.experimental import pallas as pl
from jax.experimental.pallas import tpu as pltpu
from jax.sharding import PartitionSpec as P

QUERY_HEADS = 18
KEY_VALUE_HEADS = 6
HEAD_DIMENSION = 64


norm_eps = 1e-05
rope_base = 10000.0


def rope_tables(positions, head_width):
    half_width = head_width // 2
    exponents = jnp.arange(half_width, dtype=jnp.float32) * (2.0 / head_width)
    angles = positions.astype(jnp.float32)[:, None] * (rope_base ** (-exponents))[None, :]
    return (jnp.cos(angles), jnp.sin(angles))


def apply_rotary(value_rows, cosine_table, sine_table):
    half_width = value_rows.shape[-1] // 2
    front_half = value_rows[..., :half_width]
    back_half = value_rows[..., half_width:]
    cos_wide = cosine_table[:, None, :]
    sin_wide = sine_table[:, None, :]
    return jnp.concatenate(
        [
            front_half * cos_wide - back_half * sin_wide,
            front_half * sin_wide + back_half * cos_wide,
        ],
        axis=-1,
    )


def allowed_mask(query_pos, key_pos, live_len):
    causal = key_pos[None, :] <= query_pos[:, None]
    present = key_pos[None, :] < live_len[:, None]
    return (causal[None, :, :] & present[:, None, :])[:, None, None, :, :]


def over_blocks(piece_len, unit_len, step_fn, running):
    block_length = math.gcd(piece_len, unit_len * max(1, 512 // unit_len))
    number_of_blocks = piece_len // block_length

    def loop_step(block_number, state):
        return step_fn(state, block_number * block_length, block_length)

    return lax.fori_loop(0, number_of_blocks, loop_step, running)


def collect(shards):
    wide = (
        lax.all_gather(shards[0], "seq", axis=1, tiled=True),
        lax.all_gather(shards[1], "seq", axis=1, tiled=True),
        lax.all_gather(shards[2], "seq", axis=1, tiled=True),
        lax.all_gather(shards[3], "seq", axis=1, tiled=True),
        lax.all_gather(shards[4], "seq", axis=1, tiled=True),
        lax.all_gather(shards[5], "seq", axis=1, tiled=True),
        lax.all_gather(shards[6], "seq", axis=1, tiled=True),
        lax.all_gather(shards[7], "seq", axis=0, tiled=True),
        lax.all_gather(shards[8], "seq", axis=0, tiled=True),
    )
    whole = (
        lax.all_gather(wide[0], "dp", axis=0, tiled=True),
        lax.all_gather(wide[1], "dp", axis=0, tiled=True),
        lax.all_gather(wide[2], "dp", axis=0, tiled=True),
        lax.all_gather(wide[3], "dp", axis=0, tiled=True),
        lax.all_gather(wide[4], "dp", axis=0, tiled=True),
        lax.all_gather(wide[5], "dp", axis=0, tiled=True),
        lax.all_gather(wide[6], "dp", axis=0, tiled=True),
    )
    return tuple(whole) + (wide[7], wide[8])


def reduce_grads(grad_sums):
    summed = (
        lax.psum_scatter(grad_sums[0], "seq", scatter_dimension=1, tiled=True),
        lax.psum_scatter(grad_sums[1], "seq", scatter_dimension=1, tiled=True),
        lax.psum_scatter(grad_sums[2], "seq", scatter_dimension=1, tiled=True),
        lax.psum_scatter(grad_sums[3], "seq", scatter_dimension=1, tiled=True),
        lax.psum_scatter(grad_sums[4], "seq", scatter_dimension=1, tiled=True),
        lax.psum_scatter(grad_sums[5], "seq", scatter_dimension=1, tiled=True),
        lax.psum_scatter(grad_sums[6], "seq", scatter_dimension=1, tiled=True),
        lax.psum_scatter(grad_sums[7], "seq", scatter_dimension=0, tiled=True),
        lax.psum_scatter(grad_sums[8], "seq", scatter_dimension=0, tiled=True),
    )
    owned = (
        lax.psum_scatter(summed[0], "dp", scatter_dimension=0, tiled=True),
        lax.psum_scatter(summed[1], "dp", scatter_dimension=0, tiled=True),
        lax.psum_scatter(summed[2], "dp", scatter_dimension=0, tiled=True),
        lax.psum_scatter(summed[3], "dp", scatter_dimension=0, tiled=True),
        lax.psum_scatter(summed[4], "dp", scatter_dimension=0, tiled=True),
        lax.psum_scatter(summed[5], "dp", scatter_dimension=0, tiled=True),
        lax.psum_scatter(summed[6], "dp", scatter_dimension=0, tiled=True),
    )
    return (tuple(owned), summed[7], summed[8])


def forward_slot(weights, tok_part, live_len, query_pos, cosine_table, sine_table):
    (
        full_query,
        full_key,
        full_value,
        full_out,
        full_gate,
        full_up,
        full_down,
        full_gain_attn,
        full_gain_ffn,
    ) = weights
    slot_position, stretched_length, model_width = tok_part.shape
    number_of_rows = slot_position * stretched_length
    query_group = QUERY_HEADS // KEY_VALUE_HEADS
    scale = HEAD_DIMENSION ** (-0.5)
    tok_float = tok_part.astype(jnp.float32).reshape(number_of_rows, model_width)
    inv_first = lax.rsqrt(jnp.mean(tok_float * tok_float, axis=-1, keepdims=True) + norm_eps)
    normed_first = tok_float * inv_first
    attention_input = (normed_first * full_gain_attn.astype(jnp.float32)).astype(jnp.bfloat16)
    unrotated_query = jnp.dot(
        attention_input, full_query, preferred_element_type=jnp.float32
    ).reshape(slot_position, stretched_length, QUERY_HEADS, HEAD_DIMENSION)
    unrotated_key = jnp.dot(attention_input, full_key, preferred_element_type=jnp.float32).reshape(
        slot_position, stretched_length, KEY_VALUE_HEADS, HEAD_DIMENSION
    )
    value_block = (
        jnp.dot(attention_input, full_value, preferred_element_type=jnp.float32)
        .astype(jnp.bfloat16)
        .reshape(slot_position, stretched_length, KEY_VALUE_HEADS * HEAD_DIMENSION)
    )
    query_b = (
        apply_rotary(unrotated_query, cosine_table, sine_table)
        .astype(jnp.bfloat16)
        .reshape(slot_position, stretched_length, KEY_VALUE_HEADS, query_group, HEAD_DIMENSION)
    )
    key_block = (
        apply_rotary(unrotated_key, cosine_table, sine_table)
        .astype(jnp.bfloat16)
        .reshape(slot_position, stretched_length, KEY_VALUE_HEADS * HEAD_DIMENSION)
    )
    empty_denominator = jnp.zeros(
        (slot_position, KEY_VALUE_HEADS, query_group, stretched_length), jnp.float32
    )
    empty_numerator = jnp.zeros(
        (slot_position, KEY_VALUE_HEADS, query_group, stretched_length, HEAD_DIMENSION), jnp.float32
    )
    key_piece = lax.all_gather(key_block, "seq", axis=1, tiled=True)
    value_piece = lax.all_gather(value_block, "seq", axis=1, tiled=True)

    def one_block(partial_value, offset, block_length):
        denominator, numerator = partial_value
        key_blk = lax.dynamic_slice_in_dim(key_piece, offset, block_length, 1).reshape(
            slot_position, block_length, KEY_VALUE_HEADS, HEAD_DIMENSION
        )
        value_blk = lax.dynamic_slice_in_dim(value_piece, offset, block_length, 1).reshape(
            slot_position, block_length, KEY_VALUE_HEADS, HEAD_DIMENSION
        )
        allowed = allowed_mask(
            query_pos, offset + jnp.arange(block_length, dtype=jnp.int32), live_len
        )
        scores = (
            jnp.einsum("schgd,snhd->shgcn", query_b, key_blk, preferred_element_type=jnp.float32)
            * scale
        )
        exp_scores = jnp.where(allowed, jnp.exp(scores), 0.0)
        denominator = denominator + jnp.sum(exp_scores, axis=-1)
        numerator = numerator + jnp.einsum(
            "shgcn,snhd->shgcd",
            exp_scores.astype(jnp.bfloat16),
            value_blk,
            preferred_element_type=jnp.float32,
        )
        return (denominator, numerator)

    denominator, numerator = over_blocks(
        key_piece.shape[1], stretched_length, one_block, (empty_denominator, empty_numerator)
    )
    attn_float = jnp.transpose(numerator / denominator[..., None], (0, 3, 1, 2, 4)).reshape(
        number_of_rows, QUERY_HEADS * HEAD_DIMENSION
    )
    attn_b = attn_float.astype(jnp.bfloat16)
    hidden = tok_float + jnp.dot(attn_b, full_out, preferred_element_type=jnp.float32)
    inv_second = lax.rsqrt(jnp.mean(hidden * hidden, axis=-1, keepdims=True) + norm_eps)
    normed_second = hidden * inv_second
    ffn_in = (normed_second * full_gain_ffn.astype(jnp.float32)).astype(jnp.bfloat16)
    gate_proj = jnp.dot(ffn_in, full_gate, preferred_element_type=jnp.float32)
    up_proj = jnp.dot(ffn_in, full_up, preferred_element_type=jnp.float32)
    hid_b = (jax.nn.silu(gate_proj) * up_proj).astype(jnp.bfloat16)
    valid_rows = (query_pos[None, :] < live_len[:, None]).reshape(number_of_rows, 1)
    out_float = jnp.where(
        valid_rows, hidden + jnp.dot(hid_b, full_down, preferred_element_type=jnp.float32), 0.0
    )
    saved = (
        attention_input,
        inv_first,
        normed_first,
        query_b,
        key_block,
        value_block,
        attn_float,
        attn_b,
        denominator,
        normed_second,
        inv_second,
        ffn_in,
        gate_proj,
        up_proj,
        hid_b,
    )
    return (out_float, valid_rows, saved)


def backward_slot(weights, saved, cotangent, live_len, query_pos, cosine_table, sine_table):
    (
        full_query,
        full_key,
        full_value,
        full_out,
        full_gate,
        full_up,
        full_down,
        full_gain_attn,
        full_gain_ffn,
    ) = weights
    (
        attention_input,
        inv_first,
        normed_first,
        query_b,
        key_block,
        value_block,
        attn_float,
        attn_b,
        denominator,
        normed_second,
        inv_second,
        ffn_in,
        gate_proj,
        up_proj,
        hid_b,
    ) = saved
    slot_position = query_b.shape[0]
    stretched_length = query_b.shape[1]
    number_of_rows = slot_position * stretched_length
    query_group = QUERY_HEADS // KEY_VALUE_HEADS
    scale = HEAD_DIMENSION ** (-0.5)
    cot_b = cotangent.astype(jnp.bfloat16)
    grad_down = jnp.einsum("rf,rd->fd", hid_b, cot_b, preferred_element_type=jnp.float32)
    grad_hid = jnp.einsum("rd,fd->rf", cot_b, full_down, preferred_element_type=jnp.float32)
    sigmoid_gate = jax.nn.sigmoid(gate_proj)
    grad_gate_b = (
        grad_hid * up_proj * sigmoid_gate * (1.0 + gate_proj * (1.0 - sigmoid_gate))
    ).astype(jnp.bfloat16)
    grad_up_b = (grad_hid * gate_proj * sigmoid_gate).astype(jnp.bfloat16)
    grad_gate = jnp.einsum("rd,rf->df", ffn_in, grad_gate_b, preferred_element_type=jnp.float32)
    grad_up = jnp.einsum("rd,rf->df", ffn_in, grad_up_b, preferred_element_type=jnp.float32)
    grad_ffn_in = jnp.einsum(
        "rf,df->rd", grad_gate_b, full_gate, preferred_element_type=jnp.float32
    ) + jnp.einsum("rf,df->rd", grad_up_b, full_up, preferred_element_type=jnp.float32)
    grad_gain_ffn = jnp.sum(grad_ffn_in * normed_second, axis=0)
    grad_normed = grad_ffn_in * full_gain_ffn.astype(jnp.float32)
    grad_hidden = cotangent + inv_second * (
        grad_normed - normed_second * jnp.mean(grad_normed * normed_second, axis=-1, keepdims=True)
    )
    grad_proj_b = grad_hidden.astype(jnp.bfloat16)
    grad_out = jnp.einsum("rq,rd->qd", attn_b, grad_proj_b, preferred_element_type=jnp.float32)
    grad_attn_b = jnp.einsum(
        "rd,qd->rq", grad_proj_b, full_out, preferred_element_type=jnp.float32
    ).astype(jnp.bfloat16)
    den_rows = jnp.transpose(denominator, (0, 3, 1, 2)).reshape(number_of_rows, QUERY_HEADS)
    grad_heads_float = grad_attn_b.astype(jnp.float32).reshape(
        number_of_rows, QUERY_HEADS, HEAD_DIMENSION
    )
    softmax_ratio = (
        jnp.sum(
            grad_heads_float * attn_float.reshape(number_of_rows, QUERY_HEADS, HEAD_DIMENSION),
            axis=-1,
        )
        / den_rows
    ).reshape(slot_position, stretched_length, QUERY_HEADS)
    scaled_gradient = (
        (grad_heads_float / den_rows[..., None])
        .astype(jnp.bfloat16)
        .reshape(slot_position, stretched_length, QUERY_HEADS * HEAD_DIMENSION)
    )
    ratio_all = lax.all_gather(softmax_ratio, "seq", axis=1, tiled=True)
    head_gradient = scaled_gradient.reshape(
        slot_position, stretched_length, KEY_VALUE_HEADS, query_group, HEAD_DIMENSION
    )
    local_softmax_ratio = jnp.transpose(
        softmax_ratio.reshape(slot_position, stretched_length, KEY_VALUE_HEADS, query_group),
        (0, 2, 3, 1),
    )[..., None]
    empty_query = jnp.zeros(
        (slot_position, KEY_VALUE_HEADS, query_group, stretched_length, HEAD_DIMENSION), jnp.float32
    )
    key_piece = lax.all_gather(key_block, "seq", axis=1, tiled=True)
    value_piece = lax.all_gather(value_block, "seq", axis=1, tiled=True)

    def one_block(partial_value, offset, block_length):
        key_blk = lax.dynamic_slice_in_dim(key_piece, offset, block_length, 1).reshape(
            slot_position, block_length, KEY_VALUE_HEADS, HEAD_DIMENSION
        )
        value_blk = lax.dynamic_slice_in_dim(value_piece, offset, block_length, 1).reshape(
            slot_position, block_length, KEY_VALUE_HEADS, HEAD_DIMENSION
        )
        allowed = allowed_mask(
            query_pos, offset + jnp.arange(block_length, dtype=jnp.int32), live_len
        )
        scores = (
            jnp.einsum("schgd,snhd->shgcn", query_b, key_blk, preferred_element_type=jnp.float32)
            * scale
        )
        exp_scores = jnp.where(allowed, jnp.exp(scores), 0.0)
        grad_prob = jnp.einsum(
            "schgd,snhd->shgcn", head_gradient, value_blk, preferred_element_type=jnp.float32
        )
        grad_score = (exp_scores * (grad_prob - local_softmax_ratio)).astype(jnp.bfloat16)
        return (
            partial_value
            + jnp.einsum(
                "shgcn,snhd->shgcd", grad_score, key_blk, preferred_element_type=jnp.float32
            )
            * scale
        )

    grad_query = over_blocks(key_piece.shape[1], stretched_length, one_block, empty_query)
    query_flat = query_b.reshape(slot_position, stretched_length, QUERY_HEADS * HEAD_DIMENSION)
    per_head_keys = key_block.reshape(
        slot_position, stretched_length, KEY_VALUE_HEADS, HEAD_DIMENSION
    )
    per_head_values = value_block.reshape(
        slot_position, stretched_length, KEY_VALUE_HEADS, HEAD_DIMENSION
    )
    empty_key_value = jnp.zeros(
        (slot_position, KEY_VALUE_HEADS, stretched_length, HEAD_DIMENSION), jnp.float32
    )
    query_piece = lax.all_gather(query_flat, "seq", axis=1, tiled=True)
    grad_piece = lax.all_gather(scaled_gradient, "seq", axis=1, tiled=True)

    def one_block(partial_value, offset, block_length):
        grad_key, value_gradient = partial_value
        query_blk = lax.dynamic_slice_in_dim(query_piece, offset, block_length, 1).reshape(
            slot_position, block_length, KEY_VALUE_HEADS, query_group, HEAD_DIMENSION
        )
        grad_blk = lax.dynamic_slice_in_dim(grad_piece, offset, block_length, 1).reshape(
            slot_position, block_length, KEY_VALUE_HEADS, query_group, HEAD_DIMENSION
        )
        ratio_blk = lax.dynamic_slice_in_dim(ratio_all, offset, block_length, 1).reshape(
            slot_position, block_length, KEY_VALUE_HEADS, query_group
        )
        ratio_blk = jnp.transpose(ratio_blk, (0, 2, 3, 1))[..., None]
        remote_pos = offset + jnp.arange(block_length, dtype=jnp.int32)
        allowed = allowed_mask(remote_pos, query_pos, live_len)
        scores = (
            jnp.einsum(
                "snhgd,schd->shgnc", query_blk, per_head_keys, preferred_element_type=jnp.float32
            )
            * scale
        )
        exp_scores = jnp.where(allowed, jnp.exp(scores), 0.0)
        value_gradient = value_gradient + jnp.einsum(
            "shgnc,snhgd->shcd",
            exp_scores.astype(jnp.bfloat16),
            grad_blk,
            preferred_element_type=jnp.float32,
        )
        grad_prob = jnp.einsum(
            "snhgd,schd->shgnc", grad_blk, per_head_values, preferred_element_type=jnp.float32
        )
        grad_score = (exp_scores * (grad_prob - ratio_blk)).astype(jnp.bfloat16)
        grad_key = (
            grad_key
            + jnp.einsum(
                "shgnc,snhgd->shcd", grad_score, query_blk, preferred_element_type=jnp.float32
            )
            * scale
        )
        return (grad_key, value_gradient)

    grad_key, value_gradient = over_blocks(
        query_piece.shape[1], stretched_length, one_block, (empty_key_value, empty_key_value)
    )
    grad_query = jnp.transpose(grad_query, (0, 3, 1, 2, 4)).reshape(
        slot_position, stretched_length, QUERY_HEADS, HEAD_DIMENSION
    )
    grad_query_b = (
        apply_rotary(grad_query, cosine_table, -sine_table)
        .astype(jnp.bfloat16)
        .reshape(number_of_rows, QUERY_HEADS * HEAD_DIMENSION)
    )
    grad_key_b = (
        apply_rotary(jnp.transpose(grad_key, (0, 2, 1, 3)), cosine_table, -sine_table)
        .astype(jnp.bfloat16)
        .reshape(number_of_rows, KEY_VALUE_HEADS * HEAD_DIMENSION)
    )
    grad_value_b = (
        jnp.transpose(value_gradient, (0, 2, 1, 3))
        .astype(jnp.bfloat16)
        .reshape(number_of_rows, KEY_VALUE_HEADS * HEAD_DIMENSION)
    )
    grad_wq = jnp.einsum(
        "rd,rq->dq", attention_input, grad_query_b, preferred_element_type=jnp.float32
    )
    grad_wk = jnp.einsum(
        "rd,rq->dq", attention_input, grad_key_b, preferred_element_type=jnp.float32
    )
    grad_wv = jnp.einsum(
        "rd,rq->dq", attention_input, grad_value_b, preferred_element_type=jnp.float32
    )
    grad_attn_in = jnp.einsum(
        "rq,dq->rd", grad_query_b, full_query, preferred_element_type=jnp.float32
    )
    grad_attn_in = grad_attn_in + jnp.einsum(
        "rq,dq->rd", grad_key_b, full_key, preferred_element_type=jnp.float32
    )
    grad_attn_in = grad_attn_in + jnp.einsum(
        "rq,dq->rd", grad_value_b, full_value, preferred_element_type=jnp.float32
    )
    grad_gain_attn = jnp.sum(grad_attn_in * normed_first, axis=0)
    grad_first = grad_attn_in * full_gain_attn.astype(jnp.float32)
    grad_tokens = grad_hidden + inv_first * (
        grad_first - normed_first * jnp.mean(grad_first * normed_first, axis=-1, keepdims=True)
    )
    return (
        (
            grad_wq,
            grad_wk,
            grad_wv,
            grad_out,
            grad_gate,
            grad_up,
            grad_down,
            grad_gain_attn,
            grad_gain_ffn,
        ),
        grad_tokens,
    )


def per_device(
    tokens,
    teacher,
    lengths,
    w_query,
    key_weight,
    value_weight,
    w_out,
    w_gate,
    w_up,
    w_down,
    gain_attn,
    gain_ffn,
):
    shards = (w_query, key_weight, value_weight, w_out, w_gate, w_up, w_down, gain_attn, gain_ffn)
    slot_count, stretched_length, model_width = tokens.shape
    total_tokens = slot_count * lax.axis_size("dp") * stretched_length * lax.axis_size("seq")
    query_pos = lax.axis_index("seq") * stretched_length + jnp.arange(
        stretched_length, dtype=jnp.int32
    )
    cosine_table, sine_table = rope_tables(query_pos, HEAD_DIMENSION)
    out_rows = []
    stored = []
    differences = []
    squares_local = jnp.zeros((), jnp.float32)
    count_local = jnp.zeros((), jnp.float32)
    for micro in range(slot_count):
        weights = collect(shards)
        live_len = lengths[micro : micro + 1]
        out_float, valid_rows, saved = forward_slot(
            weights, tokens[micro : micro + 1], live_len, query_pos, cosine_table, sine_table
        )
        teach_float = teacher[micro].astype(jnp.float32)
        difference = jnp.where(valid_rows, out_float - teach_float, 0.0)
        squares_local = squares_local + jnp.sum(difference * difference)
        count_local = count_local + jnp.sum(valid_rows.astype(jnp.float32))
        out_rows.append(out_float.astype(jnp.bfloat16).reshape(1, stretched_length, model_width))
        stored.append(saved)
        differences.append(difference)
    loss_sum, count_sum = lax.psum((squares_local, count_local), ("dp", "seq"))
    loss = loss_sum / count_sum
    factor = total_tokens / count_sum
    grad_sums = None
    token_grads = []
    for micro in range(slot_count):
        weights = collect(shards)
        grads, grad_tokens = backward_slot(
            weights,
            stored[micro],
            factor * differences[micro],
            lengths[micro : micro + 1],
            query_pos,
            cosine_table,
            sine_table,
        )
        grad_sums = grads if grad_sums is None else jax.tree.map(jnp.add, grad_sums, grads)
        token_grads.append(grad_tokens.reshape(1, stretched_length, model_width))
    owned, gain_part_attn, gain_part_ffn = reduce_grads(grad_sums)
    gain_totals = lax.psum((gain_part_attn, gain_part_ffn), "dp")
    output = jnp.concatenate(out_rows, axis=0)
    tokens_grad = jnp.concatenate(token_grads, axis=0)
    return (
        output,
        loss,
        tokens_grad,
        owned[0],
        owned[1],
        owned[2],
        owned[3],
        owned[4],
        owned[5],
        owned[6],
        gain_totals[0],
        gain_totals[1],
    )


MESH_ID = pl.DeviceIdType.MESH
VMEM_MOST = 64 * 1024 * 1024 - 128 * 1024


class Place(tuple):
    def with_line(self):
        z = self[2]
        self.line = (0,) + tuple(pick(z, v) for v in ((1, -1, -1, -1), (2, 1, 1, -2), (3, 2, -2, -3)))
        self.sign = (0,) + tuple(jnp.where(offset > 0, 1, -1) for offset in self.line[1:])
        return self


def position():
    row = lax.axis_index("dp")
    column = lax.axis_index("seq")
    return Place((lax.rem(column, 2), row // 2, column // 2, lax.rem(row, 2))).with_line()


def mesh_place(x, y, z, c):
    return (2 * y + c, 2 * z + x)


def step_to(place, axis, sign=1):
    x, y, z, c = place
    if axis == "x":
        return (1 - x, y, z, c)
    if axis == "y":
        return (x, 1 - y, z, c)
    if axis == "z":
        return (x, y, z + sign, c)
    return (x, y, z, 1 - c)


def pick(z, values):
    return sum(jnp.where(z == i, v, 0) for i, v in enumerate(values) if v)


def shifted(place, rel):
    x, y, z, c = place
    dx, dy, rank = rel
    return ((1 - x) if dx else x, (1 - y) if dy else y, z + place.line[rank], c)


def on_line(z):
    return jnp.logical_and(z >= 0, z < 4)


def greet(place, lines):
    x, y, z, c = place
    d, s = mesh_place(*place)
    barrier = pltpu.get_barrier_semaphore()

    def signal(who):
        pl.semaphore_signal(barrier, inc=1, device_id=who, device_id_type=MESH_ID)

    if lines:
        for k in range(1, 8):
            signal((d, lax.rem(s + k, 8)))
        for k in range(1, 4):
            signal((lax.rem(d + k, 4), s))
        pl.semaphore_wait(barrier, 10)
        return
    for axis in "xyc":
        signal(mesh_place(*step_to(place, axis)))
    pl.when(z < 3)(lambda: signal(mesh_place(x, y, z + 1, c)))
    pl.when(z > 0)(lambda: signal(mesh_place(x, y, z - 1, c)))
    pl.semaphore_wait(barrier, 3 + jnp.where(z > 0, 1, 0) + jnp.where(z < 3, 1, 0))


def wait_bytes(region, sem):
    pltpu.make_async_copy(region, region, sem).wait()


def spread_order(order):
    held = [((0, 0, 0), -1)]
    for level, axis in enumerate(order):
        new = []
        if axis == "z":
            new = [((rel[0], rel[1], rank), level) for rank in (1, 2, 3) for rel, _ in held]
        else:
            new = [((1, rel[1], rel[2]) if axis == "x" else (rel[0], 1, rel[2]), level) for rel, _ in held]
        held = held + new
    return held


class Spread:
    def __init__(self, place, order, own, spot, sems, job, pair=None, amount=None):
        self.place, self.order, self.own, self.spot = place, order, own, spot
        self.recv, self.send, self.recv_core, self.send_core = sems
        self.job, self.pair, self.amount = job, pair, amount
        self.pieces = spread_order(order)

    def number(self, who):
        x, y, z, _ = who
        return z * 4 + y * 2 + x

    def go(self, rel, level, target):
        who = shifted(self.place, rel)
        pltpu.make_async_remote_copy(
            src_ref=self.own if level < 0 else self.spot(who),
            dst_ref=self.spot(who),
            send_sem=self.send.at[self.job],
            recv_sem=self.recv.at[self.job, self.number(who)],
            device_id=mesh_place(*target),
            device_id_type=MESH_ID,
        ).start()

    def to_core(self, rel):
        who = shifted(self.place, rel)
        pltpu.make_async_remote_copy(
            src_ref=self.pair(who),
            dst_ref=self.pair(who),
            send_sem=self.send_core.at[self.job],
            recv_sem=self.recv_core.at[self.job],
            device_id=mesh_place(*step_to(self.place, "c")),
            device_id_type=MESH_ID,
        ).start()

    def steps(self):
        out = []
        arrived = set()
        z = self.place[2]
        for rel, level in self.pieces:

            def run(rel=rel, level=level):
                arrived.add(rel)
                who = shifted(self.place, rel)
                if level >= 0:
                    there = self.spot(who)
                    pltpu.make_async_copy(there, there, self.recv.at[self.job, self.number(who)]).wait()
                if level >= 0 and self.order[level] == "z":
                    on = z - self.place.sign[rel[2]]
                    pl.when(on_line(on))(lambda: self.go(rel, level, (self.place[0], self.place[1], on, self.place[3])))
                for axis in self.order[level + 1:]:
                    if axis == "z":
                        pl.when(z < 3)(lambda: self.go(rel, level, step_to(self.place, "z", 1)))
                        pl.when(z > 0)(lambda: self.go(rel, level, step_to(self.place, "z", -1)))
                    else:
                        self.go(rel, level, step_to(self.place, axis))
                if self.pair is not None and (1 - rel[0], rel[1], rel[2]) in arrived:
                    self.to_core(rel)

            out.append(run)
        return out

    def sent(self):
        total = [0, 0]
        for i, z in enumerate((0, 1)):
            for rel, level in self.pieces:
                if level >= 0 and self.order[level] == "z":
                    offset = (0, ((1, -1)[z]), ((2, 1)[z]), ((3, 2)[z]))[rel[2]]
                    on = z - (1 if offset > 0 else -1)
                    total[i] += 0 <= on < 4
                for axis in self.order[level + 1:]:
                    total[i] += (1, 2)[z] if axis == "z" else 1
        return total

    def wait_core(self):
        wait_bytes(self.amount(16), self.recv_core.at[self.job])

    def finish(self):
        ends, inner = self.sent()
        z = self.place[2]
        at_end = jnp.logical_or(z == 0, z == 3)
        pl.when(at_end)(lambda: wait_bytes(self.amount(ends), self.send.at[self.job]))
        pl.when(jnp.logical_not(at_end))(lambda: wait_bytes(self.amount(inner), self.send.at[self.job]))
        if self.pair is not None:
            wait_bytes(self.amount(16), self.send_core.at[self.job])


def fold_pieces(order):
    out = []
    for dx in (0, 1):
        for dy in (0, 1) if "y" in order else (0,):
            for rank in (0, 1, 2, 3):
                differs = {"x": dx, "y": dy, "z": rank}
                stage = next((i for i, axis in enumerate(order) if differs[axis]), len(order))
                out.append(((dx, dy, rank), stage))
    return sorted(out, key=lambda item: (item[1], -item[0][2], -item[0][0] - item[0][1]))


def fold_slots(order):
    base, starts = 0, []
    for level, axis in enumerate(order):
        starts.append(base)
        after = order[level + 1:]
        wide = (4 if "z" in after else 1) * (2 if "x" in after else 1) * (2 if "y" in after else 1)
        base += wide * 5 if axis == "z" else wide
    return starts, base


class Fold:
    def __init__(self, place, order, mine, arrived, sems, job, out, amount, ready=None):
        self.place, self.order, self.mine, self.arrived = place, order, mine, arrived
        self.send, self.recv = sems
        self.job, self.out, self.amount, self.ready = job, out, amount, ready
        self.pieces = fold_pieces(order)
        self.base, self.slots = fold_slots(order)

    def slot(self, level, rel, last):
        index = 0
        at_z = self.place[2] + self.place.line[rel[2]]
        for other in self.order[level + 1:]:
            size = 4 if other == "z" else 2
            index = index * size + (at_z if other == "z" else (rel[0] if other == "x" else rel[1]))
        if self.order[level] == "z":
            index = index * 5 + (4 if last is True else (at_z if last is False else jnp.where(last, 4, at_z)))
        return self.base[level] + index

    def take(self, mine, slot):
        there = self.arrived.at[slot]
        pltpu.make_async_copy(there, there, self.recv.at[self.job, slot]).wait()
        mine[...] = mine[...] + self.arrived[slot]

    def steps(self):
        out = []
        present = set()
        z = self.place[2]
        for rel, stage in self.pieces:

            def run(rel=rel, stage=stage):
                if self.ready is not None and rel[1] not in present:
                    present.add(rel[1])
                    self.ready(rel[1])
                mine = self.mine(shifted(self.place, rel))
                offset, sign = self.place.line[rel[2]], self.place.sign[rel[2]]
                for level in range(min(stage + 1, len(self.order))):
                    if self.order[level] == "z":
                        if level < stage:
                            pl.when(z > 0)(lambda: self.take(mine, self.slot(level, rel, False)))
                            pl.when(z < 3)(lambda: self.take(mine, self.slot(level, rel, True)))
                        else:
                            behind = z - sign
                            pl.when(on_line(behind))(lambda: self.take(mine, self.slot(level, rel, False)))
                    elif level < stage:
                        self.take(mine, self.slot(level, rel, False))
                if stage == len(self.order):
                    self.out(mine[...].astype(jnp.float32))
                    return
                axis = self.order[stage]
                if axis == "z":
                    target = (self.place[0], self.place[1], z + sign, self.place[3])
                else:
                    target = step_to(self.place, axis)
                slot = self.slot(stage, rel, offset == -1 if axis == "z" else False)
                pltpu.make_async_remote_copy(
                    src_ref=mine,
                    dst_ref=self.arrived.at[slot],
                    send_sem=self.send.at[self.job],
                    recv_sem=self.recv.at[self.job, slot],
                    device_id=mesh_place(*target),
                    device_id_type=MESH_ID,
                ).start()

            out.append(run)
        return out

    def finish(self):
        wait_bytes(self.amount(len(self.pieces) - 1), self.send.at[self.job])


CAT_JOBS = (("cat", 0, 96, "xzy"), ("cat", 96, 96, "yzx"), ("cat", 192, 96, "zxy"))
FFN_JOBS = (
    ("gate", 0, 144, "xzy"), ("up", 0, 96, "yzx"), ("down", 0, 384, "zxy"),
    ("gate", 144, 144, "xzy"), ("up", 96, 96, "yzx"), ("down", 384, 384, "zxy"), ("up", 192, 96, "zxy"),
)
KV_JOBS = tuple((slot, 256 * third, "xz" if (slot, third) == (1, 2) else "zx") for slot in (0, 1) for third in (0, 1, 2))
FOLD_FFN = tuple(job[:3] + (job[3][::-1],) for job in FFN_JOBS)
FOLD_CAT = tuple(job[:3] + (job[3][::-1],) for job in CAT_JOBS)
FOLD_KV = tuple((slot, row, order[::-1]) for slot, row, order in KV_JOBS)
FFN_NAMES = ("gate", "up", "down")


def job_shape(job):
    return (144, job[2]) if job[0] == "down" else (job[2], 384)


def piece_of(ref, job, paired=False):
    name, first, count, _ = job
    double = 2 if paired else 1

    def spot(who):
        x, y, z, c = who
        d, s = mesh_place(0 if paired else x, y, z, c)
        if name == "down":
            return ref.at[
                pl.ds(pl.multiple_of(s * 144, 16), 144 * double), pl.ds(pl.multiple_of(d * 768 + first, 128), count)
            ]
        return ref.at[
            pl.ds(pl.multiple_of(d * 288 + first, 8), count), pl.ds(pl.multiple_of(s * 384, 128), 384 * double)
        ]

    return spot


def region(ref, elements, rows, columns):
    units = elements // 2048
    wide = max(k for k in range(1, columns // 128 + 1) if units % k == 0 and units // k <= rows // 16)
    return ref.at[pl.ds(0, units // wide * 16), pl.ds(0, wide * 128)]


def amount_of(ref, job):
    rows, columns = job_shape(job)
    return lambda pieces: region(ref, pieces * rows * columns, *ref.shape)


def own_part(ref, job):
    name, first, count, _ = job
    return ref.at[:, pl.ds(first, count)] if name == "down" else ref.at[pl.ds(first, count), :]


def kv_spot(ref, slot, row):
    def spot(who):
        _, s = mesh_place(*who)
        return ref.at[slot, pl.ds(row, 256), pl.ds(pl.multiple_of(s * 128, 128), 128)]

    return spot


def kv_amount(ref):
    return lambda pieces: ref.at[0, pl.ds(0, 32 * pieces), :]


def make_spreads(place, jobs, shards, wholes, sems):
    return [
        Spread(
            place, job[3], own_part(shards[job[0]], job), piece_of(wholes[job[0]], job), sems, j,
            piece_of(wholes[job[0]], job, True), amount_of(wholes[job[0]], job),
        )
        for j, job in enumerate(jobs)
    ]


def make_kv_spreads(place, own, whole, sems):
    return [
        Spread(
            place, order, own.at[pl.ds(row, 256), pl.ds(slot * 128, 128)], kv_spot(whole, slot, row),
            (sems[0], sems[1], None, None), j, None, kv_amount(whole),
        )
        for j, (slot, row, order) in enumerate(KV_JOBS)
    ]


def spread_sems(jobs):
    n = len(jobs)
    return [
        pltpu.SemaphoreType.DMA((n, 16)), pltpu.SemaphoreType.DMA((n,)),
        pltpu.SemaphoreType.DMA((n,)), pltpu.SemaphoreType.DMA((n,)),
    ]


def fold_scratch(jobs, paired):
    n = len(jobs)
    most = max(fold_slots(job[3])[1] for job in jobs)
    scratch = [
        pltpu.SemaphoreType.DMA((n,)), pltpu.SemaphoreType.DMA((n, most)),
        pltpu.SemaphoreType.DMA((n, 2)), pltpu.SemaphoreType.DMA((n, 2)), pltpu.SemaphoreType.DMA((n, 2)),
    ]
    for job in jobs:
        rows, columns = job_shape(job)
        block = (2, 1152, columns) if job[0] == "down" else (2, rows, 3072)
        scratch += [
            pltpu.VMEM(block, jnp.bfloat16), pltpu.VMEM((fold_slots(job[3])[1], rows, columns), jnp.bfloat16)
        ]
        scratch += [pltpu.VMEM(block, jnp.bfloat16)] if paired else []
    return scratch


class JobFold:
    def __init__(self, place, job, j, sums, owned, scratch, paired):
        self.place, self.job, self.j, self.sums, self.paired = place, job, j, sums, paired
        send, recv, self.load_sem, self.core_send, self.core_recv = scratch[:5]
        each = 3 if paired else 2
        self.acc, arrived = scratch[5 + each * j: 7 + each * j]
        self.other = scratch[7 + each * j] if paired else None
        name, first, count, order = job

        def mine(who):
            x, y, z, c = who
            s = 2 * z + x
            if name == "down":
                return self.acc.at[y, pl.ds(pl.multiple_of(s * 144, 16), 144), :]
            return self.acc.at[y, :, pl.ds(pl.multiple_of(s * 384, 128), 384)]

        def out(value):
            if name == "down":
                owned[:, first: first + count] = value
            else:
                owned[first: first + count, :] = value

        self.fold = Fold(place, order, mine, arrived, (send, recv), j, out, amount_of(sums, job), self.ready)

    def block(self, y, c):
        name, first, count, _ = self.job
        d = 2 * y + c if self.paired else y
        if name == "down":
            return self.sums.at[:, pl.ds(pl.multiple_of(d * 768 + first, 128), count)]
        return self.sums.at[pl.ds(pl.multiple_of(d * 288 + first, 8), count), :]

    def local_copy(self, dy):
        x, y, z, c = self.place
        at = (1 - y) if dy else y
        return pltpu.make_async_copy(self.block(at, c), self.acc.at[at], self.load_sem.at[self.j, dy])

    def core_copy(self, dy):
        x, y, z, c = self.place
        at = (1 - y) if dy else y
        return pltpu.make_async_remote_copy(
            src_ref=self.block(at, 1 - c),
            dst_ref=self.other.at[at],
            send_sem=self.core_send.at[self.j, dy],
            recv_sem=self.core_recv.at[self.j, dy],
            device_id=mesh_place(x, y, z, 1 - c),
            device_id_type=MESH_ID,
        )

    def begin(self, dy):
        if self.paired:
            self.core_copy(dy).start()
        self.local_copy(dy).start()

    def ready(self, dy):
        y = self.place[1]
        at = (1 - y) if dy else y
        self.local_copy(dy).wait()
        if not self.paired:
            return
        self.core_copy(dy).wait_recv()

        def add(k, _):
            if self.job[0] == "down":
                part = (at, pl.ds(pl.multiple_of(k * 144, 16), 144), slice(None))
            else:
                part = (at, slice(None), pl.ds(pl.multiple_of(k * 384, 128), 384))
            self.acc[part] = self.acc[part] + self.other[part]
            return _

        lax.fori_loop(0, 8, add, 0)

    def finish(self):
        self.fold.finish()
        for dy in (0, 1) if self.paired else ():
            self.core_copy(dy).wait_send()


class Notes:
    def __init__(self, place, tile_of, own, by_seq, by_dp, sems):
        self.d, self.s = mesh_place(*place)
        self.tile_of, self.own, self.by_seq, self.by_dp = tile_of, own, by_seq, by_dp
        self.seq_send, self.seq_recv, self.dp_send, self.dp_recv = sems

    def along_seq(self, k):
        peer = lax.rem(self.s + k, 8)
        return pltpu.make_async_remote_copy(
            src_ref=self.tile_of(peer), dst_ref=self.by_seq.at[self.s], send_sem=self.seq_send.at[k],
            recv_sem=self.seq_recv.at[self.s], device_id=(self.d, peer), device_id_type=MESH_ID,
        )

    def along_dp(self, k):
        peer = lax.rem(self.d + k, 4)
        return pltpu.make_async_remote_copy(
            src_ref=self.own, dst_ref=self.by_dp.at[self.d], send_sem=self.dp_send.at[k],
            recv_sem=self.dp_recv.at[self.d], device_id=(peer, self.s), device_id_type=MESH_ID,
        )

    def wait_seq(self):
        for k in range(1, 8):
            peer = lax.rem(self.s + k, 8)
            there = self.by_seq.at[peer]
            pltpu.make_async_copy(there, there, self.seq_recv.at[peer]).wait()

    def wait_dp(self):
        for k in range(1, 4):
            peer = lax.rem(self.d + k, 4)
            there = self.by_dp.at[peer]
            pltpu.make_async_copy(there, there, self.dp_recv.at[peer]).wait()


NOTE_SEMS = [
    pltpu.SemaphoreType.DMA((8,)), pltpu.SemaphoreType.DMA((8,)),
    pltpu.SemaphoreType.DMA((4,)), pltpu.SemaphoreType.DMA((4,)),
]


FORWARD_PLAN = (
    (0, 100, 200,),
    (108, 1, 2, 101, 102, 8, 201, 204, 208, 4, 3, 202, 9, 104, 103, 205, 10, 109, 110, 209, 5, 105, 206, 203,
        11, 210, 6, 212, 106, 112, 207, 7, 213, 107,),
    (10500, 113, 211, 114, 10000, 10600, 214, 115, 14, 111, 10100, 10200, 10300, 10400, 12, 215, 15, 13,),
    (20000, 20100, 20200, 20300, 20400, 20500,),
    (10002, 10001, 20001, 20101, 20002, 20004, 10504, 20201, 20104, 10204, 20301, 20204, 10102, 20401, 10501,
        20304, 10101, 10008, 10201, 20502, 10604, 20501, 20404, 10108, 10302, 10301, 10601, 10402, 10401,
        20102, 10508, 10004, 10208, 20202, 10308, 10408, 20302, 10608, 10104, 20402, 20005, 10202, 10009,
        20105, 10502, 20205, 10209, 10304, 10003, 10404, 10010, 10602, 20503, 20504, 20305, 20405, 10509,
        10103, 10309, 10505, 10205, 20003, 10609, 10303, 10109, 10110, 10310, 20103, 20006, 10605, 20203,
        10403, 20505, 20106, 10005, 20303, 10210, 20206, 10512, 10409, 10410, 10510, 10212, 20306, 10613,
        20406, 10506, 10203, 10105, 10503, 10612, 10206, 10305, 10610, 10012, 10405, 20403, 10603, 10606,
        20107, 10011, 10213, 20007, 10006, 10312, 20506, 20207, 10513, 10111, 10112, 20307, 10311, 10507,
        20507, 10511, 10411, 20407,),
    (
        (1, (10211, 10306, 10412,)),
        (2, (10207, 10106, 10013, 10607,)),
        (3, (10406,)),
        (5, (10007,)),
        (8, (10113,)),
        (9, (10107, 10514,)),
        (11, (10307, 10313,)),
    ),
    (10407, 10413, 10214, 10611, 10614, 10014, 10114, 10515, 10414, 10215, 10314, 10615, 10015, 10115, 10415, 10315,),
)
BACKWARD_PLAN = (
    (10100, 10101,),
    (
        (0, (10300,)),
        (3, (10000,)),
        (5, (10102, 10500,)),
        (8, (10200,)),
        (9, (10400,)),
    ),
    (10401, 20500, 10103, 10105, 10104, 20000, 10001, 10302, 20501, 20502, 10201, 10501, 10106, 10002, 20300,
        20100, 20200, 20400, 10202, 10502, 10600, 20504, 20503, 10003, 10304, 10306, 20001, 20101, 20201,
        20301, 20401, 10107, 10108, 10109, 10110, 20402, 20505, 10301, 10303, 10305, 20002, 20102, 20202,
        20302, 10203, 10503, 10004, 20506, 20303, 20304, 10204, 10402, 10504, 10005, 10111, 20003, 20103,
        20203, 20403, 20004, 20204, 20404, 20005, 20205, 10602, 10205, 10604, 20305, 10403, 10505, 10006,
        20405, 10307, 10308, 10601, 10603, 20006, 20104, 20105, 20106, 10112, 20206, 10206, 10309, 10404,
        20306, 10506, 10007, 10008, 20007, 20406, 10113, 10009, 10207, 10208, 10209, 10405, 10507, 10508,
        10509, 20107, 20307, 10310, 10605, 20407, 10010, 20507, 10406, 10210, 10011, 10407, 10408, 10409,
        20207,),
    (
        (0, (10311, 10606,)),
        (2, (10312, 10607, 10608, 10609,)),
        (3, (10012,)),
        (4, (10410,)),
        (7, (10510,)),
    ),
    (10412, 10411, 10313, 100, 10013, 200, 101, 201, 10114, 10211, 102, 202,),
    (10610, 103, 203, 10511, 10413, 104, 204,),
    (10212, 105, 205, 106, 206, 107, 207, 10213, 0, 1, 2, 10611, 3, 10512, 10513, 208, 5, 10612, 108,),
    (109, 209, 7, 110, 10613, 4, 6, 112, 111, 113, 10314, 210, 10014, 10115, 211, 8, 10, 114, 212,),
    (9, 213, 10214, 10514, 214, 10414, 10315, 12, 10015, 11, 115, 13, 215, 10215, 10515, 14, 10614, 15, 10415,
        10615,),
)


def dot(a, b):
    return jnp.dot(a, b, preferred_element_type=jnp.float32)


def dot_t(a, b):
    return lax.dot_general(a, b, (((1,), (1,)), ((), ())), preferred_element_type=jnp.float32)


def t_dot(a, b):
    return lax.dot_general(a, b, (((0,), (0,)), ((), ())), preferred_element_type=jnp.float32)


def repeat(count, body):
    def step(k, nothing):
        body(k)
        return nothing

    lax.fori_loop(0, count, step, 0)


def rows_at(k, size, base=0):
    return pl.ds(pl.multiple_of(base + k * size, 16), size)


def lanes_at(k, size, base=0):
    return pl.ds(pl.multiple_of(base + k * size, 128), size)


def rotate(u, cosine, sine):
    front, back = u[:32], u[32:]
    return jnp.concatenate([front * cosine - back * sine, front * sine + back * cosine], axis=0)


def probabilities(keys, query, limit, chunk):
    scores = t_dot(keys, query) * (HEAD_DIMENSION ** (-0.5))
    key_pos = chunk * 256 + lax.broadcasted_iota(jnp.int32, (256, 384), 0)
    return jnp.where(key_pos <= limit, jnp.exp(scores), 0.0)


def heads_wide(ref, group, lanes):
    return jnp.concatenate(
        [ref[pl.ds(pl.multiple_of(group * 192 + 64 * i, 64), 64), lanes] for i in range(3)], axis=1
    )


def three_wide(row):
    return jnp.concatenate([row] * 3, axis=1)


def forward_body(
    cat, note, x, cosine, sine, limit, gate, up, down,
    gate_w, up_w, down_w, wcat, notes, attn_in_t, hidden, query, keys_values, attn, denom,
    attn_in, raw, own_kv, weights, proj, seq_in, dp_in, own_sems, note_a, note_b, note_c, note_d, *sems
):
    place = position()
    d, s = mesh_place(*place)
    greet(place, True)
    shards = dict(zip(FFN_NAMES, (gate, up, down)))
    wholes = dict(zip(FFN_NAMES, (gate_w, up_w, down_w)))
    cat_spreads = make_spreads(place, CAT_JOBS, {"cat": cat}, {"cat": weights}, sems[:4])
    ffn_spreads = make_spreads(place, FFN_JOBS, shards, wholes, sems[4:8])
    kv_spreads = make_kv_spreads(place, own_kv, keys_values, sems[8:10])
    steps = [[spread.steps() for spread in family] for family in (cat_spreads, ffn_spreads, kv_spreads)]

    def run(tokens):
        for token in tokens:
            steps[token // 10000][token // 100 % 100][token % 100]()

    tiles = Notes(place, lambda peer: note, note, seq_in, dp_in, (note_a, note_b, note_c, note_d))
    run(FORWARD_PLAN[0])
    for k in range(1, 8):
        tiles.along_seq(k).start()
    for k in range(1, 4):
        tiles.along_dp(k).start()
    own = [
        pltpu.make_async_copy(
            shards[name], piece_of(wholes[name], (name, 0, 768 if name == "down" else 288, ""))(place), own_sems.at[k]
        )
        for k, name in enumerate(FFN_NAMES)
    ]
    for copy in own:
        copy.start()
    weights[rows_at(d, 288), lanes_at(s, 384)] = cat[...]
    for copy in own:
        copy.wait()
    run(FORWARD_PLAN[1])
    tiles.wait_seq()
    tiles.wait_dp()
    seq_in[s] = note[...]
    dp_in[d] = note[...]
    gains = seq_in[0]
    for k in range(1, 8):
        gains = gains + seq_in[k]
    notes[0:8, :] = gains
    notes[8:16, :] = dp_in[0] + dp_in[1] + dp_in[2] + dp_in[3]

    def norm(k):
        rows = rows_at(k, 32)
        part = x[rows, :].astype(jnp.float32)
        scale = lax.rsqrt(jnp.mean(part * part, axis=-1, keepdims=True) + norm_eps)
        attn_in[rows, :] = (part * scale * notes[0:1, :]).astype(jnp.bfloat16)

    repeat(8, norm)
    attn_in_t[...] = attn_in[...].T
    run(FORWARD_PLAN[2])
    for spread in cat_spreads:
        spread.wait_core()

    def project(b):
        block = dot(attn_in[...], weights[:, lanes_at(b, 384)][:, :256]).T
        raw[rows_at(b, 144), :] = block[:144]
        raw[rows_at(b, 48, 1152), :] = block[144:192]
        raw[rows_at(b, 48, 1536), :] = block[192:240]

    repeat(8, project)
    out_copy = pltpu.make_async_copy(weights, wcat, own_sems.at[3])
    out_copy.start()

    def turn(ref, rows_of):
        def one(h):
            ref[rows_at(h, 64), :] = rotate(raw[rows_of(h), :], cosine[...], sine[...]).astype(jnp.bfloat16)

        return one

    repeat(6, turn(own_kv, lambda h: rows_at(h, 64, 1152)))
    own_kv[384:768, :] = raw[1536:1920, :].astype(jnp.bfloat16)
    repeat(18, turn(query, lambda h: rows_at(h, 64)))
    run(FORWARD_PLAN[3])
    here = lanes_at(s, 128)
    for slot in range(2):
        keys_values[slot, :, here] = own_kv[:, slot * 128: slot * 128 + 128]
    run(FORWARD_PLAN[4])

    def attend(slot, group):
        lanes = lanes_at(slot, 128)
        bound = three_wide(limit[:, lanes])
        wide = heads_wide(query, group, lanes)

        def one_chunk(chunk, carry):
            total, numer = carry
            cols = lanes_at(chunk, 256)
            expo = probabilities(keys_values[slot, rows_at(group, 64), cols], wide, bound, chunk)
            total = total + jnp.sum(expo, axis=0, keepdims=True)
            numer = numer + dot(keys_values[slot, rows_at(group, 64, 384), cols], expo.astype(jnp.bfloat16))
            return (total, numer)

        total, numer = lax.fori_loop(
            0, 4, one_chunk, (jnp.zeros((1, 384), jnp.float32), jnp.zeros((64, 384), jnp.float32)), unroll=True
        )
        mean = numer / total
        for i in range(3):
            attn[pl.ds(pl.multiple_of(group * 192 + 64 * i, 64), 64), lanes] = mean[:, i * 128: i * 128 + 128]
        denom[group, 0:3, lanes] = jnp.concatenate([total[:, i * 128: i * 128 + 128] for i in range(3)], axis=0)

    def unit(k):
        attend(k // 6, lax.rem(k, 6))
        for at, tokens in FORWARD_PLAN[5]:
            pl.when(k == at)(lambda tokens=tokens: run(tokens))

    repeat(12, unit)

    def out_project(b):
        block = t_dot(attn[...].astype(jnp.bfloat16), weights[:, lanes_at(b, 384)][:, 128:]).T
        proj[rows_at(b, 144), :] = block[112:256]

    repeat(8, out_project)
    hidden[...] = x[...].astype(jnp.float32) + proj[...].T
    run(FORWARD_PLAN[6])
    for spread in cat_spreads + ffn_spreads + kv_spreads:
        spread.finish()
    for spread in ffn_spreads:
        spread.wait_core()
    for k in range(1, 8):
        tiles.along_seq(k).wait_send()
    for k in range(1, 4):
        tiles.along_dp(k).wait_send()
    out_copy.wait()


def forward_call(cat, note, x, cosine, sine, limit, gate, up, down):
    vmem, anywhere = pl.BlockSpec(memory_space=pltpu.VMEM), pl.BlockSpec(memory_space=pl.ANY)
    return pl.pallas_call(
        forward_body,
        out_shape=[jax.ShapeDtypeStruct((1152, 3072), jnp.bfloat16)] * 4
        + [
            jax.ShapeDtypeStruct((16, 1152), jnp.float32),
            jax.ShapeDtypeStruct((1152, 256), jnp.bfloat16),
            jax.ShapeDtypeStruct((256, 1152), jnp.float32),
            jax.ShapeDtypeStruct((1152, 256), jnp.bfloat16),
            jax.ShapeDtypeStruct((2, 768, 1024), jnp.bfloat16),
            jax.ShapeDtypeStruct((1152, 256), jnp.float32),
            jax.ShapeDtypeStruct((6, 8, 256), jnp.float32),
        ],
        in_specs=[vmem] * 9,
        out_specs=[anywhere] * 4 + [vmem] * 7,
        scratch_shapes=[
            pltpu.VMEM((256, 1152), jnp.bfloat16),
            pltpu.VMEM((1920, 256), jnp.float32),
            pltpu.VMEM((768, 256), jnp.bfloat16),
            pltpu.VMEM((1152, 3072), jnp.bfloat16),
            pltpu.VMEM((1152, 256), jnp.float32),
            pltpu.VMEM((8, 8, 1152), jnp.float32),
            pltpu.VMEM((4, 8, 1152), jnp.float32),
            pltpu.SemaphoreType.DMA((4,)),
        ]
        + NOTE_SEMS
        + spread_sems(CAT_JOBS)
        + spread_sems(FFN_JOBS)
        + spread_sems(KV_JOBS)[:2],
        compiler_params=pltpu.CompilerParams(
            collective_id=3, has_side_effects=True, vmem_limit_bytes=48 * 1024 * 1024
        ),
        name="attention_forward",
    )(cat, note, x, cosine, sine, limit, gate, up, down)


def backward_body(
    grad_hidden, attn_in_t, wcat, keys_values, query, attn, denom, cosine, sine, limit, x, scales, small,
    grad_gate, grad_up, grad_down,
    own_gate, own_up, own_down, own_cat, grad_tokens, totals, grad_cat,
    weights, whole_kv, part_kv, turned, total, own_kv, left, grad_t, note, seq_in, dp_in, row_sum,
    load, store, kv_send, kv_recv, kv_arrived, note_a, note_b, note_c, note_d, *scratch
):
    place = position()
    d, s = mesh_place(*place)
    greet(place, True)
    sums = dict(zip(FFN_NAMES, (grad_gate, grad_up, grad_down)))
    owned = dict(zip(FFN_NAMES, (own_gate, own_up, own_down)))
    split = len(fold_scratch(FOLD_FFN, False))
    folds = [
        JobFold(place, job, j, sums[job[0]], owned[job[0]], scratch[:split], False) for j, job in enumerate(FOLD_FFN)
    ]
    cat_folds = [JobFold(place, job, j, grad_cat, own_cat, scratch[split:], True) for j, job in enumerate(FOLD_CAT)]
    tiles = Notes(place, lambda peer: note, row_sum, seq_in, dp_in, (note_a, note_b, note_c, note_d))

    def kv_fold(j, slot, row, order):
        def out(value):
            own_kv[row: row + 256, slot * 128: slot * 128 + 128] = value

        spot = kv_spot(part_kv, slot, row)
        return Fold(place, order, lambda who: spot(who), kv_arrived.at[j], (kv_send, kv_recv), j, out, kv_amount(part_kv))

    kv_folds = [kv_fold(j, *job) for j, job in enumerate(FOLD_KV)]
    steps = [
        [fold.fold.steps() for fold in cat_folds],
        [fold.fold.steps() for fold in folds],
        [fold.steps() for fold in kv_folds],
    ]

    def run(tokens):
        for token in tokens:
            steps[token // 10000][token // 100 % 100][token % 100]()

    for dy in (1, 0):
        for fold in folds:
            fold.begin(dy)

    def block_load(b):
        return pltpu.make_async_copy(wcat.at[:, lanes_at(b, 384)], weights.at[:, lanes_at(b, 384)], load.at[b])

    repeat(8, lambda b: block_load(b).start())
    kv_in = pltpu.make_async_copy(keys_values, whole_kv, load.at[8])
    kv_in.start()
    grad_t[...] = grad_hidden[...].T.astype(jnp.bfloat16)
    total[...] = jnp.zeros_like(total)

    def out_rows(b):
        return jnp.concatenate([jnp.zeros((112, 256), jnp.bfloat16), grad_t[rows_at(b, 144), :]], axis=0)

    def out_back(b):
        block_load(b).wait()
        total[...] += dot(weights[:, lanes_at(b, 384)][:, 128:], out_rows(b))

    repeat(8, out_back)
    run(BACKWARD_PLAN[0])
    kv_in.wait()
    scale = HEAD_DIMENSION ** (-0.5)

    def attend_back(slot, group):
        lanes = lanes_at(slot, 128)
        bound = three_wide(limit[:, lanes])
        wide = heads_wide(query, group, lanes)
        grads, ratios = [], []
        for i in range(3):
            rows = pl.ds(pl.multiple_of(group * 192 + 64 * i, 64), 64)
            grad = total[rows, lanes].astype(jnp.bfloat16).astype(jnp.float32)
            bottom = denom[group, i: i + 1, lanes]
            ratios.append(jnp.sum(grad * attn[rows, lanes], axis=0, keepdims=True) / bottom)
            grads.append((grad / bottom).astype(jnp.bfloat16))
        grads, ratios = jnp.concatenate(grads, axis=1), jnp.concatenate(ratios, axis=1)

        def one_chunk(chunk, sum_query):
            cols = lanes_at(chunk, 256)
            keys = whole_kv[slot, rows_at(group, 64), cols]
            values = whole_kv[slot, rows_at(group, 64, 384), cols]
            expo = probabilities(keys, wide, bound, chunk)
            grad_prob = t_dot(values, grads)
            grad_score = (expo * (grad_prob - ratios)).astype(jnp.bfloat16)
            part_kv[slot, rows_at(group, 64), cols] = (dot_t(wide, grad_score) * scale).astype(jnp.bfloat16)
            part_kv[slot, rows_at(group, 64, 384), cols] = dot_t(grads, expo.astype(jnp.bfloat16)).astype(jnp.bfloat16)
            return sum_query + dot(keys, grad_score)

        sum_query = lax.fori_loop(0, 4, one_chunk, jnp.zeros((64, 384), jnp.float32), unroll=True) * scale
        for i in range(3):
            total[pl.ds(pl.multiple_of(group * 192 + 64 * i, 64), 64), lanes] = sum_query[:, i * 128: i * 128 + 128]

    def unit(k):
        attend_back(k // 6, lax.rem(k, 6))
        for at, tokens in BACKWARD_PLAN[1]:
            pl.when(k == at)(lambda tokens=tokens: run(tokens))

    repeat(12, unit)
    run(BACKWARD_PLAN[2])

    def turn_back(ref, source, count):
        def one(h):
            rows = rows_at(h, 64)
            ref[rows, :] = rotate(source[rows, :], cosine[...], -sine[...]).astype(ref.dtype)

        repeat(count, one)

    turn_back(turned, total, 18)
    turn_back(own_kv, own_kv, 6)
    total[...] = jnp.zeros_like(total)

    def last_block(b):
        rows = jnp.concatenate(
            [
                turned[rows_at(b, 144), :],
                own_kv[rows_at(b, 48), :].astype(jnp.bfloat16),
                own_kv[rows_at(b, 48, 384), :].astype(jnp.bfloat16),
                jnp.zeros((16, 256), jnp.bfloat16),
            ],
            axis=0,
        )
        total[...] += dot(weights[:, lanes_at(b, 384)][:, :256], rows)
        slot = lax.rem(b, 2)
        out = pltpu.make_async_copy(left.at[slot], grad_cat.at[:, lanes_at(b, 384)], store.at[slot])
        pl.when(b >= 2)(lambda: out.wait())
        grad = dot_t(attn_in_t[...], rows)
        out_grad = dot_t(attn[...].astype(jnp.bfloat16), out_rows(b))
        left[slot, :, 0:128] = grad[:, :128].astype(jnp.bfloat16)
        left[slot, :, 128:256] = (grad[:, 128:] + out_grad[:, :128]).astype(jnp.bfloat16)
        left[slot, :, 256:384] = out_grad[:, 128:].astype(jnp.bfloat16)
        out.start()
        for at, tokens in BACKWARD_PLAN[3]:
            pl.when(b == at)(lambda tokens=tokens: run(tokens))

    repeat(8, last_block)
    for slot in range(2):
        pltpu.make_async_copy(left.at[slot], grad_cat.at[:, pl.ds((6 + slot) * 384, 384)], store.at[slot]).wait()
    for dy in (1, 0):
        for fold in cat_folds:
            fold.begin(dy)
    run(BACKWARD_PLAN[4])
    grad_tokens[...] = total[...].T
    note[...] = small[...]

    def finish_rows(k):
        rows = rows_at(k, 32)
        grad = grad_tokens[rows, :]
        scale_in = scales[rows, 0:1]
        normed = x[rows, :].astype(jnp.float32) * scale_in
        note[0:1, :] += jnp.sum(grad * normed, axis=0, keepdims=True)
        grad = grad * small[3:4, :]
        inner = grad - normed * jnp.mean(grad * normed, axis=-1, keepdims=True)
        grad_tokens[rows, :] = grad_hidden[rows, :] + scale_in * inner

    repeat(8, finish_rows)
    run(BACKWARD_PLAN[5])
    for k in range(1, 8):
        tiles.along_seq(k).start()
    run(BACKWARD_PLAN[6])
    tiles.wait_seq()
    seq_in[s] = note[...]
    along = seq_in[0]
    for k in range(1, 8):
        along = along + seq_in[k]
    row_sum[...] = along
    run(BACKWARD_PLAN[7])
    for k in range(1, 4):
        tiles.along_dp(k).start()
    run(BACKWARD_PLAN[8])
    tiles.wait_dp()
    dp_in[d] = row_sum[...]
    totals[...] = dp_in[0] + dp_in[1] + dp_in[2] + dp_in[3]
    for fold in folds + kv_folds + cat_folds:
        fold.finish()
    for k in range(1, 8):
        tiles.along_seq(k).wait_send()
    for k in range(1, 4):
        tiles.along_dp(k).wait_send()


def backward_call(
    grad_hidden, attn_in_t, wcat, keys_values, query, attn, denom, cosine, sine, limit, x, scales, small,
    grad_gate, grad_up, grad_down
):
    vmem, anywhere = pl.BlockSpec(memory_space=pltpu.VMEM), pl.BlockSpec(memory_space=pl.ANY)
    jobs = len(KV_JOBS)
    most = max(fold_slots(order)[1] for _, _, order in FOLD_KV)
    return pl.pallas_call(
        backward_body,
        out_shape=[
            jax.ShapeDtypeStruct((288, 384), jnp.float32),
            jax.ShapeDtypeStruct((288, 384), jnp.float32),
            jax.ShapeDtypeStruct((144, 768), jnp.float32),
            jax.ShapeDtypeStruct((288, 384), jnp.float32),
            jax.ShapeDtypeStruct((256, 1152), jnp.float32),
            jax.ShapeDtypeStruct((8, 1152), jnp.float32),
            jax.ShapeDtypeStruct((1152, 3072), jnp.bfloat16),
        ],
        in_specs=[vmem, vmem, anywhere, anywhere] + [vmem] * 9 + [anywhere] * 3,
        out_specs=[vmem] * 6 + [anywhere],
        scratch_shapes=[
            pltpu.VMEM((1152, 3072), jnp.bfloat16),
            pltpu.VMEM((2, 768, 1024), jnp.bfloat16),
            pltpu.VMEM((2, 768, 1024), jnp.bfloat16),
            pltpu.VMEM((1152, 256), jnp.bfloat16),
            pltpu.VMEM((1152, 256), jnp.float32),
            pltpu.VMEM((768, 256), jnp.float32),
            pltpu.VMEM((2, 1152, 384), jnp.bfloat16),
            pltpu.VMEM((1152, 256), jnp.bfloat16),
            pltpu.VMEM((8, 1152), jnp.float32),
            pltpu.VMEM((8, 8, 1152), jnp.float32),
            pltpu.VMEM((4, 8, 1152), jnp.float32),
            pltpu.VMEM((8, 1152), jnp.float32),
            pltpu.SemaphoreType.DMA((9,)),
            pltpu.SemaphoreType.DMA((2,)),
            pltpu.SemaphoreType.DMA((jobs,)),
            pltpu.SemaphoreType.DMA((jobs, most)),
            pltpu.VMEM((jobs, most, 256, 128), jnp.bfloat16),
        ]
        + NOTE_SEMS
        + fold_scratch(FOLD_FFN, False)
        + fold_scratch(FOLD_CAT, True),
        compiler_params=pltpu.CompilerParams(
            collective_id=4, has_side_effects=True, vmem_limit_bytes=VMEM_MOST
        ),
        name="attention_backward",
    )(
        grad_hidden, attn_in_t, wcat, keys_values, query, attn, denom, cosine, sine, limit, x, scales, small,
        grad_gate, grad_up, grad_down,
    )


def per_device_fast(
    tokens, teacher, lengths, w_query, key_weight, value_weight, w_out, w_gate, w_up, w_down, gain_attn, gain_ffn
):
    slots, part, width = tokens.shape
    rows = slots * part
    total_tokens = slots * lax.axis_size("dp") * part * lax.axis_size("seq")
    positions = lax.axis_index("seq") * part + jnp.arange(part, dtype=jnp.int32)
    cosine, sine = rope_tables(positions, HEAD_DIMENSION)
    cosine_t = jnp.concatenate([cosine.T] * slots, axis=1)
    sine_t = jnp.concatenate([sine.T] * slots, axis=1)
    limit = jnp.minimum(positions[None, :], lengths[:, None] - 1).reshape(1, rows)
    note = lax.dynamic_update_slice(
        jnp.zeros((8, width), jnp.float32),
        jnp.stack([gain_attn, gain_ffn]).astype(jnp.float32),
        (0, lax.axis_index("seq") * gain_attn.shape[0]),
    )
    note = note.at[2].set(jnp.sum(lengths).astype(jnp.float32))
    x_b = tokens.reshape(rows, width)
    gate_w, up_w, down_t, cat, notes, attn_in_t, hidden, query, keys_values, attn, denom = forward_call(
        jnp.concatenate([w_query, key_weight, value_weight, w_out], axis=1),
        note, x_b, cosine_t, sine_t, limit, w_gate, w_up, w_down.T,
    )
    gain_a, gain_f = notes[0:1], notes[1:2]
    count = notes[10, 0]
    factor = total_tokens / count
    r2 = lax.rsqrt(jnp.mean(hidden * hidden, axis=-1, keepdims=True) + norm_eps)
    n2 = hidden * r2
    ffn_in = (n2 * gain_f).astype(jnp.bfloat16)
    gate = dot(ffn_in, gate_w)
    up = dot(ffn_in, up_w)
    sig = jax.nn.sigmoid(gate)
    hid = (gate * sig * up).astype(jnp.bfloat16)
    valid = (positions[None, :] < lengths[:, None]).reshape(rows, 1)
    out_f = jnp.where(valid, hidden + dot_t(hid, down_t), 0.0)
    diff = jnp.where(valid, out_f - teacher.reshape(rows, width).astype(jnp.float32), 0.0)
    squares = jnp.sum(diff * diff)
    cot = factor * diff
    cot_b = cot.astype(jnp.bfloat16)
    grad_hid = dot(cot_b, down_t)
    grad_gate_b = (grad_hid * up * sig * (1.0 + gate * (1.0 - sig))).astype(jnp.bfloat16)
    grad_up_b = (grad_hid * gate * sig).astype(jnp.bfloat16)
    core = lax.rem(lax.axis_index("dp"), 2)

    def swap(value):
        return lax.ppermute(value, "dp", [(0, 1), (1, 0), (2, 3), (3, 2)])

    def lane(value, which):
        parts = value.reshape(rows, 2, 2, value.shape[1] // 4)
        return lax.dynamic_index_in_dim(parts, which, 2, keepdims=False).reshape(rows, -1)

    def over_cores(value):
        return jnp.concatenate([value, swap(value)], axis=0)

    def lane_over_cores(value):
        return jnp.concatenate([lane(value, core), swap(lane(value, 1 - core))], axis=0)

    ffn_lane = lane_over_cores(ffn_in)
    grad_down_t = t_dot(over_cores(cot_b), lane_over_cores(hid)).astype(jnp.bfloat16)
    grad_gate_w = t_dot(ffn_lane, over_cores(grad_gate_b)).astype(jnp.bfloat16)
    grad_up_w = t_dot(ffn_lane, over_cores(grad_up_b)).astype(jnp.bfloat16)
    grad_ffn_in = dot_t(grad_gate_b, gate_w) + dot_t(grad_up_b, up_w)
    part_gain_f = jnp.sum(grad_ffn_in * n2, axis=0)
    gn = grad_ffn_in * gain_f
    grad_hidden = cot + r2 * (gn - n2 * jnp.mean(gn * n2, axis=-1, keepdims=True))
    x = x_b.astype(jnp.float32)
    r1 = lax.rsqrt(jnp.mean(x * x, axis=-1, keepdims=True) + norm_eps)
    small = jnp.concatenate(
        [
            jnp.zeros((1, width), jnp.float32),
            part_gain_f[None, :],
            jnp.broadcast_to(squares, (1, width)),
            gain_a,
            jnp.zeros((4, width), jnp.float32),
        ],
        axis=0,
    )
    own_gate, own_up, own_down_t, own_cat, grad_tokens, totals, _ = backward_call(
        grad_hidden, attn_in_t, cat, keys_values, query, attn, denom, cosine_t, sine_t, limit,
        x_b, jnp.broadcast_to(r1, (rows, 128)), small, grad_gate_w, grad_up_w, grad_down_t,
    )
    own_gains = lax.dynamic_slice(
        totals, (0, lax.axis_index("seq") * gain_attn.shape[0]), (2, gain_attn.shape[0])
    )
    return (
        out_f.astype(jnp.bfloat16).reshape(tokens.shape),
        totals[2, 0] / count,
        grad_tokens.reshape(tokens.shape),
        own_cat[:, :144],
        own_cat[:, 144:192],
        own_cat[:, 192:240],
        own_cat[:, 240:],
        own_gate,
        own_up,
        own_down_t.T,
        own_gains[0],
        own_gains[1],
    )


def solution(mesh):
    placed = (
        P("dp", "seq", None),
        P("dp", "seq", None),
        P("dp"),
        P("dp", "seq"),
        P("dp", "seq"),
        P("dp", "seq"),
        P("dp", "seq"),
        P("dp", "seq"),
        P("dp", "seq"),
        P("dp", "seq"),
        P("seq"),
        P("seq"),
    )
    fits = mesh.shape["dp"] == 4 and mesh.shape["seq"] == 8
    return jax.shard_map(
        per_device_fast if fits else per_device,
        mesh=mesh,
        in_specs=placed,
        out_specs=(
            P("dp", "seq", None),
            P(),
            P("dp", "seq", None),
            P("dp", "seq"),
            P("dp", "seq"),
            P("dp", "seq"),
            P("dp", "seq"),
            P("dp", "seq"),
            P("dp", "seq"),
            P("dp", "seq"),
            P("seq"),
            P("seq"),
        ),
        check_vma=False,
    )
```

```python
import functools
import math

import jax
import jax.numpy as jnp
from jax import lax
from jax.experimental import pallas as pl
from jax.experimental.pallas import tpu as pltpu
from jax.sharding import PartitionSpec as P

QUERY_HEADS = 18
KEY_VALUE_HEADS = 6
HEAD_DIMENSION = 64


norm_eps = 1e-05
rope_base = 10000.0


def rope_tables(positions, head_width):
    half_width = head_width // 2
    exponents = jnp.arange(half_width, dtype=jnp.float32) * (2.0 / head_width)
    angles = positions.astype(jnp.float32)[:, None] * (rope_base ** (-exponents))[None, :]
    return (jnp.cos(angles), jnp.sin(angles))


def apply_rotary(value_rows, cosine_table, sine_table):
    half_width = value_rows.shape[-1] // 2
    front_half = value_rows[..., :half_width]
    back_half = value_rows[..., half_width:]
    cos_wide = cosine_table[:, None, :]
    sin_wide = sine_table[:, None, :]
    return jnp.concatenate(
        [
            front_half * cos_wide - back_half * sin_wide,
            front_half * sin_wide + back_half * cos_wide,
        ],
        axis=-1,
    )


def allowed_mask(query_pos, key_pos, live_len):
    causal = key_pos[None, :] <= query_pos[:, None]
    present = key_pos[None, :] < live_len[:, None]
    return (causal[None, :, :] & present[:, None, :])[:, None, None, :, :]


def over_blocks(piece_len, unit_len, step_fn, running):
    block_length = math.gcd(piece_len, unit_len * max(1, 512 // unit_len))
    number_of_blocks = piece_len // block_length

    def loop_step(block_number, state):
        return step_fn(state, block_number * block_length, block_length)

    return lax.fori_loop(0, number_of_blocks, loop_step, running)


def collect(shards):
    wide = (
        lax.all_gather(shards[0], "seq", axis=1, tiled=True),
        lax.all_gather(shards[1], "seq", axis=1, tiled=True),
        lax.all_gather(shards[2], "seq", axis=1, tiled=True),
        lax.all_gather(shards[3], "seq", axis=1, tiled=True),
        lax.all_gather(shards[4], "seq", axis=1, tiled=True),
        lax.all_gather(shards[5], "seq", axis=1, tiled=True),
        lax.all_gather(shards[6], "seq", axis=1, tiled=True),
        lax.all_gather(shards[7], "seq", axis=0, tiled=True),
        lax.all_gather(shards[8], "seq", axis=0, tiled=True),
    )
    whole = (
        lax.all_gather(wide[0], "dp", axis=0, tiled=True),
        lax.all_gather(wide[1], "dp", axis=0, tiled=True),
        lax.all_gather(wide[2], "dp", axis=0, tiled=True),
        lax.all_gather(wide[3], "dp", axis=0, tiled=True),
        lax.all_gather(wide[4], "dp", axis=0, tiled=True),
        lax.all_gather(wide[5], "dp", axis=0, tiled=True),
        lax.all_gather(wide[6], "dp", axis=0, tiled=True),
    )
    return tuple(whole) + (wide[7], wide[8])


def reduce_grads(grad_sums):
    summed = (
        lax.psum_scatter(grad_sums[0], "seq", scatter_dimension=1, tiled=True),
        lax.psum_scatter(grad_sums[1], "seq", scatter_dimension=1, tiled=True),
        lax.psum_scatter(grad_sums[2], "seq", scatter_dimension=1, tiled=True),
        lax.psum_scatter(grad_sums[3], "seq", scatter_dimension=1, tiled=True),
        lax.psum_scatter(grad_sums[4], "seq", scatter_dimension=1, tiled=True),
        lax.psum_scatter(grad_sums[5], "seq", scatter_dimension=1, tiled=True),
        lax.psum_scatter(grad_sums[6], "seq", scatter_dimension=1, tiled=True),
        lax.psum_scatter(grad_sums[7], "seq", scatter_dimension=0, tiled=True),
        lax.psum_scatter(grad_sums[8], "seq", scatter_dimension=0, tiled=True),
    )
    owned = (
        lax.psum_scatter(summed[0], "dp", scatter_dimension=0, tiled=True),
        lax.psum_scatter(summed[1], "dp", scatter_dimension=0, tiled=True),
        lax.psum_scatter(summed[2], "dp", scatter_dimension=0, tiled=True),
        lax.psum_scatter(summed[3], "dp", scatter_dimension=0, tiled=True),
        lax.psum_scatter(summed[4], "dp", scatter_dimension=0, tiled=True),
        lax.psum_scatter(summed[5], "dp", scatter_dimension=0, tiled=True),
        lax.psum_scatter(summed[6], "dp", scatter_dimension=0, tiled=True),
    )
    return (tuple(owned), summed[7], summed[8])


def forward_slot(weights, tok_part, live_len, query_pos, cosine_table, sine_table):
    (
        full_query,
        full_key,
        full_value,
        full_out,
        full_gate,
        full_up,
        full_down,
        full_gain_attn,
        full_gain_ffn,
    ) = weights
    slot_position, stretched_length, model_width = tok_part.shape
    number_of_rows = slot_position * stretched_length
    query_group = QUERY_HEADS // KEY_VALUE_HEADS
    scale = HEAD_DIMENSION ** (-0.5)
    tok_float = tok_part.astype(jnp.float32).reshape(number_of_rows, model_width)
    inv_first = lax.rsqrt(jnp.mean(tok_float * tok_float, axis=-1, keepdims=True) + norm_eps)
    normed_first = tok_float * inv_first
    attention_input = (normed_first * full_gain_attn.astype(jnp.float32)).astype(jnp.bfloat16)
    unrotated_query = jnp.dot(
        attention_input, full_query, preferred_element_type=jnp.float32
    ).reshape(slot_position, stretched_length, QUERY_HEADS, HEAD_DIMENSION)
    unrotated_key = jnp.dot(attention_input, full_key, preferred_element_type=jnp.float32).reshape(
        slot_position, stretched_length, KEY_VALUE_HEADS, HEAD_DIMENSION
    )
    value_block = (
        jnp.dot(attention_input, full_value, preferred_element_type=jnp.float32)
        .astype(jnp.bfloat16)
        .reshape(slot_position, stretched_length, KEY_VALUE_HEADS * HEAD_DIMENSION)
    )
    query_b = (
        apply_rotary(unrotated_query, cosine_table, sine_table)
        .astype(jnp.bfloat16)
        .reshape(slot_position, stretched_length, KEY_VALUE_HEADS, query_group, HEAD_DIMENSION)
    )
    key_block = (
        apply_rotary(unrotated_key, cosine_table, sine_table)
        .astype(jnp.bfloat16)
        .reshape(slot_position, stretched_length, KEY_VALUE_HEADS * HEAD_DIMENSION)
    )
    empty_denominator = jnp.zeros(
        (slot_position, KEY_VALUE_HEADS, query_group, stretched_length), jnp.float32
    )
    empty_numerator = jnp.zeros(
        (slot_position, KEY_VALUE_HEADS, query_group, stretched_length, HEAD_DIMENSION), jnp.float32
    )
    key_piece = lax.all_gather(key_block, "seq", axis=1, tiled=True)
    value_piece = lax.all_gather(value_block, "seq", axis=1, tiled=True)

    def one_block(partial_value, offset, block_length):
        denominator, numerator = partial_value
        key_blk = lax.dynamic_slice_in_dim(key_piece, offset, block_length, 1).reshape(
            slot_position, block_length, KEY_VALUE_HEADS, HEAD_DIMENSION
        )
        value_blk = lax.dynamic_slice_in_dim(value_piece, offset, block_length, 1).reshape(
            slot_position, block_length, KEY_VALUE_HEADS, HEAD_DIMENSION
        )
        allowed = allowed_mask(
            query_pos, offset + jnp.arange(block_length, dtype=jnp.int32), live_len
        )
        scores = (
            jnp.einsum("schgd,snhd->shgcn", query_b, key_blk, preferred_element_type=jnp.float32)
            * scale
        )
        exp_scores = jnp.where(allowed, jnp.exp(scores), 0.0)
        denominator = denominator + jnp.sum(exp_scores, axis=-1)
        numerator = numerator + jnp.einsum(
            "shgcn,snhd->shgcd",
            exp_scores.astype(jnp.bfloat16),
            value_blk,
            preferred_element_type=jnp.float32,
        )
        return (denominator, numerator)

    denominator, numerator = over_blocks(
        key_piece.shape[1], stretched_length, one_block, (empty_denominator, empty_numerator)
    )
    attn_float = jnp.transpose(numerator / denominator[..., None], (0, 3, 1, 2, 4)).reshape(
        number_of_rows, QUERY_HEADS * HEAD_DIMENSION
    )
    attn_b = attn_float.astype(jnp.bfloat16)
    hidden = tok_float + jnp.dot(attn_b, full_out, preferred_element_type=jnp.float32)
    inv_second = lax.rsqrt(jnp.mean(hidden * hidden, axis=-1, keepdims=True) + norm_eps)
    normed_second = hidden * inv_second
    ffn_in = (normed_second * full_gain_ffn.astype(jnp.float32)).astype(jnp.bfloat16)
    gate_proj = jnp.dot(ffn_in, full_gate, preferred_element_type=jnp.float32)
    up_proj = jnp.dot(ffn_in, full_up, preferred_element_type=jnp.float32)
    hid_b = (jax.nn.silu(gate_proj) * up_proj).astype(jnp.bfloat16)
    valid_rows = (query_pos[None, :] < live_len[:, None]).reshape(number_of_rows, 1)
    out_float = jnp.where(
        valid_rows, hidden + jnp.dot(hid_b, full_down, preferred_element_type=jnp.float32), 0.0
    )
    saved = (
        attention_input,
        inv_first,
        normed_first,
        query_b,
        key_block,
        value_block,
        attn_float,
        attn_b,
        denominator,
        normed_second,
        inv_second,
        ffn_in,
        gate_proj,
        up_proj,
        hid_b,
    )
    return (out_float, valid_rows, saved)


def backward_slot(weights, saved, cotangent, live_len, query_pos, cosine_table, sine_table):
    (
        full_query,
        full_key,
        full_value,
        full_out,
        full_gate,
        full_up,
        full_down,
        full_gain_attn,
        full_gain_ffn,
    ) = weights
    (
        attention_input,
        inv_first,
        normed_first,
        query_b,
        key_block,
        value_block,
        attn_float,
        attn_b,
        denominator,
        normed_second,
        inv_second,
        ffn_in,
        gate_proj,
        up_proj,
        hid_b,
    ) = saved
    slot_position = query_b.shape[0]
    stretched_length = query_b.shape[1]
    number_of_rows = slot_position * stretched_length
    query_group = QUERY_HEADS // KEY_VALUE_HEADS
    scale = HEAD_DIMENSION ** (-0.5)
    cot_b = cotangent.astype(jnp.bfloat16)
    grad_down = jnp.einsum("rf,rd->fd", hid_b, cot_b, preferred_element_type=jnp.float32)
    grad_hid = jnp.einsum("rd,fd->rf", cot_b, full_down, preferred_element_type=jnp.float32)
    sigmoid_gate = jax.nn.sigmoid(gate_proj)
    grad_gate_b = (
        grad_hid * up_proj * sigmoid_gate * (1.0 + gate_proj * (1.0 - sigmoid_gate))
    ).astype(jnp.bfloat16)
    grad_up_b = (grad_hid * gate_proj * sigmoid_gate).astype(jnp.bfloat16)
    grad_gate = jnp.einsum("rd,rf->df", ffn_in, grad_gate_b, preferred_element_type=jnp.float32)
    grad_up = jnp.einsum("rd,rf->df", ffn_in, grad_up_b, preferred_element_type=jnp.float32)
    grad_ffn_in = jnp.einsum(
        "rf,df->rd", grad_gate_b, full_gate, preferred_element_type=jnp.float32
    ) + jnp.einsum("rf,df->rd", grad_up_b, full_up, preferred_element_type=jnp.float32)
    grad_gain_ffn = jnp.sum(grad_ffn_in * normed_second, axis=0)
    grad_normed = grad_ffn_in * full_gain_ffn.astype(jnp.float32)
    grad_hidden = cotangent + inv_second * (
        grad_normed - normed_second * jnp.mean(grad_normed * normed_second, axis=-1, keepdims=True)
    )
    grad_proj_b = grad_hidden.astype(jnp.bfloat16)
    grad_out = jnp.einsum("rq,rd->qd", attn_b, grad_proj_b, preferred_element_type=jnp.float32)
    grad_attn_b = jnp.einsum(
        "rd,qd->rq", grad_proj_b, full_out, preferred_element_type=jnp.float32
    ).astype(jnp.bfloat16)
    den_rows = jnp.transpose(denominator, (0, 3, 1, 2)).reshape(number_of_rows, QUERY_HEADS)
    grad_heads_float = grad_attn_b.astype(jnp.float32).reshape(
        number_of_rows, QUERY_HEADS, HEAD_DIMENSION
    )
    softmax_ratio = (
        jnp.sum(
            grad_heads_float * attn_float.reshape(number_of_rows, QUERY_HEADS, HEAD_DIMENSION),
            axis=-1,
        )
        / den_rows
    ).reshape(slot_position, stretched_length, QUERY_HEADS)
    scaled_gradient = (
        (grad_heads_float / den_rows[..., None])
        .astype(jnp.bfloat16)
        .reshape(slot_position, stretched_length, QUERY_HEADS * HEAD_DIMENSION)
    )
    ratio_all = lax.all_gather(softmax_ratio, "seq", axis=1, tiled=True)
    head_gradient = scaled_gradient.reshape(
        slot_position, stretched_length, KEY_VALUE_HEADS, query_group, HEAD_DIMENSION
    )
    local_softmax_ratio = jnp.transpose(
        softmax_ratio.reshape(slot_position, stretched_length, KEY_VALUE_HEADS, query_group),
        (0, 2, 3, 1),
    )[..., None]
    empty_query = jnp.zeros(
        (slot_position, KEY_VALUE_HEADS, query_group, stretched_length, HEAD_DIMENSION), jnp.float32
    )
    key_piece = lax.all_gather(key_block, "seq", axis=1, tiled=True)
    value_piece = lax.all_gather(value_block, "seq", axis=1, tiled=True)

    def one_block(partial_value, offset, block_length):
        key_blk = lax.dynamic_slice_in_dim(key_piece, offset, block_length, 1).reshape(
            slot_position, block_length, KEY_VALUE_HEADS, HEAD_DIMENSION
        )
        value_blk = lax.dynamic_slice_in_dim(value_piece, offset, block_length, 1).reshape(
            slot_position, block_length, KEY_VALUE_HEADS, HEAD_DIMENSION
        )
        allowed = allowed_mask(
            query_pos, offset + jnp.arange(block_length, dtype=jnp.int32), live_len
        )
        scores = (
            jnp.einsum("schgd,snhd->shgcn", query_b, key_blk, preferred_element_type=jnp.float32)
            * scale
        )
        exp_scores = jnp.where(allowed, jnp.exp(scores), 0.0)
        grad_prob = jnp.einsum(
            "schgd,snhd->shgcn", head_gradient, value_blk, preferred_element_type=jnp.float32
        )
        grad_score = (exp_scores * (grad_prob - local_softmax_ratio)).astype(jnp.bfloat16)
        return (
            partial_value
            + jnp.einsum(
                "shgcn,snhd->shgcd", grad_score, key_blk, preferred_element_type=jnp.float32
            )
            * scale
        )

    grad_query = over_blocks(key_piece.shape[1], stretched_length, one_block, empty_query)
    query_flat = query_b.reshape(slot_position, stretched_length, QUERY_HEADS * HEAD_DIMENSION)
    per_head_keys = key_block.reshape(
        slot_position, stretched_length, KEY_VALUE_HEADS, HEAD_DIMENSION
    )
    per_head_values = value_block.reshape(
        slot_position, stretched_length, KEY_VALUE_HEADS, HEAD_DIMENSION
    )
    empty_key_value = jnp.zeros(
        (slot_position, KEY_VALUE_HEADS, stretched_length, HEAD_DIMENSION), jnp.float32
    )
    query_piece = lax.all_gather(query_flat, "seq", axis=1, tiled=True)
    grad_piece = lax.all_gather(scaled_gradient, "seq", axis=1, tiled=True)

    def one_block(partial_value, offset, block_length):
        grad_key, value_gradient = partial_value
        query_blk = lax.dynamic_slice_in_dim(query_piece, offset, block_length, 1).reshape(
            slot_position, block_length, KEY_VALUE_HEADS, query_group, HEAD_DIMENSION
        )
        grad_blk = lax.dynamic_slice_in_dim(grad_piece, offset, block_length, 1).reshape(
            slot_position, block_length, KEY_VALUE_HEADS, query_group, HEAD_DIMENSION
        )
        ratio_blk = lax.dynamic_slice_in_dim(ratio_all, offset, block_length, 1).reshape(
            slot_position, block_length, KEY_VALUE_HEADS, query_group
        )
        ratio_blk = jnp.transpose(ratio_blk, (0, 2, 3, 1))[..., None]
        remote_pos = offset + jnp.arange(block_length, dtype=jnp.int32)
        allowed = allowed_mask(remote_pos, query_pos, live_len)
        scores = (
            jnp.einsum(
                "snhgd,schd->shgnc", query_blk, per_head_keys, preferred_element_type=jnp.float32
            )
            * scale
        )
        exp_scores = jnp.where(allowed, jnp.exp(scores), 0.0)
        value_gradient = value_gradient + jnp.einsum(
            "shgnc,snhgd->shcd",
            exp_scores.astype(jnp.bfloat16),
            grad_blk,
            preferred_element_type=jnp.float32,
        )
        grad_prob = jnp.einsum(
            "snhgd,schd->shgnc", grad_blk, per_head_values, preferred_element_type=jnp.float32
        )
        grad_score = (exp_scores * (grad_prob - ratio_blk)).astype(jnp.bfloat16)
        grad_key = (
            grad_key
            + jnp.einsum(
                "shgnc,snhgd->shcd", grad_score, query_blk, preferred_element_type=jnp.float32
            )
            * scale
        )
        return (grad_key, value_gradient)

    grad_key, value_gradient = over_blocks(
        query_piece.shape[1], stretched_length, one_block, (empty_key_value, empty_key_value)
    )
    grad_query = jnp.transpose(grad_query, (0, 3, 1, 2, 4)).reshape(
        slot_position, stretched_length, QUERY_HEADS, HEAD_DIMENSION
    )
    grad_query_b = (
        apply_rotary(grad_query, cosine_table, -sine_table)
        .astype(jnp.bfloat16)
        .reshape(number_of_rows, QUERY_HEADS * HEAD_DIMENSION)
    )
    grad_key_b = (
        apply_rotary(jnp.transpose(grad_key, (0, 2, 1, 3)), cosine_table, -sine_table)
        .astype(jnp.bfloat16)
        .reshape(number_of_rows, KEY_VALUE_HEADS * HEAD_DIMENSION)
    )
    grad_value_b = (
        jnp.transpose(value_gradient, (0, 2, 1, 3))
        .astype(jnp.bfloat16)
        .reshape(number_of_rows, KEY_VALUE_HEADS * HEAD_DIMENSION)
    )
    grad_wq = jnp.einsum(
        "rd,rq->dq", attention_input, grad_query_b, preferred_element_type=jnp.float32
    )
    grad_wk = jnp.einsum(
        "rd,rq->dq", attention_input, grad_key_b, preferred_element_type=jnp.float32
    )
    grad_wv = jnp.einsum(
        "rd,rq->dq", attention_input, grad_value_b, preferred_element_type=jnp.float32
    )
    grad_attn_in = jnp.einsum(
        "rq,dq->rd", grad_query_b, full_query, preferred_element_type=jnp.float32
    )
    grad_attn_in = grad_attn_in + jnp.einsum(
        "rq,dq->rd", grad_key_b, full_key, preferred_element_type=jnp.float32
    )
    grad_attn_in = grad_attn_in + jnp.einsum(
        "rq,dq->rd", grad_value_b, full_value, preferred_element_type=jnp.float32
    )
    grad_gain_attn = jnp.sum(grad_attn_in * normed_first, axis=0)
    grad_first = grad_attn_in * full_gain_attn.astype(jnp.float32)
    grad_tokens = grad_hidden + inv_first * (
        grad_first - normed_first * jnp.mean(grad_first * normed_first, axis=-1, keepdims=True)
    )
    return (
        (
            grad_wq,
            grad_wk,
            grad_wv,
            grad_out,
            grad_gate,
            grad_up,
            grad_down,
            grad_gain_attn,
            grad_gain_ffn,
        ),
        grad_tokens,
    )


def per_device(
    tokens,
    teacher,
    lengths,
    w_query,
    key_weight,
    value_weight,
    w_out,
    w_gate,
    w_up,
    w_down,
    gain_attn,
    gain_ffn,
):
    shards = (w_query, key_weight, value_weight, w_out, w_gate, w_up, w_down, gain_attn, gain_ffn)
    slot_count, stretched_length, model_width = tokens.shape
    total_tokens = slot_count * lax.axis_size("dp") * stretched_length * lax.axis_size("seq")
    query_pos = lax.axis_index("seq") * stretched_length + jnp.arange(
        stretched_length, dtype=jnp.int32
    )
    cosine_table, sine_table = rope_tables(query_pos, HEAD_DIMENSION)
    out_rows = []
    stored = []
    differences = []
    squares_local = jnp.zeros((), jnp.float32)
    count_local = jnp.zeros((), jnp.float32)
    for micro in range(slot_count):
        weights = collect(shards)
        live_len = lengths[micro : micro + 1]
        out_float, valid_rows, saved = forward_slot(
            weights, tokens[micro : micro + 1], live_len, query_pos, cosine_table, sine_table
        )
        teach_float = teacher[micro].astype(jnp.float32)
        difference = jnp.where(valid_rows, out_float - teach_float, 0.0)
        squares_local = squares_local + jnp.sum(difference * difference)
        count_local = count_local + jnp.sum(valid_rows.astype(jnp.float32))
        out_rows.append(out_float.astype(jnp.bfloat16).reshape(1, stretched_length, model_width))
        stored.append(saved)
        differences.append(difference)
    loss_sum, count_sum = lax.psum((squares_local, count_local), ("dp", "seq"))
    loss = loss_sum / count_sum
    factor = total_tokens / count_sum
    grad_sums = None
    token_grads = []
    for micro in range(slot_count):
        weights = collect(shards)
        grads, grad_tokens = backward_slot(
            weights,
            stored[micro],
            factor * differences[micro],
            lengths[micro : micro + 1],
            query_pos,
            cosine_table,
            sine_table,
        )
        grad_sums = grads if grad_sums is None else jax.tree.map(jnp.add, grad_sums, grads)
        token_grads.append(grad_tokens.reshape(1, stretched_length, model_width))
    owned, gain_part_attn, gain_part_ffn = reduce_grads(grad_sums)
    gain_totals = lax.psum((gain_part_attn, gain_part_ffn), "dp")
    output = jnp.concatenate(out_rows, axis=0)
    tokens_grad = jnp.concatenate(token_grads, axis=0)
    return (
        output,
        loss,
        tokens_grad,
        owned[0],
        owned[1],
        owned[2],
        owned[3],
        owned[4],
        owned[5],
        owned[6],
        gain_totals[0],
        gain_totals[1],
    )


MESH_ID = pl.DeviceIdType.MESH
VMEM_MOST = 64 * 1024 * 1024 - 128 * 1024


class Place(tuple):
    def with_line(self):
        z = self[2]
        self.line = (0,) + tuple(pick(z, v) for v in ((1, -1, -1, -1), (2, 1, 1, -2), (3, 2, -2, -3)))
        self.sign = (0,) + tuple(jnp.where(offset > 0, 1, -1) for offset in self.line[1:])
        return self


def position():
    row = lax.axis_index("dp")
    column = lax.axis_index("seq")
    return Place((lax.rem(column, 2), row // 2, column // 2, lax.rem(row, 2))).with_line()


def mesh_place(x, y, z, c):
    return (2 * y + c, 2 * z + x)


def step_to(place, axis, sign=1):
    x, y, z, c = place
    if axis == "x":
        return (1 - x, y, z, c)
    if axis == "y":
        return (x, 1 - y, z, c)
    if axis == "z":
        return (x, y, z + sign, c)
    return (x, y, z, 1 - c)


def pick(z, values):
    return sum(jnp.where(z == i, v, 0) for i, v in enumerate(values) if v)


def shifted(place, rel):
    x, y, z, c = place
    dx, dy, rank = rel
    return ((1 - x) if dx else x, (1 - y) if dy else y, z + place.line[rank], c)


def on_line(z):
    return jnp.logical_and(z >= 0, z < 4)


def greet(place, lines):
    x, y, z, c = place
    d, s = mesh_place(*place)
    barrier = pltpu.get_barrier_semaphore()

    def signal(who):
        pl.semaphore_signal(barrier, inc=1, device_id=who, device_id_type=MESH_ID)

    if lines:
        for k in range(1, 8):
            signal((d, lax.rem(s + k, 8)))
        for k in range(1, 4):
            signal((lax.rem(d + k, 4), s))
        pl.semaphore_wait(barrier, 10)
        return
    for axis in "xyc":
        signal(mesh_place(*step_to(place, axis)))
    pl.when(z < 3)(lambda: signal(mesh_place(x, y, z + 1, c)))
    pl.when(z > 0)(lambda: signal(mesh_place(x, y, z - 1, c)))
    pl.semaphore_wait(barrier, 3 + jnp.where(z > 0, 1, 0) + jnp.where(z < 3, 1, 0))


def wait_bytes(region, sem):
    pltpu.make_async_copy(region, region, sem).wait()


def spread_order(order):
    held = [((0, 0, 0), -1)]
    for level, axis in enumerate(order):
        new = []
        if axis == "z":
            new = [((rel[0], rel[1], rank), level) for rank in (1, 2, 3) for rel, _ in held]
        else:
            new = [((1, rel[1], rel[2]) if axis == "x" else (rel[0], 1, rel[2]), level) for rel, _ in held]
        held = held + new
    return held


class Spread:
    def __init__(self, place, order, own, spot, sems, job, pair=None, amount=None):
        self.place, self.order, self.own, self.spot = place, order, own, spot
        self.recv, self.send, self.recv_core, self.send_core = sems
        self.job, self.pair, self.amount = job, pair, amount
        self.pieces = spread_order(order)

    def number(self, who):
        x, y, z, _ = who
        return z * 4 + y * 2 + x

    def go(self, rel, level, target):
        who = shifted(self.place, rel)
        pltpu.make_async_remote_copy(
            src_ref=self.own if level < 0 else self.spot(who),
            dst_ref=self.spot(who),
            send_sem=self.send.at[self.job],
            recv_sem=self.recv.at[self.job, self.number(who)],
            device_id=mesh_place(*target),
            device_id_type=MESH_ID,
        ).start()

    def to_core(self, rel):
        who = shifted(self.place, rel)
        pltpu.make_async_remote_copy(
            src_ref=self.pair(who),
            dst_ref=self.pair(who),
            send_sem=self.send_core.at[self.job],
            recv_sem=self.recv_core.at[self.job],
            device_id=mesh_place(*step_to(self.place, "c")),
            device_id_type=MESH_ID,
        ).start()

    def steps(self):
        out = []
        arrived = set()
        z = self.place[2]
        for rel, level in self.pieces:

            def run(rel=rel, level=level):
                arrived.add(rel)
                who = shifted(self.place, rel)
                if level >= 0:
                    there = self.spot(who)
                    pltpu.make_async_copy(there, there, self.recv.at[self.job, self.number(who)]).wait()
                if level >= 0 and self.order[level] == "z":
                    on = z - self.place.sign[rel[2]]
                    pl.when(on_line(on))(lambda: self.go(rel, level, (self.place[0], self.place[1], on, self.place[3])))
                for axis in self.order[level + 1:]:
                    if axis == "z":
                        pl.when(z < 3)(lambda: self.go(rel, level, step_to(self.place, "z", 1)))
                        pl.when(z > 0)(lambda: self.go(rel, level, step_to(self.place, "z", -1)))
                    else:
                        self.go(rel, level, step_to(self.place, axis))
                if self.pair is not None and (1 - rel[0], rel[1], rel[2]) in arrived:
                    self.to_core(rel)

            out.append(run)
        return out

    def sent(self):
        total = [0, 0]
        for i, z in enumerate((0, 1)):
            for rel, level in self.pieces:
                if level >= 0 and self.order[level] == "z":
                    offset = (0, ((1, -1)[z]), ((2, 1)[z]), ((3, 2)[z]))[rel[2]]
                    on = z - (1 if offset > 0 else -1)
                    total[i] += 0 <= on < 4
                for axis in self.order[level + 1:]:
                    total[i] += (1, 2)[z] if axis == "z" else 1
        return total

    def wait_core(self):
        wait_bytes(self.amount(16), self.recv_core.at[self.job])

    def finish(self):
        ends, inner = self.sent()
        z = self.place[2]
        at_end = jnp.logical_or(z == 0, z == 3)
        pl.when(at_end)(lambda: wait_bytes(self.amount(ends), self.send.at[self.job]))
        pl.when(jnp.logical_not(at_end))(lambda: wait_bytes(self.amount(inner), self.send.at[self.job]))
        if self.pair is not None:
            wait_bytes(self.amount(16), self.send_core.at[self.job])


def fold_pieces(order):
    out = []
    for dx in (0, 1):
        for dy in (0, 1) if "y" in order else (0,):
            for rank in (0, 1, 2, 3):
                differs = {"x": dx, "y": dy, "z": rank}
                stage = next((i for i, axis in enumerate(order) if differs[axis]), len(order))
                out.append(((dx, dy, rank), stage))
    return sorted(out, key=lambda item: (item[1], -item[0][2], -item[0][0] - item[0][1]))


def fold_slots(order):
    base, starts = 0, []
    for level, axis in enumerate(order):
        starts.append(base)
        after = order[level + 1:]
        wide = (4 if "z" in after else 1) * (2 if "x" in after else 1) * (2 if "y" in after else 1)
        base += wide * 5 if axis == "z" else wide
    return starts, base


class Fold:
    def __init__(self, place, order, mine, arrived, sems, job, out, amount, ready=None):
        self.place, self.order, self.mine, self.arrived = place, order, mine, arrived
        self.send, self.recv = sems
        self.job, self.out, self.amount, self.ready = job, out, amount, ready
        self.pieces = fold_pieces(order)
        self.base, self.slots = fold_slots(order)

    def slot(self, level, rel, last):
        index = 0
        at_z = self.place[2] + self.place.line[rel[2]]
        for other in self.order[level + 1:]:
            size = 4 if other == "z" else 2
            index = index * size + (at_z if other == "z" else (rel[0] if other == "x" else rel[1]))
        if self.order[level] == "z":
            index = index * 5 + (4 if last is True else (at_z if last is False else jnp.where(last, 4, at_z)))
        return self.base[level] + index

    def take(self, mine, slot):
        there = self.arrived.at[slot]
        pltpu.make_async_copy(there, there, self.recv.at[self.job, slot]).wait()
        mine[...] = mine[...] + self.arrived[slot]

    def steps(self):
        out = []
        present = set()
        z = self.place[2]
        for rel, stage in self.pieces:

            def run(rel=rel, stage=stage):
                if self.ready is not None and rel[1] not in present:
                    present.add(rel[1])
                    self.ready(rel[1])
                mine = self.mine(shifted(self.place, rel))
                offset, sign = self.place.line[rel[2]], self.place.sign[rel[2]]
                for level in range(min(stage + 1, len(self.order))):
                    if self.order[level] == "z":
                        if level < stage:
                            pl.when(z > 0)(lambda: self.take(mine, self.slot(level, rel, False)))
                            pl.when(z < 3)(lambda: self.take(mine, self.slot(level, rel, True)))
                        else:
                            behind = z - sign
                            pl.when(on_line(behind))(lambda: self.take(mine, self.slot(level, rel, False)))
                    elif level < stage:
                        self.take(mine, self.slot(level, rel, False))
                if stage == len(self.order):
                    self.out(mine[...].astype(jnp.float32))
                    return
                axis = self.order[stage]
                if axis == "z":
                    target = (self.place[0], self.place[1], z + sign, self.place[3])
                else:
                    target = step_to(self.place, axis)
                slot = self.slot(stage, rel, offset == -1 if axis == "z" else False)
                pltpu.make_async_remote_copy(
                    src_ref=mine,
                    dst_ref=self.arrived.at[slot],
                    send_sem=self.send.at[self.job],
                    recv_sem=self.recv.at[self.job, slot],
                    device_id=mesh_place(*target),
                    device_id_type=MESH_ID,
                ).start()

            out.append(run)
        return out

    def finish(self):
        wait_bytes(self.amount(len(self.pieces) - 1), self.send.at[self.job])


CAT_JOBS = (("cat", 0, 96, "xzy"), ("cat", 96, 96, "yzx"), ("cat", 192, 96, "zxy"))
FFN_JOBS = (
    ("gate", 0, 144, "xzy"), ("up", 0, 96, "yzx"), ("down", 0, 384, "zxy"),
    ("gate", 144, 144, "xzy"), ("up", 96, 96, "yzx"), ("down", 384, 384, "zxy"), ("up", 192, 96, "zxy"),
)
KV_JOBS = tuple((slot, 256 * third, "xz" if (slot, third) == (1, 2) else "zx") for slot in (0, 1) for third in (0, 1, 2))
FOLD_FFN = tuple(job[:3] + (job[3][::-1],) for job in FFN_JOBS)
FOLD_CAT = tuple(job[:3] + (job[3][::-1],) for job in CAT_JOBS)
FOLD_KV = tuple((slot, row, order[::-1]) for slot, row, order in KV_JOBS)
FFN_NAMES = ("gate", "up", "down")


def job_shape(job):
    return (144, job[2]) if job[0] == "down" else (job[2], 384)


def piece_of(ref, job, paired=False):
    name, first, count, _ = job
    double = 2 if paired else 1

    def spot(who):
        x, y, z, c = who
        d, s = mesh_place(0 if paired else x, y, z, c)
        if name == "down":
            return ref.at[
                pl.ds(pl.multiple_of(s * 144, 16), 144 * double), pl.ds(pl.multiple_of(d * 768 + first, 128), count)
            ]
        return ref.at[
            pl.ds(pl.multiple_of(d * 288 + first, 8), count), pl.ds(pl.multiple_of(s * 384, 128), 384 * double)
        ]

    return spot


def region(ref, elements, rows, columns):
    units = elements // 2048
    wide = max(k for k in range(1, columns // 128 + 1) if units % k == 0 and units // k <= rows // 16)
    return ref.at[pl.ds(0, units // wide * 16), pl.ds(0, wide * 128)]


def amount_of(ref, job):
    rows, columns = job_shape(job)
    return lambda pieces: region(ref, pieces * rows * columns, *ref.shape)


def own_part(ref, job):
    name, first, count, _ = job
    return ref.at[:, pl.ds(first, count)] if name == "down" else ref.at[pl.ds(first, count), :]


def kv_spot(ref, slot, row):
    def spot(who):
        _, s = mesh_place(*who)
        return ref.at[slot, pl.ds(row, 256), pl.ds(pl.multiple_of(s * 128, 128), 128)]

    return spot


def kv_amount(ref):
    return lambda pieces: ref.at[0, pl.ds(0, 32 * pieces), :]


def make_spreads(place, jobs, shards, wholes, sems):
    return [
        Spread(
            place, job[3], own_part(shards[job[0]], job), piece_of(wholes[job[0]], job), sems, j,
            piece_of(wholes[job[0]], job, True), amount_of(wholes[job[0]], job),
        )
        for j, job in enumerate(jobs)
    ]


def make_kv_spreads(place, own, whole, sems):
    return [
        Spread(
            place, order, own.at[pl.ds(row, 256), pl.ds(slot * 128, 128)], kv_spot(whole, slot, row),
            (sems[0], sems[1], None, None), j, None, kv_amount(whole),
        )
        for j, (slot, row, order) in enumerate(KV_JOBS)
    ]


def spread_sems(jobs):
    n = len(jobs)
    return [
        pltpu.SemaphoreType.DMA((n, 16)), pltpu.SemaphoreType.DMA((n,)),
        pltpu.SemaphoreType.DMA((n,)), pltpu.SemaphoreType.DMA((n,)),
    ]


def fold_scratch(jobs, paired):
    n = len(jobs)
    most = max(fold_slots(job[3])[1] for job in jobs)
    scratch = [
        pltpu.SemaphoreType.DMA((n,)), pltpu.SemaphoreType.DMA((n, most)),
        pltpu.SemaphoreType.DMA((n, 2)), pltpu.SemaphoreType.DMA((n, 2)), pltpu.SemaphoreType.DMA((n, 2)),
    ]
    for job in jobs:
        rows, columns = job_shape(job)
        block = (2, 1152, columns) if job[0] == "down" else (2, rows, 3072)
        scratch += [
            pltpu.VMEM(block, jnp.bfloat16), pltpu.VMEM((fold_slots(job[3])[1], rows, columns), jnp.bfloat16)
        ]
        scratch += [pltpu.VMEM(block, jnp.bfloat16)] if paired else []
    return scratch


class JobFold:
    def __init__(self, place, job, j, sums, owned, scratch, paired):
        self.place, self.job, self.j, self.sums, self.paired = place, job, j, sums, paired
        send, recv, self.load_sem, self.core_send, self.core_recv = scratch[:5]
        each = 3 if paired else 2
        self.acc, arrived = scratch[5 + each * j: 7 + each * j]
        self.other = scratch[7 + each * j] if paired else None
        name, first, count, order = job

        def mine(who):
            x, y, z, c = who
            s = 2 * z + x
            if name == "down":
                return self.acc.at[y, pl.ds(pl.multiple_of(s * 144, 16), 144), :]
            return self.acc.at[y, :, pl.ds(pl.multiple_of(s * 384, 128), 384)]

        def out(value):
            if name == "down":
                owned[:, first: first + count] = value
            else:
                owned[first: first + count, :] = value

        self.fold = Fold(place, order, mine, arrived, (send, recv), j, out, amount_of(sums, job), self.ready)

    def block(self, y, c):
        name, first, count, _ = self.job
        d = 2 * y + c if self.paired else y
        if name == "down":
            return self.sums.at[:, pl.ds(pl.multiple_of(d * 768 + first, 128), count)]
        return self.sums.at[pl.ds(pl.multiple_of(d * 288 + first, 8), count), :]

    def local_copy(self, dy):
        x, y, z, c = self.place
        at = (1 - y) if dy else y
        return pltpu.make_async_copy(self.block(at, c), self.acc.at[at], self.load_sem.at[self.j, dy])

    def core_copy(self, dy):
        x, y, z, c = self.place
        at = (1 - y) if dy else y
        return pltpu.make_async_remote_copy(
            src_ref=self.block(at, 1 - c),
            dst_ref=self.other.at[at],
            send_sem=self.core_send.at[self.j, dy],
            recv_sem=self.core_recv.at[self.j, dy],
            device_id=mesh_place(x, y, z, 1 - c),
            device_id_type=MESH_ID,
        )

    def begin(self, dy):
        if self.paired:
            self.core_copy(dy).start()
        self.local_copy(dy).start()

    def ready(self, dy):
        y = self.place[1]
        at = (1 - y) if dy else y
        self.local_copy(dy).wait()
        if not self.paired:
            return
        self.core_copy(dy).wait_recv()

        def add(k, _):
            if self.job[0] == "down":
                part = (at, pl.ds(pl.multiple_of(k * 144, 16), 144), slice(None))
            else:
                part = (at, slice(None), pl.ds(pl.multiple_of(k * 384, 128), 384))
            self.acc[part] = self.acc[part] + self.other[part]
            return _

        lax.fori_loop(0, 8, add, 0)

    def finish(self):
        self.fold.finish()
        for dy in (0, 1) if self.paired else ():
            self.core_copy(dy).wait_send()


class Notes:
    def __init__(self, place, tile_of, own, by_seq, by_dp, sems):
        self.d, self.s = mesh_place(*place)
        self.tile_of, self.own, self.by_seq, self.by_dp = tile_of, own, by_seq, by_dp
        self.seq_send, self.seq_recv, self.dp_send, self.dp_recv = sems

    def along_seq(self, k):
        peer = lax.rem(self.s + k, 8)
        return pltpu.make_async_remote_copy(
            src_ref=self.tile_of(peer), dst_ref=self.by_seq.at[self.s], send_sem=self.seq_send.at[k],
            recv_sem=self.seq_recv.at[self.s], device_id=(self.d, peer), device_id_type=MESH_ID,
        )

    def along_dp(self, k):
        peer = lax.rem(self.d + k, 4)
        return pltpu.make_async_remote_copy(
            src_ref=self.own, dst_ref=self.by_dp.at[self.d], send_sem=self.dp_send.at[k],
            recv_sem=self.dp_recv.at[self.d], device_id=(peer, self.s), device_id_type=MESH_ID,
        )

    def wait_seq(self):
        for k in range(1, 8):
            peer = lax.rem(self.s + k, 8)
            there = self.by_seq.at[peer]
            pltpu.make_async_copy(there, there, self.seq_recv.at[peer]).wait()

    def wait_dp(self):
        for k in range(1, 4):
            peer = lax.rem(self.d + k, 4)
            there = self.by_dp.at[peer]
            pltpu.make_async_copy(there, there, self.dp_recv.at[peer]).wait()


NOTE_SEMS = [
    pltpu.SemaphoreType.DMA((8,)), pltpu.SemaphoreType.DMA((8,)),
    pltpu.SemaphoreType.DMA((4,)), pltpu.SemaphoreType.DMA((4,)),
]


FORWARD_PLAN = (
    (0, 100, 200,),
    (108, 1, 2, 101, 102, 8, 201, 204, 208, 4, 3, 202, 9, 104, 103, 205, 10, 109, 110, 209, 5, 105, 206, 203,
        11, 210, 6, 212, 106, 112, 207, 7, 213, 107,),
    (10500, 113, 211, 114, 10000, 10600, 214, 115, 14, 111, 10100, 10200, 10300, 10400, 12, 215, 15, 13,),
    (20000, 20100, 20200, 20300, 20400, 20500,),
    (10002, 10001, 20001, 20101, 20002, 20004, 10504, 20201, 20104, 10204, 20301, 20204, 10102, 20401, 10501,
        20304, 10101, 10008, 10201, 20502, 10604, 20501, 20404, 10108, 10302, 10301, 10601, 10402, 10401,
        20102, 10508, 10004, 10208, 20202, 10308, 10408, 20302, 10608, 10104, 20402, 20005, 10202, 10009,
        20105, 10502, 20205, 10209, 10304, 10003, 10404, 10010, 10602, 20503, 20504, 20305, 20405, 10509,
        10103, 10309, 10505, 10205, 20003, 10609, 10303, 10109, 10110, 10310, 20103, 20006, 10605, 20203,
        10403, 20505, 20106, 10005, 20303, 10210, 20206, 10512, 10409, 10410, 10510, 10212, 20306, 10613,
        20406, 10506, 10203, 10105, 10503, 10612, 10206, 10305, 10610, 10012, 10405, 20403, 10603, 10606,
        20107, 10011, 10213, 20007, 10006, 10312, 20506, 20207, 10513, 10111, 10112, 20307, 10311, 10507,
        20507, 10511, 10411, 20407,),
    (
        (1, (10211, 10306, 10412,)),
        (2, (10207, 10106, 10013, 10607,)),
        (3, (10406,)),
        (5, (10007,)),
        (8, (10113,)),
        (9, (10107, 10514,)),
        (11, (10307, 10313,)),
    ),
    (10407, 10413, 10214, 10611, 10614, 10014, 10114, 10515, 10414, 10215, 10314, 10615, 10015, 10115, 10415, 10315,),
)
BACKWARD_PLAN = (
    (10100, 10101,),
    (
        (0, (10300,)),
        (3, (10000,)),
        (5, (10102, 10500,)),
        (8, (10200,)),
        (9, (10400,)),
    ),
    (10401, 20500, 10103, 10105, 10104, 20000, 10001, 10302, 20501, 20502, 10201, 10501, 10106, 10002, 20300,
        20100, 20200, 20400, 10202, 10502, 10600, 20504, 20503, 10003, 10304, 10306, 20001, 20101, 20201,
        20301, 20401, 10107, 10108, 10109, 10110, 20402, 20505, 10301, 10303, 10305, 20002, 20102, 20202,
        20302, 10203, 10503, 10004, 20506, 20303, 20304, 10204, 10402, 10504, 10005, 10111, 20003, 20103,
        20203, 20403, 20004, 20204, 20404, 20005, 20205, 10602, 10205, 10604, 20305, 10403, 10505, 10006,
        20405, 10307, 10308, 10601, 10603, 20006, 20104, 20105, 20106, 10112, 20206, 10206, 10309, 10404,
        20306, 10506, 10007, 10008, 20007, 20406, 10113, 10009, 10207, 10208, 10209, 10405, 10507, 10508,
        10509, 20107, 20307, 10310, 10605, 20407, 10010, 20507, 10406, 10210, 10011, 10407, 10408, 10409,
        20207,),
    (
        (0, (10311, 10606,)),
        (2, (10312, 10607, 10608, 10609,)),
        (3, (10012,)),
        (4, (10410,)),
        (7, (10510,)),
    ),
    (10412, 10411, 10313, 100, 10013, 200, 101, 201, 10114, 10211, 102, 202,),
    (10610, 103, 203, 10511, 10413, 104, 204,),
    (10212, 105, 205, 106, 206, 107, 207, 10213, 0, 1, 2, 10611, 3, 10512, 10513, 208, 5, 10612, 108,),
    (109, 209, 7, 110, 10613, 4, 6, 112, 111, 113, 10314, 210, 10014, 10115, 211, 8, 10, 114, 212,),
    (9, 213, 10214, 10514, 214, 10414, 10315, 12, 10015, 11, 115, 13, 215, 10215, 10515, 14, 10614, 15, 10415,
        10615,),
)


def dot(a, b):
    return jnp.dot(a, b, preferred_element_type=jnp.float32)


def dot_t(a, b):
    return lax.dot_general(a, b, (((1,), (1,)), ((), ())), preferred_element_type=jnp.float32)


def t_dot(a, b):
    return lax.dot_general(a, b, (((0,), (0,)), ((), ())), preferred_element_type=jnp.float32)


def repeat(count, body):
    def step(k, nothing):
        body(k)
        return nothing

    lax.fori_loop(0, count, step, 0)


def rows_at(k, size, base=0):
    return pl.ds(pl.multiple_of(base + k * size, 16), size)


def lanes_at(k, size, base=0):
    return pl.ds(pl.multiple_of(base + k * size, 128), size)


def rotate(u, cosine, sine):
    front, back = u[:32], u[32:]
    return jnp.concatenate([front * cosine - back * sine, front * sine + back * cosine], axis=0)


def probabilities(keys, query, limit, chunk):
    scores = t_dot(keys, query) * (HEAD_DIMENSION ** (-0.5))
    key_pos = chunk * 256 + lax.broadcasted_iota(jnp.int32, (256, 384), 0)
    return jnp.where(key_pos <= limit, jnp.exp(scores), 0.0)


def heads_wide(ref, group, lanes):
    return jnp.concatenate(
        [ref[pl.ds(pl.multiple_of(group * 192 + 64 * i, 64), 64), lanes] for i in range(3)], axis=1
    )


def three_wide(row):
    return jnp.concatenate([row] * 3, axis=1)


def forward_body(
    cat, note, x, cosine, sine, limit, gate, up, down,
    gate_w, up_w, down_w, wcat, notes, attn_in_t, hidden, query, keys_values, attn, denom,
    attn_in, raw, own_kv, weights, proj, seq_in, dp_in, own_sems, note_a, note_b, note_c, note_d, *sems
):
    place = position()
    d, s = mesh_place(*place)
    greet(place, True)
    shards = dict(zip(FFN_NAMES, (gate, up, down)))
    wholes = dict(zip(FFN_NAMES, (gate_w, up_w, down_w)))
    cat_spreads = make_spreads(place, CAT_JOBS, {"cat": cat}, {"cat": weights}, sems[:4])
    ffn_spreads = make_spreads(place, FFN_JOBS, shards, wholes, sems[4:8])
    kv_spreads = make_kv_spreads(place, own_kv, keys_values, sems[8:10])
    steps = [[spread.steps() for spread in family] for family in (cat_spreads, ffn_spreads, kv_spreads)]

    def run(tokens):
        for token in tokens:
            steps[token // 10000][token // 100 % 100][token % 100]()

    tiles = Notes(place, lambda peer: note, note, seq_in, dp_in, (note_a, note_b, note_c, note_d))
    run(FORWARD_PLAN[0])
    for k in range(1, 8):
        tiles.along_seq(k).start()
    for k in range(1, 4):
        tiles.along_dp(k).start()
    own = [
        pltpu.make_async_copy(
            shards[name], piece_of(wholes[name], (name, 0, 768 if name == "down" else 288, ""))(place), own_sems.at[k]
        )
        for k, name in enumerate(FFN_NAMES)
    ]
    for copy in own:
        copy.start()
    weights[rows_at(d, 288), lanes_at(s, 384)] = cat[...]
    for copy in own:
        copy.wait()
    run(FORWARD_PLAN[1])
    tiles.wait_seq()
    tiles.wait_dp()
    seq_in[s] = note[...]
    dp_in[d] = note[...]
    gains = seq_in[0]
    for k in range(1, 8):
        gains = gains + seq_in[k]
    notes[0:8, :] = gains
    notes[8:16, :] = dp_in[0] + dp_in[1] + dp_in[2] + dp_in[3]

    def norm(k):
        rows = rows_at(k, 32)
        part = x[rows, :].astype(jnp.float32)
        scale = lax.rsqrt(jnp.mean(part * part, axis=-1, keepdims=True) + norm_eps)
        attn_in[rows, :] = (part * scale * notes[0:1, :]).astype(jnp.bfloat16)

    repeat(8, norm)
    attn_in_t[...] = attn_in[...].T
    run(FORWARD_PLAN[2])
    for spread in cat_spreads:
        spread.wait_core()

    def project(b):
        block = dot(attn_in[...], weights[:, lanes_at(b, 384)][:, :256]).T
        raw[rows_at(b, 144), :] = block[:144]
        raw[rows_at(b, 48, 1152), :] = block[144:192]
        raw[rows_at(b, 48, 1536), :] = block[192:240]

    repeat(8, project)
    out_copy = pltpu.make_async_copy(weights, wcat, own_sems.at[3])
    out_copy.start()

    def turn(ref, rows_of):
        def one(h):
            ref[rows_at(h, 64), :] = rotate(raw[rows_of(h), :], cosine[...], sine[...]).astype(jnp.bfloat16)

        return one

    repeat(6, turn(own_kv, lambda h: rows_at(h, 64, 1152)))
    own_kv[384:768, :] = raw[1536:1920, :].astype(jnp.bfloat16)
    repeat(18, turn(query, lambda h: rows_at(h, 64)))
    run(FORWARD_PLAN[3])
    here = lanes_at(s, 128)
    for slot in range(2):
        keys_values[slot, :, here] = own_kv[:, slot * 128: slot * 128 + 128]
    run(FORWARD_PLAN[4])

    def attend(slot, group):
        lanes = lanes_at(slot, 128)
        bound = three_wide(limit[:, lanes])
        wide = heads_wide(query, group, lanes)

        def one_chunk(chunk, carry):
            total, numer = carry
            cols = lanes_at(chunk, 256)
            expo = probabilities(keys_values[slot, rows_at(group, 64), cols], wide, bound, chunk)
            total = total + jnp.sum(expo, axis=0, keepdims=True)
            numer = numer + dot(keys_values[slot, rows_at(group, 64, 384), cols], expo.astype(jnp.bfloat16))
            return (total, numer)

        total, numer = lax.fori_loop(
            0, 4, one_chunk, (jnp.zeros((1, 384), jnp.float32), jnp.zeros((64, 384), jnp.float32)), unroll=True
        )
        mean = numer / total
        for i in range(3):
            attn[pl.ds(pl.multiple_of(group * 192 + 64 * i, 64), 64), lanes] = mean[:, i * 128: i * 128 + 128]
        denom[group, 0:3, lanes] = jnp.concatenate([total[:, i * 128: i * 128 + 128] for i in range(3)], axis=0)

    def unit(k):
        attend(k // 6, lax.rem(k, 6))
        for at, tokens in FORWARD_PLAN[5]:
            pl.when(k == at)(lambda tokens=tokens: run(tokens))

    repeat(12, unit)

    def out_project(b):
        block = t_dot(attn[...].astype(jnp.bfloat16), weights[:, lanes_at(b, 384)][:, 128:]).T
        proj[rows_at(b, 144), :] = block[112:256]

    repeat(8, out_project)
    hidden[...] = x[...].astype(jnp.float32) + proj[...].T
    run(FORWARD_PLAN[6])
    for spread in cat_spreads + ffn_spreads + kv_spreads:
        spread.finish()
    for spread in ffn_spreads:
        spread.wait_core()
    for k in range(1, 8):
        tiles.along_seq(k).wait_send()
    for k in range(1, 4):
        tiles.along_dp(k).wait_send()
    out_copy.wait()


def forward_call(cat, note, x, cosine, sine, limit, gate, up, down):
    vmem, anywhere = pl.BlockSpec(memory_space=pltpu.VMEM), pl.BlockSpec(memory_space=pl.ANY)
    return pl.pallas_call(
        forward_body,
        out_shape=[jax.ShapeDtypeStruct((1152, 3072), jnp.bfloat16)] * 4
        + [
            jax.ShapeDtypeStruct((16, 1152), jnp.float32),
            jax.ShapeDtypeStruct((1152, 256), jnp.bfloat16),
            jax.ShapeDtypeStruct((256, 1152), jnp.float32),
            jax.ShapeDtypeStruct((1152, 256), jnp.bfloat16),
            jax.ShapeDtypeStruct((2, 768, 1024), jnp.bfloat16),
            jax.ShapeDtypeStruct((1152, 256), jnp.float32),
            jax.ShapeDtypeStruct((6, 8, 256), jnp.float32),
        ],
        in_specs=[vmem] * 9,
        out_specs=[anywhere] * 4 + [vmem] * 7,
        scratch_shapes=[
            pltpu.VMEM((256, 1152), jnp.bfloat16),
            pltpu.VMEM((1920, 256), jnp.float32),
            pltpu.VMEM((768, 256), jnp.bfloat16),
            pltpu.VMEM((1152, 3072), jnp.bfloat16),
            pltpu.VMEM((1152, 256), jnp.float32),
            pltpu.VMEM((8, 8, 1152), jnp.float32),
            pltpu.VMEM((4, 8, 1152), jnp.float32),
            pltpu.SemaphoreType.DMA((4,)),
        ]
        + NOTE_SEMS
        + spread_sems(CAT_JOBS)
        + spread_sems(FFN_JOBS)
        + spread_sems(KV_JOBS)[:2],
        compiler_params=pltpu.CompilerParams(
            collective_id=3, has_side_effects=True, vmem_limit_bytes=48 * 1024 * 1024
        ),
        name="attention_forward",
    )(cat, note, x, cosine, sine, limit, gate, up, down)


def ffn_body(
    total_tokens, hidden, teacher, valid, notes, gate_w, up_w, down_w,
    out, grad_hidden, small, gate_sums, up_sums, down_sums,
    w_gate, w_up, w_down, gate, up, hid, grads_gate, grads_up, inputs_t, cot_t, inputs, cot_b, acc, cot, rate,
    sums_gate, sums_up, sums_down, load, swap_send, swap_recv, store
):
    place = position()
    x, y, z, c = place
    other = mesh_place(x, y, z, 1 - c)
    barrier = pltpu.get_barrier_semaphore()
    pl.semaphore_signal(barrier, inc=1, device_id=other, device_id_type=MESH_ID)
    pl.semaphore_wait(barrier, 1)
    columns = lambda j: lanes_at(j, 768)

    def load_copy(k, source, target, j):
        return pltpu.make_async_copy(source.at[:, columns(j)], target.at[:, columns(j)], load.at[k, j])

    def loads(j):
        return [load_copy(k, *pair, j) for k, pair in enumerate(((gate_w, w_gate), (up_w, w_up), (down_w, w_down)))]

    for j in range(4):
        for copy in loads(j):
            copy.start()

    def swap(source, target, k):
        return pltpu.make_async_remote_copy(
            src_ref=source, dst_ref=target, send_sem=swap_send.at[k], recv_sem=swap_recv.at[k],
            device_id=other, device_id_type=MESH_ID,
        )

    own, theirs = pl.ds(0, 256), pl.ds(256, 256)
    swap_inputs = swap(inputs_t.at[:, own], inputs_t.at[:, theirs], 0)
    swap_cot = swap(cot_t.at[:, own], cot_t.at[:, theirs], 1)

    def swap_hid(i, core):
        at = columns(core + 2 * i)
        return swap(hid.at[own, at], hid.at[theirs, at], 2 + i)

    def swap_grads(ref, j, k):
        return swap(ref.at[own, columns(j)], ref.at[theirs, columns(j)], k + j)

    def norm(k):
        rows = rows_at(k, 32)
        part = hidden[rows, :]
        scale = lax.rsqrt(jnp.mean(part * part, axis=-1, keepdims=True) + norm_eps)
        rate[rows, :] = jnp.broadcast_to(scale, (32, 128))
        inputs[rows, :] = (part * scale * notes[1:2, :]).astype(jnp.bfloat16)

    repeat(8, norm)
    inputs_t[:, 0:256] = inputs[...].T
    acc[...] = jnp.zeros_like(acc)

    def forward(j):
        for copy in loads(j):
            copy.wait()
        at = columns(j)
        gate_part = dot(inputs[...], w_gate[:, at])
        up_part = dot(inputs[...], w_up[:, at])
        gate[:, at] = gate_part
        up[:, at] = up_part
        hid[0:256, at] = (gate_part * jax.nn.sigmoid(gate_part) * up_part).astype(jnp.bfloat16)
        acc[...] += dot_t(hid[0:256, at], w_down[:, at])

    repeat(4, forward)
    swap_inputs.start()
    for i in range(2):
        swap_hid(i, 1 - c).start()
    factor = total_tokens / notes[10:11, :]
    small[...] = jnp.zeros_like(small)

    def losses(k):
        rows = rows_at(k, 32)
        live = valid[rows, 0:1] > 0.0
        value = jnp.where(live, hidden[rows, :] + acc[rows, :], 0.0)
        out[rows, :] = value.astype(jnp.bfloat16)
        diff = jnp.where(live, value - teacher[rows, :].astype(jnp.float32), 0.0)
        small[2:3, :] += jnp.sum(diff * diff, axis=0, keepdims=True)
        grad = factor * diff
        cot[rows, :] = grad
        cot_b[rows, :] = grad.astype(jnp.bfloat16)

    repeat(8, losses)
    cot_t[:, 0:256] = cot_b[...].T
    acc[...] = jnp.zeros_like(acc)

    def backward(j):
        at = columns(j)
        grad_hid = dot(cot_b[...], w_down[:, at])
        gate_part = gate[:, at]
        sig = jax.nn.sigmoid(gate_part)
        grads_gate[0:256, at] = (
            grad_hid * up[:, at] * sig * (1.0 + gate_part * (1.0 - sig))
        ).astype(jnp.bfloat16)
        grads_up[0:256, at] = (grad_hid * gate_part * sig).astype(jnp.bfloat16)
        acc[...] += dot_t(grads_gate[0:256, at], w_gate[:, at]) + dot_t(grads_up[0:256, at], w_up[:, at])
        swap_grads(grads_gate, j, 4).start()
        swap_grads(grads_up, j, 8).start()
        pl.when(j == 0)(swap_cot.start)

    repeat(4, backward)

    def finish_rows(k):
        rows = rows_at(k, 32)
        scale = rate[rows, 0:1]
        normed = hidden[rows, :] * scale
        grad = acc[rows, :]
        small[1:2, :] += jnp.sum(grad * normed, axis=0, keepdims=True)
        grad = grad * notes[1:2, :]
        inner = grad - normed * jnp.mean(grad * normed, axis=-1, keepdims=True)
        grad_hidden[rows, :] = cot[rows, :] + scale * inner

    repeat(8, finish_rows)
    small[2:3, :] = jnp.broadcast_to(jnp.sum(small[2:3, :], axis=-1, keepdims=True), (1, 1152))
    small[3:4, :] = notes[0:1, :]
    swap_cot.wait_recv()
    swap_inputs.wait_recv()

    def stored(k, source, target, i):
        at = columns(i)
        return pltpu.make_async_copy(source.at[:, at], target.at[:, at], store.at[k, i])

    def down_grads(i):
        swap_hid(i, c).wait_recv()
        sums_down[:, columns(i)] = dot(cot_t[...], hid[:, columns(c + 2 * i)]).astype(jnp.bfloat16)
        stored(0, sums_down, down_sums, i).start()

    repeat(2, down_grads)

    def wide_grads(j):
        at = columns(j)
        swap_grads(grads_gate, j, 4).wait_recv()
        swap_grads(grads_up, j, 8).wait_recv()
        for half in range(2):
            rows = rows_at(c + 2 * half, 288)
            kept = slice(288 * half, 288 * half + 288)
            sums_gate[kept, at] = dot(inputs_t[rows, :], grads_gate[:, at]).astype(jnp.bfloat16)
            sums_up[kept, at] = dot(inputs_t[rows, :], grads_up[:, at]).astype(jnp.bfloat16)
        stored(1, sums_gate, gate_sums, j).start()
        stored(2, sums_up, up_sums, j).start()

    repeat(4, wide_grads)
    swap_inputs.wait_send()
    swap_cot.wait_send()
    for i in range(2):
        swap_hid(i, 1 - c).wait_send()
        stored(0, sums_down, down_sums, i).wait()
    for j in range(4):
        swap_grads(grads_gate, j, 4).wait_send()
        swap_grads(grads_up, j, 8).wait_send()
        stored(1, sums_gate, gate_sums, j).wait()
        stored(2, sums_up, up_sums, j).wait()


def ffn_call(total_tokens, hidden, teacher, valid, notes, gate_w, up_w, down_w):
    vmem, anywhere = pl.BlockSpec(memory_space=pltpu.VMEM), pl.BlockSpec(memory_space=pl.ANY)
    whole = pltpu.VMEM((1152, 3072), jnp.bfloat16)
    both = pltpu.VMEM((512, 3072), jnp.bfloat16)
    return pl.pallas_call(
        functools.partial(ffn_body, total_tokens),
        out_shape=[
            jax.ShapeDtypeStruct((256, 1152), jnp.bfloat16),
            jax.ShapeDtypeStruct((256, 1152), jnp.float32),
            jax.ShapeDtypeStruct((8, 1152), jnp.float32),
            jax.ShapeDtypeStruct((576, 3072), jnp.bfloat16),
            jax.ShapeDtypeStruct((576, 3072), jnp.bfloat16),
            jax.ShapeDtypeStruct((1152, 1536), jnp.bfloat16),
        ],
        in_specs=[vmem] * 4 + [anywhere] * 3,
        out_specs=[vmem] * 3 + [anywhere] * 3,
        scratch_shapes=[whole] * 3
        + [pltpu.VMEM((256, 3072), jnp.float32)] * 2
        + [both] * 3
        + [pltpu.VMEM((1152, 512), jnp.bfloat16)] * 2
        + [pltpu.VMEM((256, 1152), jnp.bfloat16)] * 2
        + [pltpu.VMEM((256, 1152), jnp.float32)] * 2
        + [pltpu.VMEM((256, 128), jnp.float32)]
        + [pltpu.VMEM((576, 3072), jnp.bfloat16)] * 2
        + [
            pltpu.VMEM((1152, 1536), jnp.bfloat16),
            pltpu.SemaphoreType.DMA((3, 4)),
            pltpu.SemaphoreType.DMA((12,)),
            pltpu.SemaphoreType.DMA((12,)),
            pltpu.SemaphoreType.DMA((3, 4)),
        ],
        compiler_params=pltpu.CompilerParams(
            collective_id=5, has_side_effects=True, vmem_limit_bytes=VMEM_MOST
        ),
        name="feed_forward",
    )(hidden, teacher, valid, notes, gate_w, up_w, down_w)


def backward_body(
    grad_hidden, attn_in_t, wcat, keys_values, query, attn, denom, cosine, sine, limit, x, scales, small,
    grad_gate, grad_up, grad_down,
    own_gate, own_up, own_down, own_cat, grad_tokens, totals, grad_cat,
    weights, whole_kv, part_kv, turned, total, own_kv, left, grad_t, note, seq_in, dp_in, row_sum,
    load, store, kv_send, kv_recv, kv_arrived, note_a, note_b, note_c, note_d, *scratch
):
    place = position()
    d, s = mesh_place(*place)
    greet(place, True)
    sums = dict(zip(FFN_NAMES, (grad_gate, grad_up, grad_down)))
    owned = dict(zip(FFN_NAMES, (own_gate, own_up, own_down)))
    split = len(fold_scratch(FOLD_FFN, False))
    folds = [
        JobFold(place, job, j, sums[job[0]], owned[job[0]], scratch[:split], False) for j, job in enumerate(FOLD_FFN)
    ]
    cat_folds = [JobFold(place, job, j, grad_cat, own_cat, scratch[split:], True) for j, job in enumerate(FOLD_CAT)]
    tiles = Notes(place, lambda peer: note, row_sum, seq_in, dp_in, (note_a, note_b, note_c, note_d))

    def kv_fold(j, slot, row, order):
        def out(value):
            own_kv[row: row + 256, slot * 128: slot * 128 + 128] = value

        spot = kv_spot(part_kv, slot, row)
        return Fold(place, order, lambda who: spot(who), kv_arrived.at[j], (kv_send, kv_recv), j, out, kv_amount(part_kv))

    kv_folds = [kv_fold(j, *job) for j, job in enumerate(FOLD_KV)]
    steps = [
        [fold.fold.steps() for fold in cat_folds],
        [fold.fold.steps() for fold in folds],
        [fold.steps() for fold in kv_folds],
    ]

    def run(tokens):
        for token in tokens:
            steps[token // 10000][token // 100 % 100][token % 100]()

    for dy in (1, 0):
        for fold in folds:
            fold.begin(dy)

    def block_load(b):
        return pltpu.make_async_copy(wcat.at[:, lanes_at(b, 384)], weights.at[:, lanes_at(b, 384)], load.at[b])

    repeat(8, lambda b: block_load(b).start())
    kv_in = pltpu.make_async_copy(keys_values, whole_kv, load.at[8])
    kv_in.start()
    grad_t[...] = grad_hidden[...].T.astype(jnp.bfloat16)
    total[...] = jnp.zeros_like(total)

    def out_rows(b):
        return jnp.concatenate([jnp.zeros((112, 256), jnp.bfloat16), grad_t[rows_at(b, 144), :]], axis=0)

    def out_back(b):
        block_load(b).wait()
        total[...] += dot(weights[:, lanes_at(b, 384)][:, 128:], out_rows(b))

    repeat(8, out_back)
    run(BACKWARD_PLAN[0])
    kv_in.wait()
    scale = HEAD_DIMENSION ** (-0.5)

    def attend_back(slot, group):
        lanes = lanes_at(slot, 128)
        bound = three_wide(limit[:, lanes])
        wide = heads_wide(query, group, lanes)
        grads, ratios = [], []
        for i in range(3):
            rows = pl.ds(pl.multiple_of(group * 192 + 64 * i, 64), 64)
            grad = total[rows, lanes].astype(jnp.bfloat16).astype(jnp.float32)
            bottom = denom[group, i: i + 1, lanes]
            ratios.append(jnp.sum(grad * attn[rows, lanes], axis=0, keepdims=True) / bottom)
            grads.append((grad / bottom).astype(jnp.bfloat16))
        grads, ratios = jnp.concatenate(grads, axis=1), jnp.concatenate(ratios, axis=1)

        def one_chunk(chunk, sum_query):
            cols = lanes_at(chunk, 256)
            keys = whole_kv[slot, rows_at(group, 64), cols]
            values = whole_kv[slot, rows_at(group, 64, 384), cols]
            expo = probabilities(keys, wide, bound, chunk)
            grad_prob = t_dot(values, grads)
            grad_score = (expo * (grad_prob - ratios)).astype(jnp.bfloat16)
            part_kv[slot, rows_at(group, 64), cols] = (dot_t(wide, grad_score) * scale).astype(jnp.bfloat16)
            part_kv[slot, rows_at(group, 64, 384), cols] = dot_t(grads, expo.astype(jnp.bfloat16)).astype(jnp.bfloat16)
            return sum_query + dot(keys, grad_score)

        sum_query = lax.fori_loop(0, 4, one_chunk, jnp.zeros((64, 384), jnp.float32), unroll=True) * scale
        for i in range(3):
            total[pl.ds(pl.multiple_of(group * 192 + 64 * i, 64), 64), lanes] = sum_query[:, i * 128: i * 128 + 128]

    def unit(k):
        attend_back(k // 6, lax.rem(k, 6))
        for at, tokens in BACKWARD_PLAN[1]:
            pl.when(k == at)(lambda tokens=tokens: run(tokens))

    repeat(12, unit)
    run(BACKWARD_PLAN[2])

    def turn_back(ref, source, count):
        def one(h):
            rows = rows_at(h, 64)
            ref[rows, :] = rotate(source[rows, :], cosine[...], -sine[...]).astype(ref.dtype)

        repeat(count, one)

    turn_back(turned, total, 18)
    turn_back(own_kv, own_kv, 6)
    total[...] = jnp.zeros_like(total)

    def last_block(b):
        rows = jnp.concatenate(
            [
                turned[rows_at(b, 144), :],
                own_kv[rows_at(b, 48), :].astype(jnp.bfloat16),
                own_kv[rows_at(b, 48, 384), :].astype(jnp.bfloat16),
                jnp.zeros((16, 256), jnp.bfloat16),
            ],
            axis=0,
        )
        total[...] += dot(weights[:, lanes_at(b, 384)][:, :256], rows)
        slot = lax.rem(b, 2)
        out = pltpu.make_async_copy(left.at[slot], grad_cat.at[:, lanes_at(b, 384)], store.at[slot])
        pl.when(b >= 2)(lambda: out.wait())
        grad = dot_t(attn_in_t[...], rows)
        out_grad = dot_t(attn[...].astype(jnp.bfloat16), out_rows(b))
        left[slot, :, 0:128] = grad[:, :128].astype(jnp.bfloat16)
        left[slot, :, 128:256] = (grad[:, 128:] + out_grad[:, :128]).astype(jnp.bfloat16)
        left[slot, :, 256:384] = out_grad[:, 128:].astype(jnp.bfloat16)
        out.start()
        for at, tokens in BACKWARD_PLAN[3]:
            pl.when(b == at)(lambda tokens=tokens: run(tokens))

    repeat(8, last_block)
    for slot in range(2):
        pltpu.make_async_copy(left.at[slot], grad_cat.at[:, pl.ds((6 + slot) * 384, 384)], store.at[slot]).wait()
    for dy in (1, 0):
        for fold in cat_folds:
            fold.begin(dy)
    run(BACKWARD_PLAN[4])
    grad_tokens[...] = total[...].T
    note[...] = small[...]

    def finish_rows(k):
        rows = rows_at(k, 32)
        grad = grad_tokens[rows, :]
        scale_in = scales[rows, 0:1]
        normed = x[rows, :].astype(jnp.float32) * scale_in
        note[0:1, :] += jnp.sum(grad * normed, axis=0, keepdims=True)
        grad = grad * small[3:4, :]
        inner = grad - normed * jnp.mean(grad * normed, axis=-1, keepdims=True)
        grad_tokens[rows, :] = grad_hidden[rows, :] + scale_in * inner

    repeat(8, finish_rows)
    run(BACKWARD_PLAN[5])
    for k in range(1, 8):
        tiles.along_seq(k).start()
    run(BACKWARD_PLAN[6])
    tiles.wait_seq()
    seq_in[s] = note[...]
    along = seq_in[0]
    for k in range(1, 8):
        along = along + seq_in[k]
    row_sum[...] = along
    run(BACKWARD_PLAN[7])
    for k in range(1, 4):
        tiles.along_dp(k).start()
    run(BACKWARD_PLAN[8])
    tiles.wait_dp()
    dp_in[d] = row_sum[...]
    totals[...] = dp_in[0] + dp_in[1] + dp_in[2] + dp_in[3]
    for fold in folds + kv_folds + cat_folds:
        fold.finish()
    for k in range(1, 8):
        tiles.along_seq(k).wait_send()
    for k in range(1, 4):
        tiles.along_dp(k).wait_send()


def backward_call(
    grad_hidden, attn_in_t, wcat, keys_values, query, attn, denom, cosine, sine, limit, x, scales, small,
    grad_gate, grad_up, grad_down
):
    vmem, anywhere = pl.BlockSpec(memory_space=pltpu.VMEM), pl.BlockSpec(memory_space=pl.ANY)
    jobs = len(KV_JOBS)
    most = max(fold_slots(order)[1] for _, _, order in FOLD_KV)
    return pl.pallas_call(
        backward_body,
        out_shape=[
            jax.ShapeDtypeStruct((288, 384), jnp.float32),
            jax.ShapeDtypeStruct((288, 384), jnp.float32),
            jax.ShapeDtypeStruct((144, 768), jnp.float32),
            jax.ShapeDtypeStruct((288, 384), jnp.float32),
            jax.ShapeDtypeStruct((256, 1152), jnp.float32),
            jax.ShapeDtypeStruct((8, 1152), jnp.float32),
            jax.ShapeDtypeStruct((1152, 3072), jnp.bfloat16),
        ],
        in_specs=[vmem, vmem, anywhere, anywhere] + [vmem] * 9 + [anywhere] * 3,
        out_specs=[vmem] * 6 + [anywhere],
        scratch_shapes=[
            pltpu.VMEM((1152, 3072), jnp.bfloat16),
            pltpu.VMEM((2, 768, 1024), jnp.bfloat16),
            pltpu.VMEM((2, 768, 1024), jnp.bfloat16),
            pltpu.VMEM((1152, 256), jnp.bfloat16),
            pltpu.VMEM((1152, 256), jnp.float32),
            pltpu.VMEM((768, 256), jnp.float32),
            pltpu.VMEM((2, 1152, 384), jnp.bfloat16),
            pltpu.VMEM((1152, 256), jnp.bfloat16),
            pltpu.VMEM((8, 1152), jnp.float32),
            pltpu.VMEM((8, 8, 1152), jnp.float32),
            pltpu.VMEM((4, 8, 1152), jnp.float32),
            pltpu.VMEM((8, 1152), jnp.float32),
            pltpu.SemaphoreType.DMA((9,)),
            pltpu.SemaphoreType.DMA((2,)),
            pltpu.SemaphoreType.DMA((jobs,)),
            pltpu.SemaphoreType.DMA((jobs, most)),
            pltpu.VMEM((jobs, most, 256, 128), jnp.bfloat16),
        ]
        + NOTE_SEMS
        + fold_scratch(FOLD_FFN, False)
        + fold_scratch(FOLD_CAT, True),
        compiler_params=pltpu.CompilerParams(
            collective_id=4, has_side_effects=True, vmem_limit_bytes=VMEM_MOST
        ),
        name="attention_backward",
    )(
        grad_hidden, attn_in_t, wcat, keys_values, query, attn, denom, cosine, sine, limit, x, scales, small,
        grad_gate, grad_up, grad_down,
    )


def per_device_fast(
    tokens, teacher, lengths, w_query, key_weight, value_weight, w_out, w_gate, w_up, w_down, gain_attn, gain_ffn
):
    slots, part, width = tokens.shape
    rows = slots * part
    own_columns = gain_attn.shape[0]
    first_column = lax.axis_index("seq") * own_columns
    total_tokens = slots * lax.axis_size("dp") * part * lax.axis_size("seq")
    positions = lax.axis_index("seq") * part + jnp.arange(part, dtype=jnp.int32)
    cosine, sine = rope_tables(positions, HEAD_DIMENSION)
    cosine_t = jnp.concatenate([cosine.T] * slots, axis=1)
    sine_t = jnp.concatenate([sine.T] * slots, axis=1)
    limit = jnp.minimum(positions[None, :], lengths[:, None] - 1).reshape(1, rows)
    valid = (positions[None, :] < lengths[:, None]).astype(jnp.float32).reshape(rows, 1)
    note = lax.dynamic_update_slice(
        jnp.zeros((8, width), jnp.float32),
        jnp.stack([gain_attn, gain_ffn]).astype(jnp.float32),
        (0, first_column),
    )
    note = note.at[2].set(jnp.sum(lengths).astype(jnp.float32))
    x_b = tokens.reshape(rows, width)
    gate_w, up_w, down_t, cat, notes, attn_in_t, hidden, query, keys_values, attn, denom = forward_call(
        jnp.concatenate([w_query, key_weight, value_weight, w_out], axis=1),
        note, x_b, cosine_t, sine_t, limit, w_gate, w_up, w_down.T,
    )
    output, grad_hidden, small, gate_sums, up_sums, down_sums = ffn_call(
        float(total_tokens), hidden, teacher.reshape(rows, width), jnp.broadcast_to(valid, (rows, 128)), notes,
        gate_w, up_w, down_t,
    )
    x = x_b.astype(jnp.float32)
    r1 = lax.rsqrt(jnp.mean(x * x, axis=-1, keepdims=True) + norm_eps)
    own_gate, own_up, own_down_t, own_cat, grad_tokens, totals, _ = backward_call(
        grad_hidden, attn_in_t, cat, keys_values, query, attn, denom, cosine_t, sine_t, limit,
        x_b, jnp.broadcast_to(r1, (rows, 128)), small, gate_sums, up_sums, down_sums,
    )
    own_gains = lax.dynamic_slice(totals, (0, first_column), (2, own_columns))
    return (
        output.reshape(tokens.shape),
        totals[2, 0] / notes[10, 0],
        grad_tokens.reshape(tokens.shape),
        own_cat[:, :144],
        own_cat[:, 144:192],
        own_cat[:, 192:240],
        own_cat[:, 240:],
        own_gate,
        own_up,
        own_down_t.T,
        own_gains[0],
        own_gains[1],
    )


def solution(mesh):
    placed = (
        P("dp", "seq", None),
        P("dp", "seq", None),
        P("dp"),
        P("dp", "seq"),
        P("dp", "seq"),
        P("dp", "seq"),
        P("dp", "seq"),
        P("dp", "seq"),
        P("dp", "seq"),
        P("dp", "seq"),
        P("seq"),
        P("seq"),
    )
    fits = mesh.shape["dp"] == 4 and mesh.shape["seq"] == 8
    return jax.shard_map(
        per_device_fast if fits else per_device,
        mesh=mesh,
        in_specs=placed,
        out_specs=(
            P("dp", "seq", None),
            P(),
            P("dp", "seq", None),
            P("dp", "seq"),
            P("dp", "seq"),
            P("dp", "seq"),
            P("dp", "seq"),
            P("dp", "seq"),
            P("dp", "seq"),
            P("dp", "seq"),
            P("seq"),
            P("seq"),
        ),
        check_vma=False,
    )
```

```python
import functools
import math

import jax
import jax.numpy as jnp
from jax import lax
from jax.experimental import pallas as pl
from jax.experimental.pallas import tpu as pltpu
from jax.sharding import PartitionSpec as P

QUERY_HEADS = 18
KEY_VALUE_HEADS = 6
HEAD_DIMENSION = 64


norm_eps = 1e-05
rope_base = 10000.0


def rope_tables(positions, head_width):
    half_width = head_width // 2
    exponents = jnp.arange(half_width, dtype=jnp.float32) * (2.0 / head_width)
    angles = positions.astype(jnp.float32)[:, None] * (rope_base ** (-exponents))[None, :]
    return (jnp.cos(angles), jnp.sin(angles))


def apply_rotary(value_rows, cosine_table, sine_table):
    half_width = value_rows.shape[-1] // 2
    front_half = value_rows[..., :half_width]
    back_half = value_rows[..., half_width:]
    cos_wide = cosine_table[:, None, :]
    sin_wide = sine_table[:, None, :]
    return jnp.concatenate(
        [
            front_half * cos_wide - back_half * sin_wide,
            front_half * sin_wide + back_half * cos_wide,
        ],
        axis=-1,
    )


def allowed_mask(query_pos, key_pos, live_len):
    causal = key_pos[None, :] <= query_pos[:, None]
    present = key_pos[None, :] < live_len[:, None]
    return (causal[None, :, :] & present[:, None, :])[:, None, None, :, :]


def over_blocks(piece_len, unit_len, step_fn, running):
    block_length = math.gcd(piece_len, unit_len * max(1, 512 // unit_len))
    number_of_blocks = piece_len // block_length

    def loop_step(block_number, state):
        return step_fn(state, block_number * block_length, block_length)

    return lax.fori_loop(0, number_of_blocks, loop_step, running)


def collect(shards):
    wide = (
        lax.all_gather(shards[0], "seq", axis=1, tiled=True),
        lax.all_gather(shards[1], "seq", axis=1, tiled=True),
        lax.all_gather(shards[2], "seq", axis=1, tiled=True),
        lax.all_gather(shards[3], "seq", axis=1, tiled=True),
        lax.all_gather(shards[4], "seq", axis=1, tiled=True),
        lax.all_gather(shards[5], "seq", axis=1, tiled=True),
        lax.all_gather(shards[6], "seq", axis=1, tiled=True),
        lax.all_gather(shards[7], "seq", axis=0, tiled=True),
        lax.all_gather(shards[8], "seq", axis=0, tiled=True),
    )
    whole = (
        lax.all_gather(wide[0], "dp", axis=0, tiled=True),
        lax.all_gather(wide[1], "dp", axis=0, tiled=True),
        lax.all_gather(wide[2], "dp", axis=0, tiled=True),
        lax.all_gather(wide[3], "dp", axis=0, tiled=True),
        lax.all_gather(wide[4], "dp", axis=0, tiled=True),
        lax.all_gather(wide[5], "dp", axis=0, tiled=True),
        lax.all_gather(wide[6], "dp", axis=0, tiled=True),
    )
    return tuple(whole) + (wide[7], wide[8])


def reduce_grads(grad_sums):
    summed = (
        lax.psum_scatter(grad_sums[0], "seq", scatter_dimension=1, tiled=True),
        lax.psum_scatter(grad_sums[1], "seq", scatter_dimension=1, tiled=True),
        lax.psum_scatter(grad_sums[2], "seq", scatter_dimension=1, tiled=True),
        lax.psum_scatter(grad_sums[3], "seq", scatter_dimension=1, tiled=True),
        lax.psum_scatter(grad_sums[4], "seq", scatter_dimension=1, tiled=True),
        lax.psum_scatter(grad_sums[5], "seq", scatter_dimension=1, tiled=True),
        lax.psum_scatter(grad_sums[6], "seq", scatter_dimension=1, tiled=True),
        lax.psum_scatter(grad_sums[7], "seq", scatter_dimension=0, tiled=True),
        lax.psum_scatter(grad_sums[8], "seq", scatter_dimension=0, tiled=True),
    )
    owned = (
        lax.psum_scatter(summed[0], "dp", scatter_dimension=0, tiled=True),
        lax.psum_scatter(summed[1], "dp", scatter_dimension=0, tiled=True),
        lax.psum_scatter(summed[2], "dp", scatter_dimension=0, tiled=True),
        lax.psum_scatter(summed[3], "dp", scatter_dimension=0, tiled=True),
        lax.psum_scatter(summed[4], "dp", scatter_dimension=0, tiled=True),
        lax.psum_scatter(summed[5], "dp", scatter_dimension=0, tiled=True),
        lax.psum_scatter(summed[6], "dp", scatter_dimension=0, tiled=True),
    )
    return (tuple(owned), summed[7], summed[8])


def forward_slot(weights, tok_part, live_len, query_pos, cosine_table, sine_table):
    (
        full_query,
        full_key,
        full_value,
        full_out,
        full_gate,
        full_up,
        full_down,
        full_gain_attn,
        full_gain_ffn,
    ) = weights
    slot_position, stretched_length, model_width = tok_part.shape
    number_of_rows = slot_position * stretched_length
    query_group = QUERY_HEADS // KEY_VALUE_HEADS
    scale = HEAD_DIMENSION ** (-0.5)
    tok_float = tok_part.astype(jnp.float32).reshape(number_of_rows, model_width)
    inv_first = lax.rsqrt(jnp.mean(tok_float * tok_float, axis=-1, keepdims=True) + norm_eps)
    normed_first = tok_float * inv_first
    attention_input = (normed_first * full_gain_attn.astype(jnp.float32)).astype(jnp.bfloat16)
    unrotated_query = jnp.dot(
        attention_input, full_query, preferred_element_type=jnp.float32
    ).reshape(slot_position, stretched_length, QUERY_HEADS, HEAD_DIMENSION)
    unrotated_key = jnp.dot(attention_input, full_key, preferred_element_type=jnp.float32).reshape(
        slot_position, stretched_length, KEY_VALUE_HEADS, HEAD_DIMENSION
    )
    value_block = (
        jnp.dot(attention_input, full_value, preferred_element_type=jnp.float32)
        .astype(jnp.bfloat16)
        .reshape(slot_position, stretched_length, KEY_VALUE_HEADS * HEAD_DIMENSION)
    )
    query_b = (
        apply_rotary(unrotated_query, cosine_table, sine_table)
        .astype(jnp.bfloat16)
        .reshape(slot_position, stretched_length, KEY_VALUE_HEADS, query_group, HEAD_DIMENSION)
    )
    key_block = (
        apply_rotary(unrotated_key, cosine_table, sine_table)
        .astype(jnp.bfloat16)
        .reshape(slot_position, stretched_length, KEY_VALUE_HEADS * HEAD_DIMENSION)
    )
    empty_denominator = jnp.zeros(
        (slot_position, KEY_VALUE_HEADS, query_group, stretched_length), jnp.float32
    )
    empty_numerator = jnp.zeros(
        (slot_position, KEY_VALUE_HEADS, query_group, stretched_length, HEAD_DIMENSION), jnp.float32
    )
    key_piece = lax.all_gather(key_block, "seq", axis=1, tiled=True)
    value_piece = lax.all_gather(value_block, "seq", axis=1, tiled=True)

    def one_block(partial_value, offset, block_length):
        denominator, numerator = partial_value
        key_blk = lax.dynamic_slice_in_dim(key_piece, offset, block_length, 1).reshape(
            slot_position, block_length, KEY_VALUE_HEADS, HEAD_DIMENSION
        )
        value_blk = lax.dynamic_slice_in_dim(value_piece, offset, block_length, 1).reshape(
            slot_position, block_length, KEY_VALUE_HEADS, HEAD_DIMENSION
        )
        allowed = allowed_mask(
            query_pos, offset + jnp.arange(block_length, dtype=jnp.int32), live_len
        )
        scores = (
            jnp.einsum("schgd,snhd->shgcn", query_b, key_blk, preferred_element_type=jnp.float32)
            * scale
        )
        exp_scores = jnp.where(allowed, jnp.exp(scores), 0.0)
        denominator = denominator + jnp.sum(exp_scores, axis=-1)
        numerator = numerator + jnp.einsum(
            "shgcn,snhd->shgcd",
            exp_scores.astype(jnp.bfloat16),
            value_blk,
            preferred_element_type=jnp.float32,
        )
        return (denominator, numerator)

    denominator, numerator = over_blocks(
        key_piece.shape[1], stretched_length, one_block, (empty_denominator, empty_numerator)
    )
    attn_float = jnp.transpose(numerator / denominator[..., None], (0, 3, 1, 2, 4)).reshape(
        number_of_rows, QUERY_HEADS * HEAD_DIMENSION
    )
    attn_b = attn_float.astype(jnp.bfloat16)
    hidden = tok_float + jnp.dot(attn_b, full_out, preferred_element_type=jnp.float32)
    inv_second = lax.rsqrt(jnp.mean(hidden * hidden, axis=-1, keepdims=True) + norm_eps)
    normed_second = hidden * inv_second
    ffn_in = (normed_second * full_gain_ffn.astype(jnp.float32)).astype(jnp.bfloat16)
    gate_proj = jnp.dot(ffn_in, full_gate, preferred_element_type=jnp.float32)
    up_proj = jnp.dot(ffn_in, full_up, preferred_element_type=jnp.float32)
    hid_b = (jax.nn.silu(gate_proj) * up_proj).astype(jnp.bfloat16)
    valid_rows = (query_pos[None, :] < live_len[:, None]).reshape(number_of_rows, 1)
    out_float = jnp.where(
        valid_rows, hidden + jnp.dot(hid_b, full_down, preferred_element_type=jnp.float32), 0.0
    )
    saved = (
        attention_input,
        inv_first,
        normed_first,
        query_b,
        key_block,
        value_block,
        attn_float,
        attn_b,
        denominator,
        normed_second,
        inv_second,
        ffn_in,
        gate_proj,
        up_proj,
        hid_b,
    )
    return (out_float, valid_rows, saved)


def backward_slot(weights, saved, cotangent, live_len, query_pos, cosine_table, sine_table):
    (
        full_query,
        full_key,
        full_value,
        full_out,
        full_gate,
        full_up,
        full_down,
        full_gain_attn,
        full_gain_ffn,
    ) = weights
    (
        attention_input,
        inv_first,
        normed_first,
        query_b,
        key_block,
        value_block,
        attn_float,
        attn_b,
        denominator,
        normed_second,
        inv_second,
        ffn_in,
        gate_proj,
        up_proj,
        hid_b,
    ) = saved
    slot_position = query_b.shape[0]
    stretched_length = query_b.shape[1]
    number_of_rows = slot_position * stretched_length
    query_group = QUERY_HEADS // KEY_VALUE_HEADS
    scale = HEAD_DIMENSION ** (-0.5)
    cot_b = cotangent.astype(jnp.bfloat16)
    grad_down = jnp.einsum("rf,rd->fd", hid_b, cot_b, preferred_element_type=jnp.float32)
    grad_hid = jnp.einsum("rd,fd->rf", cot_b, full_down, preferred_element_type=jnp.float32)
    sigmoid_gate = jax.nn.sigmoid(gate_proj)
    grad_gate_b = (
        grad_hid * up_proj * sigmoid_gate * (1.0 + gate_proj * (1.0 - sigmoid_gate))
    ).astype(jnp.bfloat16)
    grad_up_b = (grad_hid * gate_proj * sigmoid_gate).astype(jnp.bfloat16)
    grad_gate = jnp.einsum("rd,rf->df", ffn_in, grad_gate_b, preferred_element_type=jnp.float32)
    grad_up = jnp.einsum("rd,rf->df", ffn_in, grad_up_b, preferred_element_type=jnp.float32)
    grad_ffn_in = jnp.einsum(
        "rf,df->rd", grad_gate_b, full_gate, preferred_element_type=jnp.float32
    ) + jnp.einsum("rf,df->rd", grad_up_b, full_up, preferred_element_type=jnp.float32)
    grad_gain_ffn = jnp.sum(grad_ffn_in * normed_second, axis=0)
    grad_normed = grad_ffn_in * full_gain_ffn.astype(jnp.float32)
    grad_hidden = cotangent + inv_second * (
        grad_normed - normed_second * jnp.mean(grad_normed * normed_second, axis=-1, keepdims=True)
    )
    grad_proj_b = grad_hidden.astype(jnp.bfloat16)
    grad_out = jnp.einsum("rq,rd->qd", attn_b, grad_proj_b, preferred_element_type=jnp.float32)
    grad_attn_b = jnp.einsum(
        "rd,qd->rq", grad_proj_b, full_out, preferred_element_type=jnp.float32
    ).astype(jnp.bfloat16)
    den_rows = jnp.transpose(denominator, (0, 3, 1, 2)).reshape(number_of_rows, QUERY_HEADS)
    grad_heads_float = grad_attn_b.astype(jnp.float32).reshape(
        number_of_rows, QUERY_HEADS, HEAD_DIMENSION
    )
    softmax_ratio = (
        jnp.sum(
            grad_heads_float * attn_float.reshape(number_of_rows, QUERY_HEADS, HEAD_DIMENSION),
            axis=-1,
        )
        / den_rows
    ).reshape(slot_position, stretched_length, QUERY_HEADS)
    scaled_gradient = (
        (grad_heads_float / den_rows[..., None])
        .astype(jnp.bfloat16)
        .reshape(slot_position, stretched_length, QUERY_HEADS * HEAD_DIMENSION)
    )
    ratio_all = lax.all_gather(softmax_ratio, "seq", axis=1, tiled=True)
    head_gradient = scaled_gradient.reshape(
        slot_position, stretched_length, KEY_VALUE_HEADS, query_group, HEAD_DIMENSION
    )
    local_softmax_ratio = jnp.transpose(
        softmax_ratio.reshape(slot_position, stretched_length, KEY_VALUE_HEADS, query_group),
        (0, 2, 3, 1),
    )[..., None]
    empty_query = jnp.zeros(
        (slot_position, KEY_VALUE_HEADS, query_group, stretched_length, HEAD_DIMENSION), jnp.float32
    )
    key_piece = lax.all_gather(key_block, "seq", axis=1, tiled=True)
    value_piece = lax.all_gather(value_block, "seq", axis=1, tiled=True)

    def one_block(partial_value, offset, block_length):
        key_blk = lax.dynamic_slice_in_dim(key_piece, offset, block_length, 1).reshape(
            slot_position, block_length, KEY_VALUE_HEADS, HEAD_DIMENSION
        )
        value_blk = lax.dynamic_slice_in_dim(value_piece, offset, block_length, 1).reshape(
            slot_position, block_length, KEY_VALUE_HEADS, HEAD_DIMENSION
        )
        allowed = allowed_mask(
            query_pos, offset + jnp.arange(block_length, dtype=jnp.int32), live_len
        )
        scores = (
            jnp.einsum("schgd,snhd->shgcn", query_b, key_blk, preferred_element_type=jnp.float32)
            * scale
        )
        exp_scores = jnp.where(allowed, jnp.exp(scores), 0.0)
        grad_prob = jnp.einsum(
            "schgd,snhd->shgcn", head_gradient, value_blk, preferred_element_type=jnp.float32
        )
        grad_score = (exp_scores * (grad_prob - local_softmax_ratio)).astype(jnp.bfloat16)
        return (
            partial_value
            + jnp.einsum(
                "shgcn,snhd->shgcd", grad_score, key_blk, preferred_element_type=jnp.float32
            )
            * scale
        )

    grad_query = over_blocks(key_piece.shape[1], stretched_length, one_block, empty_query)
    query_flat = query_b.reshape(slot_position, stretched_length, QUERY_HEADS * HEAD_DIMENSION)
    per_head_keys = key_block.reshape(
        slot_position, stretched_length, KEY_VALUE_HEADS, HEAD_DIMENSION
    )
    per_head_values = value_block.reshape(
        slot_position, stretched_length, KEY_VALUE_HEADS, HEAD_DIMENSION
    )
    empty_key_value = jnp.zeros(
        (slot_position, KEY_VALUE_HEADS, stretched_length, HEAD_DIMENSION), jnp.float32
    )
    query_piece = lax.all_gather(query_flat, "seq", axis=1, tiled=True)
    grad_piece = lax.all_gather(scaled_gradient, "seq", axis=1, tiled=True)

    def one_block(partial_value, offset, block_length):
        grad_key, value_gradient = partial_value
        query_blk = lax.dynamic_slice_in_dim(query_piece, offset, block_length, 1).reshape(
            slot_position, block_length, KEY_VALUE_HEADS, query_group, HEAD_DIMENSION
        )
        grad_blk = lax.dynamic_slice_in_dim(grad_piece, offset, block_length, 1).reshape(
            slot_position, block_length, KEY_VALUE_HEADS, query_group, HEAD_DIMENSION
        )
        ratio_blk = lax.dynamic_slice_in_dim(ratio_all, offset, block_length, 1).reshape(
            slot_position, block_length, KEY_VALUE_HEADS, query_group
        )
        ratio_blk = jnp.transpose(ratio_blk, (0, 2, 3, 1))[..., None]
        remote_pos = offset + jnp.arange(block_length, dtype=jnp.int32)
        allowed = allowed_mask(remote_pos, query_pos, live_len)
        scores = (
            jnp.einsum(
                "snhgd,schd->shgnc", query_blk, per_head_keys, preferred_element_type=jnp.float32
            )
            * scale
        )
        exp_scores = jnp.where(allowed, jnp.exp(scores), 0.0)
        value_gradient = value_gradient + jnp.einsum(
            "shgnc,snhgd->shcd",
            exp_scores.astype(jnp.bfloat16),
            grad_blk,
            preferred_element_type=jnp.float32,
        )
        grad_prob = jnp.einsum(
            "snhgd,schd->shgnc", grad_blk, per_head_values, preferred_element_type=jnp.float32
        )
        grad_score = (exp_scores * (grad_prob - ratio_blk)).astype(jnp.bfloat16)
        grad_key = (
            grad_key
            + jnp.einsum(
                "shgnc,snhgd->shcd", grad_score, query_blk, preferred_element_type=jnp.float32
            )
            * scale
        )
        return (grad_key, value_gradient)

    grad_key, value_gradient = over_blocks(
        query_piece.shape[1], stretched_length, one_block, (empty_key_value, empty_key_value)
    )
    grad_query = jnp.transpose(grad_query, (0, 3, 1, 2, 4)).reshape(
        slot_position, stretched_length, QUERY_HEADS, HEAD_DIMENSION
    )
    grad_query_b = (
        apply_rotary(grad_query, cosine_table, -sine_table)
        .astype(jnp.bfloat16)
        .reshape(number_of_rows, QUERY_HEADS * HEAD_DIMENSION)
    )
    grad_key_b = (
        apply_rotary(jnp.transpose(grad_key, (0, 2, 1, 3)), cosine_table, -sine_table)
        .astype(jnp.bfloat16)
        .reshape(number_of_rows, KEY_VALUE_HEADS * HEAD_DIMENSION)
    )
    grad_value_b = (
        jnp.transpose(value_gradient, (0, 2, 1, 3))
        .astype(jnp.bfloat16)
        .reshape(number_of_rows, KEY_VALUE_HEADS * HEAD_DIMENSION)
    )
    grad_wq = jnp.einsum(
        "rd,rq->dq", attention_input, grad_query_b, preferred_element_type=jnp.float32
    )
    grad_wk = jnp.einsum(
        "rd,rq->dq", attention_input, grad_key_b, preferred_element_type=jnp.float32
    )
    grad_wv = jnp.einsum(
        "rd,rq->dq", attention_input, grad_value_b, preferred_element_type=jnp.float32
    )
    grad_attn_in = jnp.einsum(
        "rq,dq->rd", grad_query_b, full_query, preferred_element_type=jnp.float32
    )
    grad_attn_in = grad_attn_in + jnp.einsum(
        "rq,dq->rd", grad_key_b, full_key, preferred_element_type=jnp.float32
    )
    grad_attn_in = grad_attn_in + jnp.einsum(
        "rq,dq->rd", grad_value_b, full_value, preferred_element_type=jnp.float32
    )
    grad_gain_attn = jnp.sum(grad_attn_in * normed_first, axis=0)
    grad_first = grad_attn_in * full_gain_attn.astype(jnp.float32)
    grad_tokens = grad_hidden + inv_first * (
        grad_first - normed_first * jnp.mean(grad_first * normed_first, axis=-1, keepdims=True)
    )
    return (
        (
            grad_wq,
            grad_wk,
            grad_wv,
            grad_out,
            grad_gate,
            grad_up,
            grad_down,
            grad_gain_attn,
            grad_gain_ffn,
        ),
        grad_tokens,
    )


def per_device(
    tokens,
    teacher,
    lengths,
    w_query,
    key_weight,
    value_weight,
    w_out,
    w_gate,
    w_up,
    w_down,
    gain_attn,
    gain_ffn,
):
    shards = (w_query, key_weight, value_weight, w_out, w_gate, w_up, w_down, gain_attn, gain_ffn)
    slot_count, stretched_length, model_width = tokens.shape
    total_tokens = slot_count * lax.axis_size("dp") * stretched_length * lax.axis_size("seq")
    query_pos = lax.axis_index("seq") * stretched_length + jnp.arange(
        stretched_length, dtype=jnp.int32
    )
    cosine_table, sine_table = rope_tables(query_pos, HEAD_DIMENSION)
    out_rows = []
    stored = []
    differences = []
    squares_local = jnp.zeros((), jnp.float32)
    count_local = jnp.zeros((), jnp.float32)
    for micro in range(slot_count):
        weights = collect(shards)
        live_len = lengths[micro : micro + 1]
        out_float, valid_rows, saved = forward_slot(
            weights, tokens[micro : micro + 1], live_len, query_pos, cosine_table, sine_table
        )
        teach_float = teacher[micro].astype(jnp.float32)
        difference = jnp.where(valid_rows, out_float - teach_float, 0.0)
        squares_local = squares_local + jnp.sum(difference * difference)
        count_local = count_local + jnp.sum(valid_rows.astype(jnp.float32))
        out_rows.append(out_float.astype(jnp.bfloat16).reshape(1, stretched_length, model_width))
        stored.append(saved)
        differences.append(difference)
    loss_sum, count_sum = lax.psum((squares_local, count_local), ("dp", "seq"))
    loss = loss_sum / count_sum
    factor = total_tokens / count_sum
    grad_sums = None
    token_grads = []
    for micro in range(slot_count):
        weights = collect(shards)
        grads, grad_tokens = backward_slot(
            weights,
            stored[micro],
            factor * differences[micro],
            lengths[micro : micro + 1],
            query_pos,
            cosine_table,
            sine_table,
        )
        grad_sums = grads if grad_sums is None else jax.tree.map(jnp.add, grad_sums, grads)
        token_grads.append(grad_tokens.reshape(1, stretched_length, model_width))
    owned, gain_part_attn, gain_part_ffn = reduce_grads(grad_sums)
    gain_totals = lax.psum((gain_part_attn, gain_part_ffn), "dp")
    output = jnp.concatenate(out_rows, axis=0)
    tokens_grad = jnp.concatenate(token_grads, axis=0)
    return (
        output,
        loss,
        tokens_grad,
        owned[0],
        owned[1],
        owned[2],
        owned[3],
        owned[4],
        owned[5],
        owned[6],
        gain_totals[0],
        gain_totals[1],
    )


MESH_ID = pl.DeviceIdType.MESH
VMEM_MOST = 64 * 1024 * 1024 - 128 * 1024


class Place(tuple):
    def with_line(self):
        z = self[2]
        self.line = (0,) + tuple(pick(z, v) for v in ((1, -1, -1, -1), (2, 1, 1, -2), (3, 2, -2, -3)))
        self.sign = (0,) + tuple(jnp.where(offset > 0, 1, -1) for offset in self.line[1:])
        return self


def position():
    row = lax.axis_index("dp")
    column = lax.axis_index("seq")
    return Place((lax.rem(column, 2), row // 2, column // 2, lax.rem(row, 2))).with_line()


def mesh_place(x, y, z, c):
    return (2 * y + c, 2 * z + x)


def step_to(place, axis, sign=1):
    x, y, z, c = place
    if axis == "x":
        return (1 - x, y, z, c)
    if axis == "y":
        return (x, 1 - y, z, c)
    if axis == "z":
        return (x, y, z + sign, c)
    return (x, y, z, 1 - c)


def pick(z, values):
    return sum(jnp.where(z == i, v, 0) for i, v in enumerate(values) if v)


def shifted(place, rel):
    x, y, z, c = place
    dx, dy, rank = rel
    return ((1 - x) if dx else x, (1 - y) if dy else y, z + place.line[rank], c)


def on_line(z):
    return jnp.logical_and(z >= 0, z < 4)


def greet(place, lines):
    x, y, z, c = place
    d, s = mesh_place(*place)
    barrier = pltpu.get_barrier_semaphore()

    def signal(who):
        pl.semaphore_signal(barrier, inc=1, device_id=who, device_id_type=MESH_ID)

    if lines:
        for k in range(1, 8):
            signal((d, lax.rem(s + k, 8)))
        for k in range(1, 4):
            signal((lax.rem(d + k, 4), s))
        pl.semaphore_wait(barrier, 10)
        return
    for axis in "xyc":
        signal(mesh_place(*step_to(place, axis)))
    pl.when(z < 3)(lambda: signal(mesh_place(x, y, z + 1, c)))
    pl.when(z > 0)(lambda: signal(mesh_place(x, y, z - 1, c)))
    pl.semaphore_wait(barrier, 3 + jnp.where(z > 0, 1, 0) + jnp.where(z < 3, 1, 0))


def wait_bytes(region, sem):
    pltpu.make_async_copy(region, region, sem).wait()


def spread_order(order):
    held = [((0, 0, 0), -1)]
    for level, axis in enumerate(order):
        new = []
        if axis == "z":
            new = [((rel[0], rel[1], rank), level) for rank in (1, 2, 3) for rel, _ in held]
        else:
            new = [((1, rel[1], rel[2]) if axis == "x" else (rel[0], 1, rel[2]), level) for rel, _ in held]
        held = held + new
    return held


class Spread:
    def __init__(self, place, order, own, spot, sems, job, pair=None, amount=None):
        self.place, self.order, self.own, self.spot = place, order, own, spot
        self.recv, self.send, self.recv_core, self.send_core = sems
        self.job, self.pair, self.amount = job, pair, amount
        self.pieces = spread_order(order)

    def number(self, who):
        x, y, z, _ = who
        return z * 4 + y * 2 + x

    def go(self, rel, level, target):
        who = shifted(self.place, rel)
        pltpu.make_async_remote_copy(
            src_ref=self.own if level < 0 else self.spot(who),
            dst_ref=self.spot(who),
            send_sem=self.send.at[self.job],
            recv_sem=self.recv.at[self.job, self.number(who)],
            device_id=mesh_place(*target),
            device_id_type=MESH_ID,
        ).start()

    def to_core(self, rel):
        who = shifted(self.place, rel)
        pltpu.make_async_remote_copy(
            src_ref=self.pair(who),
            dst_ref=self.pair(who),
            send_sem=self.send_core.at[self.job],
            recv_sem=self.recv_core.at[self.job],
            device_id=mesh_place(*step_to(self.place, "c")),
            device_id_type=MESH_ID,
        ).start()

    def steps(self):
        out = []
        arrived = set()
        z = self.place[2]
        for rel, level in self.pieces:

            def run(rel=rel, level=level):
                arrived.add(rel)
                who = shifted(self.place, rel)
                if level >= 0:
                    there = self.spot(who)
                    pltpu.make_async_copy(there, there, self.recv.at[self.job, self.number(who)]).wait()
                if level >= 0 and self.order[level] == "z":
                    on = z - self.place.sign[rel[2]]
                    pl.when(on_line(on))(lambda: self.go(rel, level, (self.place[0], self.place[1], on, self.place[3])))
                for axis in self.order[level + 1:]:
                    if axis == "z":
                        pl.when(z < 3)(lambda: self.go(rel, level, step_to(self.place, "z", 1)))
                        pl.when(z > 0)(lambda: self.go(rel, level, step_to(self.place, "z", -1)))
                    else:
                        self.go(rel, level, step_to(self.place, axis))
                if self.pair is not None and (1 - rel[0], rel[1], rel[2]) in arrived:
                    self.to_core(rel)

            out.append(run)
        return out

    def sent(self):
        total = [0, 0]
        for i, z in enumerate((0, 1)):
            for rel, level in self.pieces:
                if level >= 0 and self.order[level] == "z":
                    offset = (0, ((1, -1)[z]), ((2, 1)[z]), ((3, 2)[z]))[rel[2]]
                    on = z - (1 if offset > 0 else -1)
                    total[i] += 0 <= on < 4
                for axis in self.order[level + 1:]:
                    total[i] += (1, 2)[z] if axis == "z" else 1
        return total

    def wait_core(self):
        wait_bytes(self.amount(16), self.recv_core.at[self.job])

    def finish(self):
        ends, inner = self.sent()
        z = self.place[2]
        at_end = jnp.logical_or(z == 0, z == 3)
        pl.when(at_end)(lambda: wait_bytes(self.amount(ends), self.send.at[self.job]))
        pl.when(jnp.logical_not(at_end))(lambda: wait_bytes(self.amount(inner), self.send.at[self.job]))
        if self.pair is not None:
            wait_bytes(self.amount(16), self.send_core.at[self.job])


def fold_pieces(order):
    out = []
    for dx in (0, 1):
        for dy in (0, 1) if "y" in order else (0,):
            for rank in (0, 1, 2, 3):
                differs = {"x": dx, "y": dy, "z": rank}
                stage = next((i for i, axis in enumerate(order) if differs[axis]), len(order))
                out.append(((dx, dy, rank), stage))
    return sorted(out, key=lambda item: (item[1], -item[0][2], -item[0][0] - item[0][1]))


def fold_slots(order):
    base, starts = 0, []
    for level, axis in enumerate(order):
        starts.append(base)
        after = order[level + 1:]
        wide = (4 if "z" in after else 1) * (2 if "x" in after else 1) * (2 if "y" in after else 1)
        base += wide * 5 if axis == "z" else wide
    return starts, base


class Fold:
    def __init__(self, place, order, mine, arrived, sems, job, out, amount, ready=None):
        self.place, self.order, self.mine, self.arrived = place, order, mine, arrived
        self.send, self.recv = sems
        self.job, self.out, self.amount, self.ready = job, out, amount, ready
        self.pieces = fold_pieces(order)
        self.base, self.slots = fold_slots(order)

    def slot(self, level, rel, last):
        index = 0
        at_z = self.place[2] + self.place.line[rel[2]]
        for other in self.order[level + 1:]:
            size = 4 if other == "z" else 2
            index = index * size + (at_z if other == "z" else (rel[0] if other == "x" else rel[1]))
        if self.order[level] == "z":
            index = index * 5 + (4 if last is True else (at_z if last is False else jnp.where(last, 4, at_z)))
        return self.base[level] + index

    def take(self, mine, slot):
        there = self.arrived.at[slot]
        pltpu.make_async_copy(there, there, self.recv.at[self.job, slot]).wait()
        mine[...] = mine[...] + self.arrived[slot]

    def steps(self):
        out = []
        present = set()
        z = self.place[2]
        for rel, stage in self.pieces:

            def run(rel=rel, stage=stage):
                if self.ready is not None and rel[1] not in present:
                    present.add(rel[1])
                    self.ready(rel[1])
                mine = self.mine(shifted(self.place, rel))
                offset, sign = self.place.line[rel[2]], self.place.sign[rel[2]]
                for level in range(min(stage + 1, len(self.order))):
                    if self.order[level] == "z":
                        if level < stage:
                            pl.when(z > 0)(lambda: self.take(mine, self.slot(level, rel, False)))
                            pl.when(z < 3)(lambda: self.take(mine, self.slot(level, rel, True)))
                        else:
                            behind = z - sign
                            pl.when(on_line(behind))(lambda: self.take(mine, self.slot(level, rel, False)))
                    elif level < stage:
                        self.take(mine, self.slot(level, rel, False))
                if stage == len(self.order):
                    self.out(mine[...].astype(jnp.float32))
                    return
                axis = self.order[stage]
                if axis == "z":
                    target = (self.place[0], self.place[1], z + sign, self.place[3])
                else:
                    target = step_to(self.place, axis)
                slot = self.slot(stage, rel, offset == -1 if axis == "z" else False)
                pltpu.make_async_remote_copy(
                    src_ref=mine,
                    dst_ref=self.arrived.at[slot],
                    send_sem=self.send.at[self.job],
                    recv_sem=self.recv.at[self.job, slot],
                    device_id=mesh_place(*target),
                    device_id_type=MESH_ID,
                ).start()

            out.append(run)
        return out

    def finish(self):
        wait_bytes(self.amount(len(self.pieces) - 1), self.send.at[self.job])


CAT_JOBS = (("cat", 0, 96, "xzy"), ("cat", 96, 96, "yzx"), ("cat", 192, 96, "zxy"))
FFN_JOBS = (
    ("gate", 0, 144, "xzy"), ("up", 0, 96, "yzx"), ("down", 0, 384, "zxy"),
    ("gate", 144, 144, "xzy"), ("up", 96, 96, "yzx"), ("down", 384, 384, "zxy"), ("up", 192, 96, "zxy"),
)
KV_JOBS = tuple((slot, 256 * third, "xz" if (slot, third) == (1, 2) else "zx") for slot in (0, 1) for third in (0, 1, 2))
FOLD_FFN = tuple(job[:3] + (job[3][::-1],) for job in FFN_JOBS)
FOLD_CAT = tuple(job[:3] + (job[3][::-1],) for job in CAT_JOBS)
FOLD_KV = tuple((slot, row, order[::-1]) for slot, row, order in KV_JOBS)
FFN_NAMES = ("gate", "up", "down")


def job_shape(job):
    return (144, job[2]) if job[0] == "down" else (job[2], 384)


def piece_of(ref, job, paired=False):
    name, first, count, _ = job
    double = 2 if paired else 1

    def spot(who):
        x, y, z, c = who
        d, s = mesh_place(0 if paired else x, y, z, c)
        if name == "down":
            return ref.at[
                pl.ds(pl.multiple_of(s * 144, 16), 144 * double), pl.ds(pl.multiple_of(d * 768 + first, 128), count)
            ]
        return ref.at[
            pl.ds(pl.multiple_of(d * 288 + first, 8), count), pl.ds(pl.multiple_of(s * 384, 128), 384 * double)
        ]

    return spot


def region(ref, elements, rows, columns):
    units = elements // 2048
    wide = max(k for k in range(1, columns // 128 + 1) if units % k == 0 and units // k <= rows // 16)
    return ref.at[pl.ds(0, units // wide * 16), pl.ds(0, wide * 128)]


def amount_of(ref, job):
    rows, columns = job_shape(job)
    return lambda pieces: region(ref, pieces * rows * columns, *ref.shape)


def own_part(ref, job):
    name, first, count, _ = job
    return ref.at[:, pl.ds(first, count)] if name == "down" else ref.at[pl.ds(first, count), :]


def kv_spot(ref, slot, row):
    def spot(who):
        _, s = mesh_place(*who)
        return ref.at[slot, pl.ds(row, 256), pl.ds(pl.multiple_of(s * 128, 128), 128)]

    return spot


def kv_amount(ref):
    return lambda pieces: ref.at[0, pl.ds(0, 32 * pieces), :]


def make_spreads(place, jobs, shards, wholes, sems):
    return [
        Spread(
            place, job[3], own_part(shards[job[0]], job), piece_of(wholes[job[0]], job), sems, j,
            piece_of(wholes[job[0]], job, True), amount_of(wholes[job[0]], job),
        )
        for j, job in enumerate(jobs)
    ]


def make_kv_spreads(place, own, whole, sems):
    return [
        Spread(
            place, order, own.at[pl.ds(row, 256), pl.ds(slot * 128, 128)], kv_spot(whole, slot, row),
            (sems[0], sems[1], None, None), j, None, kv_amount(whole),
        )
        for j, (slot, row, order) in enumerate(KV_JOBS)
    ]


def spread_sems(jobs):
    n = len(jobs)
    return [
        pltpu.SemaphoreType.DMA((n, 16)), pltpu.SemaphoreType.DMA((n,)),
        pltpu.SemaphoreType.DMA((n,)), pltpu.SemaphoreType.DMA((n,)),
    ]


def fold_scratch(jobs, paired):
    n = len(jobs)
    most = max(fold_slots(job[3])[1] for job in jobs)
    scratch = [
        pltpu.SemaphoreType.DMA((n,)), pltpu.SemaphoreType.DMA((n, most)),
        pltpu.SemaphoreType.DMA((n, 2)), pltpu.SemaphoreType.DMA((n, 2)), pltpu.SemaphoreType.DMA((n, 2)),
    ]
    for job in jobs:
        rows, columns = job_shape(job)
        block = (2, 1152, columns) if job[0] == "down" else (2, rows, 3072)
        scratch += [
            pltpu.VMEM(block, jnp.bfloat16), pltpu.VMEM((fold_slots(job[3])[1], rows, columns), jnp.bfloat16)
        ]
        scratch += [pltpu.VMEM(block, jnp.bfloat16)] if paired else []
    return scratch


class JobFold:
    def __init__(self, place, job, j, sums, owned, scratch, paired):
        self.place, self.job, self.j, self.sums, self.paired = place, job, j, sums, paired
        send, recv, self.load_sem, self.core_send, self.core_recv = scratch[:5]
        each = 3 if paired else 2
        self.acc, arrived = scratch[5 + each * j: 7 + each * j]
        self.other = scratch[7 + each * j] if paired else None
        name, first, count, order = job

        def mine(who):
            x, y, z, c = who
            s = 2 * z + x
            if name == "down":
                return self.acc.at[y, pl.ds(pl.multiple_of(s * 144, 16), 144), :]
            return self.acc.at[y, :, pl.ds(pl.multiple_of(s * 384, 128), 384)]

        def out(value):
            if name == "down":
                owned[:, first: first + count] = value
            else:
                owned[first: first + count, :] = value

        self.fold = Fold(place, order, mine, arrived, (send, recv), j, out, amount_of(sums, job), self.ready)

    def block(self, y, c):
        name, first, count, _ = self.job
        d = 2 * y + c if self.paired else y
        if name == "down":
            return self.sums.at[:, pl.ds(pl.multiple_of(d * 768 + first, 128), count)]
        return self.sums.at[pl.ds(pl.multiple_of(d * 288 + first, 8), count), :]

    def local_copy(self, dy):
        x, y, z, c = self.place
        at = (1 - y) if dy else y
        return pltpu.make_async_copy(self.block(at, c), self.acc.at[at], self.load_sem.at[self.j, dy])

    def core_copy(self, dy):
        x, y, z, c = self.place
        at = (1 - y) if dy else y
        return pltpu.make_async_remote_copy(
            src_ref=self.block(at, 1 - c),
            dst_ref=self.other.at[at],
            send_sem=self.core_send.at[self.j, dy],
            recv_sem=self.core_recv.at[self.j, dy],
            device_id=mesh_place(x, y, z, 1 - c),
            device_id_type=MESH_ID,
        )

    def begin(self, dy):
        if self.paired:
            self.core_copy(dy).start()
        self.local_copy(dy).start()

    def ready(self, dy):
        y = self.place[1]
        at = (1 - y) if dy else y
        self.local_copy(dy).wait()
        if not self.paired:
            return
        self.core_copy(dy).wait_recv()

        def add(k, _):
            if self.job[0] == "down":
                part = (at, pl.ds(pl.multiple_of(k * 144, 16), 144), slice(None))
            else:
                part = (at, slice(None), pl.ds(pl.multiple_of(k * 384, 128), 384))
            self.acc[part] = self.acc[part] + self.other[part]
            return _

        lax.fori_loop(0, 8, add, 0)

    def finish(self):
        self.fold.finish()
        for dy in (0, 1) if self.paired else ():
            self.core_copy(dy).wait_send()


class Notes:
    def __init__(self, place, tile_of, own, by_seq, by_dp, sems):
        self.d, self.s = mesh_place(*place)
        self.tile_of, self.own, self.by_seq, self.by_dp = tile_of, own, by_seq, by_dp
        self.seq_send, self.seq_recv, self.dp_send, self.dp_recv = sems

    def along_seq(self, k):
        peer = lax.rem(self.s + k, 8)
        return pltpu.make_async_remote_copy(
            src_ref=self.tile_of(peer), dst_ref=self.by_seq.at[self.s], send_sem=self.seq_send.at[k],
            recv_sem=self.seq_recv.at[self.s], device_id=(self.d, peer), device_id_type=MESH_ID,
        )

    def along_dp(self, k):
        peer = lax.rem(self.d + k, 4)
        return pltpu.make_async_remote_copy(
            src_ref=self.own, dst_ref=self.by_dp.at[self.d], send_sem=self.dp_send.at[k],
            recv_sem=self.dp_recv.at[self.d], device_id=(peer, self.s), device_id_type=MESH_ID,
        )

    def wait_seq(self):
        for k in range(1, 8):
            peer = lax.rem(self.s + k, 8)
            there = self.by_seq.at[peer]
            pltpu.make_async_copy(there, there, self.seq_recv.at[peer]).wait()

    def wait_dp(self):
        for k in range(1, 4):
            peer = lax.rem(self.d + k, 4)
            there = self.by_dp.at[peer]
            pltpu.make_async_copy(there, there, self.dp_recv.at[peer]).wait()


NOTE_SEMS = [
    pltpu.SemaphoreType.DMA((8,)), pltpu.SemaphoreType.DMA((8,)),
    pltpu.SemaphoreType.DMA((4,)), pltpu.SemaphoreType.DMA((4,)),
]


FORWARD_PLAN = (
    (0, 100, 200,),
    (108, 1, 2, 101, 102, 8, 201, 204, 208, 4, 3, 202, 9, 104, 103, 205, 10, 109, 110, 209, 5, 105, 206, 203,
        11, 210, 6, 212, 106, 112, 207, 7, 213, 107,),
    (10500, 113, 211, 114, 10000, 10600, 214, 115, 14, 111, 10100, 10200, 10300, 10400, 12, 215, 15, 13,),
    (20000, 20100, 20200, 20300, 20400, 20500,),
    (10002, 10001, 20001, 20101, 20002, 20004, 10504, 20201, 20104, 10204, 20301, 20204, 10102, 20401, 10501,
        20304, 10101, 10008, 10201, 20502, 10604, 20501, 20404, 10108, 10302, 10301, 10601, 10402, 10401,
        20102, 10508, 10004, 10208, 20202, 10308, 10408, 20302, 10608, 10104, 20402, 20005, 10202, 10009,
        20105, 10502, 20205, 10209, 10304, 10003, 10404, 10010, 10602, 20503, 20504, 20305, 20405, 10509,
        10103, 10309, 10505, 10205, 20003, 10609, 10303, 10109, 10110, 10310, 20103, 20006, 10605, 20203,
        10403, 20505, 20106, 10005, 20303, 10210, 20206, 10512, 10409, 10410, 10510, 10212, 20306, 10613,
        20406, 10506, 10203, 10105, 10503, 10612, 10206, 10305, 10610, 10012, 10405, 20403, 10603, 10606,
        20107, 10011, 10213, 20007, 10006, 10312, 20506, 20207, 10513, 10111, 10112, 20307, 10311, 10507,
        20507, 10511, 10411, 20407,),
    (
        (1, (10211, 10306, 10412,)),
        (2, (10207, 10106, 10013, 10607,)),
        (3, (10406,)),
        (5, (10007,)),
        (8, (10113,)),
        (9, (10107, 10514,)),
        (11, (10307, 10313,)),
    ),
    (10407, 10413, 10214, 10611, 10614, 10014, 10114, 10515, 10414, 10215, 10314, 10615, 10015, 10115, 10415, 10315,),
)
BACKWARD_PLAN = (
    (),
    (
        (0, (10400,)),
        (3, (10200,)),
        (4, (10300,)),
        (5, (10202,)),
        (6, (20000, 20100, 20200, 20001, 20101, 20002, 20201, 20102, 20202, 10600, 10000, 10001,)),
        (7, (10201, 20003, 20004, 10301, 20103, 20104,)),
        (8, (20203, 20204, 20005,)),
        (9, (10500, 20105, 10401,)),
        (10, (10303, 20006, 20205,)),
        (11, (20106, 10302,)),
    ),
    (20400, 20401, 20402, 20206, 10602, 10601, 10402, 20403, 10002, 10203, 20500, 20300, 10603, 10502, 10403,
        20301, 10100, 10003, 10204, 10305, 10304, 20302, 10604, 10004, 20501, 20303, 10404, 10501, 10503,
        20007, 10101, 20502, 20504, 20107, 20207, 20503, 20505, 20404, 20405, 10605, 10504, 10205, 10102,
        10005, 10206, 10405, 10207, 10208, 10209, 10006, 20506, 10306, 20406, 10606, 10406, 10505, 10103,
        20304, 10307, 10308, 10607, 10608, 10609, 20305, 10506, 10407, 10408, 20306, 10104, 10007, 10008,
        10009, 10309, 10507, 10508, 10509, 10105, 10409, 20407, 10010, 10310, 10410, 10210, 10106, 20507,
        10107, 10108, 10109, 20307,),
    (
        (3, (10012, 10412,)),
        (4, (10312, 10011,)),
        (5, (10311, 10610,)),
    ),
    (100, 101, 10510, 10411, 10110, 10413, 10013, 0, 10313, 200, 102, 10112, 10211,),
    (103, 104, 106, 10111, 10212, 105, 10113,),
    (10014, 10414, 1, 201, 10611, 10314, 107, 2, 202, 10213, 108, 10612, 10511, 3, 203, 205, 109, 10214, 4, 10512,),
    (204, 5, 10613, 10114, 6, 206, 10614, 110, 112, 10513, 111, 113, 7, 207, 208, 10514, 10015, 10315, 10415, 8,),
    (209, 114, 10215, 210, 9, 10, 12, 10115, 10615, 115, 211, 212, 213, 11, 13, 10515, 214, 14, 15, 215,),
)


def dot(a, b):
    return jnp.dot(a, b, preferred_element_type=jnp.float32)


def dot_t(a, b):
    return lax.dot_general(a, b, (((1,), (1,)), ((), ())), preferred_element_type=jnp.float32)


def t_dot(a, b):
    return lax.dot_general(a, b, (((0,), (0,)), ((), ())), preferred_element_type=jnp.float32)


def repeat(count, body):
    def step(k, nothing):
        body(k)
        return nothing

    lax.fori_loop(0, count, step, 0)


def rows_at(k, size, base=0):
    return pl.ds(pl.multiple_of(base + k * size, 16), size)


def lanes_at(k, size, base=0):
    return pl.ds(pl.multiple_of(base + k * size, 128), size)


def rotate(u, cosine, sine):
    front, back = u[:32], u[32:]
    return jnp.concatenate([front * cosine - back * sine, front * sine + back * cosine], axis=0)


def probabilities(keys, query, limit, chunk):
    scores = t_dot(keys, query) * (HEAD_DIMENSION ** (-0.5))
    key_pos = chunk * 256 + lax.broadcasted_iota(jnp.int32, (256, 384), 0)
    return jnp.where(key_pos <= limit, jnp.exp(scores), 0.0)


def heads_wide(ref, group, lanes):
    return jnp.concatenate(
        [ref[pl.ds(pl.multiple_of(group * 192 + 64 * i, 64), 64), lanes] for i in range(3)], axis=1
    )


def key_limit(length, s):
    query_pos = s * 128 + lax.broadcasted_iota(jnp.int32, (1, 128), 1)
    return jnp.concatenate([jnp.minimum(query_pos, length - 1)] * 3, axis=1)


def forward_body(
    lengths, query_t, key_t, value_t, out_t, gain_a, gain_f, x, cosine, sine, gate, up, down,
    gate_w, up_w, down_w, wcat, kept_in_t, kept_query, kept_kv, kept_attn, kept_denom, notes, hidden,
    tile, cat_t, cat, attn_in_t, query, keys_values, attn, denom,
    attn_in, raw, own_kv, weights, proj, seq_in, dp_in, own_sems, note_a, note_b, note_c, note_d, *sems
):
    place = position()
    d, s = mesh_place(*place)
    row = 0
    for part in (query_t, key_t, value_t, out_t):
        cat_t[row: row + part.shape[0], 0:288] = part[...].astype(jnp.float32)
        row += part.shape[0]
    cat[...] = cat_t[...].T[0:288, :].astype(jnp.bfloat16)
    tile[...] = jnp.zeros_like(tile)
    for k in range(8):
        def own_gains(k=k):
            tile[0:1, 144 * k: 144 * k + 144] = gain_a[...].astype(jnp.float32).reshape(1, 144)
            tile[1:2, 144 * k: 144 * k + 144] = gain_f[...].astype(jnp.float32).reshape(1, 144)

        pl.when(s == k)(own_gains)
    tile[2:3, :] = jnp.broadcast_to((lengths[0] + lengths[1]).astype(jnp.float32), (1, 1152))
    greet(place, True)
    shards = dict(zip(FFN_NAMES, (gate, up, down)))
    wholes = dict(zip(FFN_NAMES, (gate_w, up_w, down_w)))
    cat_spreads = make_spreads(place, CAT_JOBS, {"cat": cat}, {"cat": weights}, sems[:4])
    ffn_spreads = make_spreads(place, FFN_JOBS, shards, wholes, sems[4:8])
    kv_spreads = make_kv_spreads(place, own_kv, keys_values, sems[8:10])
    steps = [[spread.steps() for spread in family] for family in (cat_spreads, ffn_spreads, kv_spreads)]

    def run(tokens):
        for token in tokens:
            steps[token // 10000][token // 100 % 100][token % 100]()

    tiles = Notes(place, lambda peer: tile, tile, seq_in, dp_in, (note_a, note_b, note_c, note_d))
    run(FORWARD_PLAN[0])
    for k in range(1, 8):
        tiles.along_seq(k).start()
    for k in range(1, 4):
        tiles.along_dp(k).start()
    own = [
        pltpu.make_async_copy(
            shards[name], piece_of(wholes[name], (name, 0, 768 if name == "down" else 288, ""))(place), own_sems.at[k]
        )
        for k, name in enumerate(FFN_NAMES)
    ]
    for copy in own:
        copy.start()
    weights[rows_at(d, 288), lanes_at(s, 384)] = cat[...]
    for copy in own:
        copy.wait()
    run(FORWARD_PLAN[1])
    tiles.wait_seq()
    tiles.wait_dp()
    seq_in[s] = tile[...]
    dp_in[d] = tile[...]
    gains = seq_in[0]
    for k in range(1, 8):
        gains = gains + seq_in[k]
    notes[0:8, :] = gains
    notes[8:16, :] = dp_in[0] + dp_in[1] + dp_in[2] + dp_in[3]

    def norm(k):
        rows = rows_at(k, 32)
        part = x[rows, :].astype(jnp.float32)
        scale = lax.rsqrt(jnp.mean(part * part, axis=-1, keepdims=True) + norm_eps)
        attn_in[rows, :] = (part * scale * notes[0:1, :]).astype(jnp.bfloat16)

    repeat(8, norm)
    attn_in_t[...] = attn_in[...].T
    run(FORWARD_PLAN[2])
    for spread in cat_spreads:
        spread.wait_core()

    def project(b):
        block = dot(attn_in[...], weights[:, lanes_at(b, 384)][:, :256]).T
        raw[rows_at(b, 144), :] = block[:144]
        raw[rows_at(b, 48, 1152), :] = block[144:192]
        raw[rows_at(b, 48, 1536), :] = block[192:240]

    repeat(8, project)
    out_copy = pltpu.make_async_copy(weights, wcat, own_sems.at[3])
    out_copy.start()

    def turn(ref, rows_of):
        def one(h):
            ref[rows_at(h, 64), :] = rotate(raw[rows_of(h), :], cosine[...], sine[...]).astype(jnp.bfloat16)

        return one

    repeat(6, turn(own_kv, lambda h: rows_at(h, 64, 1152)))
    own_kv[384:768, :] = raw[1536:1920, :].astype(jnp.bfloat16)
    repeat(18, turn(query, lambda h: rows_at(h, 64)))
    keeps = [
        pltpu.make_async_copy(source, target, own_sems.at[4 + k])
        for k, (source, target) in enumerate(
            ((attn_in_t, kept_in_t), (query, kept_query), (keys_values, kept_kv), (attn, kept_attn), (denom, kept_denom))
        )
    ]
    keeps[0].start()
    keeps[1].start()
    run(FORWARD_PLAN[3])
    here = lanes_at(s, 128)
    for slot in range(2):
        keys_values[slot, :, here] = own_kv[:, slot * 128: slot * 128 + 128]
    run(FORWARD_PLAN[4])
    keeps[2].start()

    def attend(slot, group):
        lanes = lanes_at(slot, 128)
        bound = key_limit(lengths[slot], s)
        wide = heads_wide(query, group, lanes)

        def one_chunk(chunk, carry):
            total, numer = carry
            cols = lanes_at(chunk, 256)
            expo = probabilities(keys_values[slot, rows_at(group, 64), cols], wide, bound, chunk)
            total = total + jnp.sum(expo, axis=0, keepdims=True)
            numer = numer + dot(keys_values[slot, rows_at(group, 64, 384), cols], expo.astype(jnp.bfloat16))
            return (total, numer)

        total, numer = lax.fori_loop(
            0, 4, one_chunk, (jnp.zeros((1, 384), jnp.float32), jnp.zeros((64, 384), jnp.float32)), unroll=True
        )
        mean = numer / total
        for i in range(3):
            attn[pl.ds(pl.multiple_of(group * 192 + 64 * i, 64), 64), lanes] = mean[:, i * 128: i * 128 + 128]
        denom[group, 0:3, lanes] = jnp.concatenate([total[:, i * 128: i * 128 + 128] for i in range(3)], axis=0)

    def unit(k):
        attend(k // 6, lax.rem(k, 6))
        for at, tokens in FORWARD_PLAN[5]:
            pl.when(k == at)(lambda tokens=tokens: run(tokens))

    repeat(12, unit)
    keeps[3].start()
    keeps[4].start()

    def out_project(b):
        block = t_dot(attn[...].astype(jnp.bfloat16), weights[:, lanes_at(b, 384)][:, 128:]).T
        proj[rows_at(b, 144), :] = block[112:256]

    repeat(8, out_project)
    hidden[...] = x[...].astype(jnp.float32) + proj[...].T
    run(FORWARD_PLAN[6])
    for spread in cat_spreads + ffn_spreads + kv_spreads:
        spread.finish()
    for spread in ffn_spreads:
        spread.wait_core()
    for k in range(1, 8):
        tiles.along_seq(k).wait_send()
    for k in range(1, 4):
        tiles.along_dp(k).wait_send()
    for copy in [out_copy] + keeps:
        copy.wait()


def forward_call(lengths, shards_t, gain_a, gain_f, x, cosine, sine, gate, up, down):
    vmem, anywhere = pl.BlockSpec(memory_space=pltpu.VMEM), pl.BlockSpec(memory_space=pl.ANY)
    kept = [
        ((1152, 256), jnp.bfloat16), ((1152, 256), jnp.bfloat16), ((2, 768, 1024), jnp.bfloat16),
        ((1152, 256), jnp.float32), ((6, 8, 256), jnp.float32),
    ]
    return pl.pallas_call(
        forward_body,
        out_shape=[jax.ShapeDtypeStruct((1152, 3072), jnp.bfloat16)] * 4
        + [jax.ShapeDtypeStruct(*item) for item in kept]
        + [jax.ShapeDtypeStruct((16, 1152), jnp.float32), jax.ShapeDtypeStruct((256, 1152), jnp.float32)],
        in_specs=[pl.BlockSpec(memory_space=pltpu.SMEM)] + [vmem] * 12,
        out_specs=[anywhere] * 9 + [vmem] * 2,
        scratch_shapes=[pltpu.VMEM((8, 1152), jnp.float32), pltpu.VMEM((384, 384), jnp.float32), pltpu.VMEM((288, 384), jnp.bfloat16)]
        + [pltpu.VMEM(*item) for item in kept]
        + [
            pltpu.VMEM((256, 1152), jnp.bfloat16),
            pltpu.VMEM((1920, 256), jnp.float32),
            pltpu.VMEM((768, 256), jnp.bfloat16),
            pltpu.VMEM((1152, 3072), jnp.bfloat16),
            pltpu.VMEM((1152, 256), jnp.float32),
            pltpu.VMEM((8, 8, 1152), jnp.float32),
            pltpu.VMEM((4, 8, 1152), jnp.float32),
            pltpu.SemaphoreType.DMA((9,)),
        ]
        + NOTE_SEMS
        + spread_sems(CAT_JOBS)
        + spread_sems(FFN_JOBS)
        + spread_sems(KV_JOBS)[:2],
        compiler_params=pltpu.CompilerParams(
            collective_id=3, has_side_effects=True, vmem_limit_bytes=VMEM_MOST
        ),
        name="attention_forward",
    )(lengths, *shards_t, gain_a, gain_f, x, cosine, sine, gate, up, down)


def ffn_body(
    total_tokens, lengths, hidden, teacher, notes, gate_w, up_w, down_w,
    out, grad_hidden, small, gate_sums, up_sums, down_sums,
    w_gate, w_up, w_down, gate, up, hid, grads_gate, grads_up, inputs_t, cot_t, inputs, cot_b, acc, cot, rate,
    sums_gate, sums_up, sums_down, load, swap_send, swap_recv, store
):
    place = position()
    x, y, z, c = place
    _, s = mesh_place(*place)
    other = mesh_place(x, y, z, 1 - c)
    barrier = pltpu.get_barrier_semaphore()
    pl.semaphore_signal(barrier, inc=1, device_id=other, device_id_type=MESH_ID)
    pl.semaphore_wait(barrier, 1)
    columns = lambda j: lanes_at(j, 768)

    def load_copy(k, source, target, j):
        return pltpu.make_async_copy(source.at[:, columns(j)], target.at[:, columns(j)], load.at[k, j])

    def loads(j):
        return [load_copy(k, *pair, j) for k, pair in enumerate(((gate_w, w_gate), (up_w, w_up), (down_w, w_down)))]

    for j in range(4):
        for copy in loads(j):
            copy.start()

    def swap(source, target, k):
        return pltpu.make_async_remote_copy(
            src_ref=source, dst_ref=target, send_sem=swap_send.at[k], recv_sem=swap_recv.at[k],
            device_id=other, device_id_type=MESH_ID,
        )

    own, theirs = pl.ds(0, 256), pl.ds(256, 256)
    swap_inputs = swap(inputs_t.at[:, own], inputs_t.at[:, theirs], 0)
    swap_cot = swap(cot_t.at[:, own], cot_t.at[:, theirs], 1)

    def swap_hid(i, core):
        at = columns(core + 2 * i)
        return swap(hid.at[own, at], hid.at[theirs, at], 2 + i)

    def swap_grads(ref, j, k):
        return swap(ref.at[own, columns(j)], ref.at[theirs, columns(j)], k + j)

    def norm(k):
        rows = rows_at(k, 32)
        part = hidden[rows, :]
        scale = lax.rsqrt(jnp.mean(part * part, axis=-1, keepdims=True) + norm_eps)
        rate[rows, :] = jnp.broadcast_to(scale, (32, 128))
        inputs[rows, :] = (part * scale * notes[1:2, :]).astype(jnp.bfloat16)

    repeat(8, norm)
    inputs_t[:, 0:256] = inputs[...].T
    acc[...] = jnp.zeros_like(acc)

    def forward(j):
        for copy in loads(j):
            copy.wait()
        at = columns(j)
        gate_part = dot(inputs[...], w_gate[:, at])
        up_part = dot(inputs[...], w_up[:, at])
        gate[:, at] = gate_part
        up[:, at] = up_part
        hid[0:256, at] = (gate_part * jax.nn.sigmoid(gate_part) * up_part).astype(jnp.bfloat16)
        acc[...] += dot_t(hid[0:256, at], w_down[:, at])

    repeat(4, forward)
    swap_inputs.start()
    for i in range(2):
        swap_hid(i, 1 - c).start()
    factor = total_tokens / notes[10:11, :]
    small[...] = jnp.zeros_like(small)

    def losses(k):
        rows = rows_at(k, 32)
        first = s * 128 + lax.rem(k, 4) * 32
        live = first + lax.broadcasted_iota(jnp.int32, (32, 1), 0) < lengths[k // 4]
        value = jnp.where(live, hidden[rows, :] + acc[rows, :], 0.0)
        out[rows, :] = value.astype(jnp.bfloat16)
        diff = jnp.where(live, value - teacher[rows, :].astype(jnp.float32), 0.0)
        small[2:3, :] += jnp.sum(diff * diff, axis=0, keepdims=True)
        grad = factor * diff
        cot[rows, :] = grad
        cot_b[rows, :] = grad.astype(jnp.bfloat16)

    repeat(8, losses)
    cot_t[:, 0:256] = cot_b[...].T
    acc[...] = jnp.zeros_like(acc)

    def backward(j):
        at = columns(j)
        grad_hid = dot(cot_b[...], w_down[:, at])
        gate_part = gate[:, at]
        sig = jax.nn.sigmoid(gate_part)
        grads_gate[0:256, at] = (
            grad_hid * up[:, at] * sig * (1.0 + gate_part * (1.0 - sig))
        ).astype(jnp.bfloat16)
        grads_up[0:256, at] = (grad_hid * gate_part * sig).astype(jnp.bfloat16)
        acc[...] += dot_t(grads_gate[0:256, at], w_gate[:, at]) + dot_t(grads_up[0:256, at], w_up[:, at])
        swap_grads(grads_gate, j, 4).start()
        swap_grads(grads_up, j, 8).start()
        pl.when(j == 0)(swap_cot.start)

    repeat(4, backward)

    def finish_rows(k):
        rows = rows_at(k, 32)
        scale = rate[rows, 0:1]
        normed = hidden[rows, :] * scale
        grad = acc[rows, :]
        small[1:2, :] += jnp.sum(grad * normed, axis=0, keepdims=True)
        grad = grad * notes[1:2, :]
        inner = grad - normed * jnp.mean(grad * normed, axis=-1, keepdims=True)
        grad_hidden[rows, :] = cot[rows, :] + scale * inner

    repeat(8, finish_rows)
    small[2:3, :] = jnp.broadcast_to(jnp.sum(small[2:3, :], axis=-1, keepdims=True), (1, 1152))
    small[3:4, :] = notes[0:1, :]
    swap_cot.wait_recv()
    swap_inputs.wait_recv()

    def stored(k, source, target, i):
        at = columns(i)
        return pltpu.make_async_copy(source.at[:, at], target.at[:, at], store.at[k, i])

    def down_grads(i):
        swap_hid(i, c).wait_recv()
        sums_down[:, columns(i)] = dot(cot_t[...], hid[:, columns(c + 2 * i)]).astype(jnp.bfloat16)
        stored(0, sums_down, down_sums, i).start()

    repeat(2, down_grads)

    def wide_grads(j):
        at = columns(j)
        swap_grads(grads_gate, j, 4).wait_recv()
        swap_grads(grads_up, j, 8).wait_recv()
        for half in range(2):
            rows = rows_at(c + 2 * half, 288)
            kept = slice(288 * half, 288 * half + 288)
            sums_gate[kept, at] = dot(inputs_t[rows, :], grads_gate[:, at]).astype(jnp.bfloat16)
            sums_up[kept, at] = dot(inputs_t[rows, :], grads_up[:, at]).astype(jnp.bfloat16)
        stored(1, sums_gate, gate_sums, j).start()
        stored(2, sums_up, up_sums, j).start()

    repeat(4, wide_grads)
    swap_inputs.wait_send()
    swap_cot.wait_send()
    for i in range(2):
        swap_hid(i, 1 - c).wait_send()
        stored(0, sums_down, down_sums, i).wait()
    for j in range(4):
        swap_grads(grads_gate, j, 4).wait_send()
        swap_grads(grads_up, j, 8).wait_send()
        stored(1, sums_gate, gate_sums, j).wait()
        stored(2, sums_up, up_sums, j).wait()


def ffn_call(total_tokens, lengths, hidden, teacher, notes, gate_w, up_w, down_w):
    vmem, anywhere = pl.BlockSpec(memory_space=pltpu.VMEM), pl.BlockSpec(memory_space=pl.ANY)
    whole = pltpu.VMEM((1152, 3072), jnp.bfloat16)
    both = pltpu.VMEM((512, 3072), jnp.bfloat16)
    return pl.pallas_call(
        functools.partial(ffn_body, total_tokens),
        out_shape=[
            jax.ShapeDtypeStruct((256, 1152), jnp.bfloat16),
            jax.ShapeDtypeStruct((256, 1152), jnp.float32),
            jax.ShapeDtypeStruct((8, 1152), jnp.float32),
            jax.ShapeDtypeStruct((576, 3072), jnp.bfloat16),
            jax.ShapeDtypeStruct((576, 3072), jnp.bfloat16),
            jax.ShapeDtypeStruct((1152, 1536), jnp.bfloat16),
        ],
        in_specs=[pl.BlockSpec(memory_space=pltpu.SMEM)] + [vmem] * 3 + [anywhere] * 3,
        out_specs=[vmem] * 3 + [anywhere] * 3,
        scratch_shapes=[whole] * 3
        + [pltpu.VMEM((256, 3072), jnp.float32)] * 2
        + [both] * 3
        + [pltpu.VMEM((1152, 512), jnp.bfloat16)] * 2
        + [pltpu.VMEM((256, 1152), jnp.bfloat16)] * 2
        + [pltpu.VMEM((256, 1152), jnp.float32)] * 2
        + [pltpu.VMEM((256, 128), jnp.float32)]
        + [pltpu.VMEM((576, 3072), jnp.bfloat16)] * 2
        + [
            pltpu.VMEM((1152, 1536), jnp.bfloat16),
            pltpu.SemaphoreType.DMA((3, 4)),
            pltpu.SemaphoreType.DMA((12,)),
            pltpu.SemaphoreType.DMA((12,)),
            pltpu.SemaphoreType.DMA((3, 4)),
        ],
        compiler_params=pltpu.CompilerParams(
            collective_id=5, has_side_effects=True, vmem_limit_bytes=VMEM_MOST
        ),
        name="feed_forward",
    )(lengths, hidden, teacher, notes, gate_w, up_w, down_w)


def backward_body(
    lengths, grad_hidden, cosine, sine, small, x_in, kept_in_t, wcat, keys_values, kept_query, kept_attn, kept_denom,
    grad_gate, grad_up, grad_down,
    own_gate, own_up, own_down, own_query_t, own_key_t, own_value_t, own_out_t, grad_tokens, totals, grad_cat,
    x, attn_in_t, query, attn, denom, own_cat, weights, whole_kv, part_kv, turned, total, own_kv, left, grad_t, note, seq_in, dp_in, row_sum,
    load, store, kv_send, kv_recv, *scratch
):
    place = position()
    d, s = mesh_place(*place)
    greet(place, True)
    sums = dict(zip(FFN_NAMES, (grad_gate, grad_up, grad_down)))
    owned = dict(zip(FFN_NAMES, (own_gate, own_up, own_down)))
    kv_arrived, scratch = scratch[: len(FOLD_KV)], scratch[len(FOLD_KV):]
    note_sems, scratch = scratch[:4], scratch[4:]
    split = len(fold_scratch(FOLD_FFN, False))
    folds = [
        JobFold(place, job, j, sums[job[0]], owned[job[0]], scratch[:split], False) for j, job in enumerate(FOLD_FFN)
    ]
    cat_folds = [JobFold(place, job, j, grad_cat, own_cat, scratch[split:], True) for j, job in enumerate(FOLD_CAT)]
    tiles = Notes(place, lambda peer: note, row_sum, seq_in, dp_in, note_sems)

    def kv_fold(j, slot, row, order):
        def out(value):
            own_kv[row: row + 256, slot * 128: slot * 128 + 128] = value

        spot = kv_spot(part_kv, slot, row)
        return Fold(place, order, lambda who: spot(who), kv_arrived[j], (kv_send, kv_recv), j, out, kv_amount(part_kv))

    kv_folds = [kv_fold(j, *job) for j, job in enumerate(FOLD_KV)]
    steps = [
        [fold.fold.steps() for fold in cat_folds],
        [fold.fold.steps() for fold in folds],
        [fold.steps() for fold in kv_folds],
    ]

    def run(tokens):
        for token in tokens:
            steps[token // 10000][token // 100 % 100][token % 100]()

    for dy in (1, 0):
        for fold in folds:
            fold.begin(dy)

    def block_load(b):
        return pltpu.make_async_copy(wcat.at[:, lanes_at(b, 384)], weights.at[:, lanes_at(b, 384)], load.at[b])

    repeat(8, lambda b: block_load(b).start())
    kept = [
        pltpu.make_async_copy(source, target, load.at[8 + k])
        for k, (source, target) in enumerate(
            ((keys_values, whole_kv), (kept_query, query), (kept_attn, attn), (kept_denom, denom),
             (kept_in_t, attn_in_t), (x_in, x))
        )
    ]
    for copy in kept:
        copy.start()
    grad_t[...] = grad_hidden[...].T.astype(jnp.bfloat16)
    total[...] = jnp.zeros_like(total)

    def out_rows(b):
        return jnp.concatenate([jnp.zeros((112, 256), jnp.bfloat16), grad_t[rows_at(b, 144), :]], axis=0)

    def out_back(b):
        block_load(b).wait()
        total[...] += dot(weights[:, lanes_at(b, 384)][:, 128:], out_rows(b))

    repeat(8, out_back)
    run(BACKWARD_PLAN[0])
    for copy in kept:
        copy.wait()
    scale = HEAD_DIMENSION ** (-0.5)

    def attend_back(slot, group):
        lanes = lanes_at(slot, 128)
        bound = key_limit(lengths[slot], s)
        wide = heads_wide(query, group, lanes)
        grads, ratios = [], []
        for i in range(3):
            rows = pl.ds(pl.multiple_of(group * 192 + 64 * i, 64), 64)
            grad = total[rows, lanes].astype(jnp.bfloat16).astype(jnp.float32)
            bottom = denom[group, i: i + 1, lanes]
            ratios.append(jnp.sum(grad * attn[rows, lanes], axis=0, keepdims=True) / bottom)
            grads.append((grad / bottom).astype(jnp.bfloat16))
        grads, ratios = jnp.concatenate(grads, axis=1), jnp.concatenate(ratios, axis=1)

        def one_chunk(chunk, sum_query):
            cols = lanes_at(chunk, 256)
            keys = whole_kv[slot, rows_at(group, 64), cols]
            values = whole_kv[slot, rows_at(group, 64, 384), cols]
            expo = probabilities(keys, wide, bound, chunk)
            grad_prob = t_dot(values, grads)
            grad_score = (expo * (grad_prob - ratios)).astype(jnp.bfloat16)
            part_kv[slot, rows_at(group, 64), cols] = (dot_t(wide, grad_score) * scale).astype(jnp.bfloat16)
            part_kv[slot, rows_at(group, 64, 384), cols] = dot_t(grads, expo.astype(jnp.bfloat16)).astype(jnp.bfloat16)
            return sum_query + dot(keys, grad_score)

        sum_query = lax.fori_loop(0, 4, one_chunk, jnp.zeros((64, 384), jnp.float32), unroll=True) * scale
        for i in range(3):
            total[pl.ds(pl.multiple_of(group * 192 + 64 * i, 64), 64), lanes] = sum_query[:, i * 128: i * 128 + 128]

    def unit(k):
        attend_back(k // 6, lax.rem(k, 6))
        for at, tokens in BACKWARD_PLAN[1]:
            pl.when(k == at)(lambda tokens=tokens: run(tokens))

    repeat(12, unit)
    run(BACKWARD_PLAN[2])

    def turn_back(ref, source, count):
        def one(h):
            rows = rows_at(h, 64)
            ref[rows, :] = rotate(source[rows, :], cosine[...], -sine[...]).astype(ref.dtype)

        repeat(count, one)

    turn_back(turned, total, 18)
    turn_back(own_kv, own_kv, 6)
    total[...] = jnp.zeros_like(total)

    def last_block(b):
        rows = jnp.concatenate(
            [
                turned[rows_at(b, 144), :],
                own_kv[rows_at(b, 48), :].astype(jnp.bfloat16),
                own_kv[rows_at(b, 48, 384), :].astype(jnp.bfloat16),
                jnp.zeros((16, 256), jnp.bfloat16),
            ],
            axis=0,
        )
        total[...] += dot(weights[:, lanes_at(b, 384)][:, :256], rows)
        slot = lax.rem(b, 2)
        out = pltpu.make_async_copy(left.at[slot], grad_cat.at[:, lanes_at(b, 384)], store.at[slot])
        pl.when(b >= 2)(lambda: out.wait())
        grad = dot_t(attn_in_t[...], rows)
        out_grad = dot_t(attn[...].astype(jnp.bfloat16), out_rows(b))
        left[slot, :, 0:128] = grad[:, :128].astype(jnp.bfloat16)
        left[slot, :, 128:256] = (grad[:, 128:] + out_grad[:, :128]).astype(jnp.bfloat16)
        left[slot, :, 256:384] = out_grad[:, 128:].astype(jnp.bfloat16)
        out.start()
        for at, tokens in BACKWARD_PLAN[3]:
            pl.when(b == at)(lambda tokens=tokens: run(tokens))

    repeat(8, last_block)
    for slot in range(2):
        pltpu.make_async_copy(left.at[slot], grad_cat.at[:, pl.ds((6 + slot) * 384, 384)], store.at[slot]).wait()
    for dy in (1, 0):
        for fold in cat_folds:
            fold.begin(dy)
    run(BACKWARD_PLAN[4])
    grad_tokens[...] = total[...].T
    note[...] = small[...]

    def finish_rows(k):
        rows = rows_at(k, 32)
        grad = grad_tokens[rows, :]
        normed = x[rows, :].astype(jnp.float32)
        scale_in = lax.rsqrt(jnp.mean(normed * normed, axis=-1, keepdims=True) + norm_eps)
        normed = normed * scale_in
        note[0:1, :] += jnp.sum(grad * normed, axis=0, keepdims=True)
        grad = grad * small[3:4, :]
        inner = grad - normed * jnp.mean(grad * normed, axis=-1, keepdims=True)
        grad_tokens[rows, :] = grad_hidden[rows, :] + scale_in * inner

    repeat(8, finish_rows)
    run(BACKWARD_PLAN[5])
    for k in range(1, 8):
        tiles.along_seq(k).start()
    run(BACKWARD_PLAN[6])
    tiles.wait_seq()
    seq_in[s] = note[...]
    along = seq_in[0]
    for k in range(1, 8):
        along = along + seq_in[k]
    row_sum[...] = along
    run(BACKWARD_PLAN[7])
    for k in range(1, 4):
        tiles.along_dp(k).start()
    run(BACKWARD_PLAN[8])
    tiles.wait_dp()
    dp_in[d] = row_sum[...]
    totals[...] = dp_in[0] + dp_in[1] + dp_in[2] + dp_in[3]
    turned_cat = own_cat[...].T
    row = 0
    for ref in (own_query_t, own_key_t, own_value_t, own_out_t):
        ref[...] = turned_cat[row: row + ref.shape[0], 0:288]
        row += ref.shape[0]
    for fold in folds + kv_folds + cat_folds:
        fold.finish()
    for k in range(1, 8):
        tiles.along_seq(k).wait_send()
    for k in range(1, 4):
        tiles.along_dp(k).wait_send()


def backward_call(
    lengths, grad_hidden, cosine, sine, small, x, attn_in_t, wcat, keys_values, query, attn, denom,
    grad_gate, grad_up, grad_down
):
    vmem, anywhere = pl.BlockSpec(memory_space=pltpu.VMEM), pl.BlockSpec(memory_space=pl.ANY)
    jobs = len(KV_JOBS)
    most = max(fold_slots(order)[1] for _, _, order in FOLD_KV)
    outs = ((288, 384), (288, 384), (144, 768), (144, 288), (48, 288), (48, 288), (144, 288), (256, 1152), (8, 1152))
    return pl.pallas_call(
        backward_body,
        out_shape=[jax.ShapeDtypeStruct(shape, jnp.float32) for shape in outs]
        + [jax.ShapeDtypeStruct((1152, 3072), jnp.bfloat16)],
        in_specs=[pl.BlockSpec(memory_space=pltpu.SMEM)] + [vmem] * 4 + [anywhere] * 10,
        out_specs=[vmem] * len(outs) + [anywhere],
        scratch_shapes=[
            pltpu.VMEM((256, 1152), jnp.bfloat16),
            pltpu.VMEM((1152, 256), jnp.bfloat16),
            pltpu.VMEM((1152, 256), jnp.bfloat16),
            pltpu.VMEM((1152, 256), jnp.float32),
            pltpu.VMEM((6, 8, 256), jnp.float32),
            pltpu.VMEM((384, 384), jnp.float32),
            pltpu.VMEM((1152, 3072), jnp.bfloat16),
            pltpu.VMEM((2, 768, 1024), jnp.bfloat16),
            pltpu.VMEM((2, 768, 1024), jnp.bfloat16),
            pltpu.VMEM((1152, 256), jnp.bfloat16),
            pltpu.VMEM((1152, 256), jnp.float32),
            pltpu.VMEM((768, 256), jnp.float32),
            pltpu.VMEM((2, 1152, 384), jnp.bfloat16),
            pltpu.VMEM((1152, 256), jnp.bfloat16),
            pltpu.VMEM((8, 1152), jnp.float32),
            pltpu.VMEM((8, 8, 1152), jnp.float32),
            pltpu.VMEM((4, 8, 1152), jnp.float32),
            pltpu.VMEM((8, 1152), jnp.float32),
            pltpu.SemaphoreType.DMA((14,)),
            pltpu.SemaphoreType.DMA((2,)),
            pltpu.SemaphoreType.DMA((jobs,)),
            pltpu.SemaphoreType.DMA((jobs, most)),
        ]
        + [pltpu.VMEM((fold_slots(order)[1], 256, 128), jnp.bfloat16) for _, _, order in FOLD_KV]
        + NOTE_SEMS
        + fold_scratch(FOLD_FFN, False)
        + fold_scratch(FOLD_CAT, True),
        compiler_params=pltpu.CompilerParams(
            collective_id=4, has_side_effects=True, vmem_limit_bytes=VMEM_MOST
        ),
        name="attention_backward",
    )(
        lengths, grad_hidden, cosine, sine, small, x, attn_in_t, wcat, keys_values, query, attn, denom,
        grad_gate, grad_up, grad_down,
    )


def hand_over_body(count, *refs):
    sources, (totals, notes) = refs[:count], refs[count: count + 2]
    targets, (loss, gain_a, gain_f) = refs[count + 2: 2 * count + 2], refs[2 * count + 2: 2 * count + 5]
    sems = refs[-1]
    copies = [
        pltpu.make_async_copy(source, target, sems.at[k]) for k, (source, target) in enumerate(zip(sources, targets))
    ]
    for copy in copies:
        copy.start()
    loss[...] = totals[2:3, 0:1] / notes[10:11, 0:1]
    s = lax.axis_index("seq")
    for k in range(8):
        def own(k=k):
            gain_a[...] = totals[0:1, 144 * k: 144 * k + 144]
            gain_f[...] = totals[1:2, 144 * k: 144 * k + 144]

        pl.when(s == k)(own)
    for copy in copies:
        copy.wait()


def hand_over(results, totals, notes):
    vmem, anywhere = pl.BlockSpec(memory_space=pltpu.VMEM), pl.BlockSpec(memory_space=pl.ANY)
    count = len(results)
    return pl.pallas_call(
        functools.partial(hand_over_body, count),
        out_shape=[jax.ShapeDtypeStruct(r.shape, r.dtype) for r in results]
        + [jax.ShapeDtypeStruct(shape, jnp.float32) for shape in ((1, 1), (1, 144), (1, 144))],
        in_specs=[vmem] * (count + 2),
        out_specs=[anywhere] * count + [vmem] * 3,
        scratch_shapes=[pltpu.SemaphoreType.DMA((count,))],
        compiler_params=pltpu.CompilerParams(vmem_limit_bytes=VMEM_MOST),
        name="hand_over",
    )(*results, totals, notes)


def per_device_fast(
    tokens, teacher, lengths, w_query, key_weight, value_weight, w_out, w_gate, w_up, w_down, gain_attn, gain_ffn
):
    slots, part, width = tokens.shape
    rows = slots * part
    total_tokens = slots * lax.axis_size("dp") * part * lax.axis_size("seq")
    positions = lax.axis_index("seq") * part + jnp.arange(part, dtype=jnp.int32)
    cosine, sine = rope_tables(positions, HEAD_DIMENSION)
    cosine_t = jnp.concatenate([cosine.T] * slots, axis=1)
    sine_t = jnp.concatenate([sine.T] * slots, axis=1)
    x_b = tokens.reshape(rows, width)
    gate_w, up_w, down_t, cat, attn_in_t, query, keys_values, attn, denom, notes, hidden = forward_call(
        lengths, (w_query.T, key_weight.T, value_weight.T, w_out.T),
        gain_attn, gain_ffn, x_b, cosine_t, sine_t,
        w_gate, w_up, w_down.T,
    )
    output, grad_hidden, small, gate_sums, up_sums, down_sums = ffn_call(
        float(total_tokens), lengths, hidden, teacher.reshape(rows, width), notes, gate_w, up_w, down_t
    )
    *results, totals, _ = backward_call(
        lengths, grad_hidden, cosine_t, sine_t, small, x_b, attn_in_t, cat, keys_values, query, attn, denom,
        gate_sums, up_sums, down_sums,
    )
    (
        output, own_gate, own_up, own_down_t, own_query_t, own_key_t, own_value_t, own_out_t, grad_tokens,
        loss, own_gain_a, own_gain_f,
    ) = hand_over([output] + results, totals, notes)
    return (
        output.reshape(tokens.shape),
        loss.reshape(()),
        grad_tokens.reshape(tokens.shape),
        own_query_t.T,
        own_key_t.T,
        own_value_t.T,
        own_out_t.T,
        own_gate,
        own_up,
        own_down_t.T,
        own_gain_a.reshape(-1),
        own_gain_f.reshape(-1),
    )


def solution(mesh):
    placed = (
        P("dp", "seq", None),
        P("dp", "seq", None),
        P("dp"),
        P("dp", "seq"),
        P("dp", "seq"),
        P("dp", "seq"),
        P("dp", "seq"),
        P("dp", "seq"),
        P("dp", "seq"),
        P("dp", "seq"),
        P("seq"),
        P("seq"),
    )
    fits = mesh.shape["dp"] == 4 and mesh.shape["seq"] == 8
    return jax.shard_map(
        per_device_fast if fits else per_device,
        mesh=mesh,
        in_specs=placed,
        out_specs=(
            P("dp", "seq", None),
            P(),
            P("dp", "seq", None),
            P("dp", "seq"),
            P("dp", "seq"),
            P("dp", "seq"),
            P("dp", "seq"),
            P("dp", "seq"),
            P("dp", "seq"),
            P("dp", "seq"),
            P("seq"),
            P("seq"),
        ),
        check_vma=False,
    )
```

```python
import functools
import math

import jax
import jax.numpy as jnp
from jax import lax
from jax.experimental import pallas as pl
from jax.experimental.pallas import tpu as pltpu
from jax.sharding import PartitionSpec as P

QUERY_HEADS = 18
KEY_VALUE_HEADS = 6
HEAD_DIMENSION = 64


norm_eps = 1e-05
rope_base = 10000.0


def rope_tables(positions, head_width):
    half_width = head_width // 2
    exponents = jnp.arange(half_width, dtype=jnp.float32) * (2.0 / head_width)
    angles = positions.astype(jnp.float32)[:, None] * (rope_base ** (-exponents))[None, :]
    return (jnp.cos(angles), jnp.sin(angles))


def apply_rotary(value_rows, cosine_table, sine_table):
    half_width = value_rows.shape[-1] // 2
    front_half = value_rows[..., :half_width]
    back_half = value_rows[..., half_width:]
    cos_wide = cosine_table[:, None, :]
    sin_wide = sine_table[:, None, :]
    return jnp.concatenate(
        [
            front_half * cos_wide - back_half * sin_wide,
            front_half * sin_wide + back_half * cos_wide,
        ],
        axis=-1,
    )


def allowed_mask(query_pos, key_pos, live_len):
    causal = key_pos[None, :] <= query_pos[:, None]
    present = key_pos[None, :] < live_len[:, None]
    return (causal[None, :, :] & present[:, None, :])[:, None, None, :, :]


def over_blocks(piece_len, unit_len, step_fn, running):
    block_length = math.gcd(piece_len, unit_len * max(1, 512 // unit_len))
    number_of_blocks = piece_len // block_length

    def loop_step(block_number, state):
        return step_fn(state, block_number * block_length, block_length)

    return lax.fori_loop(0, number_of_blocks, loop_step, running)


def collect(shards):
    wide = (
        lax.all_gather(shards[0], "seq", axis=1, tiled=True),
        lax.all_gather(shards[1], "seq", axis=1, tiled=True),
        lax.all_gather(shards[2], "seq", axis=1, tiled=True),
        lax.all_gather(shards[3], "seq", axis=1, tiled=True),
        lax.all_gather(shards[4], "seq", axis=1, tiled=True),
        lax.all_gather(shards[5], "seq", axis=1, tiled=True),
        lax.all_gather(shards[6], "seq", axis=1, tiled=True),
        lax.all_gather(shards[7], "seq", axis=0, tiled=True),
        lax.all_gather(shards[8], "seq", axis=0, tiled=True),
    )
    whole = (
        lax.all_gather(wide[0], "dp", axis=0, tiled=True),
        lax.all_gather(wide[1], "dp", axis=0, tiled=True),
        lax.all_gather(wide[2], "dp", axis=0, tiled=True),
        lax.all_gather(wide[3], "dp", axis=0, tiled=True),
        lax.all_gather(wide[4], "dp", axis=0, tiled=True),
        lax.all_gather(wide[5], "dp", axis=0, tiled=True),
        lax.all_gather(wide[6], "dp", axis=0, tiled=True),
    )
    return tuple(whole) + (wide[7], wide[8])


def reduce_grads(grad_sums):
    summed = (
        lax.psum_scatter(grad_sums[0], "seq", scatter_dimension=1, tiled=True),
        lax.psum_scatter(grad_sums[1], "seq", scatter_dimension=1, tiled=True),
        lax.psum_scatter(grad_sums[2], "seq", scatter_dimension=1, tiled=True),
        lax.psum_scatter(grad_sums[3], "seq", scatter_dimension=1, tiled=True),
        lax.psum_scatter(grad_sums[4], "seq", scatter_dimension=1, tiled=True),
        lax.psum_scatter(grad_sums[5], "seq", scatter_dimension=1, tiled=True),
        lax.psum_scatter(grad_sums[6], "seq", scatter_dimension=1, tiled=True),
        lax.psum_scatter(grad_sums[7], "seq", scatter_dimension=0, tiled=True),
        lax.psum_scatter(grad_sums[8], "seq", scatter_dimension=0, tiled=True),
    )
    owned = (
        lax.psum_scatter(summed[0], "dp", scatter_dimension=0, tiled=True),
        lax.psum_scatter(summed[1], "dp", scatter_dimension=0, tiled=True),
        lax.psum_scatter(summed[2], "dp", scatter_dimension=0, tiled=True),
        lax.psum_scatter(summed[3], "dp", scatter_dimension=0, tiled=True),
        lax.psum_scatter(summed[4], "dp", scatter_dimension=0, tiled=True),
        lax.psum_scatter(summed[5], "dp", scatter_dimension=0, tiled=True),
        lax.psum_scatter(summed[6], "dp", scatter_dimension=0, tiled=True),
    )
    return (tuple(owned), summed[7], summed[8])


def forward_slot(weights, tok_part, live_len, query_pos, cosine_table, sine_table):
    (
        full_query,
        full_key,
        full_value,
        full_out,
        full_gate,
        full_up,
        full_down,
        full_gain_attn,
        full_gain_ffn,
    ) = weights
    slot_position, stretched_length, model_width = tok_part.shape
    number_of_rows = slot_position * stretched_length
    query_group = QUERY_HEADS // KEY_VALUE_HEADS
    scale = HEAD_DIMENSION ** (-0.5)
    tok_float = tok_part.astype(jnp.float32).reshape(number_of_rows, model_width)
    inv_first = lax.rsqrt(jnp.mean(tok_float * tok_float, axis=-1, keepdims=True) + norm_eps)
    normed_first = tok_float * inv_first
    attention_input = (normed_first * full_gain_attn.astype(jnp.float32)).astype(jnp.bfloat16)
    unrotated_query = jnp.dot(
        attention_input, full_query, preferred_element_type=jnp.float32
    ).reshape(slot_position, stretched_length, QUERY_HEADS, HEAD_DIMENSION)
    unrotated_key = jnp.dot(attention_input, full_key, preferred_element_type=jnp.float32).reshape(
        slot_position, stretched_length, KEY_VALUE_HEADS, HEAD_DIMENSION
    )
    value_block = (
        jnp.dot(attention_input, full_value, preferred_element_type=jnp.float32)
        .astype(jnp.bfloat16)
        .reshape(slot_position, stretched_length, KEY_VALUE_HEADS * HEAD_DIMENSION)
    )
    query_b = (
        apply_rotary(unrotated_query, cosine_table, sine_table)
        .astype(jnp.bfloat16)
        .reshape(slot_position, stretched_length, KEY_VALUE_HEADS, query_group, HEAD_DIMENSION)
    )
    key_block = (
        apply_rotary(unrotated_key, cosine_table, sine_table)
        .astype(jnp.bfloat16)
        .reshape(slot_position, stretched_length, KEY_VALUE_HEADS * HEAD_DIMENSION)
    )
    empty_denominator = jnp.zeros(
        (slot_position, KEY_VALUE_HEADS, query_group, stretched_length), jnp.float32
    )
    empty_numerator = jnp.zeros(
        (slot_position, KEY_VALUE_HEADS, query_group, stretched_length, HEAD_DIMENSION), jnp.float32
    )
    key_piece = lax.all_gather(key_block, "seq", axis=1, tiled=True)
    value_piece = lax.all_gather(value_block, "seq", axis=1, tiled=True)

    def one_block(partial_value, offset, block_length):
        denominator, numerator = partial_value
        key_blk = lax.dynamic_slice_in_dim(key_piece, offset, block_length, 1).reshape(
            slot_position, block_length, KEY_VALUE_HEADS, HEAD_DIMENSION
        )
        value_blk = lax.dynamic_slice_in_dim(value_piece, offset, block_length, 1).reshape(
            slot_position, block_length, KEY_VALUE_HEADS, HEAD_DIMENSION
        )
        allowed = allowed_mask(
            query_pos, offset + jnp.arange(block_length, dtype=jnp.int32), live_len
        )
        scores = (
            jnp.einsum("schgd,snhd->shgcn", query_b, key_blk, preferred_element_type=jnp.float32)
            * scale
        )
        exp_scores = jnp.where(allowed, jnp.exp(scores), 0.0)
        denominator = denominator + jnp.sum(exp_scores, axis=-1)
        numerator = numerator + jnp.einsum(
            "shgcn,snhd->shgcd",
            exp_scores.astype(jnp.bfloat16),
            value_blk,
            preferred_element_type=jnp.float32,
        )
        return (denominator, numerator)

    denominator, numerator = over_blocks(
        key_piece.shape[1], stretched_length, one_block, (empty_denominator, empty_numerator)
    )
    attn_float = jnp.transpose(numerator / denominator[..., None], (0, 3, 1, 2, 4)).reshape(
        number_of_rows, QUERY_HEADS * HEAD_DIMENSION
    )
    attn_b = attn_float.astype(jnp.bfloat16)
    hidden = tok_float + jnp.dot(attn_b, full_out, preferred_element_type=jnp.float32)
    inv_second = lax.rsqrt(jnp.mean(hidden * hidden, axis=-1, keepdims=True) + norm_eps)
    normed_second = hidden * inv_second
    ffn_in = (normed_second * full_gain_ffn.astype(jnp.float32)).astype(jnp.bfloat16)
    gate_proj = jnp.dot(ffn_in, full_gate, preferred_element_type=jnp.float32)
    up_proj = jnp.dot(ffn_in, full_up, preferred_element_type=jnp.float32)
    hid_b = (jax.nn.silu(gate_proj) * up_proj).astype(jnp.bfloat16)
    valid_rows = (query_pos[None, :] < live_len[:, None]).reshape(number_of_rows, 1)
    out_float = jnp.where(
        valid_rows, hidden + jnp.dot(hid_b, full_down, preferred_element_type=jnp.float32), 0.0
    )
    saved = (
        attention_input,
        inv_first,
        normed_first,
        query_b,
        key_block,
        value_block,
        attn_float,
        attn_b,
        denominator,
        normed_second,
        inv_second,
        ffn_in,
        gate_proj,
        up_proj,
        hid_b,
    )
    return (out_float, valid_rows, saved)


def backward_slot(weights, saved, cotangent, live_len, query_pos, cosine_table, sine_table):
    (
        full_query,
        full_key,
        full_value,
        full_out,
        full_gate,
        full_up,
        full_down,
        full_gain_attn,
        full_gain_ffn,
    ) = weights
    (
        attention_input,
        inv_first,
        normed_first,
        query_b,
        key_block,
        value_block,
        attn_float,
        attn_b,
        denominator,
        normed_second,
        inv_second,
        ffn_in,
        gate_proj,
        up_proj,
        hid_b,
    ) = saved
    slot_position = query_b.shape[0]
    stretched_length = query_b.shape[1]
    number_of_rows = slot_position * stretched_length
    query_group = QUERY_HEADS // KEY_VALUE_HEADS
    scale = HEAD_DIMENSION ** (-0.5)
    cot_b = cotangent.astype(jnp.bfloat16)
    grad_down = jnp.einsum("rf,rd->fd", hid_b, cot_b, preferred_element_type=jnp.float32)
    grad_hid = jnp.einsum("rd,fd->rf", cot_b, full_down, preferred_element_type=jnp.float32)
    sigmoid_gate = jax.nn.sigmoid(gate_proj)
    grad_gate_b = (
        grad_hid * up_proj * sigmoid_gate * (1.0 + gate_proj * (1.0 - sigmoid_gate))
    ).astype(jnp.bfloat16)
    grad_up_b = (grad_hid * gate_proj * sigmoid_gate).astype(jnp.bfloat16)
    grad_gate = jnp.einsum("rd,rf->df", ffn_in, grad_gate_b, preferred_element_type=jnp.float32)
    grad_up = jnp.einsum("rd,rf->df", ffn_in, grad_up_b, preferred_element_type=jnp.float32)
    grad_ffn_in = jnp.einsum(
        "rf,df->rd", grad_gate_b, full_gate, preferred_element_type=jnp.float32
    ) + jnp.einsum("rf,df->rd", grad_up_b, full_up, preferred_element_type=jnp.float32)
    grad_gain_ffn = jnp.sum(grad_ffn_in * normed_second, axis=0)
    grad_normed = grad_ffn_in * full_gain_ffn.astype(jnp.float32)
    grad_hidden = cotangent + inv_second * (
        grad_normed - normed_second * jnp.mean(grad_normed * normed_second, axis=-1, keepdims=True)
    )
    grad_proj_b = grad_hidden.astype(jnp.bfloat16)
    grad_out = jnp.einsum("rq,rd->qd", attn_b, grad_proj_b, preferred_element_type=jnp.float32)
    grad_attn_b = jnp.einsum(
        "rd,qd->rq", grad_proj_b, full_out, preferred_element_type=jnp.float32
    ).astype(jnp.bfloat16)
    den_rows = jnp.transpose(denominator, (0, 3, 1, 2)).reshape(number_of_rows, QUERY_HEADS)
    grad_heads_float = grad_attn_b.astype(jnp.float32).reshape(
        number_of_rows, QUERY_HEADS, HEAD_DIMENSION
    )
    softmax_ratio = (
        jnp.sum(
            grad_heads_float * attn_float.reshape(number_of_rows, QUERY_HEADS, HEAD_DIMENSION),
            axis=-1,
        )
        / den_rows
    ).reshape(slot_position, stretched_length, QUERY_HEADS)
    scaled_gradient = (
        (grad_heads_float / den_rows[..., None])
        .astype(jnp.bfloat16)
        .reshape(slot_position, stretched_length, QUERY_HEADS * HEAD_DIMENSION)
    )
    ratio_all = lax.all_gather(softmax_ratio, "seq", axis=1, tiled=True)
    head_gradient = scaled_gradient.reshape(
        slot_position, stretched_length, KEY_VALUE_HEADS, query_group, HEAD_DIMENSION
    )
    local_softmax_ratio = jnp.transpose(
        softmax_ratio.reshape(slot_position, stretched_length, KEY_VALUE_HEADS, query_group),
        (0, 2, 3, 1),
    )[..., None]
    empty_query = jnp.zeros(
        (slot_position, KEY_VALUE_HEADS, query_group, stretched_length, HEAD_DIMENSION), jnp.float32
    )
    key_piece = lax.all_gather(key_block, "seq", axis=1, tiled=True)
    value_piece = lax.all_gather(value_block, "seq", axis=1, tiled=True)

    def one_block(partial_value, offset, block_length):
        key_blk = lax.dynamic_slice_in_dim(key_piece, offset, block_length, 1).reshape(
            slot_position, block_length, KEY_VALUE_HEADS, HEAD_DIMENSION
        )
        value_blk = lax.dynamic_slice_in_dim(value_piece, offset, block_length, 1).reshape(
            slot_position, block_length, KEY_VALUE_HEADS, HEAD_DIMENSION
        )
        allowed = allowed_mask(
            query_pos, offset + jnp.arange(block_length, dtype=jnp.int32), live_len
        )
        scores = (
            jnp.einsum("schgd,snhd->shgcn", query_b, key_blk, preferred_element_type=jnp.float32)
            * scale
        )
        exp_scores = jnp.where(allowed, jnp.exp(scores), 0.0)
        grad_prob = jnp.einsum(
            "schgd,snhd->shgcn", head_gradient, value_blk, preferred_element_type=jnp.float32
        )
        grad_score = (exp_scores * (grad_prob - local_softmax_ratio)).astype(jnp.bfloat16)
        return (
            partial_value
            + jnp.einsum(
                "shgcn,snhd->shgcd", grad_score, key_blk, preferred_element_type=jnp.float32
            )
            * scale
        )

    grad_query = over_blocks(key_piece.shape[1], stretched_length, one_block, empty_query)
    query_flat = query_b.reshape(slot_position, stretched_length, QUERY_HEADS * HEAD_DIMENSION)
    per_head_keys = key_block.reshape(
        slot_position, stretched_length, KEY_VALUE_HEADS, HEAD_DIMENSION
    )
    per_head_values = value_block.reshape(
        slot_position, stretched_length, KEY_VALUE_HEADS, HEAD_DIMENSION
    )
    empty_key_value = jnp.zeros(
        (slot_position, KEY_VALUE_HEADS, stretched_length, HEAD_DIMENSION), jnp.float32
    )
    query_piece = lax.all_gather(query_flat, "seq", axis=1, tiled=True)
    grad_piece = lax.all_gather(scaled_gradient, "seq", axis=1, tiled=True)

    def one_block(partial_value, offset, block_length):
        grad_key, value_gradient = partial_value
        query_blk = lax.dynamic_slice_in_dim(query_piece, offset, block_length, 1).reshape(
            slot_position, block_length, KEY_VALUE_HEADS, query_group, HEAD_DIMENSION
        )
        grad_blk = lax.dynamic_slice_in_dim(grad_piece, offset, block_length, 1).reshape(
            slot_position, block_length, KEY_VALUE_HEADS, query_group, HEAD_DIMENSION
        )
        ratio_blk = lax.dynamic_slice_in_dim(ratio_all, offset, block_length, 1).reshape(
            slot_position, block_length, KEY_VALUE_HEADS, query_group
        )
        ratio_blk = jnp.transpose(ratio_blk, (0, 2, 3, 1))[..., None]
        remote_pos = offset + jnp.arange(block_length, dtype=jnp.int32)
        allowed = allowed_mask(remote_pos, query_pos, live_len)
        scores = (
            jnp.einsum(
                "snhgd,schd->shgnc", query_blk, per_head_keys, preferred_element_type=jnp.float32
            )
            * scale
        )
        exp_scores = jnp.where(allowed, jnp.exp(scores), 0.0)
        value_gradient = value_gradient + jnp.einsum(
            "shgnc,snhgd->shcd",
            exp_scores.astype(jnp.bfloat16),
            grad_blk,
            preferred_element_type=jnp.float32,
        )
        grad_prob = jnp.einsum(
            "snhgd,schd->shgnc", grad_blk, per_head_values, preferred_element_type=jnp.float32
        )
        grad_score = (exp_scores * (grad_prob - ratio_blk)).astype(jnp.bfloat16)
        grad_key = (
            grad_key
            + jnp.einsum(
                "shgnc,snhgd->shcd", grad_score, query_blk, preferred_element_type=jnp.float32
            )
            * scale
        )
        return (grad_key, value_gradient)

    grad_key, value_gradient = over_blocks(
        query_piece.shape[1], stretched_length, one_block, (empty_key_value, empty_key_value)
    )
    grad_query = jnp.transpose(grad_query, (0, 3, 1, 2, 4)).reshape(
        slot_position, stretched_length, QUERY_HEADS, HEAD_DIMENSION
    )
    grad_query_b = (
        apply_rotary(grad_query, cosine_table, -sine_table)
        .astype(jnp.bfloat16)
        .reshape(number_of_rows, QUERY_HEADS * HEAD_DIMENSION)
    )
    grad_key_b = (
        apply_rotary(jnp.transpose(grad_key, (0, 2, 1, 3)), cosine_table, -sine_table)
        .astype(jnp.bfloat16)
        .reshape(number_of_rows, KEY_VALUE_HEADS * HEAD_DIMENSION)
    )
    grad_value_b = (
        jnp.transpose(value_gradient, (0, 2, 1, 3))
        .astype(jnp.bfloat16)
        .reshape(number_of_rows, KEY_VALUE_HEADS * HEAD_DIMENSION)
    )
    grad_wq = jnp.einsum(
        "rd,rq->dq", attention_input, grad_query_b, preferred_element_type=jnp.float32
    )
    grad_wk = jnp.einsum(
        "rd,rq->dq", attention_input, grad_key_b, preferred_element_type=jnp.float32
    )
    grad_wv = jnp.einsum(
        "rd,rq->dq", attention_input, grad_value_b, preferred_element_type=jnp.float32
    )
    grad_attn_in = jnp.einsum(
        "rq,dq->rd", grad_query_b, full_query, preferred_element_type=jnp.float32
    )
    grad_attn_in = grad_attn_in + jnp.einsum(
        "rq,dq->rd", grad_key_b, full_key, preferred_element_type=jnp.float32
    )
    grad_attn_in = grad_attn_in + jnp.einsum(
        "rq,dq->rd", grad_value_b, full_value, preferred_element_type=jnp.float32
    )
    grad_gain_attn = jnp.sum(grad_attn_in * normed_first, axis=0)
    grad_first = grad_attn_in * full_gain_attn.astype(jnp.float32)
    grad_tokens = grad_hidden + inv_first * (
        grad_first - normed_first * jnp.mean(grad_first * normed_first, axis=-1, keepdims=True)
    )
    return (
        (
            grad_wq,
            grad_wk,
            grad_wv,
            grad_out,
            grad_gate,
            grad_up,
            grad_down,
            grad_gain_attn,
            grad_gain_ffn,
        ),
        grad_tokens,
    )


def per_device(
    tokens,
    teacher,
    lengths,
    w_query,
    key_weight,
    value_weight,
    w_out,
    w_gate,
    w_up,
    w_down,
    gain_attn,
    gain_ffn,
):
    shards = (w_query, key_weight, value_weight, w_out, w_gate, w_up, w_down, gain_attn, gain_ffn)
    slot_count, stretched_length, model_width = tokens.shape
    total_tokens = slot_count * lax.axis_size("dp") * stretched_length * lax.axis_size("seq")
    query_pos = lax.axis_index("seq") * stretched_length + jnp.arange(
        stretched_length, dtype=jnp.int32
    )
    cosine_table, sine_table = rope_tables(query_pos, HEAD_DIMENSION)
    out_rows = []
    stored = []
    differences = []
    squares_local = jnp.zeros((), jnp.float32)
    count_local = jnp.zeros((), jnp.float32)
    for micro in range(slot_count):
        weights = collect(shards)
        live_len = lengths[micro : micro + 1]
        out_float, valid_rows, saved = forward_slot(
            weights, tokens[micro : micro + 1], live_len, query_pos, cosine_table, sine_table
        )
        teach_float = teacher[micro].astype(jnp.float32)
        difference = jnp.where(valid_rows, out_float - teach_float, 0.0)
        squares_local = squares_local + jnp.sum(difference * difference)
        count_local = count_local + jnp.sum(valid_rows.astype(jnp.float32))
        out_rows.append(out_float.astype(jnp.bfloat16).reshape(1, stretched_length, model_width))
        stored.append(saved)
        differences.append(difference)
    loss_sum, count_sum = lax.psum((squares_local, count_local), ("dp", "seq"))
    loss = loss_sum / count_sum
    factor = total_tokens / count_sum
    grad_sums = None
    token_grads = []
    for micro in range(slot_count):
        weights = collect(shards)
        grads, grad_tokens = backward_slot(
            weights,
            stored[micro],
            factor * differences[micro],
            lengths[micro : micro + 1],
            query_pos,
            cosine_table,
            sine_table,
        )
        grad_sums = grads if grad_sums is None else jax.tree.map(jnp.add, grad_sums, grads)
        token_grads.append(grad_tokens.reshape(1, stretched_length, model_width))
    owned, gain_part_attn, gain_part_ffn = reduce_grads(grad_sums)
    gain_totals = lax.psum((gain_part_attn, gain_part_ffn), "dp")
    output = jnp.concatenate(out_rows, axis=0)
    tokens_grad = jnp.concatenate(token_grads, axis=0)
    return (
        output,
        loss,
        tokens_grad,
        owned[0],
        owned[1],
        owned[2],
        owned[3],
        owned[4],
        owned[5],
        owned[6],
        gain_totals[0],
        gain_totals[1],
    )


MESH_ID = pl.DeviceIdType.MESH
VMEM_MOST = 64 * 1024 * 1024 - 128 * 1024


class Place(tuple):
    def with_line(self):
        z = self[2]
        self.line = (0,) + tuple(pick(z, v) for v in ((1, -1, -1, -1), (2, 1, 1, -2), (3, 2, -2, -3)))
        self.sign = (0,) + tuple(jnp.where(offset > 0, 1, -1) for offset in self.line[1:])
        return self


def position():
    row = lax.axis_index("dp")
    column = lax.axis_index("seq")
    return Place((lax.rem(column, 2), row // 2, column // 2, lax.rem(row, 2))).with_line()


def mesh_place(x, y, z, c):
    return (2 * y + c, 2 * z + x)


def step_to(place, axis, sign=1):
    x, y, z, c = place
    if axis == "x":
        return (1 - x, y, z, c)
    if axis == "y":
        return (x, 1 - y, z, c)
    if axis == "z":
        return (x, y, z + sign, c)
    return (x, y, z, 1 - c)


def pick(z, values):
    return sum(jnp.where(z == i, v, 0) for i, v in enumerate(values) if v)


def shifted(place, rel):
    x, y, z, c = place
    dx, dy, rank = rel
    return ((1 - x) if dx else x, (1 - y) if dy else y, z + place.line[rank], c)


def on_line(z):
    return jnp.logical_and(z >= 0, z < 4)


def greet(place, lines):
    x, y, z, c = place
    d, s = mesh_place(*place)
    barrier = pltpu.get_barrier_semaphore()

    def signal(who):
        pl.semaphore_signal(barrier, inc=1, device_id=who, device_id_type=MESH_ID)

    if lines:
        for k in range(1, 8):
            signal((d, lax.rem(s + k, 8)))
        for k in range(1, 4):
            signal((lax.rem(d + k, 4), s))
        pl.semaphore_wait(barrier, 10)
        return
    for axis in "xyc":
        signal(mesh_place(*step_to(place, axis)))
    pl.when(z < 3)(lambda: signal(mesh_place(x, y, z + 1, c)))
    pl.when(z > 0)(lambda: signal(mesh_place(x, y, z - 1, c)))
    pl.semaphore_wait(barrier, 3 + jnp.where(z > 0, 1, 0) + jnp.where(z < 3, 1, 0))


def wait_bytes(region, sem):
    pltpu.make_async_copy(region, region, sem).wait()


def spread_order(order):
    held = [((0, 0, 0), -1)]
    for level, axis in enumerate(order):
        new = []
        if axis == "z":
            new = [((rel[0], rel[1], rank), level) for rank in (1, 2, 3) for rel, _ in held]
        else:
            new = [((1, rel[1], rel[2]) if axis == "x" else (rel[0], 1, rel[2]), level) for rel, _ in held]
        held = held + new
    return held


class Spread:
    def __init__(self, place, order, own, spot, sems, job, pair=None, amount=None):
        self.place, self.order, self.own, self.spot = place, order, own, spot
        self.recv, self.send, self.recv_core, self.send_core = sems
        self.job, self.pair, self.amount = job, pair, amount
        self.pieces = spread_order(order)

    def number(self, who):
        x, y, z, _ = who
        return z * 4 + y * 2 + x

    def go(self, rel, level, target):
        who = shifted(self.place, rel)
        pltpu.make_async_remote_copy(
            src_ref=self.own if level < 0 else self.spot(who),
            dst_ref=self.spot(who),
            send_sem=self.send.at[self.job],
            recv_sem=self.recv.at[self.job, self.number(who)],
            device_id=mesh_place(*target),
            device_id_type=MESH_ID,
        ).start()

    def to_core(self, rel):
        who = shifted(self.place, rel)
        pltpu.make_async_remote_copy(
            src_ref=self.pair(who),
            dst_ref=self.pair(who),
            send_sem=self.send_core.at[self.job],
            recv_sem=self.recv_core.at[self.job],
            device_id=mesh_place(*step_to(self.place, "c")),
            device_id_type=MESH_ID,
        ).start()

    def steps(self):
        out = []
        arrived = set()
        z = self.place[2]
        for rel, level in self.pieces:

            def run(rel=rel, level=level):
                arrived.add(rel)
                who = shifted(self.place, rel)
                if level >= 0:
                    there = self.spot(who)
                    pltpu.make_async_copy(there, there, self.recv.at[self.job, self.number(who)]).wait()
                if level >= 0 and self.order[level] == "z":
                    on = z - self.place.sign[rel[2]]
                    pl.when(on_line(on))(lambda: self.go(rel, level, (self.place[0], self.place[1], on, self.place[3])))
                for axis in self.order[level + 1:]:
                    if axis == "z":
                        pl.when(z < 3)(lambda: self.go(rel, level, step_to(self.place, "z", 1)))
                        pl.when(z > 0)(lambda: self.go(rel, level, step_to(self.place, "z", -1)))
                    else:
                        self.go(rel, level, step_to(self.place, axis))
                if self.pair is not None and (1 - rel[0], rel[1], rel[2]) in arrived:
                    self.to_core(rel)

            out.append(run)
        return out

    def sent(self):
        total = [0, 0]
        for i, z in enumerate((0, 1)):
            for rel, level in self.pieces:
                if level >= 0 and self.order[level] == "z":
                    offset = (0, ((1, -1)[z]), ((2, 1)[z]), ((3, 2)[z]))[rel[2]]
                    on = z - (1 if offset > 0 else -1)
                    total[i] += 0 <= on < 4
                for axis in self.order[level + 1:]:
                    total[i] += (1, 2)[z] if axis == "z" else 1
        return total

    def wait_core(self):
        wait_bytes(self.amount(16), self.recv_core.at[self.job])

    def finish(self):
        ends, inner = self.sent()
        z = self.place[2]
        at_end = jnp.logical_or(z == 0, z == 3)
        pl.when(at_end)(lambda: wait_bytes(self.amount(ends), self.send.at[self.job]))
        pl.when(jnp.logical_not(at_end))(lambda: wait_bytes(self.amount(inner), self.send.at[self.job]))
        if self.pair is not None:
            wait_bytes(self.amount(16), self.send_core.at[self.job])


def fold_pieces(order):
    out = []
    for dx in (0, 1):
        for dy in (0, 1) if "y" in order else (0,):
            for rank in (0, 1, 2, 3):
                differs = {"x": dx, "y": dy, "z": rank}
                stage = next((i for i, axis in enumerate(order) if differs[axis]), len(order))
                out.append(((dx, dy, rank), stage))
    return sorted(out, key=lambda item: (item[1], -item[0][2], -item[0][0] - item[0][1]))


def fold_slots(order):
    base, starts = 0, []
    for level, axis in enumerate(order):
        starts.append(base)
        after = order[level + 1:]
        wide = (4 if "z" in after else 1) * (2 if "x" in after else 1) * (2 if "y" in after else 1)
        base += wide * 5 if axis == "z" else wide
    return starts, base


class Fold:
    def __init__(self, place, order, mine, arrived, sems, job, out, amount, ready=None):
        self.place, self.order, self.mine, self.arrived = place, order, mine, arrived
        self.send, self.recv = sems
        self.job, self.out, self.amount, self.ready = job, out, amount, ready
        self.pieces = fold_pieces(order)
        self.base, self.slots = fold_slots(order)

    def slot(self, level, rel, last):
        index = 0
        at_z = self.place[2] + self.place.line[rel[2]]
        for other in self.order[level + 1:]:
            size = 4 if other == "z" else 2
            index = index * size + (at_z if other == "z" else (rel[0] if other == "x" else rel[1]))
        if self.order[level] == "z":
            index = index * 5 + (4 if last is True else (at_z if last is False else jnp.where(last, 4, at_z)))
        return self.base[level] + index

    def take(self, mine, slot):
        there = self.arrived.at[slot]
        pltpu.make_async_copy(there, there, self.recv.at[self.job, slot]).wait()
        mine[...] = mine[...] + self.arrived[slot]

    def steps(self):
        out = []
        present = set()
        z = self.place[2]
        for rel, stage in self.pieces:

            def run(rel=rel, stage=stage):
                if self.ready is not None and rel[1] not in present:
                    present.add(rel[1])
                    self.ready(rel[1])
                mine = self.mine(shifted(self.place, rel))
                offset, sign = self.place.line[rel[2]], self.place.sign[rel[2]]
                for level in range(min(stage + 1, len(self.order))):
                    if self.order[level] == "z":
                        if level < stage:
                            pl.when(z > 0)(lambda: self.take(mine, self.slot(level, rel, False)))
                            pl.when(z < 3)(lambda: self.take(mine, self.slot(level, rel, True)))
                        else:
                            behind = z - sign
                            pl.when(on_line(behind))(lambda: self.take(mine, self.slot(level, rel, False)))
                    elif level < stage:
                        self.take(mine, self.slot(level, rel, False))
                if stage == len(self.order):
                    self.out(mine[...].astype(jnp.float32))
                    return
                axis = self.order[stage]
                if axis == "z":
                    target = (self.place[0], self.place[1], z + sign, self.place[3])
                else:
                    target = step_to(self.place, axis)
                slot = self.slot(stage, rel, offset == -1 if axis == "z" else False)
                pltpu.make_async_remote_copy(
                    src_ref=mine,
                    dst_ref=self.arrived.at[slot],
                    send_sem=self.send.at[self.job],
                    recv_sem=self.recv.at[self.job, slot],
                    device_id=mesh_place(*target),
                    device_id_type=MESH_ID,
                ).start()

            out.append(run)
        return out

    def finish(self):
        wait_bytes(self.amount(len(self.pieces) - 1), self.send.at[self.job])


CAT_JOBS = (("cat", 0, 96, "xzy"), ("cat", 96, 96, "yzx"), ("cat", 192, 96, "zxy"))
FFN_JOBS = (
    ("gate", 0, 144, "xzy"), ("up", 0, 96, "yzx"), ("down", 0, 384, "zxy"),
    ("gate", 144, 144, "xzy"), ("up", 96, 96, "yzx"), ("down", 384, 384, "zxy"), ("up", 192, 96, "zyx"),
)
KV_JOBS = tuple((slot, 256 * third, "zx") for slot in (0, 1) for third in (0, 1, 2))
FOLD_FFN = tuple(job[:3] + (job[3][::-1],) for job in FFN_JOBS)
FOLD_CAT = tuple(job[:3] + (job[3][::-1],) for job in CAT_JOBS)
FOLD_KV = tuple((slot, row, order[::-1]) for slot, row, order in KV_JOBS)
FFN_NAMES = ("gate", "up", "down")


def job_shape(job):
    return (144, job[2]) if job[0] == "down" else (job[2], 384)


def piece_of(ref, job, paired=False):
    name, first, count, _ = job
    double = 2 if paired else 1

    def spot(who):
        x, y, z, c = who
        d, s = mesh_place(0 if paired else x, y, z, c)
        if name == "down":
            return ref.at[
                pl.ds(pl.multiple_of(s * 144, 16), 144 * double), pl.ds(pl.multiple_of(d * 768 + first, 128), count)
            ]
        return ref.at[
            pl.ds(pl.multiple_of(d * 288 + first, 8), count), pl.ds(pl.multiple_of(s * 384, 128), 384 * double)
        ]

    return spot


def region(ref, elements, rows, columns):
    units = elements // 2048
    wide = max(k for k in range(1, columns // 128 + 1) if units % k == 0 and units // k <= rows // 16)
    return ref.at[pl.ds(0, units // wide * 16), pl.ds(0, wide * 128)]


def amount_of(ref, job):
    rows, columns = job_shape(job)
    return lambda pieces: region(ref, pieces * rows * columns, *ref.shape)


def own_part(ref, job):
    name, first, count, _ = job
    return ref.at[:, pl.ds(first, count)] if name == "down" else ref.at[pl.ds(first, count), :]


def kv_spot(ref, slot, row):
    def spot(who):
        _, s = mesh_place(*who)
        return ref.at[slot, pl.ds(row, 256), pl.ds(pl.multiple_of(s * 128, 128), 128)]

    return spot


def kv_amount(ref):
    return lambda pieces: ref.at[0, pl.ds(0, 32 * pieces), :]


def make_spreads(place, jobs, shards, wholes, sems):
    return [
        Spread(
            place, job[3], own_part(shards[job[0]], job), piece_of(wholes[job[0]], job), sems, j,
            piece_of(wholes[job[0]], job, True), amount_of(wholes[job[0]], job),
        )
        for j, job in enumerate(jobs)
    ]


def make_kv_spreads(place, own, whole, sems):
    return [
        Spread(
            place, order, own.at[pl.ds(row, 256), pl.ds(slot * 128, 128)], kv_spot(whole, slot, row),
            (sems[0], sems[1], None, None), j, None, kv_amount(whole),
        )
        for j, (slot, row, order) in enumerate(KV_JOBS)
    ]


def spread_sems(jobs):
    n = len(jobs)
    return [
        pltpu.SemaphoreType.DMA((n, 16)), pltpu.SemaphoreType.DMA((n,)),
        pltpu.SemaphoreType.DMA((n,)), pltpu.SemaphoreType.DMA((n,)),
    ]


def fold_scratch(jobs, paired):
    n = len(jobs)
    most = max(fold_slots(job[3])[1] for job in jobs)
    scratch = [
        pltpu.SemaphoreType.DMA((n,)), pltpu.SemaphoreType.DMA((n, most)),
        pltpu.SemaphoreType.DMA((n, 2)), pltpu.SemaphoreType.DMA((n, 2)), pltpu.SemaphoreType.DMA((n, 2)),
    ]
    for job in jobs:
        rows, columns = job_shape(job)
        block = (2, 1152, columns) if job[0] == "down" else (2, rows, 3072)
        scratch += [
            pltpu.VMEM(block, jnp.bfloat16), pltpu.VMEM((fold_slots(job[3])[1], rows, columns), jnp.bfloat16)
        ]
        scratch += [pltpu.VMEM(block, jnp.bfloat16)] if paired else []
    return scratch


class JobFold:
    def __init__(self, place, job, j, sums, owned, scratch, paired):
        self.place, self.job, self.j, self.sums, self.paired = place, job, j, sums, paired
        send, recv, self.load_sem, self.core_send, self.core_recv = scratch[:5]
        each = 3 if paired else 2
        self.acc, arrived = scratch[5 + each * j: 7 + each * j]
        self.other = scratch[7 + each * j] if paired else None
        name, first, count, order = job

        def mine(who):
            x, y, z, c = who
            s = 2 * z + x
            if name == "down":
                return self.acc.at[y, pl.ds(pl.multiple_of(s * 144, 16), 144), :]
            return self.acc.at[y, :, pl.ds(pl.multiple_of(s * 384, 128), 384)]

        def out(value):
            if name == "down":
                owned[:, first: first + count] = value
            else:
                owned[first: first + count, :] = value

        self.fold = Fold(place, order, mine, arrived, (send, recv), j, out, amount_of(sums, job), self.ready)

    def block(self, y, c):
        name, first, count, _ = self.job
        d = 2 * y + c if self.paired else y
        if name == "down":
            return self.sums.at[:, pl.ds(pl.multiple_of(d * 768 + first, 128), count)]
        return self.sums.at[pl.ds(pl.multiple_of(d * 288 + first, 8), count), :]

    def local_copy(self, dy):
        x, y, z, c = self.place
        at = (1 - y) if dy else y
        return pltpu.make_async_copy(self.block(at, c), self.acc.at[at], self.load_sem.at[self.j, dy])

    def core_copy(self, dy):
        x, y, z, c = self.place
        at = (1 - y) if dy else y
        return pltpu.make_async_remote_copy(
            src_ref=self.block(at, 1 - c),
            dst_ref=self.other.at[at],
            send_sem=self.core_send.at[self.j, dy],
            recv_sem=self.core_recv.at[self.j, dy],
            device_id=mesh_place(x, y, z, 1 - c),
            device_id_type=MESH_ID,
        )

    def begin(self, dy):
        if self.paired:
            self.core_copy(dy).start()
        self.local_copy(dy).start()

    def ready(self, dy):
        y = self.place[1]
        at = (1 - y) if dy else y
        self.local_copy(dy).wait()
        if not self.paired:
            return
        self.core_copy(dy).wait_recv()

        def add(k, _):
            if self.job[0] == "down":
                part = (at, pl.ds(pl.multiple_of(k * 144, 16), 144), slice(None))
            else:
                part = (at, slice(None), pl.ds(pl.multiple_of(k * 384, 128), 384))
            self.acc[part] = self.acc[part] + self.other[part]
            return _

        lax.fori_loop(0, 8, add, 0)

    def finish(self):
        self.fold.finish()
        for dy in (0, 1) if self.paired else ():
            self.core_copy(dy).wait_send()


class Notes:
    def __init__(self, place, tile_of, own, by_seq, by_dp, sems):
        self.d, self.s = mesh_place(*place)
        self.tile_of, self.own, self.by_seq, self.by_dp = tile_of, own, by_seq, by_dp
        self.seq_send, self.seq_recv, self.dp_send, self.dp_recv = sems

    def along_seq(self, k):
        peer = lax.rem(self.s + k, 8)
        return pltpu.make_async_remote_copy(
            src_ref=self.tile_of(peer), dst_ref=self.by_seq.at[self.s], send_sem=self.seq_send.at[k],
            recv_sem=self.seq_recv.at[self.s], device_id=(self.d, peer), device_id_type=MESH_ID,
        )

    def along_dp(self, k):
        peer = lax.rem(self.d + k, 4)
        return pltpu.make_async_remote_copy(
            src_ref=self.own, dst_ref=self.by_dp.at[self.d], send_sem=self.dp_send.at[k],
            recv_sem=self.dp_recv.at[self.d], device_id=(peer, self.s), device_id_type=MESH_ID,
        )

    def wait_seq(self):
        for k in range(1, 8):
            peer = lax.rem(self.s + k, 8)
            there = self.by_seq.at[peer]
            pltpu.make_async_copy(there, there, self.seq_recv.at[peer]).wait()

    def wait_dp(self):
        for k in range(1, 4):
            peer = lax.rem(self.d + k, 4)
            there = self.by_dp.at[peer]
            pltpu.make_async_copy(there, there, self.dp_recv.at[peer]).wait()


NOTE_SEMS = [
    pltpu.SemaphoreType.DMA((8,)), pltpu.SemaphoreType.DMA((8,)),
    pltpu.SemaphoreType.DMA((4,)), pltpu.SemaphoreType.DMA((4,)),
]


FORWARD_PLAN = (
    (200, 0, 100,),
    (2, 1, 201, 204, 101, 102, 4, 202, 3, 8, 205, 208, 108, 104, 103, 203, 5, 206, 9, 109, 209, 105, 10, 110,
        6, 212, 207, 106, 210, 7, 112, 10500, 12, 11,),
    (111, 107, 213, 10200, 113, 211, 10600, 214, 13, 10000, 10300, 10400, 114, 215, 14, 115, 15,),
    (20000, 20100, 20200, 20300, 20400, 20500,),
    (10100, 20001, 20004, 20101, 20201, 20104, 20301, 20204, 10201, 10002, 10001, 20401, 20304, 10204, 20501,
        10501, 20404, 20002, 10208, 20504, 10008, 10504, 20102, 10508, 10301, 10302, 20202, 10402, 10601,
        20005, 20302, 10308, 10401, 10408, 20205, 20402, 10604, 10608, 10102, 20502, 10101, 20305, 10108,
        10202, 20405, 10004, 20505, 10502, 10209, 10009, 10010, 20105, 10205, 20003, 10003, 10304, 10509,
        20103, 10602, 20006, 10605, 10505, 20203, 10404, 10212, 10104, 10309, 10310, 20106, 20303, 20403,
        10303, 20206, 10512, 20306, 20503, 10005, 10403, 10210, 20406, 10103, 10409, 10510, 10110, 10609,
        20506, 10410, 10305, 10109, 10213, 10513, 10203, 10012, 10405, 10503, 10011, 10105, 10612, 10206,
        20007, 10506, 10606, 10013, 20107, 10603, 10613, 10312, 10610, 20207, 10311, 10006, 20307, 10211,
        10313, 20407, 10511, 20507,),
    (
        (1, (10412,)),
        (3, (10411,)),
        (4, (10007, 10207,)),
        (5, (10306, 10413, 10112, 10406, 10214,)),
        (6, (10507,)),
        (7, (10111, 10514,)),
        (8, (10607, 10106,)),
        (9, (10307,)),
        (10, (10407,)),
    ),
    (10113, 10611, 10107, 10014, 10614, 10415, 10515, 10215, 10314, 10615, 10015, 10114, 10414, 10315, 10115,),
)
BACKWARD_PLAN = (
    (
        (10100, 10101, 10102, 10104, 10103, 10300,),
        (10000, 10105, 10002, 10301,),
    ),
    (
        (1, (10001, 10500,)),
        (2, (10302, 10106, 10200,)),
        (3, (10501,)),
        (5, (10107, 10108,)),
        (6, (20000, 20100, 20001, 20002, 20101, 20200, 20201, 20102, 20003, 20103, 20202, 10303, 10003, 10109,
            10401, 20004,)),
        (7, (20203, 10502, 20104, 10004, 10400,)),
        (8, (10304, 10110,)),
        (9, (20005,)),
        (10, (20204, 20006, 10201,)),
        (11, (20105, 20106, 10503, 10402,)),
    ),
    (20500, 20300, 20400, 20401, 20301, 20302, 20402, 20303, 20403, 10305, 10202, 20205, 10504, 20007, 10111,
        20206, 10306, 10601, 10600, 20107, 20501, 20502, 20503, 10403, 10112, 10005, 10505, 10203, 10307,
        10308, 10602, 20207, 10204, 10404, 10506, 10007, 10603, 10006, 10008, 10309, 10205, 10405, 10507,
        10508, 10509, 20404, 20504, 10009, 10604, 10010, 20304, 10605, 10310, 20405, 10207, 20305, 20306,
        10206, 10208, 10209, 10407, 20406, 20505, 20506, 10311, 10012, 10510, 10312, 10011, 10210, 10113,
        20307, 10406, 10408, 10409, 10410, 20407, 10607, 10606, 10608, 10609, 20507,),
    (
        (3, (10411,)),
        (4, (10610,)),
        (7, (10412,)),
    ),
    (10511, 10211, 10114, 10313, 0, 1, 2, 3, 100, 102, 200, 201,),
    (202, 203, 10013, 101, 4, 204,),
    (206, 103, 5, 105, 205, 104, 106, 6, 7, 207, 10512, 10212, 10014, 10413, 107, 8, 208, 10611, 10115,),
    (209, 108, 9, 10314, 109, 10, 12, 10612, 110, 112, 210, 11, 13, 111, 113, 211, 212, 10414,),
    (10513, 10514, 14, 10315, 114, 10015, 10213, 10214, 10613, 213, 214, 15, 10614, 115, 215, 10515, 10415,
        10215, 10615,),
)


def dot(a, b):
    return jnp.dot(a, b, preferred_element_type=jnp.float32)


def dot_t(a, b):
    return lax.dot_general(a, b, (((1,), (1,)), ((), ())), preferred_element_type=jnp.float32)


def t_dot(a, b):
    return lax.dot_general(a, b, (((0,), (0,)), ((), ())), preferred_element_type=jnp.float32)


def repeat(count, body):
    def step(k, nothing):
        body(k)
        return nothing

    lax.fori_loop(0, count, step, 0)


def rows_at(k, size, base=0):
    return pl.ds(pl.multiple_of(base + k * size, 16), size)


def lanes_at(k, size, base=0):
    return pl.ds(pl.multiple_of(base + k * size, 128), size)


def rotate(u, cosine, sine):
    front, back = u[:32], u[32:]
    return jnp.concatenate([front * cosine - back * sine, front * sine + back * cosine], axis=0)


def probabilities(keys, query, limit, chunk):
    scores = t_dot(keys, query) * (HEAD_DIMENSION ** (-0.5))
    key_pos = chunk * 256 + lax.broadcasted_iota(jnp.int32, (256, 384), 0)
    return jnp.where(key_pos <= limit, jnp.exp(scores), 0.0)


def heads_wide(ref, group, lanes):
    return jnp.concatenate(
        [ref[pl.ds(pl.multiple_of(group * 192 + 64 * i, 64), 64), lanes] for i in range(3)], axis=1
    )


def key_limit(length, s):
    query_pos = s * 128 + lax.broadcasted_iota(jnp.int32, (1, 128), 1)
    return jnp.concatenate([jnp.minimum(query_pos, length - 1)] * 3, axis=1)


def forward_body(
    lengths, query_t, key_t, value_t, out_t, gain_a, gain_f, x, cosine, sine, gate, up, down,
    gate_w, up_w, down_w, wcat, kept_in_t, kept_query, kept_kv, kept_attn, kept_denom, notes, hidden,
    tile, cat_t, cat, attn_in_t, query, keys_values, attn, denom,
    attn_in, raw, own_kv, weights, proj, seq_in, dp_in, own_sems, note_a, note_b, note_c, note_d, *sems
):
    place = position()
    d, s = mesh_place(*place)
    row = 0
    for part in (query_t, key_t, value_t, out_t):
        cat_t[row: row + part.shape[0], 0:288] = part[...].astype(jnp.float32)
        row += part.shape[0]
    cat[...] = cat_t[...].T[0:288, :].astype(jnp.bfloat16)
    tile[...] = jnp.zeros_like(tile)
    for k in range(8):
        def own_gains(k=k):
            tile[0:1, 144 * k: 144 * k + 144] = gain_a[...].astype(jnp.float32).reshape(1, 144)
            tile[1:2, 144 * k: 144 * k + 144] = gain_f[...].astype(jnp.float32).reshape(1, 144)

        pl.when(s == k)(own_gains)
    tile[2:3, :] = jnp.broadcast_to((lengths[0] + lengths[1]).astype(jnp.float32), (1, 1152))
    greet(place, True)
    shards = dict(zip(FFN_NAMES, (gate, up, down)))
    wholes = dict(zip(FFN_NAMES, (gate_w, up_w, down_w)))
    cat_spreads = make_spreads(place, CAT_JOBS, {"cat": cat}, {"cat": weights}, sems[:4])
    ffn_spreads = make_spreads(place, FFN_JOBS, shards, wholes, sems[4:8])
    kv_spreads = make_kv_spreads(place, own_kv, keys_values, sems[8:10])
    steps = [[spread.steps() for spread in family] for family in (cat_spreads, ffn_spreads, kv_spreads)]

    def run(tokens):
        for token in tokens:
            steps[token // 10000][token // 100 % 100][token % 100]()

    tiles = Notes(place, lambda peer: tile, tile, seq_in, dp_in, (note_a, note_b, note_c, note_d))
    run(FORWARD_PLAN[0])
    for k in range(1, 8):
        tiles.along_seq(k).start()
    for k in range(1, 4):
        tiles.along_dp(k).start()
    own = [
        pltpu.make_async_copy(
            shards[name], piece_of(wholes[name], (name, 0, 768 if name == "down" else 288, ""))(place), own_sems.at[k]
        )
        for k, name in enumerate(FFN_NAMES)
    ]
    for copy in own:
        copy.start()
    weights[rows_at(d, 288), lanes_at(s, 384)] = cat[...]
    for copy in own:
        copy.wait()
    run(FORWARD_PLAN[1])
    tiles.wait_seq()
    tiles.wait_dp()
    seq_in[s] = tile[...]
    dp_in[d] = tile[...]
    gains = seq_in[0]
    for k in range(1, 8):
        gains = gains + seq_in[k]
    notes[0:8, :] = gains
    notes[8:16, :] = dp_in[0] + dp_in[1] + dp_in[2] + dp_in[3]

    def norm(k):
        rows = rows_at(k, 32)
        part = x[rows, :].astype(jnp.float32)
        scale = lax.rsqrt(jnp.mean(part * part, axis=-1, keepdims=True) + norm_eps)
        attn_in[rows, :] = (part * scale * notes[0:1, :]).astype(jnp.bfloat16)

    repeat(8, norm)
    attn_in_t[...] = attn_in[...].T
    run(FORWARD_PLAN[2])
    for spread in cat_spreads:
        spread.wait_core()

    def project(b):
        block = dot(attn_in[...], weights[:, lanes_at(b, 384)][:, :256]).T
        raw[rows_at(b, 144), :] = block[:144]
        raw[rows_at(b, 48, 1152), :] = block[144:192]
        raw[rows_at(b, 48, 1536), :] = block[192:240]

    repeat(8, project)
    out_copy = pltpu.make_async_copy(weights, wcat, own_sems.at[3])
    out_copy.start()

    def turn(ref, rows_of):
        def one(h):
            ref[rows_at(h, 64), :] = rotate(raw[rows_of(h), :], cosine[...], sine[...]).astype(jnp.bfloat16)

        return one

    repeat(6, turn(own_kv, lambda h: rows_at(h, 64, 1152)))
    own_kv[384:768, :] = raw[1536:1920, :].astype(jnp.bfloat16)
    repeat(18, turn(query, lambda h: rows_at(h, 64)))
    keeps = [
        pltpu.make_async_copy(source, target, own_sems.at[4 + k])
        for k, (source, target) in enumerate(
            ((attn_in_t, kept_in_t), (query, kept_query), (keys_values, kept_kv), (attn, kept_attn), (denom, kept_denom))
        )
    ]
    keeps[0].start()
    keeps[1].start()
    run(FORWARD_PLAN[3])
    here = lanes_at(s, 128)
    for slot in range(2):
        keys_values[slot, :, here] = own_kv[:, slot * 128: slot * 128 + 128]
    run(FORWARD_PLAN[4])
    keeps[2].start()

    def attend(slot, group):
        lanes = lanes_at(slot, 128)
        bound = key_limit(lengths[slot], s)
        wide = heads_wide(query, group, lanes)

        def one_chunk(chunk, carry):
            total, numer = carry
            cols = lanes_at(chunk, 256)
            expo = probabilities(keys_values[slot, rows_at(group, 64), cols], wide, bound, chunk)
            total = total + jnp.sum(expo, axis=0, keepdims=True)
            numer = numer + dot(keys_values[slot, rows_at(group, 64, 384), cols], expo.astype(jnp.bfloat16))
            return (total, numer)

        total, numer = lax.fori_loop(
            0, 4, one_chunk, (jnp.zeros((1, 384), jnp.float32), jnp.zeros((64, 384), jnp.float32)), unroll=True
        )
        mean = numer / total
        for i in range(3):
            attn[pl.ds(pl.multiple_of(group * 192 + 64 * i, 64), 64), lanes] = mean[:, i * 128: i * 128 + 128]
        denom[group, 0:3, lanes] = jnp.concatenate([total[:, i * 128: i * 128 + 128] for i in range(3)], axis=0)

    def unit(k):
        attend(k // 6, lax.rem(k, 6))
        for at, tokens in FORWARD_PLAN[5]:
            pl.when(k == at)(lambda tokens=tokens: run(tokens))

    repeat(12, unit)
    keeps[3].start()
    keeps[4].start()

    def out_project(b):
        block = t_dot(attn[...].astype(jnp.bfloat16), weights[:, lanes_at(b, 384)][:, 128:]).T
        proj[rows_at(b, 144), :] = block[112:256]

    repeat(8, out_project)
    hidden[...] = x[...].astype(jnp.float32) + proj[...].T
    run(FORWARD_PLAN[6])
    for spread in cat_spreads + ffn_spreads + kv_spreads:
        spread.finish()
    for spread in ffn_spreads:
        spread.wait_core()
    for k in range(1, 8):
        tiles.along_seq(k).wait_send()
    for k in range(1, 4):
        tiles.along_dp(k).wait_send()
    for copy in [out_copy] + keeps:
        copy.wait()


def forward_call(lengths, shards_t, gain_a, gain_f, x, cosine, sine, gate, up, down):
    vmem, anywhere = pl.BlockSpec(memory_space=pltpu.VMEM), pl.BlockSpec(memory_space=pl.ANY)
    kept = [
        ((1152, 256), jnp.bfloat16), ((1152, 256), jnp.bfloat16), ((2, 768, 1024), jnp.bfloat16),
        ((1152, 256), jnp.float32), ((6, 8, 256), jnp.float32),
    ]
    return pl.pallas_call(
        forward_body,
        out_shape=[jax.ShapeDtypeStruct((1152, 3072), jnp.bfloat16)] * 4
        + [jax.ShapeDtypeStruct(*item) for item in kept]
        + [jax.ShapeDtypeStruct((16, 1152), jnp.float32), jax.ShapeDtypeStruct((256, 1152), jnp.float32)],
        in_specs=[pl.BlockSpec(memory_space=pltpu.SMEM)] + [vmem] * 12,
        out_specs=[anywhere] * 9 + [vmem] * 2,
        scratch_shapes=[pltpu.VMEM((8, 1152), jnp.float32), pltpu.VMEM((384, 384), jnp.float32), pltpu.VMEM((288, 384), jnp.bfloat16)]
        + [pltpu.VMEM(*item) for item in kept]
        + [
            pltpu.VMEM((256, 1152), jnp.bfloat16),
            pltpu.VMEM((1920, 256), jnp.float32),
            pltpu.VMEM((768, 256), jnp.bfloat16),
            pltpu.VMEM((1152, 3072), jnp.bfloat16),
            pltpu.VMEM((1152, 256), jnp.float32),
            pltpu.VMEM((8, 8, 1152), jnp.float32),
            pltpu.VMEM((4, 8, 1152), jnp.float32),
            pltpu.SemaphoreType.DMA((9,)),
        ]
        + NOTE_SEMS
        + spread_sems(CAT_JOBS)
        + spread_sems(FFN_JOBS)
        + spread_sems(KV_JOBS)[:2],
        compiler_params=pltpu.CompilerParams(
            collective_id=3, has_side_effects=True, vmem_limit_bytes=VMEM_MOST
        ),
        name="attention_forward",
    )(lengths, *shards_t, gain_a, gain_f, x, cosine, sine, gate, up, down)


def ffn_body(
    total_tokens, lengths, hidden, teacher, notes, gate_w, up_w, down_w,
    out, grad_hidden, small, gate_sums, up_sums, down_sums,
    w_gate, w_up, w_down, gate, up, hid, grads_gate, grads_up, inputs_t, cot_t, inputs, cot_b, acc, cot, rate,
    sums_gate, sums_up, sums_down, load, swap_send, swap_recv, store
):
    place = position()
    x, y, z, c = place
    _, s = mesh_place(*place)
    other = mesh_place(x, y, z, 1 - c)
    barrier = pltpu.get_barrier_semaphore()
    pl.semaphore_signal(barrier, inc=1, device_id=other, device_id_type=MESH_ID)
    pl.semaphore_wait(barrier, 1)
    columns = lambda j: lanes_at(j, 768)

    def load_copy(k, source, target, j):
        return pltpu.make_async_copy(source.at[:, columns(j)], target.at[:, columns(j)], load.at[k, j])

    def loads(j):
        return [load_copy(k, *pair, j) for k, pair in enumerate(((gate_w, w_gate), (up_w, w_up), (down_w, w_down)))]

    for j in range(4):
        for copy in loads(j):
            copy.start()

    def swap(source, target, k):
        return pltpu.make_async_remote_copy(
            src_ref=source, dst_ref=target, send_sem=swap_send.at[k], recv_sem=swap_recv.at[k],
            device_id=other, device_id_type=MESH_ID,
        )

    own, theirs = pl.ds(0, 256), pl.ds(256, 256)
    swap_inputs = swap(inputs_t.at[:, own], inputs_t.at[:, theirs], 0)
    swap_cot = swap(cot_t.at[:, own], cot_t.at[:, theirs], 1)

    def swap_hid(i, core):
        at = columns(core + 2 * i)
        return swap(hid.at[own, at], hid.at[theirs, at], 2 + i)

    def swap_grads(ref, j, k):
        return swap(ref.at[own, columns(j)], ref.at[theirs, columns(j)], k + j)

    def norm(k):
        rows = rows_at(k, 32)
        part = hidden[rows, :]
        scale = lax.rsqrt(jnp.mean(part * part, axis=-1, keepdims=True) + norm_eps)
        rate[rows, :] = jnp.broadcast_to(scale, (32, 128))
        inputs[rows, :] = (part * scale * notes[1:2, :]).astype(jnp.bfloat16)

    repeat(8, norm)
    inputs_t[:, 0:256] = inputs[...].T
    acc[...] = jnp.zeros_like(acc)

    def forward(j):
        for copy in loads(j):
            copy.wait()
        at = columns(j)
        gate_part = dot(inputs[...], w_gate[:, at])
        up_part = dot(inputs[...], w_up[:, at])
        gate[:, at] = gate_part
        up[:, at] = up_part
        hid[0:256, at] = (gate_part * jax.nn.sigmoid(gate_part) * up_part).astype(jnp.bfloat16)
        acc[...] += dot_t(hid[0:256, at], w_down[:, at])

    repeat(4, forward)
    swap_inputs.start()
    for i in range(2):
        swap_hid(i, 1 - c).start()
    factor = total_tokens / notes[10:11, :]
    small[...] = jnp.zeros_like(small)

    def losses(k):
        rows = rows_at(k, 32)
        first = s * 128 + lax.rem(k, 4) * 32
        live = first + lax.broadcasted_iota(jnp.int32, (32, 1), 0) < lengths[k // 4]
        value = jnp.where(live, hidden[rows, :] + acc[rows, :], 0.0)
        out[rows, :] = value.astype(jnp.bfloat16)
        diff = jnp.where(live, value - teacher[rows, :].astype(jnp.float32), 0.0)
        small[2:3, :] += jnp.sum(diff * diff, axis=0, keepdims=True)
        grad = factor * diff
        cot[rows, :] = grad
        cot_b[rows, :] = grad.astype(jnp.bfloat16)

    repeat(8, losses)
    cot_t[:, 0:256] = cot_b[...].T
    acc[...] = jnp.zeros_like(acc)

    def backward(j):
        at = columns(j)
        grad_hid = dot(cot_b[...], w_down[:, at])
        gate_part = gate[:, at]
        sig = jax.nn.sigmoid(gate_part)
        grads_gate[0:256, at] = (
            grad_hid * up[:, at] * sig * (1.0 + gate_part * (1.0 - sig))
        ).astype(jnp.bfloat16)
        grads_up[0:256, at] = (grad_hid * gate_part * sig).astype(jnp.bfloat16)
        acc[...] += dot_t(grads_gate[0:256, at], w_gate[:, at]) + dot_t(grads_up[0:256, at], w_up[:, at])
        swap_grads(grads_gate, j, 4).start()
        swap_grads(grads_up, j, 8).start()
        pl.when(j == 0)(swap_cot.start)

    repeat(4, backward)

    def finish_rows(k):
        rows = rows_at(k, 32)
        scale = rate[rows, 0:1]
        normed = hidden[rows, :] * scale
        grad = acc[rows, :]
        small[1:2, :] += jnp.sum(grad * normed, axis=0, keepdims=True)
        grad = grad * notes[1:2, :]
        inner = grad - normed * jnp.mean(grad * normed, axis=-1, keepdims=True)
        grad_hidden[rows, :] = cot[rows, :] + scale * inner

    repeat(8, finish_rows)
    small[2:3, :] = jnp.broadcast_to(jnp.sum(small[2:3, :], axis=-1, keepdims=True), (1, 1152))
    small[3:4, :] = notes[0:1, :]
    swap_cot.wait_recv()
    swap_inputs.wait_recv()

    def stored(k, source, target, i):
        at = columns(i)
        return pltpu.make_async_copy(source.at[:, at], target.at[:, at], store.at[k, i])

    def down_grads(i):
        swap_hid(i, c).wait_recv()
        sums_down[:, columns(i)] = dot(cot_t[...], hid[:, columns(c + 2 * i)]).astype(jnp.bfloat16)
        stored(0, sums_down, down_sums, i).start()

    repeat(2, down_grads)

    def wide_grads(j):
        at = columns(j)
        swap_grads(grads_gate, j, 4).wait_recv()
        swap_grads(grads_up, j, 8).wait_recv()
        for half in range(2):
            rows = rows_at(c + 2 * half, 288)
            kept = slice(288 * half, 288 * half + 288)
            sums_gate[kept, at] = dot(inputs_t[rows, :], grads_gate[:, at]).astype(jnp.bfloat16)
            sums_up[kept, at] = dot(inputs_t[rows, :], grads_up[:, at]).astype(jnp.bfloat16)
        stored(1, sums_gate, gate_sums, j).start()
        stored(2, sums_up, up_sums, j).start()

    repeat(4, wide_grads)
    swap_inputs.wait_send()
    swap_cot.wait_send()
    for i in range(2):
        swap_hid(i, 1 - c).wait_send()
        stored(0, sums_down, down_sums, i).wait()
    for j in range(4):
        swap_grads(grads_gate, j, 4).wait_send()
        swap_grads(grads_up, j, 8).wait_send()
        stored(1, sums_gate, gate_sums, j).wait()
        stored(2, sums_up, up_sums, j).wait()


def ffn_call(total_tokens, lengths, hidden, teacher, notes, gate_w, up_w, down_w):
    vmem, anywhere = pl.BlockSpec(memory_space=pltpu.VMEM), pl.BlockSpec(memory_space=pl.ANY)
    whole = pltpu.VMEM((1152, 3072), jnp.bfloat16)
    both = pltpu.VMEM((512, 3072), jnp.bfloat16)
    return pl.pallas_call(
        functools.partial(ffn_body, total_tokens),
        out_shape=[
            jax.ShapeDtypeStruct((256, 1152), jnp.bfloat16),
            jax.ShapeDtypeStruct((256, 1152), jnp.float32),
            jax.ShapeDtypeStruct((8, 1152), jnp.float32),
            jax.ShapeDtypeStruct((576, 3072), jnp.bfloat16),
            jax.ShapeDtypeStruct((576, 3072), jnp.bfloat16),
            jax.ShapeDtypeStruct((1152, 1536), jnp.bfloat16),
        ],
        in_specs=[pl.BlockSpec(memory_space=pltpu.SMEM)] + [vmem] * 3 + [anywhere] * 3,
        out_specs=[vmem] * 3 + [anywhere] * 3,
        scratch_shapes=[whole] * 3
        + [pltpu.VMEM((256, 3072), jnp.float32)] * 2
        + [both] * 3
        + [pltpu.VMEM((1152, 512), jnp.bfloat16)] * 2
        + [pltpu.VMEM((256, 1152), jnp.bfloat16)] * 2
        + [pltpu.VMEM((256, 1152), jnp.float32)] * 2
        + [pltpu.VMEM((256, 128), jnp.float32)]
        + [pltpu.VMEM((576, 3072), jnp.bfloat16)] * 2
        + [
            pltpu.VMEM((1152, 1536), jnp.bfloat16),
            pltpu.SemaphoreType.DMA((3, 4)),
            pltpu.SemaphoreType.DMA((12,)),
            pltpu.SemaphoreType.DMA((12,)),
            pltpu.SemaphoreType.DMA((3, 4)),
        ],
        compiler_params=pltpu.CompilerParams(
            collective_id=5, has_side_effects=True, vmem_limit_bytes=VMEM_MOST
        ),
        name="feed_forward",
    )(lengths, hidden, teacher, notes, gate_w, up_w, down_w)


def backward_body(
    lengths, grad_hidden, cosine, sine, small, x_in, kept_in_t, wcat, keys_values, kept_query, kept_attn, kept_denom,
    grad_gate, grad_up, grad_down,
    own_gate, own_up, own_down, own_query_t, own_key_t, own_value_t, own_out_t, grad_tokens, totals, grad_cat,
    x, attn_in_t, query, attn, denom, own_cat, weights, whole_kv, part_kv, turned, total, own_kv, left, grad_t, note, seq_in, dp_in, row_sum,
    load, store, kv_send, kv_recv, *scratch
):
    place = position()
    d, s = mesh_place(*place)
    greet(place, True)
    sums = dict(zip(FFN_NAMES, (grad_gate, grad_up, grad_down)))
    owned = dict(zip(FFN_NAMES, (own_gate, own_up, own_down)))
    kv_arrived, scratch = scratch[: len(FOLD_KV)], scratch[len(FOLD_KV):]
    note_sems, scratch = scratch[:4], scratch[4:]
    split = len(fold_scratch(FOLD_FFN, False))
    folds = [
        JobFold(place, job, j, sums[job[0]], owned[job[0]], scratch[:split], False) for j, job in enumerate(FOLD_FFN)
    ]
    cat_folds = [JobFold(place, job, j, grad_cat, own_cat, scratch[split:], True) for j, job in enumerate(FOLD_CAT)]
    tiles = Notes(place, lambda peer: note, row_sum, seq_in, dp_in, note_sems)

    def kv_fold(j, slot, row, order):
        def out(value):
            own_kv[row: row + 256, slot * 128: slot * 128 + 128] = value

        spot = kv_spot(part_kv, slot, row)
        return Fold(place, order, lambda who: spot(who), kv_arrived[j], (kv_send, kv_recv), j, out, kv_amount(part_kv))

    kv_folds = [kv_fold(j, *job) for j, job in enumerate(FOLD_KV)]
    steps = [
        [fold.fold.steps() for fold in cat_folds],
        [fold.fold.steps() for fold in folds],
        [fold.steps() for fold in kv_folds],
    ]

    def run(tokens):
        for token in tokens:
            steps[token // 10000][token // 100 % 100][token % 100]()

    for dy in (1, 0):
        for fold in folds:
            fold.begin(dy)

    def block_load(b):
        return pltpu.make_async_copy(wcat.at[:, lanes_at(b, 384)], weights.at[:, lanes_at(b, 384)], load.at[b])

    repeat(8, lambda b: block_load(b).start())
    kept = [
        pltpu.make_async_copy(source, target, load.at[8 + k])
        for k, (source, target) in enumerate(
            ((keys_values, whole_kv), (kept_query, query), (kept_attn, attn), (kept_denom, denom),
             (kept_in_t, attn_in_t), (x_in, x))
        )
    ]
    for copy in kept:
        copy.start()
    run(BACKWARD_PLAN[0][0])
    grad_t[...] = grad_hidden[...].T.astype(jnp.bfloat16)
    total[...] = jnp.zeros_like(total)

    def out_rows(b):
        return jnp.concatenate([jnp.zeros((112, 256), jnp.bfloat16), grad_t[rows_at(b, 144), :]], axis=0)

    def out_back(b):
        block_load(b).wait()
        total[...] += dot(weights[:, lanes_at(b, 384)][:, 128:], out_rows(b))

    repeat(8, out_back)
    run(BACKWARD_PLAN[0][1])
    for copy in kept:
        copy.wait()
    scale = HEAD_DIMENSION ** (-0.5)

    def attend_back(slot, group):
        lanes = lanes_at(slot, 128)
        bound = key_limit(lengths[slot], s)
        wide = heads_wide(query, group, lanes)
        grads, ratios = [], []
        for i in range(3):
            rows = pl.ds(pl.multiple_of(group * 192 + 64 * i, 64), 64)
            grad = total[rows, lanes].astype(jnp.bfloat16).astype(jnp.float32)
            bottom = denom[group, i: i + 1, lanes]
            ratios.append(jnp.sum(grad * attn[rows, lanes], axis=0, keepdims=True) / bottom)
            grads.append((grad / bottom).astype(jnp.bfloat16))
        grads, ratios = jnp.concatenate(grads, axis=1), jnp.concatenate(ratios, axis=1)

        def one_chunk(chunk, sum_query):
            cols = lanes_at(chunk, 256)
            keys = whole_kv[slot, rows_at(group, 64), cols]
            values = whole_kv[slot, rows_at(group, 64, 384), cols]
            expo = probabilities(keys, wide, bound, chunk)
            grad_prob = t_dot(values, grads)
            grad_score = (expo * (grad_prob - ratios)).astype(jnp.bfloat16)
            part_kv[slot, rows_at(group, 64), cols] = (dot_t(wide, grad_score) * scale).astype(jnp.bfloat16)
            part_kv[slot, rows_at(group, 64, 384), cols] = dot_t(grads, expo.astype(jnp.bfloat16)).astype(jnp.bfloat16)
            return sum_query + dot(keys, grad_score)

        sum_query = lax.fori_loop(0, 4, one_chunk, jnp.zeros((64, 384), jnp.float32), unroll=True) * scale
        for i in range(3):
            total[pl.ds(pl.multiple_of(group * 192 + 64 * i, 64), 64), lanes] = sum_query[:, i * 128: i * 128 + 128]

    def unit(k):
        attend_back(k // 6, lax.rem(k, 6))
        for at, tokens in BACKWARD_PLAN[1]:
            pl.when(k == at)(lambda tokens=tokens: run(tokens))

    repeat(12, unit)
    run(BACKWARD_PLAN[2])

    def turn_back(ref, source, count):
        def one(h):
            rows = rows_at(h, 64)
            ref[rows, :] = rotate(source[rows, :], cosine[...], -sine[...]).astype(ref.dtype)

        repeat(count, one)

    turn_back(turned, total, 18)
    turn_back(own_kv, own_kv, 6)
    total[...] = jnp.zeros_like(total)

    def last_block(b):
        rows = jnp.concatenate(
            [
                turned[rows_at(b, 144), :],
                own_kv[rows_at(b, 48), :].astype(jnp.bfloat16),
                own_kv[rows_at(b, 48, 384), :].astype(jnp.bfloat16),
                jnp.zeros((16, 256), jnp.bfloat16),
            ],
            axis=0,
        )
        total[...] += dot(weights[:, lanes_at(b, 384)][:, :256], rows)
        slot = lax.rem(b, 2)
        out = pltpu.make_async_copy(left.at[slot], grad_cat.at[:, lanes_at(b, 384)], store.at[slot])
        pl.when(b >= 2)(lambda: out.wait())
        grad = dot_t(attn_in_t[...], rows)
        out_grad = dot_t(attn[...].astype(jnp.bfloat16), out_rows(b))
        left[slot, :, 0:128] = grad[:, :128].astype(jnp.bfloat16)
        left[slot, :, 128:256] = (grad[:, 128:] + out_grad[:, :128]).astype(jnp.bfloat16)
        left[slot, :, 256:384] = out_grad[:, 128:].astype(jnp.bfloat16)
        out.start()
        for at, tokens in BACKWARD_PLAN[3]:
            pl.when(b == at)(lambda tokens=tokens: run(tokens))

    repeat(8, last_block)
    for slot in range(2):
        pltpu.make_async_copy(left.at[slot], grad_cat.at[:, pl.ds((6 + slot) * 384, 384)], store.at[slot]).wait()
    for dy in (1, 0):
        for fold in cat_folds:
            fold.begin(dy)
    run(BACKWARD_PLAN[4])
    grad_tokens[...] = total[...].T
    note[...] = small[...]

    def finish_rows(k):
        rows = rows_at(k, 32)
        grad = grad_tokens[rows, :]
        normed = x[rows, :].astype(jnp.float32)
        scale_in = lax.rsqrt(jnp.mean(normed * normed, axis=-1, keepdims=True) + norm_eps)
        normed = normed * scale_in
        note[0:1, :] += jnp.sum(grad * normed, axis=0, keepdims=True)
        grad = grad * small[3:4, :]
        inner = grad - normed * jnp.mean(grad * normed, axis=-1, keepdims=True)
        grad_tokens[rows, :] = grad_hidden[rows, :] + scale_in * inner

    repeat(8, finish_rows)
    run(BACKWARD_PLAN[5])
    for k in range(1, 8):
        tiles.along_seq(k).start()
    run(BACKWARD_PLAN[6])
    tiles.wait_seq()
    seq_in[s] = note[...]
    along = seq_in[0]
    for k in range(1, 8):
        along = along + seq_in[k]
    row_sum[...] = along
    run(BACKWARD_PLAN[7])
    for k in range(1, 4):
        tiles.along_dp(k).start()
    run(BACKWARD_PLAN[8])
    tiles.wait_dp()
    dp_in[d] = row_sum[...]
    totals[...] = dp_in[0] + dp_in[1] + dp_in[2] + dp_in[3]
    turned_cat = own_cat[...].T
    row = 0
    for ref in (own_query_t, own_key_t, own_value_t, own_out_t):
        ref[...] = turned_cat[row: row + ref.shape[0], 0:288]
        row += ref.shape[0]
    for fold in folds + kv_folds + cat_folds:
        fold.finish()
    for k in range(1, 8):
        tiles.along_seq(k).wait_send()
    for k in range(1, 4):
        tiles.along_dp(k).wait_send()


def backward_call(
    lengths, grad_hidden, cosine, sine, small, x, attn_in_t, wcat, keys_values, query, attn, denom,
    grad_gate, grad_up, grad_down
):
    vmem, anywhere = pl.BlockSpec(memory_space=pltpu.VMEM), pl.BlockSpec(memory_space=pl.ANY)
    jobs = len(KV_JOBS)
    most = max(fold_slots(order)[1] for _, _, order in FOLD_KV)
    outs = ((288, 384), (288, 384), (144, 768), (144, 288), (48, 288), (48, 288), (144, 288), (256, 1152), (8, 1152))
    return pl.pallas_call(
        backward_body,
        out_shape=[jax.ShapeDtypeStruct(shape, jnp.float32) for shape in outs]
        + [jax.ShapeDtypeStruct((1152, 3072), jnp.bfloat16)],
        in_specs=[pl.BlockSpec(memory_space=pltpu.SMEM)] + [vmem] * 4 + [anywhere] * 10,
        out_specs=[vmem] * len(outs) + [anywhere],
        scratch_shapes=[
            pltpu.VMEM((256, 1152), jnp.bfloat16),
            pltpu.VMEM((1152, 256), jnp.bfloat16),
            pltpu.VMEM((1152, 256), jnp.bfloat16),
            pltpu.VMEM((1152, 256), jnp.float32),
            pltpu.VMEM((6, 8, 256), jnp.float32),
            pltpu.VMEM((384, 384), jnp.float32),
            pltpu.VMEM((1152, 3072), jnp.bfloat16),
            pltpu.VMEM((2, 768, 1024), jnp.bfloat16),
            pltpu.VMEM((2, 768, 1024), jnp.bfloat16),
            pltpu.VMEM((1152, 256), jnp.bfloat16),
            pltpu.VMEM((1152, 256), jnp.float32),
            pltpu.VMEM((768, 256), jnp.float32),
            pltpu.VMEM((2, 1152, 384), jnp.bfloat16),
            pltpu.VMEM((1152, 256), jnp.bfloat16),
            pltpu.VMEM((8, 1152), jnp.float32),
            pltpu.VMEM((8, 8, 1152), jnp.float32),
            pltpu.VMEM((4, 8, 1152), jnp.float32),
            pltpu.VMEM((8, 1152), jnp.float32),
            pltpu.SemaphoreType.DMA((14,)),
            pltpu.SemaphoreType.DMA((2,)),
            pltpu.SemaphoreType.DMA((jobs,)),
            pltpu.SemaphoreType.DMA((jobs, most)),
        ]
        + [pltpu.VMEM((fold_slots(order)[1], 256, 128), jnp.bfloat16) for _, _, order in FOLD_KV]
        + NOTE_SEMS
        + fold_scratch(FOLD_FFN, False)
        + fold_scratch(FOLD_CAT, True),
        compiler_params=pltpu.CompilerParams(
            collective_id=4, has_side_effects=True, vmem_limit_bytes=VMEM_MOST
        ),
        name="attention_backward",
    )(
        lengths, grad_hidden, cosine, sine, small, x, attn_in_t, wcat, keys_values, query, attn, denom,
        grad_gate, grad_up, grad_down,
    )


def hand_over_body(count, *refs):
    sources, (totals, notes) = refs[:count], refs[count: count + 2]
    targets, (loss, gain_a, gain_f) = refs[count + 2: 2 * count + 2], refs[2 * count + 2: 2 * count + 5]
    held, (into, out) = refs[2 * count + 5: 3 * count + 5], refs[-2:]
    reads = [pltpu.make_async_copy(source, there, into.at[k]) for k, (source, there) in enumerate(zip(sources, held))]
    copies = [pltpu.make_async_copy(there, target, out.at[k]) for k, (there, target) in enumerate(zip(held, targets))]
    for read in reads:
        read.start()
    loss[...] = totals[2:3, 0:1] / notes[10:11, 0:1]
    s = lax.axis_index("seq")
    for k in range(8):
        def own(k=k):
            gain_a[...] = totals[0:1, 144 * k: 144 * k + 144]
            gain_f[...] = totals[1:2, 144 * k: 144 * k + 144]

        pl.when(s == k)(own)
    for read, copy in zip(reads, copies):
        read.wait()
        copy.start()
    for copy in copies:
        copy.wait()


def hand_over(results, totals, notes):
    vmem, anywhere = pl.BlockSpec(memory_space=pltpu.VMEM), pl.BlockSpec(memory_space=pl.ANY)
    count = len(results)
    return pl.pallas_call(
        functools.partial(hand_over_body, count),
        out_shape=[jax.ShapeDtypeStruct(r.shape, r.dtype) for r in results]
        + [jax.ShapeDtypeStruct(shape, jnp.float32) for shape in ((1, 1), (1, 144), (1, 144))],
        in_specs=[anywhere] * count + [vmem] * 2,
        out_specs=[anywhere] * count + [vmem] * 3,
        scratch_shapes=[pltpu.VMEM(r.shape, r.dtype) for r in results]
        + [pltpu.SemaphoreType.DMA((count,)), pltpu.SemaphoreType.DMA((count,))],
        compiler_params=pltpu.CompilerParams(vmem_limit_bytes=VMEM_MOST),
        name="hand_over",
    )(*results, totals, notes)


def per_device_fast(
    tokens, teacher, lengths, w_query, key_weight, value_weight, w_out, w_gate, w_up, w_down, gain_attn, gain_ffn
):
    slots, part, width = tokens.shape
    rows = slots * part
    total_tokens = slots * lax.axis_size("dp") * part * lax.axis_size("seq")
    positions = lax.axis_index("seq") * part + jnp.arange(part, dtype=jnp.int32)
    cosine, sine = rope_tables(positions, HEAD_DIMENSION)
    cosine_t = jnp.concatenate([cosine.T] * slots, axis=1)
    sine_t = jnp.concatenate([sine.T] * slots, axis=1)
    x_b = tokens.reshape(rows, width)
    gate_w, up_w, down_t, cat, attn_in_t, query, keys_values, attn, denom, notes, hidden = forward_call(
        lengths, (w_query.T, key_weight.T, value_weight.T, w_out.T),
        gain_attn, gain_ffn, x_b, cosine_t, sine_t,
        w_gate, w_up, w_down.T,
    )
    output, grad_hidden, small, gate_sums, up_sums, down_sums = ffn_call(
        float(total_tokens), lengths, hidden, teacher.reshape(rows, width), notes, gate_w, up_w, down_t
    )
    *results, totals, _ = backward_call(
        lengths, grad_hidden, cosine_t, sine_t, small, x_b, attn_in_t, cat, keys_values, query, attn, denom,
        gate_sums, up_sums, down_sums,
    )
    (
        output, own_gate, own_up, own_down_t, own_query_t, own_key_t, own_value_t, own_out_t, grad_tokens,
        loss, own_gain_a, own_gain_f,
    ) = hand_over([output] + results, totals, notes)
    return (
        output.reshape(tokens.shape),
        loss.reshape(()),
        grad_tokens.reshape(tokens.shape),
        own_query_t.T,
        own_key_t.T,
        own_value_t.T,
        own_out_t.T,
        own_gate,
        own_up,
        own_down_t.T,
        own_gain_a.reshape(-1),
        own_gain_f.reshape(-1),
    )


def solution(mesh):
    placed = (
        P("dp", "seq", None),
        P("dp", "seq", None),
        P("dp"),
        P("dp", "seq"),
        P("dp", "seq"),
        P("dp", "seq"),
        P("dp", "seq"),
        P("dp", "seq"),
        P("dp", "seq"),
        P("dp", "seq"),
        P("seq"),
        P("seq"),
    )
    fits = mesh.shape["dp"] == 4 and mesh.shape["seq"] == 8
    return jax.shard_map(
        per_device_fast if fits else per_device,
        mesh=mesh,
        in_specs=placed,
        out_specs=(
            P("dp", "seq", None),
            P(),
            P("dp", "seq", None),
            P("dp", "seq"),
            P("dp", "seq"),
            P("dp", "seq"),
            P("dp", "seq"),
            P("dp", "seq"),
            P("dp", "seq"),
            P("dp", "seq"),
            P("seq"),
            P("seq"),
        ),
        check_vma=False,
    )
```

```python
import functools
import math

import jax
import jax.numpy as jnp
from jax import lax
from jax.experimental import pallas as pl
from jax.experimental.pallas import tpu as pltpu
from jax.sharding import PartitionSpec as P

QUERY_HEADS = 18
KEY_VALUE_HEADS = 6
HEAD_DIMENSION = 64


norm_eps = 1e-05
rope_base = 10000.0


def rope_tables(positions, head_width):
    half_width = head_width // 2
    exponents = jnp.arange(half_width, dtype=jnp.float32) * (2.0 / head_width)
    angles = positions.astype(jnp.float32)[:, None] * (rope_base ** (-exponents))[None, :]
    return (jnp.cos(angles), jnp.sin(angles))


def apply_rotary(value_rows, cosine_table, sine_table):
    half_width = value_rows.shape[-1] // 2
    front_half = value_rows[..., :half_width]
    back_half = value_rows[..., half_width:]
    cos_wide = cosine_table[:, None, :]
    sin_wide = sine_table[:, None, :]
    return jnp.concatenate(
        [
            front_half * cos_wide - back_half * sin_wide,
            front_half * sin_wide + back_half * cos_wide,
        ],
        axis=-1,
    )


def allowed_mask(query_pos, key_pos, live_len):
    causal = key_pos[None, :] <= query_pos[:, None]
    present = key_pos[None, :] < live_len[:, None]
    return (causal[None, :, :] & present[:, None, :])[:, None, None, :, :]


def over_blocks(piece_len, unit_len, step_fn, running):
    block_length = math.gcd(piece_len, unit_len * max(1, 512 // unit_len))
    number_of_blocks = piece_len // block_length

    def loop_step(block_number, state):
        return step_fn(state, block_number * block_length, block_length)

    return lax.fori_loop(0, number_of_blocks, loop_step, running)


def collect(shards):
    wide = (
        lax.all_gather(shards[0], "seq", axis=1, tiled=True),
        lax.all_gather(shards[1], "seq", axis=1, tiled=True),
        lax.all_gather(shards[2], "seq", axis=1, tiled=True),
        lax.all_gather(shards[3], "seq", axis=1, tiled=True),
        lax.all_gather(shards[4], "seq", axis=1, tiled=True),
        lax.all_gather(shards[5], "seq", axis=1, tiled=True),
        lax.all_gather(shards[6], "seq", axis=1, tiled=True),
        lax.all_gather(shards[7], "seq", axis=0, tiled=True),
        lax.all_gather(shards[8], "seq", axis=0, tiled=True),
    )
    whole = (
        lax.all_gather(wide[0], "dp", axis=0, tiled=True),
        lax.all_gather(wide[1], "dp", axis=0, tiled=True),
        lax.all_gather(wide[2], "dp", axis=0, tiled=True),
        lax.all_gather(wide[3], "dp", axis=0, tiled=True),
        lax.all_gather(wide[4], "dp", axis=0, tiled=True),
        lax.all_gather(wide[5], "dp", axis=0, tiled=True),
        lax.all_gather(wide[6], "dp", axis=0, tiled=True),
    )
    return tuple(whole) + (wide[7], wide[8])


def reduce_grads(grad_sums):
    summed = (
        lax.psum_scatter(grad_sums[0], "seq", scatter_dimension=1, tiled=True),
        lax.psum_scatter(grad_sums[1], "seq", scatter_dimension=1, tiled=True),
        lax.psum_scatter(grad_sums[2], "seq", scatter_dimension=1, tiled=True),
        lax.psum_scatter(grad_sums[3], "seq", scatter_dimension=1, tiled=True),
        lax.psum_scatter(grad_sums[4], "seq", scatter_dimension=1, tiled=True),
        lax.psum_scatter(grad_sums[5], "seq", scatter_dimension=1, tiled=True),
        lax.psum_scatter(grad_sums[6], "seq", scatter_dimension=1, tiled=True),
        lax.psum_scatter(grad_sums[7], "seq", scatter_dimension=0, tiled=True),
        lax.psum_scatter(grad_sums[8], "seq", scatter_dimension=0, tiled=True),
    )
    owned = (
        lax.psum_scatter(summed[0], "dp", scatter_dimension=0, tiled=True),
        lax.psum_scatter(summed[1], "dp", scatter_dimension=0, tiled=True),
        lax.psum_scatter(summed[2], "dp", scatter_dimension=0, tiled=True),
        lax.psum_scatter(summed[3], "dp", scatter_dimension=0, tiled=True),
        lax.psum_scatter(summed[4], "dp", scatter_dimension=0, tiled=True),
        lax.psum_scatter(summed[5], "dp", scatter_dimension=0, tiled=True),
        lax.psum_scatter(summed[6], "dp", scatter_dimension=0, tiled=True),
    )
    return (tuple(owned), summed[7], summed[8])


def forward_slot(weights, tok_part, live_len, query_pos, cosine_table, sine_table):
    (
        full_query,
        full_key,
        full_value,
        full_out,
        full_gate,
        full_up,
        full_down,
        full_gain_attn,
        full_gain_ffn,
    ) = weights
    slot_position, stretched_length, model_width = tok_part.shape
    number_of_rows = slot_position * stretched_length
    query_group = QUERY_HEADS // KEY_VALUE_HEADS
    scale = HEAD_DIMENSION ** (-0.5)
    tok_float = tok_part.astype(jnp.float32).reshape(number_of_rows, model_width)
    inv_first = lax.rsqrt(jnp.mean(tok_float * tok_float, axis=-1, keepdims=True) + norm_eps)
    normed_first = tok_float * inv_first
    attention_input = (normed_first * full_gain_attn.astype(jnp.float32)).astype(jnp.bfloat16)
    unrotated_query = jnp.dot(
        attention_input, full_query, preferred_element_type=jnp.float32
    ).reshape(slot_position, stretched_length, QUERY_HEADS, HEAD_DIMENSION)
    unrotated_key = jnp.dot(attention_input, full_key, preferred_element_type=jnp.float32).reshape(
        slot_position, stretched_length, KEY_VALUE_HEADS, HEAD_DIMENSION
    )
    value_block = (
        jnp.dot(attention_input, full_value, preferred_element_type=jnp.float32)
        .astype(jnp.bfloat16)
        .reshape(slot_position, stretched_length, KEY_VALUE_HEADS * HEAD_DIMENSION)
    )
    query_b = (
        apply_rotary(unrotated_query, cosine_table, sine_table)
        .astype(jnp.bfloat16)
        .reshape(slot_position, stretched_length, KEY_VALUE_HEADS, query_group, HEAD_DIMENSION)
    )
    key_block = (
        apply_rotary(unrotated_key, cosine_table, sine_table)
        .astype(jnp.bfloat16)
        .reshape(slot_position, stretched_length, KEY_VALUE_HEADS * HEAD_DIMENSION)
    )
    empty_denominator = jnp.zeros(
        (slot_position, KEY_VALUE_HEADS, query_group, stretched_length), jnp.float32
    )
    empty_numerator = jnp.zeros(
        (slot_position, KEY_VALUE_HEADS, query_group, stretched_length, HEAD_DIMENSION), jnp.float32
    )
    key_piece = lax.all_gather(key_block, "seq", axis=1, tiled=True)
    value_piece = lax.all_gather(value_block, "seq", axis=1, tiled=True)

    def one_block(partial_value, offset, block_length):
        denominator, numerator = partial_value
        key_blk = lax.dynamic_slice_in_dim(key_piece, offset, block_length, 1).reshape(
            slot_position, block_length, KEY_VALUE_HEADS, HEAD_DIMENSION
        )
        value_blk = lax.dynamic_slice_in_dim(value_piece, offset, block_length, 1).reshape(
            slot_position, block_length, KEY_VALUE_HEADS, HEAD_DIMENSION
        )
        allowed = allowed_mask(
            query_pos, offset + jnp.arange(block_length, dtype=jnp.int32), live_len
        )
        scores = (
            jnp.einsum("schgd,snhd->shgcn", query_b, key_blk, preferred_element_type=jnp.float32)
            * scale
        )
        exp_scores = jnp.where(allowed, jnp.exp(scores), 0.0)
        denominator = denominator + jnp.sum(exp_scores, axis=-1)
        numerator = numerator + jnp.einsum(
            "shgcn,snhd->shgcd",
            exp_scores.astype(jnp.bfloat16),
            value_blk,
            preferred_element_type=jnp.float32,
        )
        return (denominator, numerator)

    denominator, numerator = over_blocks(
        key_piece.shape[1], stretched_length, one_block, (empty_denominator, empty_numerator)
    )
    attn_float = jnp.transpose(numerator / denominator[..., None], (0, 3, 1, 2, 4)).reshape(
        number_of_rows, QUERY_HEADS * HEAD_DIMENSION
    )
    attn_b = attn_float.astype(jnp.bfloat16)
    hidden = tok_float + jnp.dot(attn_b, full_out, preferred_element_type=jnp.float32)
    inv_second = lax.rsqrt(jnp.mean(hidden * hidden, axis=-1, keepdims=True) + norm_eps)
    normed_second = hidden * inv_second
    ffn_in = (normed_second * full_gain_ffn.astype(jnp.float32)).astype(jnp.bfloat16)
    gate_proj = jnp.dot(ffn_in, full_gate, preferred_element_type=jnp.float32)
    up_proj = jnp.dot(ffn_in, full_up, preferred_element_type=jnp.float32)
    hid_b = (jax.nn.silu(gate_proj) * up_proj).astype(jnp.bfloat16)
    valid_rows = (query_pos[None, :] < live_len[:, None]).reshape(number_of_rows, 1)
    out_float = jnp.where(
        valid_rows, hidden + jnp.dot(hid_b, full_down, preferred_element_type=jnp.float32), 0.0
    )
    saved = (
        attention_input,
        inv_first,
        normed_first,
        query_b,
        key_block,
        value_block,
        attn_float,
        attn_b,
        denominator,
        normed_second,
        inv_second,
        ffn_in,
        gate_proj,
        up_proj,
        hid_b,
    )
    return (out_float, valid_rows, saved)


def backward_slot(weights, saved, cotangent, live_len, query_pos, cosine_table, sine_table):
    (
        full_query,
        full_key,
        full_value,
        full_out,
        full_gate,
        full_up,
        full_down,
        full_gain_attn,
        full_gain_ffn,
    ) = weights
    (
        attention_input,
        inv_first,
        normed_first,
        query_b,
        key_block,
        value_block,
        attn_float,
        attn_b,
        denominator,
        normed_second,
        inv_second,
        ffn_in,
        gate_proj,
        up_proj,
        hid_b,
    ) = saved
    slot_position = query_b.shape[0]
    stretched_length = query_b.shape[1]
    number_of_rows = slot_position * stretched_length
    query_group = QUERY_HEADS // KEY_VALUE_HEADS
    scale = HEAD_DIMENSION ** (-0.5)
    cot_b = cotangent.astype(jnp.bfloat16)
    grad_down = jnp.einsum("rf,rd->fd", hid_b, cot_b, preferred_element_type=jnp.float32)
    grad_hid = jnp.einsum("rd,fd->rf", cot_b, full_down, preferred_element_type=jnp.float32)
    sigmoid_gate = jax.nn.sigmoid(gate_proj)
    grad_gate_b = (
        grad_hid * up_proj * sigmoid_gate * (1.0 + gate_proj * (1.0 - sigmoid_gate))
    ).astype(jnp.bfloat16)
    grad_up_b = (grad_hid * gate_proj * sigmoid_gate).astype(jnp.bfloat16)
    grad_gate = jnp.einsum("rd,rf->df", ffn_in, grad_gate_b, preferred_element_type=jnp.float32)
    grad_up = jnp.einsum("rd,rf->df", ffn_in, grad_up_b, preferred_element_type=jnp.float32)
    grad_ffn_in = jnp.einsum(
        "rf,df->rd", grad_gate_b, full_gate, preferred_element_type=jnp.float32
    ) + jnp.einsum("rf,df->rd", grad_up_b, full_up, preferred_element_type=jnp.float32)
    grad_gain_ffn = jnp.sum(grad_ffn_in * normed_second, axis=0)
    grad_normed = grad_ffn_in * full_gain_ffn.astype(jnp.float32)
    grad_hidden = cotangent + inv_second * (
        grad_normed - normed_second * jnp.mean(grad_normed * normed_second, axis=-1, keepdims=True)
    )
    grad_proj_b = grad_hidden.astype(jnp.bfloat16)
    grad_out = jnp.einsum("rq,rd->qd", attn_b, grad_proj_b, preferred_element_type=jnp.float32)
    grad_attn_b = jnp.einsum(
        "rd,qd->rq", grad_proj_b, full_out, preferred_element_type=jnp.float32
    ).astype(jnp.bfloat16)
    den_rows = jnp.transpose(denominator, (0, 3, 1, 2)).reshape(number_of_rows, QUERY_HEADS)
    grad_heads_float = grad_attn_b.astype(jnp.float32).reshape(
        number_of_rows, QUERY_HEADS, HEAD_DIMENSION
    )
    softmax_ratio = (
        jnp.sum(
            grad_heads_float * attn_float.reshape(number_of_rows, QUERY_HEADS, HEAD_DIMENSION),
            axis=-1,
        )
        / den_rows
    ).reshape(slot_position, stretched_length, QUERY_HEADS)
    scaled_gradient = (
        (grad_heads_float / den_rows[..., None])
        .astype(jnp.bfloat16)
        .reshape(slot_position, stretched_length, QUERY_HEADS * HEAD_DIMENSION)
    )
    ratio_all = lax.all_gather(softmax_ratio, "seq", axis=1, tiled=True)
    head_gradient = scaled_gradient.reshape(
        slot_position, stretched_length, KEY_VALUE_HEADS, query_group, HEAD_DIMENSION
    )
    local_softmax_ratio = jnp.transpose(
        softmax_ratio.reshape(slot_position, stretched_length, KEY_VALUE_HEADS, query_group),
        (0, 2, 3, 1),
    )[..., None]
    empty_query = jnp.zeros(
        (slot_position, KEY_VALUE_HEADS, query_group, stretched_length, HEAD_DIMENSION), jnp.float32
    )
    key_piece = lax.all_gather(key_block, "seq", axis=1, tiled=True)
    value_piece = lax.all_gather(value_block, "seq", axis=1, tiled=True)

    def one_block(partial_value, offset, block_length):
        key_blk = lax.dynamic_slice_in_dim(key_piece, offset, block_length, 1).reshape(
            slot_position, block_length, KEY_VALUE_HEADS, HEAD_DIMENSION
        )
        value_blk = lax.dynamic_slice_in_dim(value_piece, offset, block_length, 1).reshape(
            slot_position, block_length, KEY_VALUE_HEADS, HEAD_DIMENSION
        )
        allowed = allowed_mask(
            query_pos, offset + jnp.arange(block_length, dtype=jnp.int32), live_len
        )
        scores = (
            jnp.einsum("schgd,snhd->shgcn", query_b, key_blk, preferred_element_type=jnp.float32)
            * scale
        )
        exp_scores = jnp.where(allowed, jnp.exp(scores), 0.0)
        grad_prob = jnp.einsum(
            "schgd,snhd->shgcn", head_gradient, value_blk, preferred_element_type=jnp.float32
        )
        grad_score = (exp_scores * (grad_prob - local_softmax_ratio)).astype(jnp.bfloat16)
        return (
            partial_value
            + jnp.einsum(
                "shgcn,snhd->shgcd", grad_score, key_blk, preferred_element_type=jnp.float32
            )
            * scale
        )

    grad_query = over_blocks(key_piece.shape[1], stretched_length, one_block, empty_query)
    query_flat = query_b.reshape(slot_position, stretched_length, QUERY_HEADS * HEAD_DIMENSION)
    per_head_keys = key_block.reshape(
        slot_position, stretched_length, KEY_VALUE_HEADS, HEAD_DIMENSION
    )
    per_head_values = value_block.reshape(
        slot_position, stretched_length, KEY_VALUE_HEADS, HEAD_DIMENSION
    )
    empty_key_value = jnp.zeros(
        (slot_position, KEY_VALUE_HEADS, stretched_length, HEAD_DIMENSION), jnp.float32
    )
    query_piece = lax.all_gather(query_flat, "seq", axis=1, tiled=True)
    grad_piece = lax.all_gather(scaled_gradient, "seq", axis=1, tiled=True)

    def one_block(partial_value, offset, block_length):
        grad_key, value_gradient = partial_value
        query_blk = lax.dynamic_slice_in_dim(query_piece, offset, block_length, 1).reshape(
            slot_position, block_length, KEY_VALUE_HEADS, query_group, HEAD_DIMENSION
        )
        grad_blk = lax.dynamic_slice_in_dim(grad_piece, offset, block_length, 1).reshape(
            slot_position, block_length, KEY_VALUE_HEADS, query_group, HEAD_DIMENSION
        )
        ratio_blk = lax.dynamic_slice_in_dim(ratio_all, offset, block_length, 1).reshape(
            slot_position, block_length, KEY_VALUE_HEADS, query_group
        )
        ratio_blk = jnp.transpose(ratio_blk, (0, 2, 3, 1))[..., None]
        remote_pos = offset + jnp.arange(block_length, dtype=jnp.int32)
        allowed = allowed_mask(remote_pos, query_pos, live_len)
        scores = (
            jnp.einsum(
                "snhgd,schd->shgnc", query_blk, per_head_keys, preferred_element_type=jnp.float32
            )
            * scale
        )
        exp_scores = jnp.where(allowed, jnp.exp(scores), 0.0)
        value_gradient = value_gradient + jnp.einsum(
            "shgnc,snhgd->shcd",
            exp_scores.astype(jnp.bfloat16),
            grad_blk,
            preferred_element_type=jnp.float32,
        )
        grad_prob = jnp.einsum(
            "snhgd,schd->shgnc", grad_blk, per_head_values, preferred_element_type=jnp.float32
        )
        grad_score = (exp_scores * (grad_prob - ratio_blk)).astype(jnp.bfloat16)
        grad_key = (
            grad_key
            + jnp.einsum(
                "shgnc,snhgd->shcd", grad_score, query_blk, preferred_element_type=jnp.float32
            )
            * scale
        )
        return (grad_key, value_gradient)

    grad_key, value_gradient = over_blocks(
        query_piece.shape[1], stretched_length, one_block, (empty_key_value, empty_key_value)
    )
    grad_query = jnp.transpose(grad_query, (0, 3, 1, 2, 4)).reshape(
        slot_position, stretched_length, QUERY_HEADS, HEAD_DIMENSION
    )
    grad_query_b = (
        apply_rotary(grad_query, cosine_table, -sine_table)
        .astype(jnp.bfloat16)
        .reshape(number_of_rows, QUERY_HEADS * HEAD_DIMENSION)
    )
    grad_key_b = (
        apply_rotary(jnp.transpose(grad_key, (0, 2, 1, 3)), cosine_table, -sine_table)
        .astype(jnp.bfloat16)
        .reshape(number_of_rows, KEY_VALUE_HEADS * HEAD_DIMENSION)
    )
    grad_value_b = (
        jnp.transpose(value_gradient, (0, 2, 1, 3))
        .astype(jnp.bfloat16)
        .reshape(number_of_rows, KEY_VALUE_HEADS * HEAD_DIMENSION)
    )
    grad_wq = jnp.einsum(
        "rd,rq->dq", attention_input, grad_query_b, preferred_element_type=jnp.float32
    )
    grad_wk = jnp.einsum(
        "rd,rq->dq", attention_input, grad_key_b, preferred_element_type=jnp.float32
    )
    grad_wv = jnp.einsum(
        "rd,rq->dq", attention_input, grad_value_b, preferred_element_type=jnp.float32
    )
    grad_attn_in = jnp.einsum(
        "rq,dq->rd", grad_query_b, full_query, preferred_element_type=jnp.float32
    )
    grad_attn_in = grad_attn_in + jnp.einsum(
        "rq,dq->rd", grad_key_b, full_key, preferred_element_type=jnp.float32
    )
    grad_attn_in = grad_attn_in + jnp.einsum(
        "rq,dq->rd", grad_value_b, full_value, preferred_element_type=jnp.float32
    )
    grad_gain_attn = jnp.sum(grad_attn_in * normed_first, axis=0)
    grad_first = grad_attn_in * full_gain_attn.astype(jnp.float32)
    grad_tokens = grad_hidden + inv_first * (
        grad_first - normed_first * jnp.mean(grad_first * normed_first, axis=-1, keepdims=True)
    )
    return (
        (
            grad_wq,
            grad_wk,
            grad_wv,
            grad_out,
            grad_gate,
            grad_up,
            grad_down,
            grad_gain_attn,
            grad_gain_ffn,
        ),
        grad_tokens,
    )


def per_device(
    tokens,
    teacher,
    lengths,
    w_query,
    key_weight,
    value_weight,
    w_out,
    w_gate,
    w_up,
    w_down,
    gain_attn,
    gain_ffn,
):
    shards = (w_query, key_weight, value_weight, w_out, w_gate, w_up, w_down, gain_attn, gain_ffn)
    slot_count, stretched_length, model_width = tokens.shape
    total_tokens = slot_count * lax.axis_size("dp") * stretched_length * lax.axis_size("seq")
    query_pos = lax.axis_index("seq") * stretched_length + jnp.arange(
        stretched_length, dtype=jnp.int32
    )
    cosine_table, sine_table = rope_tables(query_pos, HEAD_DIMENSION)
    out_rows = []
    stored = []
    differences = []
    squares_local = jnp.zeros((), jnp.float32)
    count_local = jnp.zeros((), jnp.float32)
    for micro in range(slot_count):
        weights = collect(shards)
        live_len = lengths[micro : micro + 1]
        out_float, valid_rows, saved = forward_slot(
            weights, tokens[micro : micro + 1], live_len, query_pos, cosine_table, sine_table
        )
        teach_float = teacher[micro].astype(jnp.float32)
        difference = jnp.where(valid_rows, out_float - teach_float, 0.0)
        squares_local = squares_local + jnp.sum(difference * difference)
        count_local = count_local + jnp.sum(valid_rows.astype(jnp.float32))
        out_rows.append(out_float.astype(jnp.bfloat16).reshape(1, stretched_length, model_width))
        stored.append(saved)
        differences.append(difference)
    loss_sum, count_sum = lax.psum((squares_local, count_local), ("dp", "seq"))
    loss = loss_sum / count_sum
    factor = total_tokens / count_sum
    grad_sums = None
    token_grads = []
    for micro in range(slot_count):
        weights = collect(shards)
        grads, grad_tokens = backward_slot(
            weights,
            stored[micro],
            factor * differences[micro],
            lengths[micro : micro + 1],
            query_pos,
            cosine_table,
            sine_table,
        )
        grad_sums = grads if grad_sums is None else jax.tree.map(jnp.add, grad_sums, grads)
        token_grads.append(grad_tokens.reshape(1, stretched_length, model_width))
    owned, gain_part_attn, gain_part_ffn = reduce_grads(grad_sums)
    gain_totals = lax.psum((gain_part_attn, gain_part_ffn), "dp")
    output = jnp.concatenate(out_rows, axis=0)
    tokens_grad = jnp.concatenate(token_grads, axis=0)
    return (
        output,
        loss,
        tokens_grad,
        owned[0],
        owned[1],
        owned[2],
        owned[3],
        owned[4],
        owned[5],
        owned[6],
        gain_totals[0],
        gain_totals[1],
    )


MESH_ID = pl.DeviceIdType.MESH
VMEM_MOST = 64 * 1024 * 1024 - 128 * 1024


class Place(tuple):
    def with_line(self):
        z = self[2]
        self.line = (0,) + tuple(pick(z, v) for v in ((1, -1, -1, -1), (2, 1, 1, -2), (3, 2, -2, -3)))
        self.sign = (0,) + tuple(jnp.where(offset > 0, 1, -1) for offset in self.line[1:])
        return self


def position():
    row = lax.axis_index("dp")
    column = lax.axis_index("seq")
    return Place((lax.rem(column, 2), row // 2, column // 2, lax.rem(row, 2))).with_line()


def mesh_place(x, y, z, c):
    return (2 * y + c, 2 * z + x)


def step_to(place, axis, sign=1):
    x, y, z, c = place
    if axis == "x":
        return (1 - x, y, z, c)
    if axis == "y":
        return (x, 1 - y, z, c)
    if axis == "z":
        return (x, y, z + sign, c)
    return (x, y, z, 1 - c)


def pick(z, values):
    return sum(jnp.where(z == i, v, 0) for i, v in enumerate(values) if v)


def shifted(place, rel):
    x, y, z, c = place
    dx, dy, rank = rel
    return ((1 - x) if dx else x, (1 - y) if dy else y, z + place.line[rank], c)


def on_line(z):
    return jnp.logical_and(z >= 0, z < 4)


def greet(place, lines):
    x, y, z, c = place
    d, s = mesh_place(*place)
    barrier = pltpu.get_barrier_semaphore()

    def signal(who):
        pl.semaphore_signal(barrier, inc=1, device_id=who, device_id_type=MESH_ID)

    if lines:
        for k in range(1, 8):
            signal((d, lax.rem(s + k, 8)))
        for k in range(1, 4):
            signal((lax.rem(d + k, 4), s))
        pl.semaphore_wait(barrier, 10)
        return
    for axis in "xyc":
        signal(mesh_place(*step_to(place, axis)))
    pl.when(z < 3)(lambda: signal(mesh_place(x, y, z + 1, c)))
    pl.when(z > 0)(lambda: signal(mesh_place(x, y, z - 1, c)))
    pl.semaphore_wait(barrier, 3 + jnp.where(z > 0, 1, 0) + jnp.where(z < 3, 1, 0))


def wait_bytes(region, sem):
    pltpu.make_async_copy(region, region, sem).wait()


def spread_order(order):
    held = [((0, 0, 0), -1)]
    for level, axis in enumerate(order):
        new = []
        if axis == "z":
            new = [((rel[0], rel[1], rank), level) for rank in (1, 2, 3) for rel, _ in held]
        else:
            new = [((1, rel[1], rel[2]) if axis == "x" else (rel[0], 1, rel[2]), level) for rel, _ in held]
        held = held + new
    return held


class Spread:
    def __init__(self, place, order, own, spot, sems, job, pair=None, amount=None):
        self.place, self.order, self.own, self.spot = place, order, own, spot
        self.recv, self.send, self.recv_core, self.send_core = sems
        self.job, self.pair, self.amount = job, pair, amount
        self.pieces = spread_order(order)

    def number(self, who):
        x, y, z, _ = who
        return z * 4 + y * 2 + x

    def go(self, rel, level, target):
        who = shifted(self.place, rel)
        pltpu.make_async_remote_copy(
            src_ref=self.own if level < 0 else self.spot(who),
            dst_ref=self.spot(who),
            send_sem=self.send.at[self.job],
            recv_sem=self.recv.at[self.job, self.number(who)],
            device_id=mesh_place(*target),
            device_id_type=MESH_ID,
        ).start()

    def to_core(self, rel):
        who = shifted(self.place, rel)
        pltpu.make_async_remote_copy(
            src_ref=self.pair(who),
            dst_ref=self.pair(who),
            send_sem=self.send_core.at[self.job],
            recv_sem=self.recv_core.at[self.job],
            device_id=mesh_place(*step_to(self.place, "c")),
            device_id_type=MESH_ID,
        ).start()

    def steps(self):
        out = []
        arrived = set()
        z = self.place[2]
        for rel, level in self.pieces:

            def run(rel=rel, level=level):
                arrived.add(rel)
                who = shifted(self.place, rel)
                if level >= 0:
                    there = self.spot(who)
                    pltpu.make_async_copy(there, there, self.recv.at[self.job, self.number(who)]).wait()
                if level >= 0 and self.order[level] == "z":
                    on = z - self.place.sign[rel[2]]
                    pl.when(on_line(on))(lambda: self.go(rel, level, (self.place[0], self.place[1], on, self.place[3])))
                for axis in self.order[level + 1:]:
                    if axis == "z":
                        pl.when(z < 3)(lambda: self.go(rel, level, step_to(self.place, "z", 1)))
                        pl.when(z > 0)(lambda: self.go(rel, level, step_to(self.place, "z", -1)))
                    else:
                        self.go(rel, level, step_to(self.place, axis))
                if self.pair is not None and (1 - rel[0], rel[1], rel[2]) in arrived:
                    self.to_core(rel)

            out.append(run)
        return out

    def sent(self):
        total = [0, 0]
        for i, z in enumerate((0, 1)):
            for rel, level in self.pieces:
                if level >= 0 and self.order[level] == "z":
                    offset = (0, ((1, -1)[z]), ((2, 1)[z]), ((3, 2)[z]))[rel[2]]
                    on = z - (1 if offset > 0 else -1)
                    total[i] += 0 <= on < 4
                for axis in self.order[level + 1:]:
                    total[i] += (1, 2)[z] if axis == "z" else 1
        return total

    def wait_core(self):
        wait_bytes(self.amount(16), self.recv_core.at[self.job])

    def finish(self):
        ends, inner = self.sent()
        z = self.place[2]
        at_end = jnp.logical_or(z == 0, z == 3)
        pl.when(at_end)(lambda: wait_bytes(self.amount(ends), self.send.at[self.job]))
        pl.when(jnp.logical_not(at_end))(lambda: wait_bytes(self.amount(inner), self.send.at[self.job]))
        if self.pair is not None:
            wait_bytes(self.amount(16), self.send_core.at[self.job])


def fold_pieces(order):
    out = []
    for dx in (0, 1):
        for dy in (0, 1) if "y" in order else (0,):
            for rank in (0, 1, 2, 3):
                differs = {"x": dx, "y": dy, "z": rank}
                stage = next((i for i, axis in enumerate(order) if differs[axis]), len(order))
                out.append(((dx, dy, rank), stage))
    return sorted(out, key=lambda item: (item[1], -item[0][2], -item[0][0] - item[0][1]))


def fold_slots(order):
    base, starts = 0, []
    for level, axis in enumerate(order):
        starts.append(base)
        after = order[level + 1:]
        wide = (4 if "z" in after else 1) * (2 if "x" in after else 1) * (2 if "y" in after else 1)
        base += wide * 5 if axis == "z" else wide
    return starts, base


class Fold:
    def __init__(self, place, order, mine, arrived, sems, job, out, amount, ready=None):
        self.place, self.order, self.mine, self.arrived = place, order, mine, arrived
        self.send, self.recv = sems
        self.job, self.out, self.amount, self.ready = job, out, amount, ready
        self.pieces = fold_pieces(order)
        self.base, self.slots = fold_slots(order)

    def slot(self, level, rel, last):
        index = 0
        at_z = self.place[2] + self.place.line[rel[2]]
        for other in self.order[level + 1:]:
            size = 4 if other == "z" else 2
            index = index * size + (at_z if other == "z" else (rel[0] if other == "x" else rel[1]))
        if self.order[level] == "z":
            index = index * 5 + (4 if last is True else (at_z if last is False else jnp.where(last, 4, at_z)))
        return self.base[level] + index

    def take(self, mine, slot):
        there = self.arrived.at[slot]
        pltpu.make_async_copy(there, there, self.recv.at[self.job, slot]).wait()
        mine[...] = mine[...] + self.arrived[slot]

    def steps(self):
        out = []
        present = set()
        z = self.place[2]
        for rel, stage in self.pieces:

            def run(rel=rel, stage=stage):
                if self.ready is not None and rel[1] not in present:
                    present.add(rel[1])
                    self.ready(rel[1])
                mine = self.mine(shifted(self.place, rel))
                offset, sign = self.place.line[rel[2]], self.place.sign[rel[2]]
                for level in range(min(stage + 1, len(self.order))):
                    if self.order[level] == "z":
                        if level < stage:
                            pl.when(z > 0)(lambda: self.take(mine, self.slot(level, rel, False)))
                            pl.when(z < 3)(lambda: self.take(mine, self.slot(level, rel, True)))
                        else:
                            behind = z - sign
                            pl.when(on_line(behind))(lambda: self.take(mine, self.slot(level, rel, False)))
                    elif level < stage:
                        self.take(mine, self.slot(level, rel, False))
                if stage == len(self.order):
                    self.out(mine[...].astype(jnp.float32))
                    return
                axis = self.order[stage]
                if axis == "z":
                    target = (self.place[0], self.place[1], z + sign, self.place[3])
                else:
                    target = step_to(self.place, axis)
                slot = self.slot(stage, rel, offset == -1 if axis == "z" else False)
                pltpu.make_async_remote_copy(
                    src_ref=mine,
                    dst_ref=self.arrived.at[slot],
                    send_sem=self.send.at[self.job],
                    recv_sem=self.recv.at[self.job, slot],
                    device_id=mesh_place(*target),
                    device_id_type=MESH_ID,
                ).start()

            out.append(run)
        return out

    def finish(self):
        wait_bytes(self.amount(len(self.pieces) - 1), self.send.at[self.job])


CAT_JOBS = (("cat", 0, 96, "xzy"), ("cat", 96, 96, "yzx"), ("cat", 192, 96, "zxy"))
FFN_JOBS = (
    ("gate", 0, 144, "xzy"), ("up", 0, 96, "yzx"), ("down", 0, 384, "zxy"),
    ("gate", 144, 144, "xzy"), ("up", 96, 96, "yzx"), ("down", 384, 384, "zxy"), ("up", 192, 96, "zyx"),
)
KV_JOBS = tuple((slot, 256 * third, "zx") for slot in (0, 1) for third in (0, 1, 2))
FOLD_FFN = tuple(job[:3] + (job[3][::-1],) for job in FFN_JOBS)
FOLD_CAT = tuple(job[:3] + (job[3][::-1],) for job in CAT_JOBS)
FOLD_KV = tuple((slot, row, order[::-1]) for slot, row, order in KV_JOBS)
FFN_NAMES = ("gate", "up", "down")


def job_shape(job):
    return (144, job[2]) if job[0] == "down" else (job[2], 384)


def piece_of(ref, job, paired=False):
    name, first, count, _ = job
    double = 2 if paired else 1

    def spot(who):
        x, y, z, c = who
        d, s = mesh_place(0 if paired else x, y, z, c)
        if name == "down":
            return ref.at[
                pl.ds(pl.multiple_of(s * 144, 16), 144 * double), pl.ds(pl.multiple_of(d * 768 + first, 128), count)
            ]
        return ref.at[
            pl.ds(pl.multiple_of(d * 288 + first, 8), count), pl.ds(pl.multiple_of(s * 384, 128), 384 * double)
        ]

    return spot


def region(ref, elements, rows, columns):
    units = elements // 2048
    wide = max(k for k in range(1, columns // 128 + 1) if units % k == 0 and units // k <= rows // 16)
    return ref.at[pl.ds(0, units // wide * 16), pl.ds(0, wide * 128)]


def amount_of(ref, job):
    rows, columns = job_shape(job)
    return lambda pieces: region(ref, pieces * rows * columns, *ref.shape)


def own_part(ref, job):
    name, first, count, _ = job
    return ref.at[:, pl.ds(first, count)] if name == "down" else ref.at[pl.ds(first, count), :]


def kv_spot(ref, slot, row):
    def spot(who):
        _, s = mesh_place(*who)
        return ref.at[slot, pl.ds(row, 256), pl.ds(pl.multiple_of(s * 128, 128), 128)]

    return spot


def kv_amount(ref):
    return lambda pieces: ref.at[0, pl.ds(0, 32 * pieces), :]


def make_spreads(place, jobs, shards, wholes, sems):
    return [
        Spread(
            place, job[3], own_part(shards[job[0]], job), piece_of(wholes[job[0]], job), sems, j,
            piece_of(wholes[job[0]], job, True), amount_of(wholes[job[0]], job),
        )
        for j, job in enumerate(jobs)
    ]


def make_kv_spreads(place, own, whole, sems):
    return [
        Spread(
            place, order, own.at[pl.ds(row, 256), pl.ds(slot * 128, 128)], kv_spot(whole, slot, row),
            (sems[0], sems[1], None, None), j, None, kv_amount(whole),
        )
        for j, (slot, row, order) in enumerate(KV_JOBS)
    ]


def spread_sems(jobs):
    n = len(jobs)
    return [
        pltpu.SemaphoreType.DMA((n, 16)), pltpu.SemaphoreType.DMA((n,)),
        pltpu.SemaphoreType.DMA((n,)), pltpu.SemaphoreType.DMA((n,)),
    ]


def fold_scratch(jobs, paired):
    n = len(jobs)
    most = max(fold_slots(job[3])[1] for job in jobs)
    scratch = [
        pltpu.SemaphoreType.DMA((n,)), pltpu.SemaphoreType.DMA((n, most)),
        pltpu.SemaphoreType.DMA((n, 2)), pltpu.SemaphoreType.DMA((n, 2)), pltpu.SemaphoreType.DMA((n, 2)),
    ]
    for job in jobs:
        rows, columns = job_shape(job)
        block = (2, 1152, columns) if job[0] == "down" else (2, rows, 3072)
        scratch += [
            pltpu.VMEM(block, jnp.bfloat16), pltpu.VMEM((fold_slots(job[3])[1], rows, columns), jnp.bfloat16)
        ]
        scratch += [pltpu.VMEM(block, jnp.bfloat16)] if paired else []
    return scratch


class JobFold:
    def __init__(self, place, job, j, sums, owned, scratch, paired):
        self.place, self.job, self.j, self.sums, self.paired = place, job, j, sums, paired
        send, recv, self.load_sem, self.core_send, self.core_recv = scratch[:5]
        each = 3 if paired else 2
        self.acc, arrived = scratch[5 + each * j: 7 + each * j]
        self.other = scratch[7 + each * j] if paired else None
        name, first, count, order = job

        def mine(who):
            x, y, z, c = who
            s = 2 * z + x
            if name == "down":
                return self.acc.at[y, pl.ds(pl.multiple_of(s * 144, 16), 144), :]
            return self.acc.at[y, :, pl.ds(pl.multiple_of(s * 384, 128), 384)]

        def out(value):
            if name == "down":
                owned[:, first: first + count] = value
            else:
                owned[first: first + count, :] = value

        self.fold = Fold(place, order, mine, arrived, (send, recv), j, out, amount_of(sums, job), self.ready)

    def block(self, y, c):
        name, first, count, _ = self.job
        d = 2 * y + c if self.paired else y
        if name == "down":
            return self.sums.at[:, pl.ds(pl.multiple_of(d * 768 + first, 128), count)]
        return self.sums.at[pl.ds(pl.multiple_of(d * 288 + first, 8), count), :]

    def local_copy(self, dy):
        x, y, z, c = self.place
        at = (1 - y) if dy else y
        return pltpu.make_async_copy(self.block(at, c), self.acc.at[at], self.load_sem.at[self.j, dy])

    def core_copy(self, dy):
        x, y, z, c = self.place
        at = (1 - y) if dy else y
        return pltpu.make_async_remote_copy(
            src_ref=self.block(at, 1 - c),
            dst_ref=self.other.at[at],
            send_sem=self.core_send.at[self.j, dy],
            recv_sem=self.core_recv.at[self.j, dy],
            device_id=mesh_place(x, y, z, 1 - c),
            device_id_type=MESH_ID,
        )

    def begin(self, dy):
        if self.paired:
            self.core_copy(dy).start()
        self.local_copy(dy).start()

    def ready(self, dy):
        y = self.place[1]
        at = (1 - y) if dy else y
        self.local_copy(dy).wait()
        if not self.paired:
            return
        self.core_copy(dy).wait_recv()

        def add(k, _):
            if self.job[0] == "down":
                part = (at, pl.ds(pl.multiple_of(k * 144, 16), 144), slice(None))
            else:
                part = (at, slice(None), pl.ds(pl.multiple_of(k * 384, 128), 384))
            self.acc[part] = self.acc[part] + self.other[part]
            return _

        lax.fori_loop(0, 8, add, 0)

    def finish(self):
        self.fold.finish()
        for dy in (0, 1) if self.paired else ():
            self.core_copy(dy).wait_send()


class Notes:
    def __init__(self, place, tile_of, own, by_seq, by_dp, sems):
        self.d, self.s = mesh_place(*place)
        self.tile_of, self.own, self.by_seq, self.by_dp = tile_of, own, by_seq, by_dp
        self.seq_send, self.seq_recv, self.dp_send, self.dp_recv = sems

    def along_seq(self, k):
        peer = lax.rem(self.s + k, 8)
        return pltpu.make_async_remote_copy(
            src_ref=self.tile_of(peer), dst_ref=self.by_seq.at[self.s], send_sem=self.seq_send.at[k],
            recv_sem=self.seq_recv.at[self.s], device_id=(self.d, peer), device_id_type=MESH_ID,
        )

    def along_dp(self, k):
        peer = lax.rem(self.d + k, 4)
        return pltpu.make_async_remote_copy(
            src_ref=self.own, dst_ref=self.by_dp.at[self.d], send_sem=self.dp_send.at[k],
            recv_sem=self.dp_recv.at[self.d], device_id=(peer, self.s), device_id_type=MESH_ID,
        )

    def wait_seq(self):
        for k in range(1, 8):
            peer = lax.rem(self.s + k, 8)
            there = self.by_seq.at[peer]
            pltpu.make_async_copy(there, there, self.seq_recv.at[peer]).wait()

    def wait_dp(self):
        for k in range(1, 4):
            peer = lax.rem(self.d + k, 4)
            there = self.by_dp.at[peer]
            pltpu.make_async_copy(there, there, self.dp_recv.at[peer]).wait()


NOTE_SEMS = [
    pltpu.SemaphoreType.DMA((8,)), pltpu.SemaphoreType.DMA((8,)),
    pltpu.SemaphoreType.DMA((4,)), pltpu.SemaphoreType.DMA((4,)),
]


FORWARD_PLAN = (
    (200, 0, 100,),
    (2, 1, 201, 204, 101, 102, 4, 202, 3, 8, 205, 208, 108, 104, 103, 203, 5, 206, 9, 109, 209, 105, 10, 110,
        6, 212, 207, 106, 210, 7, 112, 10500, 12, 11,),
    (111, 107, 213, 10200, 113, 211, 10600, 214, 13, 10000, 10300, 10400, 114, 215, 14, 115, 15,),
    (20000, 20100, 20200, 20300, 20400, 20500,),
    (10100, 20001, 20004, 20101, 20201, 20104, 20301, 20204, 10201, 10002, 10001, 20401, 20304, 10204, 20501,
        10501, 20404, 20002, 10208, 20504, 10008, 10504, 20102, 10508, 10301, 10302, 20202, 10402, 10601,
        20005, 20302, 10308, 10401, 10408, 20205, 20402, 10604, 10608, 10102, 20502, 10101, 20305, 10108,
        10202, 20405, 10004, 20505, 10502, 10209, 10009, 10010, 20105, 10205, 20003, 10003, 10304, 10509,
        20103, 10602, 20006, 10605, 10505, 20203, 10404, 10212, 10104, 10309, 10310, 20106, 20303, 20403,
        10303, 20206, 10512, 20306, 20503, 10005, 10403, 10210, 20406, 10103, 10409, 10510, 10110, 10609,
        20506, 10410, 10305, 10109, 10213, 10513, 10203, 10012, 10405, 10503, 10011, 10105, 10612, 10206,
        20007, 10506, 10606, 10013, 20107, 10603, 10613, 10312, 10610, 20207, 10311, 10006, 20307, 10211,
        10313, 20407, 10511, 20507,),
    (
        (1, (10412,)),
        (3, (10411,)),
        (4, (10007, 10207,)),
        (5, (10306, 10413, 10112, 10406, 10214,)),
        (6, (10507,)),
        (7, (10111, 10514,)),
        (8, (10607, 10106,)),
        (9, (10307,)),
        (10, (10407,)),
    ),
    (10113, 10611, 10107, 10014, 10614, 10415, 10515, 10215, 10314, 10615, 10015, 10114, 10414, 10315, 10115,),
)
BACKWARD_PLAN = (
    (
        (10100, 10102, 10101, 10103, 10104, 10106, 10105, 10400, 10200,),
        (10401, 10107, 10108, 10109, 10110, 10201,),
    ),
    (
        (0, (10000, 10402, 10300,)),
        (1, (10301,)),
        (2, (10202,)),
        (3, (10204,)),
        (4, (10403,)),
        (5, (10112,)),
        (6, (20000, 20100, 20200, 20001, 20101, 20201, 20002, 20102, 20202, 20003, 20103, 20203, 10111, 10203,
            10500, 10302, 10002, 20004,)),
        (7, (10113, 20104,)),
        (8, (10404, 20204,)),
        (9, (20005, 20105, 10501, 10303,)),
        (10, (10601, 20006, 20205,)),
        (11, (20106,)),
    ),
    (20500, 20501, 20502, 20503, 20300, 20400, 20401, 20402, 20403, 20301, 20206, 10600, 10602, 10502, 10405,
        10304, 10306, 10004, 10205, 10406, 10407, 10408, 20302, 20303, 10305, 10410, 20007, 10001, 10003,
        10005, 10503, 10006, 10409, 20107, 10604, 20504, 20505, 20207, 20506, 10206, 10207, 10208, 10209,
        10210, 10603, 10504, 10007, 10008, 10307, 10308, 10010, 10505, 20304, 10009, 10310, 20404, 10605,
        10412, 10114, 10506, 10606, 20305, 20306, 20405, 10411, 10507, 10508, 10509, 10309, 20406, 10510,
        10012, 20507, 10607, 10608, 10609, 10011, 10610, 10312, 10211, 20407, 10311, 10413, 20307,),
    (
        (0, (10013,)),
        (5, (10313, 10115,)),
    ),
    (10511, 10414, 10212, 10014, 10611, 10213, 10214, 10314, 200, 201, 202,),
    (203, 205, 204, 206, 0, 1,),
    (10415, 2, 207, 3, 208, 10512, 4, 5, 10612, 10015, 6, 10613, 10614, 10513, 209, 10514, 7,),
    (10315, 10215, 100, 102, 210, 104, 106, 8, 101, 103, 211, 105, 9, 107, 10, 11, 212,),
    (10615, 12, 10515, 13, 213, 214, 108, 109, 110, 14, 112, 215, 111, 113, 114, 15, 115,),
)


def dot(a, b):
    return jnp.dot(a, b, preferred_element_type=jnp.float32)


def dot_t(a, b):
    return lax.dot_general(a, b, (((1,), (1,)), ((), ())), preferred_element_type=jnp.float32)


def t_dot(a, b):
    return lax.dot_general(a, b, (((0,), (0,)), ((), ())), preferred_element_type=jnp.float32)


def repeat(count, body):
    def step(k, nothing):
        body(k)
        return nothing

    lax.fori_loop(0, count, step, 0)


def rows_at(k, size, base=0):
    return pl.ds(pl.multiple_of(base + k * size, 16), size)


def lanes_at(k, size, base=0):
    return pl.ds(pl.multiple_of(base + k * size, 128), size)


def rotate(u, cosine, sine):
    front, back = u[:32], u[32:]
    return jnp.concatenate([front * cosine - back * sine, front * sine + back * cosine], axis=0)


def probabilities(keys, query, limit, chunk):
    scores = t_dot(keys, query) * (HEAD_DIMENSION ** (-0.5))
    key_pos = chunk * 256 + lax.broadcasted_iota(jnp.int32, (256, 384), 0)
    return jnp.where(key_pos <= limit, jnp.exp(scores), 0.0)


def heads_wide(ref, group, lanes):
    return jnp.concatenate(
        [ref[pl.ds(pl.multiple_of(group * 192 + 64 * i, 64), 64), lanes] for i in range(3)], axis=1
    )


def key_limit(length, s):
    query_pos = s * 128 + lax.broadcasted_iota(jnp.int32, (1, 128), 1)
    return jnp.concatenate([jnp.minimum(query_pos, length - 1)] * 3, axis=1)


def forward_body(
    lengths, query_t, key_t, value_t, out_t, gain_a, gain_f, x, cosine, sine, gate, up, down,
    gate_w, up_w, down_w, wcat, kept_in_t, kept_query, kept_kv, kept_attn, kept_denom, notes, hidden,
    tile, cat_t, cat, attn_in_t, query, keys_values, attn, denom,
    attn_in, raw, own_kv, weights, proj, seq_in, dp_in, own_sems, note_a, note_b, note_c, note_d, *sems
):
    place = position()
    d, s = mesh_place(*place)
    row = 0
    for part in (query_t, key_t, value_t, out_t):
        cat_t[row: row + part.shape[0], 0:288] = part[...].astype(jnp.float32)
        row += part.shape[0]
    cat[...] = cat_t[...].T[0:288, :].astype(jnp.bfloat16)
    tile[...] = jnp.zeros_like(tile)
    for k in range(8):
        def own_gains(k=k):
            tile[0:1, 144 * k: 144 * k + 144] = gain_a[...].astype(jnp.float32).reshape(1, 144)
            tile[1:2, 144 * k: 144 * k + 144] = gain_f[...].astype(jnp.float32).reshape(1, 144)

        pl.when(s == k)(own_gains)
    tile[2:3, :] = jnp.broadcast_to((lengths[0] + lengths[1]).astype(jnp.float32), (1, 1152))
    greet(place, True)
    shards = dict(zip(FFN_NAMES, (gate, up, down)))
    wholes = dict(zip(FFN_NAMES, (gate_w, up_w, down_w)))
    cat_spreads = make_spreads(place, CAT_JOBS, {"cat": cat}, {"cat": weights}, sems[:4])
    ffn_spreads = make_spreads(place, FFN_JOBS, shards, wholes, sems[4:8])
    kv_spreads = make_kv_spreads(place, own_kv, keys_values, sems[8:10])
    steps = [[spread.steps() for spread in family] for family in (cat_spreads, ffn_spreads, kv_spreads)]

    def run(tokens):
        for token in tokens:
            steps[token // 10000][token // 100 % 100][token % 100]()

    tiles = Notes(place, lambda peer: tile, tile, seq_in, dp_in, (note_a, note_b, note_c, note_d))
    run(FORWARD_PLAN[0])
    for k in range(1, 8):
        tiles.along_seq(k).start()
    for k in range(1, 4):
        tiles.along_dp(k).start()
    own = [
        pltpu.make_async_copy(
            shards[name], piece_of(wholes[name], (name, 0, 768 if name == "down" else 288, ""))(place), own_sems.at[k]
        )
        for k, name in enumerate(FFN_NAMES)
    ]
    for copy in own:
        copy.start()
    weights[rows_at(d, 288), lanes_at(s, 384)] = cat[...]
    for copy in own:
        copy.wait()
    run(FORWARD_PLAN[1])
    tiles.wait_seq()
    tiles.wait_dp()
    seq_in[s] = tile[...]
    dp_in[d] = tile[...]
    gains = seq_in[0]
    for k in range(1, 8):
        gains = gains + seq_in[k]
    notes[0:8, :] = gains
    notes[8:16, :] = dp_in[0] + dp_in[1] + dp_in[2] + dp_in[3]

    def norm(k):
        rows = rows_at(k, 32)
        part = x[rows, :].astype(jnp.float32)
        scale = lax.rsqrt(jnp.mean(part * part, axis=-1, keepdims=True) + norm_eps)
        attn_in[rows, :] = (part * scale * notes[0:1, :]).astype(jnp.bfloat16)

    repeat(8, norm)
    attn_in_t[...] = attn_in[...].T
    run(FORWARD_PLAN[2])
    for spread in cat_spreads:
        spread.wait_core()

    def project(b):
        block = dot(attn_in[...], weights[:, lanes_at(b, 384)][:, :256]).T
        raw[rows_at(b, 144), :] = block[:144]
        raw[rows_at(b, 48, 1152), :] = block[144:192]
        raw[rows_at(b, 48, 1536), :] = block[192:240]

    repeat(8, project)
    out_copy = pltpu.make_async_copy(weights, wcat, own_sems.at[3])
    out_copy.start()

    def turn(ref, rows_of):
        def one(h):
            ref[rows_at(h, 64), :] = rotate(raw[rows_of(h), :], cosine[...], sine[...]).astype(jnp.bfloat16)

        return one

    repeat(6, turn(own_kv, lambda h: rows_at(h, 64, 1152)))
    own_kv[384:768, :] = raw[1536:1920, :].astype(jnp.bfloat16)
    repeat(18, turn(query, lambda h: rows_at(h, 64)))
    keeps = [
        pltpu.make_async_copy(source, target, own_sems.at[4 + k])
        for k, (source, target) in enumerate(
            ((attn_in_t, kept_in_t), (query, kept_query), (keys_values, kept_kv), (attn, kept_attn), (denom, kept_denom))
        )
    ]
    keeps[0].start()
    keeps[1].start()
    run(FORWARD_PLAN[3])
    here = lanes_at(s, 128)
    for slot in range(2):
        keys_values[slot, :, here] = own_kv[:, slot * 128: slot * 128 + 128]
    run(FORWARD_PLAN[4])
    keeps[2].start()

    def attend(slot, group):
        lanes = lanes_at(slot, 128)
        bound = key_limit(lengths[slot], s)
        wide = heads_wide(query, group, lanes)

        def one_chunk(chunk, carry):
            total, numer = carry
            cols = lanes_at(chunk, 256)
            expo = probabilities(keys_values[slot, rows_at(group, 64), cols], wide, bound, chunk)
            total = total + jnp.sum(expo, axis=0, keepdims=True)
            numer = numer + dot(keys_values[slot, rows_at(group, 64, 384), cols], expo.astype(jnp.bfloat16))
            return (total, numer)

        total, numer = lax.fori_loop(
            0, 4, one_chunk, (jnp.zeros((1, 384), jnp.float32), jnp.zeros((64, 384), jnp.float32)), unroll=True
        )
        mean = numer / total
        for i in range(3):
            attn[pl.ds(pl.multiple_of(group * 192 + 64 * i, 64), 64), lanes] = mean[:, i * 128: i * 128 + 128]
        denom[group, 0:3, lanes] = jnp.concatenate([total[:, i * 128: i * 128 + 128] for i in range(3)], axis=0)

    def unit(k):
        attend(k // 6, lax.rem(k, 6))
        for at, tokens in FORWARD_PLAN[5]:
            pl.when(k == at)(lambda tokens=tokens: run(tokens))

    repeat(12, unit)
    keeps[3].start()
    keeps[4].start()

    def out_project(b):
        block = t_dot(attn[...].astype(jnp.bfloat16), weights[:, lanes_at(b, 384)][:, 128:]).T
        proj[rows_at(b, 144), :] = block[112:256]

    repeat(8, out_project)
    hidden[...] = x[...].astype(jnp.float32) + proj[...].T
    run(FORWARD_PLAN[6])
    for spread in cat_spreads + ffn_spreads + kv_spreads:
        spread.finish()
    for spread in ffn_spreads:
        spread.wait_core()
    for k in range(1, 8):
        tiles.along_seq(k).wait_send()
    for k in range(1, 4):
        tiles.along_dp(k).wait_send()
    for copy in [out_copy] + keeps:
        copy.wait()


def forward_call(lengths, shards_t, gain_a, gain_f, x, cosine, sine, gate, up, down):
    vmem, anywhere = pl.BlockSpec(memory_space=pltpu.VMEM), pl.BlockSpec(memory_space=pl.ANY)
    kept = [
        ((1152, 256), jnp.bfloat16), ((1152, 256), jnp.bfloat16), ((2, 768, 1024), jnp.bfloat16),
        ((1152, 256), jnp.float32), ((6, 8, 256), jnp.float32),
    ]
    return pl.pallas_call(
        forward_body,
        out_shape=[jax.ShapeDtypeStruct((1152, 3072), jnp.bfloat16)] * 4
        + [jax.ShapeDtypeStruct(*item) for item in kept]
        + [jax.ShapeDtypeStruct((16, 1152), jnp.float32), jax.ShapeDtypeStruct((256, 1152), jnp.float32)],
        in_specs=[pl.BlockSpec(memory_space=pltpu.SMEM)] + [vmem] * 12,
        out_specs=[anywhere] * 9 + [vmem] * 2,
        scratch_shapes=[pltpu.VMEM((8, 1152), jnp.float32), pltpu.VMEM((384, 384), jnp.float32), pltpu.VMEM((288, 384), jnp.bfloat16)]
        + [pltpu.VMEM(*item) for item in kept]
        + [
            pltpu.VMEM((256, 1152), jnp.bfloat16),
            pltpu.VMEM((1920, 256), jnp.float32),
            pltpu.VMEM((768, 256), jnp.bfloat16),
            pltpu.VMEM((1152, 3072), jnp.bfloat16),
            pltpu.VMEM((1152, 256), jnp.float32),
            pltpu.VMEM((8, 8, 1152), jnp.float32),
            pltpu.VMEM((4, 8, 1152), jnp.float32),
            pltpu.SemaphoreType.DMA((9,)),
        ]
        + NOTE_SEMS
        + spread_sems(CAT_JOBS)
        + spread_sems(FFN_JOBS)
        + spread_sems(KV_JOBS)[:2],
        compiler_params=pltpu.CompilerParams(
            collective_id=3, has_side_effects=True, vmem_limit_bytes=VMEM_MOST
        ),
        name="attention_forward",
    )(lengths, *shards_t, gain_a, gain_f, x, cosine, sine, gate, up, down)


def ffn_body(
    total_tokens, lengths, hidden, teacher, notes, gate_w, up_w, down_w,
    out, grad_hidden, small, gate_sums, up_sums, down_sums,
    w_gate, w_up, w_down, gate, up, hid, grads_gate, grads_up, inputs_t, cot_t, inputs, cot_b, acc, cot, rate,
    sums_gate, sums_up, sums_down, load, swap_send, swap_recv, store
):
    place = position()
    x, y, z, c = place
    _, s = mesh_place(*place)
    other = mesh_place(x, y, z, 1 - c)
    barrier = pltpu.get_barrier_semaphore()
    pl.semaphore_signal(barrier, inc=1, device_id=other, device_id_type=MESH_ID)
    pl.semaphore_wait(barrier, 1)
    columns = lambda j: lanes_at(j, 768)

    def load_copy(k, source, target, j):
        return pltpu.make_async_copy(source.at[:, columns(j)], target.at[:, columns(j)], load.at[k, j])

    def loads(j):
        return [load_copy(k, *pair, j) for k, pair in enumerate(((gate_w, w_gate), (up_w, w_up), (down_w, w_down)))]

    for j in range(4):
        for copy in loads(j):
            copy.start()

    def swap(source, target, k):
        return pltpu.make_async_remote_copy(
            src_ref=source, dst_ref=target, send_sem=swap_send.at[k], recv_sem=swap_recv.at[k],
            device_id=other, device_id_type=MESH_ID,
        )

    own, theirs = pl.ds(0, 256), pl.ds(256, 256)
    swap_inputs = swap(inputs_t.at[:, own], inputs_t.at[:, theirs], 0)
    swap_cot = swap(cot_t.at[:, own], cot_t.at[:, theirs], 1)

    def swap_hid(i, core):
        at = columns(core + 2 * i)
        return swap(hid.at[own, at], hid.at[theirs, at], 2 + i)

    def swap_grads(ref, j, k):
        return swap(ref.at[own, columns(j)], ref.at[theirs, columns(j)], k + j)

    def norm(k):
        rows = rows_at(k, 32)
        part = hidden[rows, :]
        scale = lax.rsqrt(jnp.mean(part * part, axis=-1, keepdims=True) + norm_eps)
        rate[rows, :] = jnp.broadcast_to(scale, (32, 128))
        inputs[rows, :] = (part * scale * notes[1:2, :]).astype(jnp.bfloat16)

    repeat(8, norm)
    inputs_t[:, 0:256] = inputs[...].T
    acc[...] = jnp.zeros_like(acc)

    def forward(j):
        for copy in loads(j):
            copy.wait()
        at = columns(j)
        gate_part = dot(inputs[...], w_gate[:, at])
        up_part = dot(inputs[...], w_up[:, at])
        gate[:, at] = gate_part
        up[:, at] = up_part
        hid[0:256, at] = (gate_part * jax.nn.sigmoid(gate_part) * up_part).astype(jnp.bfloat16)
        acc[...] += dot_t(hid[0:256, at], w_down[:, at])

    repeat(4, forward)
    swap_inputs.start()
    for i in range(2):
        swap_hid(i, 1 - c).start()
    factor = total_tokens / notes[10:11, :]
    small[...] = jnp.zeros_like(small)

    def losses(k):
        rows = rows_at(k, 32)
        first = s * 128 + lax.rem(k, 4) * 32
        live = first + lax.broadcasted_iota(jnp.int32, (32, 1), 0) < lengths[k // 4]
        value = jnp.where(live, hidden[rows, :] + acc[rows, :], 0.0)
        out[rows, :] = value.astype(jnp.bfloat16)
        diff = jnp.where(live, value - teacher[rows, :].astype(jnp.float32), 0.0)
        small[2:3, :] += jnp.sum(diff * diff, axis=0, keepdims=True)
        grad = factor * diff
        cot[rows, :] = grad
        cot_b[rows, :] = grad.astype(jnp.bfloat16)

    repeat(8, losses)
    cot_t[:, 0:256] = cot_b[...].T
    acc[...] = jnp.zeros_like(acc)

    def backward(j):
        at = columns(j)
        grad_hid = dot(cot_b[...], w_down[:, at])
        gate_part = gate[:, at]
        sig = jax.nn.sigmoid(gate_part)
        grads_gate[0:256, at] = (
            grad_hid * up[:, at] * sig * (1.0 + gate_part * (1.0 - sig))
        ).astype(jnp.bfloat16)
        grads_up[0:256, at] = (grad_hid * gate_part * sig).astype(jnp.bfloat16)
        acc[...] += dot_t(grads_gate[0:256, at], w_gate[:, at]) + dot_t(grads_up[0:256, at], w_up[:, at])
        swap_grads(grads_gate, j, 4).start()
        swap_grads(grads_up, j, 8).start()
        pl.when(j == 0)(swap_cot.start)

    repeat(4, backward)

    def finish_rows(k):
        rows = rows_at(k, 32)
        scale = rate[rows, 0:1]
        normed = hidden[rows, :] * scale
        grad = acc[rows, :]
        small[1:2, :] += jnp.sum(grad * normed, axis=0, keepdims=True)
        grad = grad * notes[1:2, :]
        inner = grad - normed * jnp.mean(grad * normed, axis=-1, keepdims=True)
        grad_hidden[rows, :] = cot[rows, :] + scale * inner

    repeat(8, finish_rows)
    small[2:3, :] = jnp.broadcast_to(jnp.sum(small[2:3, :], axis=-1, keepdims=True), (1, 1152))
    small[3:4, :] = notes[0:1, :]
    swap_cot.wait_recv()
    swap_inputs.wait_recv()

    def stored(k, source, target, i):
        at = columns(i)
        return pltpu.make_async_copy(source.at[:, at], target.at[:, at], store.at[k, i])

    def down_grads(i):
        swap_hid(i, c).wait_recv()
        sums_down[:, columns(i)] = dot(cot_t[...], hid[:, columns(c + 2 * i)]).astype(jnp.bfloat16)
        stored(0, sums_down, down_sums, i).start()

    repeat(2, down_grads)

    def wide_grads(j):
        at = columns(j)
        swap_grads(grads_gate, j, 4).wait_recv()
        swap_grads(grads_up, j, 8).wait_recv()
        for half in range(2):
            rows = rows_at(c + 2 * half, 288)
            kept = slice(288 * half, 288 * half + 288)
            sums_gate[kept, at] = dot(inputs_t[rows, :], grads_gate[:, at]).astype(jnp.bfloat16)
            sums_up[kept, at] = dot(inputs_t[rows, :], grads_up[:, at]).astype(jnp.bfloat16)
        stored(1, sums_gate, gate_sums, j).start()
        stored(2, sums_up, up_sums, j).start()

    repeat(4, wide_grads)
    swap_inputs.wait_send()
    swap_cot.wait_send()
    for i in range(2):
        swap_hid(i, 1 - c).wait_send()
        stored(0, sums_down, down_sums, i).wait()
    for j in range(4):
        swap_grads(grads_gate, j, 4).wait_send()
        swap_grads(grads_up, j, 8).wait_send()
        stored(1, sums_gate, gate_sums, j).wait()
        stored(2, sums_up, up_sums, j).wait()


def ffn_call(total_tokens, lengths, hidden, teacher, notes, gate_w, up_w, down_w):
    vmem, anywhere = pl.BlockSpec(memory_space=pltpu.VMEM), pl.BlockSpec(memory_space=pl.ANY)
    whole = pltpu.VMEM((1152, 3072), jnp.bfloat16)
    both = pltpu.VMEM((512, 3072), jnp.bfloat16)
    return pl.pallas_call(
        functools.partial(ffn_body, total_tokens),
        out_shape=[
            jax.ShapeDtypeStruct((256, 1152), jnp.bfloat16),
            jax.ShapeDtypeStruct((256, 1152), jnp.float32),
            jax.ShapeDtypeStruct((8, 1152), jnp.float32),
            jax.ShapeDtypeStruct((576, 3072), jnp.bfloat16),
            jax.ShapeDtypeStruct((576, 3072), jnp.bfloat16),
            jax.ShapeDtypeStruct((1152, 1536), jnp.bfloat16),
        ],
        in_specs=[pl.BlockSpec(memory_space=pltpu.SMEM)] + [vmem] * 3 + [anywhere] * 3,
        out_specs=[vmem] * 3 + [anywhere] * 3,
        scratch_shapes=[whole] * 3
        + [pltpu.VMEM((256, 3072), jnp.float32)] * 2
        + [both] * 3
        + [pltpu.VMEM((1152, 512), jnp.bfloat16)] * 2
        + [pltpu.VMEM((256, 1152), jnp.bfloat16)] * 2
        + [pltpu.VMEM((256, 1152), jnp.float32)] * 2
        + [pltpu.VMEM((256, 128), jnp.float32)]
        + [pltpu.VMEM((576, 3072), jnp.bfloat16)] * 2
        + [
            pltpu.VMEM((1152, 1536), jnp.bfloat16),
            pltpu.SemaphoreType.DMA((3, 4)),
            pltpu.SemaphoreType.DMA((12,)),
            pltpu.SemaphoreType.DMA((12,)),
            pltpu.SemaphoreType.DMA((3, 4)),
        ],
        compiler_params=pltpu.CompilerParams(
            collective_id=5, has_side_effects=True, vmem_limit_bytes=VMEM_MOST
        ),
        name="feed_forward",
    )(lengths, hidden, teacher, notes, gate_w, up_w, down_w)


def backward_body(
    lengths, grad_hidden, cosine, sine, small, x_in, kept_in_t, wcat, keys_values, kept_query, kept_attn, kept_denom,
    grad_gate, grad_up, grad_down,
    own_gate, own_up, own_down, own_query_t, own_key_t, own_value_t, own_out_t, grad_tokens, totals, grad_cat,
    x, attn_in_t, query, attn, denom, own_cat, weights, whole_kv, part_kv, turned, total, own_kv, left, grad_t, note, seq_in, dp_in, row_sum,
    load, store, kv_send, kv_recv, *scratch
):
    place = position()
    d, s = mesh_place(*place)
    greet(place, True)
    sums = dict(zip(FFN_NAMES, (grad_gate, grad_up, grad_down)))
    owned = dict(zip(FFN_NAMES, (own_gate, own_up, own_down)))
    kv_arrived, scratch = scratch[: len(FOLD_KV)], scratch[len(FOLD_KV):]
    note_sems, scratch = scratch[:4], scratch[4:]
    split = len(fold_scratch(FOLD_FFN, False))
    folds = [
        JobFold(place, job, j, sums[job[0]], owned[job[0]], scratch[:split], False) for j, job in enumerate(FOLD_FFN)
    ]
    cat_folds = [JobFold(place, job, j, grad_cat, own_cat, scratch[split:], True) for j, job in enumerate(FOLD_CAT)]
    tiles = Notes(place, lambda peer: note, row_sum, seq_in, dp_in, note_sems)

    def kv_fold(j, slot, row, order):
        def out(value):
            own_kv[row: row + 256, slot * 128: slot * 128 + 128] = value

        spot = kv_spot(part_kv, slot, row)
        return Fold(place, order, lambda who: spot(who), kv_arrived[j], (kv_send, kv_recv), j, out, kv_amount(part_kv))

    kv_folds = [kv_fold(j, *job) for j, job in enumerate(FOLD_KV)]
    steps = [
        [fold.fold.steps() for fold in cat_folds],
        [fold.fold.steps() for fold in folds],
        [fold.steps() for fold in kv_folds],
    ]

    def run(tokens):
        for token in tokens:
            steps[token // 10000][token // 100 % 100][token % 100]()

    for dy in (1, 0):
        for fold in folds:
            fold.begin(dy)

    def block_load(b):
        return pltpu.make_async_copy(wcat.at[:, lanes_at(b, 384)], weights.at[:, lanes_at(b, 384)], load.at[b])

    repeat(8, lambda b: block_load(b).start())
    kept = [
        pltpu.make_async_copy(source, target, load.at[8 + k])
        for k, (source, target) in enumerate(
            ((keys_values, whole_kv), (kept_query, query), (kept_attn, attn), (kept_denom, denom),
             (kept_in_t, attn_in_t), (x_in, x))
        )
    ]
    for copy in kept:
        copy.start()
    run(BACKWARD_PLAN[0][0])
    grad_t[...] = grad_hidden[...].T.astype(jnp.bfloat16)
    total[...] = jnp.zeros_like(total)

    def out_rows(b):
        return jnp.concatenate([jnp.zeros((112, 256), jnp.bfloat16), grad_t[rows_at(b, 144), :]], axis=0)

    def out_back(b):
        block_load(b).wait()
        total[...] += dot(weights[:, lanes_at(b, 384)][:, 128:], out_rows(b))

    repeat(8, out_back)
    run(BACKWARD_PLAN[0][1])
    for copy in kept:
        copy.wait()
    scale = HEAD_DIMENSION ** (-0.5)

    def attend_back(slot, group):
        lanes = lanes_at(slot, 128)
        bound = key_limit(lengths[slot], s)
        wide = heads_wide(query, group, lanes)
        grads, ratios = [], []
        for i in range(3):
            rows = pl.ds(pl.multiple_of(group * 192 + 64 * i, 64), 64)
            grad = total[rows, lanes].astype(jnp.bfloat16).astype(jnp.float32)
            bottom = denom[group, i: i + 1, lanes]
            ratios.append(jnp.sum(grad * attn[rows, lanes], axis=0, keepdims=True) / bottom)
            grads.append((grad / bottom).astype(jnp.bfloat16))
        grads, ratios = jnp.concatenate(grads, axis=1), jnp.concatenate(ratios, axis=1)

        def one_chunk(chunk, sum_query):
            cols = lanes_at(chunk, 256)
            keys = whole_kv[slot, rows_at(group, 64), cols]
            values = whole_kv[slot, rows_at(group, 64, 384), cols]
            expo = probabilities(keys, wide, bound, chunk)
            grad_prob = t_dot(values, grads)
            grad_score = (expo * (grad_prob - ratios)).astype(jnp.bfloat16)
            part_kv[slot, rows_at(group, 64), cols] = (dot_t(wide, grad_score) * scale).astype(jnp.bfloat16)
            part_kv[slot, rows_at(group, 64, 384), cols] = dot_t(grads, expo.astype(jnp.bfloat16)).astype(jnp.bfloat16)
            return sum_query + dot(keys, grad_score)

        sum_query = lax.fori_loop(0, 4, one_chunk, jnp.zeros((64, 384), jnp.float32), unroll=True) * scale
        for i in range(3):
            total[pl.ds(pl.multiple_of(group * 192 + 64 * i, 64), 64), lanes] = sum_query[:, i * 128: i * 128 + 128]

    def unit(k):
        attend_back(k // 6, lax.rem(k, 6))
        for at, tokens in BACKWARD_PLAN[1]:
            pl.when(k == at)(lambda tokens=tokens: run(tokens))

    repeat(12, unit)
    run(BACKWARD_PLAN[2])

    def turn_back(ref, source, count):
        def one(h):
            rows = rows_at(h, 64)
            ref[rows, :] = rotate(source[rows, :], cosine[...], -sine[...]).astype(ref.dtype)

        repeat(count, one)

    turn_back(turned, total, 18)
    turn_back(own_kv, own_kv, 6)
    total[...] = jnp.zeros_like(total)

    def last_block(b):
        rows = jnp.concatenate(
            [
                turned[rows_at(b, 144), :],
                own_kv[rows_at(b, 48), :].astype(jnp.bfloat16),
                own_kv[rows_at(b, 48, 384), :].astype(jnp.bfloat16),
                jnp.zeros((16, 256), jnp.bfloat16),
            ],
            axis=0,
        )
        total[...] += dot(weights[:, lanes_at(b, 384)][:, :256], rows)
        slot = lax.rem(b, 2)
        out = pltpu.make_async_copy(left.at[slot], grad_cat.at[:, lanes_at(b, 384)], store.at[slot])
        pl.when(b >= 2)(lambda: out.wait())
        grad = dot_t(attn_in_t[...], rows)
        out_grad = dot_t(attn[...].astype(jnp.bfloat16), out_rows(b))
        left[slot, :, 0:128] = grad[:, :128].astype(jnp.bfloat16)
        left[slot, :, 128:256] = (grad[:, 128:] + out_grad[:, :128]).astype(jnp.bfloat16)
        left[slot, :, 256:384] = out_grad[:, 128:].astype(jnp.bfloat16)
        out.start()
        for at, tokens in BACKWARD_PLAN[3]:
            pl.when(b == at)(lambda tokens=tokens: run(tokens))

    repeat(8, last_block)
    for slot in range(2):
        pltpu.make_async_copy(left.at[slot], grad_cat.at[:, pl.ds((6 + slot) * 384, 384)], store.at[slot]).wait()
    for dy in (1, 0):
        for fold in cat_folds:
            fold.begin(dy)
    run(BACKWARD_PLAN[4])
    grad_tokens[...] = total[...].T
    note[...] = small[...]

    def finish_rows(k):
        rows = rows_at(k, 32)
        grad = grad_tokens[rows, :]
        normed = x[rows, :].astype(jnp.float32)
        scale_in = lax.rsqrt(jnp.mean(normed * normed, axis=-1, keepdims=True) + norm_eps)
        normed = normed * scale_in
        note[0:1, :] += jnp.sum(grad * normed, axis=0, keepdims=True)
        grad = grad * small[3:4, :]
        inner = grad - normed * jnp.mean(grad * normed, axis=-1, keepdims=True)
        grad_tokens[rows, :] = grad_hidden[rows, :] + scale_in * inner

    repeat(8, finish_rows)
    run(BACKWARD_PLAN[5])
    for k in range(1, 8):
        tiles.along_seq(k).start()
    run(BACKWARD_PLAN[6])
    tiles.wait_seq()
    seq_in[s] = note[...]
    along = seq_in[0]
    for k in range(1, 8):
        along = along + seq_in[k]
    row_sum[...] = along
    run(BACKWARD_PLAN[7])
    for k in range(1, 4):
        tiles.along_dp(k).start()
    run(BACKWARD_PLAN[8])
    tiles.wait_dp()
    dp_in[d] = row_sum[...]
    totals[...] = dp_in[0] + dp_in[1] + dp_in[2] + dp_in[3]
    turned_cat = own_cat[...].T
    row = 0
    for ref in (own_query_t, own_key_t, own_value_t, own_out_t):
        ref[...] = turned_cat[row: row + ref.shape[0], 0:288]
        row += ref.shape[0]
    for fold in folds + kv_folds + cat_folds:
        fold.finish()
    for k in range(1, 8):
        tiles.along_seq(k).wait_send()
    for k in range(1, 4):
        tiles.along_dp(k).wait_send()


def backward_call(
    lengths, grad_hidden, cosine, sine, small, x, attn_in_t, wcat, keys_values, query, attn, denom,
    grad_gate, grad_up, grad_down
):
    vmem, anywhere = pl.BlockSpec(memory_space=pltpu.VMEM), pl.BlockSpec(memory_space=pl.ANY)
    jobs = len(KV_JOBS)
    most = max(fold_slots(order)[1] for _, _, order in FOLD_KV)
    outs = ((288, 384), (288, 384), (144, 768), (144, 288), (48, 288), (48, 288), (144, 288), (256, 1152), (8, 1152))
    return pl.pallas_call(
        backward_body,
        out_shape=[jax.ShapeDtypeStruct(shape, jnp.float32) for shape in outs]
        + [jax.ShapeDtypeStruct((1152, 3072), jnp.bfloat16)],
        in_specs=[pl.BlockSpec(memory_space=pltpu.SMEM)] + [vmem] * 4 + [anywhere] * 10,
        out_specs=[vmem] * len(outs) + [anywhere],
        scratch_shapes=[
            pltpu.VMEM((256, 1152), jnp.bfloat16),
            pltpu.VMEM((1152, 256), jnp.bfloat16),
            pltpu.VMEM((1152, 256), jnp.bfloat16),
            pltpu.VMEM((1152, 256), jnp.float32),
            pltpu.VMEM((6, 8, 256), jnp.float32),
            pltpu.VMEM((384, 384), jnp.float32),
            pltpu.VMEM((1152, 3072), jnp.bfloat16),
            pltpu.VMEM((2, 768, 1024), jnp.bfloat16),
            pltpu.VMEM((2, 768, 1024), jnp.bfloat16),
            pltpu.VMEM((1152, 256), jnp.bfloat16),
            pltpu.VMEM((1152, 256), jnp.float32),
            pltpu.VMEM((768, 256), jnp.float32),
            pltpu.VMEM((2, 1152, 384), jnp.bfloat16),
            pltpu.VMEM((1152, 256), jnp.bfloat16),
            pltpu.VMEM((8, 1152), jnp.float32),
            pltpu.VMEM((8, 8, 1152), jnp.float32),
            pltpu.VMEM((4, 8, 1152), jnp.float32),
            pltpu.VMEM((8, 1152), jnp.float32),
            pltpu.SemaphoreType.DMA((14,)),
            pltpu.SemaphoreType.DMA((2,)),
            pltpu.SemaphoreType.DMA((jobs,)),
            pltpu.SemaphoreType.DMA((jobs, most)),
        ]
        + [pltpu.VMEM((fold_slots(order)[1], 256, 128), jnp.bfloat16) for _, _, order in FOLD_KV]
        + NOTE_SEMS
        + fold_scratch(FOLD_FFN, False)
        + fold_scratch(FOLD_CAT, True),
        compiler_params=pltpu.CompilerParams(
            collective_id=4, has_side_effects=True, vmem_limit_bytes=VMEM_MOST
        ),
        name="attention_backward",
    )(
        lengths, grad_hidden, cosine, sine, small, x, attn_in_t, wcat, keys_values, query, attn, denom,
        grad_gate, grad_up, grad_down,
    )


def hand_over_body(count, *refs):
    sources, (totals, notes) = refs[:count], refs[count: count + 2]
    targets, (loss, gain_a, gain_f) = refs[count + 2: 2 * count + 2], refs[2 * count + 2: 2 * count + 5]
    held, (into, out) = refs[2 * count + 5: 3 * count + 5], refs[-2:]
    reads = [pltpu.make_async_copy(source, there, into.at[k]) for k, (source, there) in enumerate(zip(sources, held))]
    copies = [pltpu.make_async_copy(there, target, out.at[k]) for k, (there, target) in enumerate(zip(held, targets))]
    for read in reads:
        read.start()
    loss[...] = totals[2:3, 0:1] / notes[10:11, 0:1]
    s = lax.axis_index("seq")
    for k in range(8):
        def own(k=k):
            gain_a[...] = totals[0:1, 144 * k: 144 * k + 144]
            gain_f[...] = totals[1:2, 144 * k: 144 * k + 144]

        pl.when(s == k)(own)
    for read, copy in zip(reads, copies):
        read.wait()
        copy.start()
    for copy in copies:
        copy.wait()


def hand_over(results, totals, notes):
    vmem, anywhere = pl.BlockSpec(memory_space=pltpu.VMEM), pl.BlockSpec(memory_space=pl.ANY)
    count = len(results)
    return pl.pallas_call(
        functools.partial(hand_over_body, count),
        out_shape=[jax.ShapeDtypeStruct(r.shape, r.dtype) for r in results]
        + [jax.ShapeDtypeStruct(shape, jnp.float32) for shape in ((1, 1), (1, 144), (1, 144))],
        in_specs=[anywhere] * count + [vmem] * 2,
        out_specs=[anywhere] * count + [vmem] * 3,
        scratch_shapes=[pltpu.VMEM(r.shape, r.dtype) for r in results]
        + [pltpu.SemaphoreType.DMA((count,)), pltpu.SemaphoreType.DMA((count,))],
        compiler_params=pltpu.CompilerParams(vmem_limit_bytes=VMEM_MOST),
        name="hand_over",
    )(*results, totals, notes)


def per_device_fast(
    tokens, teacher, lengths, w_query, key_weight, value_weight, w_out, w_gate, w_up, w_down, gain_attn, gain_ffn
):
    slots, part, width = tokens.shape
    rows = slots * part
    total_tokens = slots * lax.axis_size("dp") * part * lax.axis_size("seq")
    positions = lax.axis_index("seq") * part + jnp.arange(part, dtype=jnp.int32)
    cosine, sine = rope_tables(positions, HEAD_DIMENSION)
    cosine_t = jnp.concatenate([cosine.T] * slots, axis=1)
    sine_t = jnp.concatenate([sine.T] * slots, axis=1)
    x_b = tokens.reshape(rows, width)
    gate_w, up_w, down_t, cat, attn_in_t, query, keys_values, attn, denom, notes, hidden = forward_call(
        lengths, (w_query.T, key_weight.T, value_weight.T, w_out.T),
        gain_attn, gain_ffn, x_b, cosine_t, sine_t,
        w_gate, w_up, w_down.T,
    )
    output, grad_hidden, small, gate_sums, up_sums, down_sums = ffn_call(
        float(total_tokens), lengths, hidden, teacher.reshape(rows, width), notes, gate_w, up_w, down_t
    )
    *results, totals, _ = backward_call(
        lengths, grad_hidden, cosine_t, sine_t, small, x_b, attn_in_t, cat, keys_values, query, attn, denom,
        gate_sums, up_sums, down_sums,
    )
    (
        output, own_gate, own_up, own_down_t, own_query_t, own_key_t, own_value_t, own_out_t, grad_tokens,
        loss, own_gain_a, own_gain_f,
    ) = hand_over([output] + results, totals, notes)
    return (
        output.reshape(tokens.shape),
        loss.reshape(()),
        grad_tokens.reshape(tokens.shape),
        own_query_t.T,
        own_key_t.T,
        own_value_t.T,
        own_out_t.T,
        own_gate,
        own_up,
        own_down_t.T,
        own_gain_a.reshape(-1),
        own_gain_f.reshape(-1),
    )


def solution(mesh):
    placed = (
        P("dp", "seq", None),
        P("dp", "seq", None),
        P("dp"),
        P("dp", "seq"),
        P("dp", "seq"),
        P("dp", "seq"),
        P("dp", "seq"),
        P("dp", "seq"),
        P("dp", "seq"),
        P("dp", "seq"),
        P("seq"),
        P("seq"),
    )
    fits = mesh.shape["dp"] == 4 and mesh.shape["seq"] == 8
    return jax.shard_map(
        per_device_fast if fits else per_device,
        mesh=mesh,
        in_specs=placed,
        out_specs=(
            P("dp", "seq", None),
            P(),
            P("dp", "seq", None),
            P("dp", "seq"),
            P("dp", "seq"),
            P("dp", "seq"),
            P("dp", "seq"),
            P("dp", "seq"),
            P("dp", "seq"),
            P("dp", "seq"),
            P("seq"),
            P("seq"),
        ),
        check_vma=False,
    )
```

```python
import functools
import math

import jax
import jax.numpy as jnp
from jax import lax
from jax.experimental import pallas as pl
from jax.experimental.pallas import tpu as pltpu
from jax.sharding import PartitionSpec as P

QUERY_HEADS = 18
KEY_VALUE_HEADS = 6
HEAD_DIMENSION = 64


norm_eps = 1e-05
rope_base = 10000.0


def rope_tables(positions, head_width):
    half_width = head_width // 2
    exponents = jnp.arange(half_width, dtype=jnp.float32) * (2.0 / head_width)
    angles = positions.astype(jnp.float32)[:, None] * (rope_base ** (-exponents))[None, :]
    return (jnp.cos(angles), jnp.sin(angles))


def apply_rotary(value_rows, cosine_table, sine_table):
    half_width = value_rows.shape[-1] // 2
    front_half = value_rows[..., :half_width]
    back_half = value_rows[..., half_width:]
    cos_wide = cosine_table[:, None, :]
    sin_wide = sine_table[:, None, :]
    return jnp.concatenate(
        [
            front_half * cos_wide - back_half * sin_wide,
            front_half * sin_wide + back_half * cos_wide,
        ],
        axis=-1,
    )


def allowed_mask(query_pos, key_pos, live_len):
    causal = key_pos[None, :] <= query_pos[:, None]
    present = key_pos[None, :] < live_len[:, None]
    return (causal[None, :, :] & present[:, None, :])[:, None, None, :, :]


def over_blocks(piece_len, unit_len, step_fn, running):
    block_length = math.gcd(piece_len, unit_len * max(1, 512 // unit_len))
    number_of_blocks = piece_len // block_length

    def loop_step(block_number, state):
        return step_fn(state, block_number * block_length, block_length)

    return lax.fori_loop(0, number_of_blocks, loop_step, running)


def collect(shards):
    wide = (
        lax.all_gather(shards[0], "seq", axis=1, tiled=True),
        lax.all_gather(shards[1], "seq", axis=1, tiled=True),
        lax.all_gather(shards[2], "seq", axis=1, tiled=True),
        lax.all_gather(shards[3], "seq", axis=1, tiled=True),
        lax.all_gather(shards[4], "seq", axis=1, tiled=True),
        lax.all_gather(shards[5], "seq", axis=1, tiled=True),
        lax.all_gather(shards[6], "seq", axis=1, tiled=True),
        lax.all_gather(shards[7], "seq", axis=0, tiled=True),
        lax.all_gather(shards[8], "seq", axis=0, tiled=True),
    )
    whole = (
        lax.all_gather(wide[0], "dp", axis=0, tiled=True),
        lax.all_gather(wide[1], "dp", axis=0, tiled=True),
        lax.all_gather(wide[2], "dp", axis=0, tiled=True),
        lax.all_gather(wide[3], "dp", axis=0, tiled=True),
        lax.all_gather(wide[4], "dp", axis=0, tiled=True),
        lax.all_gather(wide[5], "dp", axis=0, tiled=True),
        lax.all_gather(wide[6], "dp", axis=0, tiled=True),
    )
    return tuple(whole) + (wide[7], wide[8])


def reduce_grads(grad_sums):
    summed = (
        lax.psum_scatter(grad_sums[0], "seq", scatter_dimension=1, tiled=True),
        lax.psum_scatter(grad_sums[1], "seq", scatter_dimension=1, tiled=True),
        lax.psum_scatter(grad_sums[2], "seq", scatter_dimension=1, tiled=True),
        lax.psum_scatter(grad_sums[3], "seq", scatter_dimension=1, tiled=True),
        lax.psum_scatter(grad_sums[4], "seq", scatter_dimension=1, tiled=True),
        lax.psum_scatter(grad_sums[5], "seq", scatter_dimension=1, tiled=True),
        lax.psum_scatter(grad_sums[6], "seq", scatter_dimension=1, tiled=True),
        lax.psum_scatter(grad_sums[7], "seq", scatter_dimension=0, tiled=True),
        lax.psum_scatter(grad_sums[8], "seq", scatter_dimension=0, tiled=True),
    )
    owned = (
        lax.psum_scatter(summed[0], "dp", scatter_dimension=0, tiled=True),
        lax.psum_scatter(summed[1], "dp", scatter_dimension=0, tiled=True),
        lax.psum_scatter(summed[2], "dp", scatter_dimension=0, tiled=True),
        lax.psum_scatter(summed[3], "dp", scatter_dimension=0, tiled=True),
        lax.psum_scatter(summed[4], "dp", scatter_dimension=0, tiled=True),
        lax.psum_scatter(summed[5], "dp", scatter_dimension=0, tiled=True),
        lax.psum_scatter(summed[6], "dp", scatter_dimension=0, tiled=True),
    )
    return (tuple(owned), summed[7], summed[8])


def forward_slot(weights, tok_part, live_len, query_pos, cosine_table, sine_table):
    (
        full_query,
        full_key,
        full_value,
        full_out,
        full_gate,
        full_up,
        full_down,
        full_gain_attn,
        full_gain_ffn,
    ) = weights
    slot_position, stretched_length, model_width = tok_part.shape
    number_of_rows = slot_position * stretched_length
    query_group = QUERY_HEADS // KEY_VALUE_HEADS
    scale = HEAD_DIMENSION ** (-0.5)
    tok_float = tok_part.astype(jnp.float32).reshape(number_of_rows, model_width)
    inv_first = lax.rsqrt(jnp.mean(tok_float * tok_float, axis=-1, keepdims=True) + norm_eps)
    normed_first = tok_float * inv_first
    attention_input = (normed_first * full_gain_attn.astype(jnp.float32)).astype(jnp.bfloat16)
    unrotated_query = jnp.dot(
        attention_input, full_query, preferred_element_type=jnp.float32
    ).reshape(slot_position, stretched_length, QUERY_HEADS, HEAD_DIMENSION)
    unrotated_key = jnp.dot(attention_input, full_key, preferred_element_type=jnp.float32).reshape(
        slot_position, stretched_length, KEY_VALUE_HEADS, HEAD_DIMENSION
    )
    value_block = (
        jnp.dot(attention_input, full_value, preferred_element_type=jnp.float32)
        .astype(jnp.bfloat16)
        .reshape(slot_position, stretched_length, KEY_VALUE_HEADS * HEAD_DIMENSION)
    )
    query_b = (
        apply_rotary(unrotated_query, cosine_table, sine_table)
        .astype(jnp.bfloat16)
        .reshape(slot_position, stretched_length, KEY_VALUE_HEADS, query_group, HEAD_DIMENSION)
    )
    key_block = (
        apply_rotary(unrotated_key, cosine_table, sine_table)
        .astype(jnp.bfloat16)
        .reshape(slot_position, stretched_length, KEY_VALUE_HEADS * HEAD_DIMENSION)
    )
    empty_denominator = jnp.zeros(
        (slot_position, KEY_VALUE_HEADS, query_group, stretched_length), jnp.float32
    )
    empty_numerator = jnp.zeros(
        (slot_position, KEY_VALUE_HEADS, query_group, stretched_length, HEAD_DIMENSION), jnp.float32
    )
    key_piece = lax.all_gather(key_block, "seq", axis=1, tiled=True)
    value_piece = lax.all_gather(value_block, "seq", axis=1, tiled=True)

    def one_block(partial_value, offset, block_length):
        denominator, numerator = partial_value
        key_blk = lax.dynamic_slice_in_dim(key_piece, offset, block_length, 1).reshape(
            slot_position, block_length, KEY_VALUE_HEADS, HEAD_DIMENSION
        )
        value_blk = lax.dynamic_slice_in_dim(value_piece, offset, block_length, 1).reshape(
            slot_position, block_length, KEY_VALUE_HEADS, HEAD_DIMENSION
        )
        allowed = allowed_mask(
            query_pos, offset + jnp.arange(block_length, dtype=jnp.int32), live_len
        )
        scores = (
            jnp.einsum("schgd,snhd->shgcn", query_b, key_blk, preferred_element_type=jnp.float32)
            * scale
        )
        exp_scores = jnp.where(allowed, jnp.exp(scores), 0.0)
        denominator = denominator + jnp.sum(exp_scores, axis=-1)
        numerator = numerator + jnp.einsum(
            "shgcn,snhd->shgcd",
            exp_scores.astype(jnp.bfloat16),
            value_blk,
            preferred_element_type=jnp.float32,
        )
        return (denominator, numerator)

    denominator, numerator = over_blocks(
        key_piece.shape[1], stretched_length, one_block, (empty_denominator, empty_numerator)
    )
    attn_float = jnp.transpose(numerator / denominator[..., None], (0, 3, 1, 2, 4)).reshape(
        number_of_rows, QUERY_HEADS * HEAD_DIMENSION
    )
    attn_b = attn_float.astype(jnp.bfloat16)
    hidden = tok_float + jnp.dot(attn_b, full_out, preferred_element_type=jnp.float32)
    inv_second = lax.rsqrt(jnp.mean(hidden * hidden, axis=-1, keepdims=True) + norm_eps)
    normed_second = hidden * inv_second
    ffn_in = (normed_second * full_gain_ffn.astype(jnp.float32)).astype(jnp.bfloat16)
    gate_proj = jnp.dot(ffn_in, full_gate, preferred_element_type=jnp.float32)
    up_proj = jnp.dot(ffn_in, full_up, preferred_element_type=jnp.float32)
    hid_b = (jax.nn.silu(gate_proj) * up_proj).astype(jnp.bfloat16)
    valid_rows = (query_pos[None, :] < live_len[:, None]).reshape(number_of_rows, 1)
    out_float = jnp.where(
        valid_rows, hidden + jnp.dot(hid_b, full_down, preferred_element_type=jnp.float32), 0.0
    )
    saved = (
        attention_input,
        inv_first,
        normed_first,
        query_b,
        key_block,
        value_block,
        attn_float,
        attn_b,
        denominator,
        normed_second,
        inv_second,
        ffn_in,
        gate_proj,
        up_proj,
        hid_b,
    )
    return (out_float, valid_rows, saved)


def backward_slot(weights, saved, cotangent, live_len, query_pos, cosine_table, sine_table):
    (
        full_query,
        full_key,
        full_value,
        full_out,
        full_gate,
        full_up,
        full_down,
        full_gain_attn,
        full_gain_ffn,
    ) = weights
    (
        attention_input,
        inv_first,
        normed_first,
        query_b,
        key_block,
        value_block,
        attn_float,
        attn_b,
        denominator,
        normed_second,
        inv_second,
        ffn_in,
        gate_proj,
        up_proj,
        hid_b,
    ) = saved
    slot_position = query_b.shape[0]
    stretched_length = query_b.shape[1]
    number_of_rows = slot_position * stretched_length
    query_group = QUERY_HEADS // KEY_VALUE_HEADS
    scale = HEAD_DIMENSION ** (-0.5)
    cot_b = cotangent.astype(jnp.bfloat16)
    grad_down = jnp.einsum("rf,rd->fd", hid_b, cot_b, preferred_element_type=jnp.float32)
    grad_hid = jnp.einsum("rd,fd->rf", cot_b, full_down, preferred_element_type=jnp.float32)
    sigmoid_gate = jax.nn.sigmoid(gate_proj)
    grad_gate_b = (
        grad_hid * up_proj * sigmoid_gate * (1.0 + gate_proj * (1.0 - sigmoid_gate))
    ).astype(jnp.bfloat16)
    grad_up_b = (grad_hid * gate_proj * sigmoid_gate).astype(jnp.bfloat16)
    grad_gate = jnp.einsum("rd,rf->df", ffn_in, grad_gate_b, preferred_element_type=jnp.float32)
    grad_up = jnp.einsum("rd,rf->df", ffn_in, grad_up_b, preferred_element_type=jnp.float32)
    grad_ffn_in = jnp.einsum(
        "rf,df->rd", grad_gate_b, full_gate, preferred_element_type=jnp.float32
    ) + jnp.einsum("rf,df->rd", grad_up_b, full_up, preferred_element_type=jnp.float32)
    grad_gain_ffn = jnp.sum(grad_ffn_in * normed_second, axis=0)
    grad_normed = grad_ffn_in * full_gain_ffn.astype(jnp.float32)
    grad_hidden = cotangent + inv_second * (
        grad_normed - normed_second * jnp.mean(grad_normed * normed_second, axis=-1, keepdims=True)
    )
    grad_proj_b = grad_hidden.astype(jnp.bfloat16)
    grad_out = jnp.einsum("rq,rd->qd", attn_b, grad_proj_b, preferred_element_type=jnp.float32)
    grad_attn_b = jnp.einsum(
        "rd,qd->rq", grad_proj_b, full_out, preferred_element_type=jnp.float32
    ).astype(jnp.bfloat16)
    den_rows = jnp.transpose(denominator, (0, 3, 1, 2)).reshape(number_of_rows, QUERY_HEADS)
    grad_heads_float = grad_attn_b.astype(jnp.float32).reshape(
        number_of_rows, QUERY_HEADS, HEAD_DIMENSION
    )
    softmax_ratio = (
        jnp.sum(
            grad_heads_float * attn_float.reshape(number_of_rows, QUERY_HEADS, HEAD_DIMENSION),
            axis=-1,
        )
        / den_rows
    ).reshape(slot_position, stretched_length, QUERY_HEADS)
    scaled_gradient = (
        (grad_heads_float / den_rows[..., None])
        .astype(jnp.bfloat16)
        .reshape(slot_position, stretched_length, QUERY_HEADS * HEAD_DIMENSION)
    )
    ratio_all = lax.all_gather(softmax_ratio, "seq", axis=1, tiled=True)
    head_gradient = scaled_gradient.reshape(
        slot_position, stretched_length, KEY_VALUE_HEADS, query_group, HEAD_DIMENSION
    )
    local_softmax_ratio = jnp.transpose(
        softmax_ratio.reshape(slot_position, stretched_length, KEY_VALUE_HEADS, query_group),
        (0, 2, 3, 1),
    )[..., None]
    empty_query = jnp.zeros(
        (slot_position, KEY_VALUE_HEADS, query_group, stretched_length, HEAD_DIMENSION), jnp.float32
    )
    key_piece = lax.all_gather(key_block, "seq", axis=1, tiled=True)
    value_piece = lax.all_gather(value_block, "seq", axis=1, tiled=True)

    def one_block(partial_value, offset, block_length):
        key_blk = lax.dynamic_slice_in_dim(key_piece, offset, block_length, 1).reshape(
            slot_position, block_length, KEY_VALUE_HEADS, HEAD_DIMENSION
        )
        value_blk = lax.dynamic_slice_in_dim(value_piece, offset, block_length, 1).reshape(
            slot_position, block_length, KEY_VALUE_HEADS, HEAD_DIMENSION
        )
        allowed = allowed_mask(
            query_pos, offset + jnp.arange(block_length, dtype=jnp.int32), live_len
        )
        scores = (
            jnp.einsum("schgd,snhd->shgcn", query_b, key_blk, preferred_element_type=jnp.float32)
            * scale
        )
        exp_scores = jnp.where(allowed, jnp.exp(scores), 0.0)
        grad_prob = jnp.einsum(
            "schgd,snhd->shgcn", head_gradient, value_blk, preferred_element_type=jnp.float32
        )
        grad_score = (exp_scores * (grad_prob - local_softmax_ratio)).astype(jnp.bfloat16)
        return (
            partial_value
            + jnp.einsum(
                "shgcn,snhd->shgcd", grad_score, key_blk, preferred_element_type=jnp.float32
            )
            * scale
        )

    grad_query = over_blocks(key_piece.shape[1], stretched_length, one_block, empty_query)
    query_flat = query_b.reshape(slot_position, stretched_length, QUERY_HEADS * HEAD_DIMENSION)
    per_head_keys = key_block.reshape(
        slot_position, stretched_length, KEY_VALUE_HEADS, HEAD_DIMENSION
    )
    per_head_values = value_block.reshape(
        slot_position, stretched_length, KEY_VALUE_HEADS, HEAD_DIMENSION
    )
    empty_key_value = jnp.zeros(
        (slot_position, KEY_VALUE_HEADS, stretched_length, HEAD_DIMENSION), jnp.float32
    )
    query_piece = lax.all_gather(query_flat, "seq", axis=1, tiled=True)
    grad_piece = lax.all_gather(scaled_gradient, "seq", axis=1, tiled=True)

    def one_block(partial_value, offset, block_length):
        grad_key, value_gradient = partial_value
        query_blk = lax.dynamic_slice_in_dim(query_piece, offset, block_length, 1).reshape(
            slot_position, block_length, KEY_VALUE_HEADS, query_group, HEAD_DIMENSION
        )
        grad_blk = lax.dynamic_slice_in_dim(grad_piece, offset, block_length, 1).reshape(
            slot_position, block_length, KEY_VALUE_HEADS, query_group, HEAD_DIMENSION
        )
        ratio_blk = lax.dynamic_slice_in_dim(ratio_all, offset, block_length, 1).reshape(
            slot_position, block_length, KEY_VALUE_HEADS, query_group
        )
        ratio_blk = jnp.transpose(ratio_blk, (0, 2, 3, 1))[..., None]
        remote_pos = offset + jnp.arange(block_length, dtype=jnp.int32)
        allowed = allowed_mask(remote_pos, query_pos, live_len)
        scores = (
            jnp.einsum(
                "snhgd,schd->shgnc", query_blk, per_head_keys, preferred_element_type=jnp.float32
            )
            * scale
        )
        exp_scores = jnp.where(allowed, jnp.exp(scores), 0.0)
        value_gradient = value_gradient + jnp.einsum(
            "shgnc,snhgd->shcd",
            exp_scores.astype(jnp.bfloat16),
            grad_blk,
            preferred_element_type=jnp.float32,
        )
        grad_prob = jnp.einsum(
            "snhgd,schd->shgnc", grad_blk, per_head_values, preferred_element_type=jnp.float32
        )
        grad_score = (exp_scores * (grad_prob - ratio_blk)).astype(jnp.bfloat16)
        grad_key = (
            grad_key
            + jnp.einsum(
                "shgnc,snhgd->shcd", grad_score, query_blk, preferred_element_type=jnp.float32
            )
            * scale
        )
        return (grad_key, value_gradient)

    grad_key, value_gradient = over_blocks(
        query_piece.shape[1], stretched_length, one_block, (empty_key_value, empty_key_value)
    )
    grad_query = jnp.transpose(grad_query, (0, 3, 1, 2, 4)).reshape(
        slot_position, stretched_length, QUERY_HEADS, HEAD_DIMENSION
    )
    grad_query_b = (
        apply_rotary(grad_query, cosine_table, -sine_table)
        .astype(jnp.bfloat16)
        .reshape(number_of_rows, QUERY_HEADS * HEAD_DIMENSION)
    )
    grad_key_b = (
        apply_rotary(jnp.transpose(grad_key, (0, 2, 1, 3)), cosine_table, -sine_table)
        .astype(jnp.bfloat16)
        .reshape(number_of_rows, KEY_VALUE_HEADS * HEAD_DIMENSION)
    )
    grad_value_b = (
        jnp.transpose(value_gradient, (0, 2, 1, 3))
        .astype(jnp.bfloat16)
        .reshape(number_of_rows, KEY_VALUE_HEADS * HEAD_DIMENSION)
    )
    grad_wq = jnp.einsum(
        "rd,rq->dq", attention_input, grad_query_b, preferred_element_type=jnp.float32
    )
    grad_wk = jnp.einsum(
        "rd,rq->dq", attention_input, grad_key_b, preferred_element_type=jnp.float32
    )
    grad_wv = jnp.einsum(
        "rd,rq->dq", attention_input, grad_value_b, preferred_element_type=jnp.float32
    )
    grad_attn_in = jnp.einsum(
        "rq,dq->rd", grad_query_b, full_query, preferred_element_type=jnp.float32
    )
    grad_attn_in = grad_attn_in + jnp.einsum(
        "rq,dq->rd", grad_key_b, full_key, preferred_element_type=jnp.float32
    )
    grad_attn_in = grad_attn_in + jnp.einsum(
        "rq,dq->rd", grad_value_b, full_value, preferred_element_type=jnp.float32
    )
    grad_gain_attn = jnp.sum(grad_attn_in * normed_first, axis=0)
    grad_first = grad_attn_in * full_gain_attn.astype(jnp.float32)
    grad_tokens = grad_hidden + inv_first * (
        grad_first - normed_first * jnp.mean(grad_first * normed_first, axis=-1, keepdims=True)
    )
    return (
        (
            grad_wq,
            grad_wk,
            grad_wv,
            grad_out,
            grad_gate,
            grad_up,
            grad_down,
            grad_gain_attn,
            grad_gain_ffn,
        ),
        grad_tokens,
    )


def per_device(
    tokens,
    teacher,
    lengths,
    w_query,
    key_weight,
    value_weight,
    w_out,
    w_gate,
    w_up,
    w_down,
    gain_attn,
    gain_ffn,
):
    shards = (w_query, key_weight, value_weight, w_out, w_gate, w_up, w_down, gain_attn, gain_ffn)
    slot_count, stretched_length, model_width = tokens.shape
    total_tokens = slot_count * lax.axis_size("dp") * stretched_length * lax.axis_size("seq")
    query_pos = lax.axis_index("seq") * stretched_length + jnp.arange(
        stretched_length, dtype=jnp.int32
    )
    cosine_table, sine_table = rope_tables(query_pos, HEAD_DIMENSION)
    out_rows = []
    stored = []
    differences = []
    squares_local = jnp.zeros((), jnp.float32)
    count_local = jnp.zeros((), jnp.float32)
    for micro in range(slot_count):
        weights = collect(shards)
        live_len = lengths[micro : micro + 1]
        out_float, valid_rows, saved = forward_slot(
            weights, tokens[micro : micro + 1], live_len, query_pos, cosine_table, sine_table
        )
        teach_float = teacher[micro].astype(jnp.float32)
        difference = jnp.where(valid_rows, out_float - teach_float, 0.0)
        squares_local = squares_local + jnp.sum(difference * difference)
        count_local = count_local + jnp.sum(valid_rows.astype(jnp.float32))
        out_rows.append(out_float.astype(jnp.bfloat16).reshape(1, stretched_length, model_width))
        stored.append(saved)
        differences.append(difference)
    loss_sum, count_sum = lax.psum((squares_local, count_local), ("dp", "seq"))
    loss = loss_sum / count_sum
    factor = total_tokens / count_sum
    grad_sums = None
    token_grads = []
    for micro in range(slot_count):
        weights = collect(shards)
        grads, grad_tokens = backward_slot(
            weights,
            stored[micro],
            factor * differences[micro],
            lengths[micro : micro + 1],
            query_pos,
            cosine_table,
            sine_table,
        )
        grad_sums = grads if grad_sums is None else jax.tree.map(jnp.add, grad_sums, grads)
        token_grads.append(grad_tokens.reshape(1, stretched_length, model_width))
    owned, gain_part_attn, gain_part_ffn = reduce_grads(grad_sums)
    gain_totals = lax.psum((gain_part_attn, gain_part_ffn), "dp")
    output = jnp.concatenate(out_rows, axis=0)
    tokens_grad = jnp.concatenate(token_grads, axis=0)
    return (
        output,
        loss,
        tokens_grad,
        owned[0],
        owned[1],
        owned[2],
        owned[3],
        owned[4],
        owned[5],
        owned[6],
        gain_totals[0],
        gain_totals[1],
    )


MESH_ID = pl.DeviceIdType.MESH
VMEM_MOST = 64 * 1024 * 1024 - 128 * 1024


class Place(tuple):
    def with_line(self):
        z = self[2]
        self.line = (0,) + tuple(pick(z, v) for v in ((1, -1, -1, -1), (2, 1, 1, -2), (3, 2, -2, -3)))
        self.sign = (0,) + tuple(jnp.where(offset > 0, 1, -1) for offset in self.line[1:])
        return self


def position():
    row = lax.axis_index("dp")
    column = lax.axis_index("seq")
    return Place((lax.rem(column, 2), row // 2, column // 2, lax.rem(row, 2))).with_line()


def mesh_place(x, y, z, c):
    return (2 * y + c, 2 * z + x)


def step_to(place, axis, sign=1):
    x, y, z, c = place
    if axis == "x":
        return (1 - x, y, z, c)
    if axis == "y":
        return (x, 1 - y, z, c)
    if axis == "z":
        return (x, y, z + sign, c)
    return (x, y, z, 1 - c)


def pick(z, values):
    return sum(jnp.where(z == i, v, 0) for i, v in enumerate(values) if v)


def shifted(place, rel):
    x, y, z, c = place
    dx, dy, rank = rel
    return ((1 - x) if dx else x, (1 - y) if dy else y, z + place.line[rank], c)


def on_line(z):
    return jnp.logical_and(z >= 0, z < 4)


def greet(place, lines):
    x, y, z, c = place
    d, s = mesh_place(*place)
    barrier = pltpu.get_barrier_semaphore()

    def signal(who):
        pl.semaphore_signal(barrier, inc=1, device_id=who, device_id_type=MESH_ID)

    if lines:
        for k in range(1, 8):
            signal((d, lax.rem(s + k, 8)))
        for k in range(1, 4):
            signal((lax.rem(d + k, 4), s))
        pl.semaphore_wait(barrier, 10)
        return
    for axis in "xyc":
        signal(mesh_place(*step_to(place, axis)))
    pl.when(z < 3)(lambda: signal(mesh_place(x, y, z + 1, c)))
    pl.when(z > 0)(lambda: signal(mesh_place(x, y, z - 1, c)))
    pl.semaphore_wait(barrier, 3 + jnp.where(z > 0, 1, 0) + jnp.where(z < 3, 1, 0))


def wait_bytes(region, sem):
    pltpu.make_async_copy(region, region, sem).wait()


def spread_order(order):
    held = [((0, 0, 0), -1)]
    for level, axis in enumerate(order):
        new = []
        if axis == "z":
            new = [((rel[0], rel[1], rank), level) for rank in (1, 2, 3) for rel, _ in held]
        else:
            new = [((1, rel[1], rel[2]) if axis == "x" else (rel[0], 1, rel[2]), level) for rel, _ in held]
        held = held + new
    return held


class Spread:
    def __init__(self, place, order, own, spot, sems, job, pair=None, amount=None):
        self.place, self.order, self.own, self.spot = place, order, own, spot
        self.recv, self.send, self.recv_core, self.send_core = sems
        self.job, self.pair, self.amount = job, pair, amount
        self.pieces = spread_order(order)

    def number(self, who):
        x, y, z, _ = who
        return z * 4 + y * 2 + x

    def go(self, rel, level, target):
        who = shifted(self.place, rel)
        pltpu.make_async_remote_copy(
            src_ref=self.own if level < 0 else self.spot(who),
            dst_ref=self.spot(who),
            send_sem=self.send.at[self.job],
            recv_sem=self.recv.at[self.job, self.number(who)],
            device_id=mesh_place(*target),
            device_id_type=MESH_ID,
        ).start()

    def to_core(self, rel):
        who = shifted(self.place, rel)
        pltpu.make_async_remote_copy(
            src_ref=self.pair(who),
            dst_ref=self.pair(who),
            send_sem=self.send_core.at[self.job],
            recv_sem=self.recv_core.at[self.job],
            device_id=mesh_place(*step_to(self.place, "c")),
            device_id_type=MESH_ID,
        ).start()

    def steps(self):
        out = []
        arrived = set()
        z = self.place[2]
        for rel, level in self.pieces:

            def run(rel=rel, level=level):
                arrived.add(rel)
                who = shifted(self.place, rel)
                if level >= 0:
                    there = self.spot(who)
                    pltpu.make_async_copy(there, there, self.recv.at[self.job, self.number(who)]).wait()
                if level >= 0 and self.order[level] == "z":
                    on = z - self.place.sign[rel[2]]
                    pl.when(on_line(on))(lambda: self.go(rel, level, (self.place[0], self.place[1], on, self.place[3])))
                for axis in self.order[level + 1:]:
                    if axis == "z":
                        pl.when(z < 3)(lambda: self.go(rel, level, step_to(self.place, "z", 1)))
                        pl.when(z > 0)(lambda: self.go(rel, level, step_to(self.place, "z", -1)))
                    else:
                        self.go(rel, level, step_to(self.place, axis))
                if self.pair is not None and (1 - rel[0], rel[1], rel[2]) in arrived:
                    self.to_core(rel)

            out.append(run)
        return out

    def sent(self):
        total = [0, 0]
        for i, z in enumerate((0, 1)):
            for rel, level in self.pieces:
                if level >= 0 and self.order[level] == "z":
                    offset = (0, ((1, -1)[z]), ((2, 1)[z]), ((3, 2)[z]))[rel[2]]
                    on = z - (1 if offset > 0 else -1)
                    total[i] += 0 <= on < 4
                for axis in self.order[level + 1:]:
                    total[i] += (1, 2)[z] if axis == "z" else 1
        return total

    def wait_core(self):
        wait_bytes(self.amount(16), self.recv_core.at[self.job])

    def finish(self):
        ends, inner = self.sent()
        z = self.place[2]
        at_end = jnp.logical_or(z == 0, z == 3)
        pl.when(at_end)(lambda: wait_bytes(self.amount(ends), self.send.at[self.job]))
        pl.when(jnp.logical_not(at_end))(lambda: wait_bytes(self.amount(inner), self.send.at[self.job]))
        if self.pair is not None:
            wait_bytes(self.amount(16), self.send_core.at[self.job])


def fold_pieces(order):
    out = []
    for dx in (0, 1):
        for dy in (0, 1) if "y" in order else (0,):
            for rank in (0, 1, 2, 3):
                differs = {"x": dx, "y": dy, "z": rank}
                stage = next((i for i, axis in enumerate(order) if differs[axis]), len(order))
                out.append(((dx, dy, rank), stage))
    return sorted(out, key=lambda item: (item[1], -item[0][2], -item[0][0] - item[0][1]))


def fold_slots(order):
    base, starts = 0, []
    for level, axis in enumerate(order):
        starts.append(base)
        after = order[level + 1:]
        wide = (4 if "z" in after else 1) * (2 if "x" in after else 1) * (2 if "y" in after else 1)
        base += wide * 5 if axis == "z" else wide
    return starts, base


class Fold:
    def __init__(self, place, order, mine, arrived, sems, job, out, amount, ready=None):
        self.place, self.order, self.mine, self.arrived = place, order, mine, arrived
        self.send, self.recv = sems
        self.job, self.out, self.amount, self.ready = job, out, amount, ready
        self.pieces = fold_pieces(order)
        self.base, self.slots = fold_slots(order)

    def slot(self, level, rel, last):
        index = 0
        at_z = self.place[2] + self.place.line[rel[2]]
        for other in self.order[level + 1:]:
            size = 4 if other == "z" else 2
            index = index * size + (at_z if other == "z" else (rel[0] if other == "x" else rel[1]))
        if self.order[level] == "z":
            index = index * 5 + (4 if last is True else (at_z if last is False else jnp.where(last, 4, at_z)))
        return self.base[level] + index

    def take(self, mine, slot):
        there = self.arrived.at[slot]
        pltpu.make_async_copy(there, there, self.recv.at[self.job, slot]).wait()
        mine[...] = mine[...] + self.arrived[slot]

    def steps(self):
        out = []
        present = set()
        z = self.place[2]
        for rel, stage in self.pieces:

            def run(rel=rel, stage=stage):
                if self.ready is not None and rel[1] not in present:
                    present.add(rel[1])
                    self.ready(rel[1])
                mine = self.mine(shifted(self.place, rel))
                offset, sign = self.place.line[rel[2]], self.place.sign[rel[2]]
                for level in range(min(stage + 1, len(self.order))):
                    if self.order[level] == "z":
                        if level < stage:
                            pl.when(z > 0)(lambda: self.take(mine, self.slot(level, rel, False)))
                            pl.when(z < 3)(lambda: self.take(mine, self.slot(level, rel, True)))
                        else:
                            behind = z - sign
                            pl.when(on_line(behind))(lambda: self.take(mine, self.slot(level, rel, False)))
                    elif level < stage:
                        self.take(mine, self.slot(level, rel, False))
                if stage == len(self.order):
                    self.out(mine[...].astype(jnp.float32))
                    return
                axis = self.order[stage]
                if axis == "z":
                    target = (self.place[0], self.place[1], z + sign, self.place[3])
                else:
                    target = step_to(self.place, axis)
                slot = self.slot(stage, rel, offset == -1 if axis == "z" else False)
                pltpu.make_async_remote_copy(
                    src_ref=mine,
                    dst_ref=self.arrived.at[slot],
                    send_sem=self.send.at[self.job],
                    recv_sem=self.recv.at[self.job, slot],
                    device_id=mesh_place(*target),
                    device_id_type=MESH_ID,
                ).start()

            out.append(run)
        return out

    def finish(self):
        wait_bytes(self.amount(len(self.pieces) - 1), self.send.at[self.job])


CAT_JOBS = (("cat", 0, 96, "xzy"), ("cat", 96, 96, "yzx"), ("cat", 192, 96, "zxy"))
FFN_JOBS = (
    ("gate", 0, 144, "xzy"), ("up", 0, 96, "yzx"), ("down", 0, 384, "zxy"),
    ("gate", 144, 144, "xzy"), ("up", 96, 96, "yzx"), ("down", 384, 384, "zxy"), ("up", 192, 96, "zyx"),
)
KV_JOBS = tuple((slot, 256 * third, "zx") for slot in (0, 1) for third in (0, 1, 2))
FOLD_FFN = tuple(job[:3] + (job[3][::-1],) for job in FFN_JOBS)
FOLD_CAT = tuple(job[:3] + (job[3][::-1],) for job in CAT_JOBS)
FOLD_KV = tuple((slot, row, order[::-1]) for slot, row, order in KV_JOBS)
FFN_NAMES = ("gate", "up", "down")


def job_shape(job):
    return (144, job[2]) if job[0] == "down" else (job[2], 384)


def piece_of(ref, job, paired=False):
    name, first, count, _ = job
    double = 2 if paired else 1

    def spot(who):
        x, y, z, c = who
        d, s = mesh_place(0 if paired else x, y, z, c)
        if name == "down":
            return ref.at[
                pl.ds(pl.multiple_of(s * 144, 16), 144 * double), pl.ds(pl.multiple_of(d * 768 + first, 128), count)
            ]
        return ref.at[
            pl.ds(pl.multiple_of(d * 288 + first, 8), count), pl.ds(pl.multiple_of(s * 384, 128), 384 * double)
        ]

    return spot


def region(ref, elements, rows, columns):
    units = elements // 2048
    wide = max(k for k in range(1, columns // 128 + 1) if units % k == 0 and units // k <= rows // 16)
    return ref.at[pl.ds(0, units // wide * 16), pl.ds(0, wide * 128)]


def amount_of(ref, job):
    rows, columns = job_shape(job)
    return lambda pieces: region(ref, pieces * rows * columns, *ref.shape)


def own_part(ref, job):
    name, first, count, _ = job
    return ref.at[:, pl.ds(first, count)] if name == "down" else ref.at[pl.ds(first, count), :]


def kv_spot(ref, slot, row):
    def spot(who):
        _, s = mesh_place(*who)
        return ref.at[slot, pl.ds(row, 256), pl.ds(pl.multiple_of(s * 128, 128), 128)]

    return spot


def kv_amount(ref):
    return lambda pieces: ref.at[0, pl.ds(0, 32 * pieces), :]


def make_spreads(place, jobs, shards, wholes, sems):
    return [
        Spread(
            place, job[3], own_part(shards[job[0]], job), piece_of(wholes[job[0]], job), sems, j,
            piece_of(wholes[job[0]], job, True), amount_of(wholes[job[0]], job),
        )
        for j, job in enumerate(jobs)
    ]


def make_kv_spreads(place, own, whole, sems):
    return [
        Spread(
            place, order, own.at[pl.ds(row, 256), pl.ds(slot * 128, 128)], kv_spot(whole, slot, row),
            (sems[0], sems[1], None, None), j, None, kv_amount(whole),
        )
        for j, (slot, row, order) in enumerate(KV_JOBS)
    ]


def spread_sems(jobs):
    n = len(jobs)
    return [
        pltpu.SemaphoreType.DMA((n, 16)), pltpu.SemaphoreType.DMA((n,)),
        pltpu.SemaphoreType.DMA((n,)), pltpu.SemaphoreType.DMA((n,)),
    ]


def fold_scratch(jobs, paired):
    n = len(jobs)
    most = max(fold_slots(job[3])[1] for job in jobs)
    scratch = [
        pltpu.SemaphoreType.DMA((n,)), pltpu.SemaphoreType.DMA((n, most)),
        pltpu.SemaphoreType.DMA((n, 2)), pltpu.SemaphoreType.DMA((n, 2)), pltpu.SemaphoreType.DMA((n, 2)),
    ]
    for job in jobs:
        rows, columns = job_shape(job)
        block = (2, 1152, columns) if job[0] == "down" else (2, rows, 3072)
        scratch += [
            pltpu.VMEM(block, jnp.bfloat16), pltpu.VMEM((fold_slots(job[3])[1], rows, columns), jnp.bfloat16)
        ]
        scratch += [pltpu.VMEM(block, jnp.bfloat16)] if paired else []
    return scratch


class JobFold:
    def __init__(self, place, job, j, sums, owned, scratch, paired):
        self.place, self.job, self.j, self.sums, self.paired = place, job, j, sums, paired
        send, recv, self.load_sem, self.core_send, self.core_recv = scratch[:5]
        each = 3 if paired else 2
        self.acc, arrived = scratch[5 + each * j: 7 + each * j]
        self.other = scratch[7 + each * j] if paired else None
        name, first, count, order = job

        def mine(who):
            x, y, z, c = who
            s = 2 * z + x
            if name == "down":
                return self.acc.at[y, pl.ds(pl.multiple_of(s * 144, 16), 144), :]
            return self.acc.at[y, :, pl.ds(pl.multiple_of(s * 384, 128), 384)]

        def out(value):
            if name == "down":
                owned[:, first: first + count] = value
            else:
                owned[first: first + count, :] = value

        self.fold = Fold(place, order, mine, arrived, (send, recv), j, out, amount_of(sums, job), self.ready)

    def block(self, y, c):
        name, first, count, _ = self.job
        d = 2 * y + c if self.paired else y
        if name == "down":
            return self.sums.at[:, pl.ds(pl.multiple_of(d * 768 + first, 128), count)]
        return self.sums.at[pl.ds(pl.multiple_of(d * 288 + first, 8), count), :]

    def local_copy(self, dy):
        x, y, z, c = self.place
        at = (1 - y) if dy else y
        return pltpu.make_async_copy(self.block(at, c), self.acc.at[at], self.load_sem.at[self.j, dy])

    def core_copy(self, dy):
        x, y, z, c = self.place
        at = (1 - y) if dy else y
        return pltpu.make_async_remote_copy(
            src_ref=self.block(at, 1 - c),
            dst_ref=self.other.at[at],
            send_sem=self.core_send.at[self.j, dy],
            recv_sem=self.core_recv.at[self.j, dy],
            device_id=mesh_place(x, y, z, 1 - c),
            device_id_type=MESH_ID,
        )

    def begin(self, dy):
        if self.paired:
            self.core_copy(dy).start()
        self.local_copy(dy).start()

    def ready(self, dy):
        y = self.place[1]
        at = (1 - y) if dy else y
        self.local_copy(dy).wait()
        if not self.paired:
            return
        self.core_copy(dy).wait_recv()

        def add(k, _):
            if self.job[0] == "down":
                part = (at, pl.ds(pl.multiple_of(k * 144, 16), 144), slice(None))
            else:
                part = (at, slice(None), pl.ds(pl.multiple_of(k * 384, 128), 384))
            self.acc[part] = self.acc[part] + self.other[part]
            return _

        lax.fori_loop(0, 8, add, 0)

    def finish(self):
        self.fold.finish()
        for dy in (0, 1) if self.paired else ():
            self.core_copy(dy).wait_send()


class Notes:
    def __init__(self, place, tile_of, own, by_seq, by_dp, sems):
        self.d, self.s = mesh_place(*place)
        self.tile_of, self.own, self.by_seq, self.by_dp = tile_of, own, by_seq, by_dp
        self.seq_send, self.seq_recv, self.dp_send, self.dp_recv = sems

    def along_seq(self, k):
        peer = lax.rem(self.s + k, 8)
        return pltpu.make_async_remote_copy(
            src_ref=self.tile_of(peer), dst_ref=self.by_seq.at[self.s], send_sem=self.seq_send.at[k],
            recv_sem=self.seq_recv.at[self.s], device_id=(self.d, peer), device_id_type=MESH_ID,
        )

    def along_dp(self, k):
        peer = lax.rem(self.d + k, 4)
        return pltpu.make_async_remote_copy(
            src_ref=self.own, dst_ref=self.by_dp.at[self.d], send_sem=self.dp_send.at[k],
            recv_sem=self.dp_recv.at[self.d], device_id=(peer, self.s), device_id_type=MESH_ID,
        )

    def wait_seq(self):
        for k in range(1, 8):
            peer = lax.rem(self.s + k, 8)
            there = self.by_seq.at[peer]
            pltpu.make_async_copy(there, there, self.seq_recv.at[peer]).wait()

    def wait_dp(self):
        for k in range(1, 4):
            peer = lax.rem(self.d + k, 4)
            there = self.by_dp.at[peer]
            pltpu.make_async_copy(there, there, self.dp_recv.at[peer]).wait()


NOTE_SEMS = [
    pltpu.SemaphoreType.DMA((8,)), pltpu.SemaphoreType.DMA((8,)),
    pltpu.SemaphoreType.DMA((4,)), pltpu.SemaphoreType.DMA((4,)),
]


FORWARD_PLAN = (
    (200, 0, 100,),
    (1, 2, 201, 8, 101, 102, 204, 3, 208, 4, 108, 9, 109, 104, 202, 103, 10, 205, 110, 209, 5, 105, 206, 212,
        203, 6, 11, 210, 12, 111, 112, 106, 7, 207,),
    (10500, 107, 211, 10200, 10300, 10400, 10000, 10100, 10600, 213, 113, 13, 114, 214, 215, 115, 14, 15,),
    (20200, 20300, 20500, 20400, 20000, 20100,),
    (20201, 20204, 20301, 20304, 10001, 20001, 20004, 20401, 10504, 10204, 20504, 20002, 20404, 10501, 20501,
        10201, 20101, 20104, 10102, 10101, 10108, 10008, 10002, 10301, 20202, 20005, 20302, 10302, 10508,
        10208, 10408, 10402, 10401, 20102, 10308, 10601, 20205, 20402, 20502, 10604, 20305, 10608, 10004,
        20405, 20505, 10104, 10009, 20105, 10509, 10202, 10502, 10304, 10209, 20003, 10404, 20006, 20203,
        10309, 10602, 20303, 20206, 10205, 10010, 10212, 20103, 10505, 10109, 10605, 10003, 20106, 20306,
        10512, 20403, 20503, 10110, 20406, 10310, 20506, 10103, 10005, 10303, 10609, 10409, 10105, 10410,
        10305, 10012, 10210, 10403, 10405, 10510, 10011, 20007, 10612, 10311, 10312, 10206, 20207, 10606,
        10506, 10513, 20307, 10503, 10112, 10203, 10213, 20107, 10006, 20407, 20507,),
    (
        (0, (10412,)),
        (1, (10111, 10106,)),
        (2, (10610,)),
        (3, (10306, 10511,)),
        (4, (10211,)),
        (5, (10406, 10603,)),
        (6, (10013,)),
        (7, (10613, 10411, 10514,)),
        (8, (10007,)),
        (9, (10107, 10313, 10214,)),
        (10, (10207, 10507,)),
        (11, (10307, 10607,)),
    ),
    (10407, 10113, 10611, 10014, 10413, 10614, 10314, 10114, 10414, 10515, 10215, 10015, 10115, 10615, 10415, 10315,),
)
BACKWARD_PLAN = (
    (
        (10100, 10102, 10101, 10103, 10104, 10106, 10105, 10400, 10200,),
        (10401, 10107, 10108, 10109, 10110, 10201,),
    ),
    (
        (0, (10000, 10402, 10300,)),
        (1, (10301,)),
        (2, (10202,)),
        (3, (10204,)),
        (4, (10403,)),
        (5, (10112,)),
        (6, (20000, 20100, 20200, 20001, 20101, 20201, 20002, 20102, 20202, 20003, 20103, 20203, 10111, 10203,
            10500, 10302, 10002, 20004,)),
        (7, (10113, 20104,)),
        (8, (10404, 20204,)),
        (9, (20005, 20105, 10501, 10303,)),
        (10, (10601, 20006, 20205,)),
        (11, (20106,)),
    ),
    (20500, 20501, 20502, 20503, 20300, 20400, 20401, 20402, 20403, 20301, 20206, 10600, 10602, 10502, 10405,
        10304, 10306, 10004, 10205, 10406, 10407, 10408, 20302, 20303, 10305, 10410, 20007, 10001, 10003,
        10005, 10503, 10006, 10409, 20107, 10604, 20504, 20505, 20207, 20506, 10206, 10207, 10208, 10209,
        10210, 10603, 10504, 10007, 10008, 10307, 10308, 10010, 10505, 20304, 10009, 10310, 20404, 10605,
        10412, 10114, 10506, 10606, 20305, 20306, 20405, 10411, 10507, 10508, 10509, 10309, 20406, 10510,
        10012, 20507, 10607, 10608, 10609, 10011, 10610, 10312, 10211, 20407, 10311, 10413, 20307,),
    (
        (0, (10013,)),
        (5, (10313, 10115,)),
    ),
    (10511, 10414, 10212, 10014, 10611, 10213, 10214, 10314, 200, 201, 202,),
    (203, 205, 204, 206, 0, 1,),
    (10415, 2, 207, 3, 208, 10512, 4, 5, 10612, 10015, 6, 10613, 10614, 10513, 209, 10514, 7,),
    (10315, 10215, 100, 102, 210, 104, 106, 8, 101, 103, 211, 105, 9, 107, 10, 11, 212,),
    (10615, 12, 10515, 13, 213, 214, 108, 109, 110, 14, 112, 215, 111, 113, 114, 15, 115,),
)


def dot(a, b):
    return jnp.dot(a, b, preferred_element_type=jnp.float32)


def dot_t(a, b):
    return lax.dot_general(a, b, (((1,), (1,)), ((), ())), preferred_element_type=jnp.float32)


def t_dot(a, b):
    return lax.dot_general(a, b, (((0,), (0,)), ((), ())), preferred_element_type=jnp.float32)


def repeat(count, body):
    def step(k, nothing):
        body(k)
        return nothing

    lax.fori_loop(0, count, step, 0)


def rows_at(k, size, base=0):
    return pl.ds(pl.multiple_of(base + k * size, 16), size)


def lanes_at(k, size, base=0):
    return pl.ds(pl.multiple_of(base + k * size, 128), size)


def rotate(u, cosine, sine):
    front, back = u[:32], u[32:]
    return jnp.concatenate([front * cosine - back * sine, front * sine + back * cosine], axis=0)


def probabilities(keys, query, limit, chunk):
    scores = t_dot(keys, query) * (HEAD_DIMENSION ** (-0.5))
    key_pos = chunk * 256 + lax.broadcasted_iota(jnp.int32, (256, 384), 0)
    return jnp.where(key_pos <= limit, jnp.exp(scores), 0.0)


def heads_wide(ref, group, lanes):
    return jnp.concatenate(
        [ref[pl.ds(pl.multiple_of(group * 192 + 64 * i, 64), 64), lanes] for i in range(3)], axis=1
    )


def key_limit(length, s):
    query_pos = s * 128 + lax.broadcasted_iota(jnp.int32, (1, 128), 1)
    return jnp.concatenate([jnp.minimum(query_pos, length - 1)] * 3, axis=1)


def forward_body(
    lengths, query_t, key_t, value_t, out_t, gain_a, gain_f, x, cosine, sine, gate, up, down,
    gate_w, up_w, down_w, wcat, kept_in_t, kept_query, kept_kv, kept_attn, kept_denom, notes, hidden,
    tile, cat_t, cat, attn_in_t, query, keys_values, attn, denom,
    attn_in, raw, own_kv, weights, proj, seq_in, dp_in, own_sems, note_a, note_b, note_c, note_d, *sems
):
    place = position()
    d, s = mesh_place(*place)
    row = 0
    for part in (query_t, key_t, value_t, out_t):
        cat_t[row: row + part.shape[0], 0:288] = part[...].astype(jnp.float32)
        row += part.shape[0]
    cat[...] = cat_t[...].T[0:288, :].astype(jnp.bfloat16)
    tile[...] = jnp.zeros_like(tile)
    for k in range(8):
        def own_gains(k=k):
            tile[0:1, 144 * k: 144 * k + 144] = gain_a[...].astype(jnp.float32).reshape(1, 144)
            tile[1:2, 144 * k: 144 * k + 144] = gain_f[...].astype(jnp.float32).reshape(1, 144)

        pl.when(s == k)(own_gains)
    tile[2:3, :] = jnp.broadcast_to((lengths[0] + lengths[1]).astype(jnp.float32), (1, 1152))
    greet(place, True)
    shards = dict(zip(FFN_NAMES, (gate, up, down)))
    wholes = dict(zip(FFN_NAMES, (gate_w, up_w, down_w)))
    cat_spreads = make_spreads(place, CAT_JOBS, {"cat": cat}, {"cat": weights}, sems[:4])
    ffn_spreads = make_spreads(place, FFN_JOBS, shards, wholes, sems[4:8])
    kv_spreads = make_kv_spreads(place, own_kv, keys_values, sems[8:10])
    steps = [[spread.steps() for spread in family] for family in (cat_spreads, ffn_spreads, kv_spreads)]

    def run(tokens):
        for token in tokens:
            steps[token // 10000][token // 100 % 100][token % 100]()

    tiles = Notes(place, lambda peer: tile, tile, seq_in, dp_in, (note_a, note_b, note_c, note_d))
    run(FORWARD_PLAN[0])
    for k in range(1, 8):
        tiles.along_seq(k).start()
    for k in range(1, 4):
        tiles.along_dp(k).start()
    own = [
        pltpu.make_async_copy(
            shards[name], piece_of(wholes[name], (name, 0, 768 if name == "down" else 288, ""))(place), own_sems.at[k]
        )
        for k, name in enumerate(FFN_NAMES)
    ]
    for copy in own:
        copy.start()
    weights[rows_at(d, 288), lanes_at(s, 384)] = cat[...]
    for copy in own:
        copy.wait()
    run(FORWARD_PLAN[1])
    tiles.wait_seq()
    tiles.wait_dp()
    seq_in[s] = tile[...]
    dp_in[d] = tile[...]
    gains = seq_in[0]
    for k in range(1, 8):
        gains = gains + seq_in[k]
    notes[0:8, :] = gains
    notes[8:16, :] = dp_in[0] + dp_in[1] + dp_in[2] + dp_in[3]

    def norm(k):
        rows = rows_at(k, 32)
        part = x[rows, :].astype(jnp.float32)
        scale = lax.rsqrt(jnp.mean(part * part, axis=-1, keepdims=True) + norm_eps)
        attn_in[rows, :] = (part * scale * notes[0:1, :]).astype(jnp.bfloat16)

    repeat(8, norm)
    attn_in_t[...] = attn_in[...].T
    run(FORWARD_PLAN[2])
    for spread in cat_spreads:
        spread.wait_core()

    def project(b):
        block = dot(attn_in[...], weights[:, lanes_at(b, 384)][:, :256]).T
        raw[rows_at(b, 144), :] = block[:144]
        raw[rows_at(b, 48, 1152), :] = block[144:192]
        raw[rows_at(b, 48, 1536), :] = block[192:240]

    repeat(8, project)
    out_copy = pltpu.make_async_copy(weights, wcat, own_sems.at[3])
    out_copy.start()

    def turn(ref, rows_of):
        def one(h):
            ref[rows_at(h, 64), :] = rotate(raw[rows_of(h), :], cosine[...], sine[...]).astype(jnp.bfloat16)

        return one

    repeat(6, turn(own_kv, lambda h: rows_at(h, 64, 1152)))
    own_kv[384:768, :] = raw[1536:1920, :].astype(jnp.bfloat16)
    repeat(18, turn(query, lambda h: rows_at(h, 64)))
    keeps = [
        pltpu.make_async_copy(source, target, own_sems.at[4 + k])
        for k, (source, target) in enumerate(
            ((attn_in_t, kept_in_t), (query, kept_query), (keys_values, kept_kv), (attn, kept_attn), (denom, kept_denom))
        )
    ]
    keeps[0].start()
    keeps[1].start()
    run(FORWARD_PLAN[3])
    here = lanes_at(s, 128)
    for slot in range(2):
        keys_values[slot, :, here] = own_kv[:, slot * 128: slot * 128 + 128]
    run(FORWARD_PLAN[4])
    keeps[2].start()

    def attend(slot, group):
        lanes = lanes_at(slot, 128)
        bound = key_limit(lengths[slot], s)
        wide = heads_wide(query, group, lanes)

        def one_chunk(chunk, carry):
            total, numer = carry
            cols = lanes_at(chunk, 256)
            expo = probabilities(keys_values[slot, rows_at(group, 64), cols], wide, bound, chunk)
            total = total + jnp.sum(expo, axis=0, keepdims=True)
            numer = numer + dot(keys_values[slot, rows_at(group, 64, 384), cols], expo.astype(jnp.bfloat16))
            return (total, numer)

        total, numer = lax.fori_loop(
            0, 4, one_chunk, (jnp.zeros((1, 384), jnp.float32), jnp.zeros((64, 384), jnp.float32)), unroll=True
        )
        mean = numer / total
        for i in range(3):
            attn[pl.ds(pl.multiple_of(group * 192 + 64 * i, 64), 64), lanes] = mean[:, i * 128: i * 128 + 128]
        denom[group, 0:3, lanes] = jnp.concatenate([total[:, i * 128: i * 128 + 128] for i in range(3)], axis=0)

    def unit(k):
        attend(k // 6, lax.rem(k, 6))
        for at, tokens in FORWARD_PLAN[5]:
            pl.when(k == at)(lambda tokens=tokens: run(tokens))

    repeat(12, unit)
    keeps[3].start()
    keeps[4].start()

    def out_project(b):
        block = t_dot(attn[...].astype(jnp.bfloat16), weights[:, lanes_at(b, 384)][:, 128:]).T
        proj[rows_at(b, 144), :] = block[112:256]

    repeat(8, out_project)
    hidden[...] = x[...].astype(jnp.float32) + proj[...].T
    run(FORWARD_PLAN[6])
    for spread in cat_spreads + ffn_spreads + kv_spreads:
        spread.finish()
    for spread in ffn_spreads:
        spread.wait_core()
    for k in range(1, 8):
        tiles.along_seq(k).wait_send()
    for k in range(1, 4):
        tiles.along_dp(k).wait_send()
    for copy in [out_copy] + keeps:
        copy.wait()


def forward_call(lengths, shards_t, gain_a, gain_f, x, cosine, sine, gate, up, down):
    vmem, anywhere = pl.BlockSpec(memory_space=pltpu.VMEM), pl.BlockSpec(memory_space=pl.ANY)
    kept = [
        ((1152, 256), jnp.bfloat16), ((1152, 256), jnp.bfloat16), ((2, 768, 1024), jnp.bfloat16),
        ((1152, 256), jnp.float32), ((6, 8, 256), jnp.float32),
    ]
    return pl.pallas_call(
        forward_body,
        out_shape=[jax.ShapeDtypeStruct((1152, 3072), jnp.bfloat16)] * 4
        + [jax.ShapeDtypeStruct(*item) for item in kept]
        + [jax.ShapeDtypeStruct((16, 1152), jnp.float32), jax.ShapeDtypeStruct((256, 1152), jnp.float32)],
        in_specs=[pl.BlockSpec(memory_space=pltpu.SMEM)] + [vmem] * 12,
        out_specs=[anywhere] * 9 + [vmem] * 2,
        scratch_shapes=[pltpu.VMEM((8, 1152), jnp.float32), pltpu.VMEM((384, 384), jnp.float32), pltpu.VMEM((288, 384), jnp.bfloat16)]
        + [pltpu.VMEM(*item) for item in kept]
        + [
            pltpu.VMEM((256, 1152), jnp.bfloat16),
            pltpu.VMEM((1920, 256), jnp.float32),
            pltpu.VMEM((768, 256), jnp.bfloat16),
            pltpu.VMEM((1152, 3072), jnp.bfloat16),
            pltpu.VMEM((1152, 256), jnp.float32),
            pltpu.VMEM((8, 8, 1152), jnp.float32),
            pltpu.VMEM((4, 8, 1152), jnp.float32),
            pltpu.SemaphoreType.DMA((9,)),
        ]
        + NOTE_SEMS
        + spread_sems(CAT_JOBS)
        + spread_sems(FFN_JOBS)
        + spread_sems(KV_JOBS)[:2],
        compiler_params=pltpu.CompilerParams(
            collective_id=3, has_side_effects=True, vmem_limit_bytes=VMEM_MOST
        ),
        name="attention_forward",
    )(lengths, *shards_t, gain_a, gain_f, x, cosine, sine, gate, up, down)


def ffn_body(
    total_tokens, lengths, hidden, teacher, notes, gate_w, up_w, down_w,
    out, grad_hidden, small, gate_sums, up_sums, down_sums,
    w_gate, w_up, w_down, gate, up, hid, grads_gate, grads_up, inputs_t, cot_t, inputs, cot_b, acc, cot, rate,
    sums_gate, sums_up, sums_down, load, swap_send, swap_recv, store
):
    place = position()
    x, y, z, c = place
    _, s = mesh_place(*place)
    other = mesh_place(x, y, z, 1 - c)
    barrier = pltpu.get_barrier_semaphore()
    pl.semaphore_signal(barrier, inc=1, device_id=other, device_id_type=MESH_ID)
    pl.semaphore_wait(barrier, 1)
    columns = lambda j: lanes_at(j, 768)

    def load_copy(k, source, target, j):
        return pltpu.make_async_copy(source.at[:, columns(j)], target.at[:, columns(j)], load.at[k, j])

    def loads(j):
        return [load_copy(k, *pair, j) for k, pair in enumerate(((gate_w, w_gate), (up_w, w_up), (down_w, w_down)))]

    for j in range(4):
        for copy in loads(j):
            copy.start()

    def swap(source, target, k):
        return pltpu.make_async_remote_copy(
            src_ref=source, dst_ref=target, send_sem=swap_send.at[k], recv_sem=swap_recv.at[k],
            device_id=other, device_id_type=MESH_ID,
        )

    own, theirs = pl.ds(0, 256), pl.ds(256, 256)
    swap_inputs = swap(inputs_t.at[:, own], inputs_t.at[:, theirs], 0)
    swap_cot = swap(cot_t.at[:, own], cot_t.at[:, theirs], 1)

    def swap_hid(i, core):
        at = columns(core + 2 * i)
        return swap(hid.at[own, at], hid.at[theirs, at], 2 + i)

    def swap_grads(ref, j, k):
        return swap(ref.at[own, columns(j)], ref.at[theirs, columns(j)], k + j)

    def norm(k):
        rows = rows_at(k, 32)
        part = hidden[rows, :]
        scale = lax.rsqrt(jnp.mean(part * part, axis=-1, keepdims=True) + norm_eps)
        rate[rows, :] = jnp.broadcast_to(scale, (32, 128))
        inputs[rows, :] = (part * scale * notes[1:2, :]).astype(jnp.bfloat16)

    repeat(8, norm)
    inputs_t[:, 0:256] = inputs[...].T
    acc[...] = jnp.zeros_like(acc)

    def forward(j):
        at = columns(j)
        from_gate, from_up, from_down = loads(j)
        from_gate.wait()
        gate_part = dot(inputs[...], w_gate[:, at])
        from_up.wait()
        up_part = dot(inputs[...], w_up[:, at])
        gate[:, at] = gate_part
        up[:, at] = up_part
        hid[0:256, at] = (gate_part * jax.nn.sigmoid(gate_part) * up_part).astype(jnp.bfloat16)
        from_down.wait()
        acc[...] += dot_t(hid[0:256, at], w_down[:, at])

    repeat(4, forward)
    swap_inputs.start()
    for i in range(2):
        swap_hid(i, 1 - c).start()
    factor = total_tokens / notes[10:11, :]
    small[...] = jnp.zeros_like(small)

    def losses(k):
        rows = rows_at(k, 32)
        first = s * 128 + lax.rem(k, 4) * 32
        live = first + lax.broadcasted_iota(jnp.int32, (32, 1), 0) < lengths[k // 4]
        value = jnp.where(live, hidden[rows, :] + acc[rows, :], 0.0)
        out[rows, :] = value.astype(jnp.bfloat16)
        diff = jnp.where(live, value - teacher[rows, :].astype(jnp.float32), 0.0)
        small[2:3, :] += jnp.sum(diff * diff, axis=0, keepdims=True)
        grad = factor * diff
        cot[rows, :] = grad
        cot_b[rows, :] = grad.astype(jnp.bfloat16)

    repeat(8, losses)
    cot_t[:, 0:256] = cot_b[...].T
    acc[...] = jnp.zeros_like(acc)

    def backward(j):
        at = columns(j)
        grad_hid = dot(cot_b[...], w_down[:, at])
        gate_part = gate[:, at]
        sig = jax.nn.sigmoid(gate_part)
        grads_gate[0:256, at] = (
            grad_hid * up[:, at] * sig * (1.0 + gate_part * (1.0 - sig))
        ).astype(jnp.bfloat16)
        grads_up[0:256, at] = (grad_hid * gate_part * sig).astype(jnp.bfloat16)
        acc[...] += dot_t(grads_gate[0:256, at], w_gate[:, at]) + dot_t(grads_up[0:256, at], w_up[:, at])
        swap_grads(grads_gate, j, 4).start()
        swap_grads(grads_up, j, 8).start()
        pl.when(j == 0)(swap_cot.start)

    repeat(4, backward)

    def finish_rows(k):
        rows = rows_at(k, 32)
        scale = rate[rows, 0:1]
        normed = hidden[rows, :] * scale
        grad = acc[rows, :]
        small[1:2, :] += jnp.sum(grad * normed, axis=0, keepdims=True)
        grad = grad * notes[1:2, :]
        inner = grad - normed * jnp.mean(grad * normed, axis=-1, keepdims=True)
        grad_hidden[rows, :] = cot[rows, :] + scale * inner

    repeat(8, finish_rows)
    small[2:3, :] = jnp.broadcast_to(jnp.sum(small[2:3, :], axis=-1, keepdims=True), (1, 1152))
    small[3:4, :] = notes[0:1, :]
    swap_cot.wait_recv()
    swap_inputs.wait_recv()

    def stored(k, source, target, i):
        at = columns(i)
        return pltpu.make_async_copy(source.at[:, at], target.at[:, at], store.at[k, i])

    def down_grads(i):
        swap_hid(i, c).wait_recv()
        sums_down[:, columns(i)] = dot(cot_t[...], hid[:, columns(c + 2 * i)]).astype(jnp.bfloat16)
        stored(0, sums_down, down_sums, i).start()

    repeat(2, down_grads)

    def wide_grads(j):
        at = columns(j)
        swap_grads(grads_gate, j, 4).wait_recv()
        swap_grads(grads_up, j, 8).wait_recv()
        for half in range(2):
            rows = rows_at(c + 2 * half, 288)
            kept = slice(288 * half, 288 * half + 288)
            sums_gate[kept, at] = dot(inputs_t[rows, :], grads_gate[:, at]).astype(jnp.bfloat16)
            sums_up[kept, at] = dot(inputs_t[rows, :], grads_up[:, at]).astype(jnp.bfloat16)
        stored(1, sums_gate, gate_sums, j).start()
        stored(2, sums_up, up_sums, j).start()

    repeat(4, wide_grads)
    swap_inputs.wait_send()
    swap_cot.wait_send()
    for i in range(2):
        swap_hid(i, 1 - c).wait_send()
        stored(0, sums_down, down_sums, i).wait()
    for j in range(4):
        swap_grads(grads_gate, j, 4).wait_send()
        swap_grads(grads_up, j, 8).wait_send()
        stored(1, sums_gate, gate_sums, j).wait()
        stored(2, sums_up, up_sums, j).wait()


def ffn_call(total_tokens, lengths, hidden, teacher, notes, gate_w, up_w, down_w):
    vmem, anywhere = pl.BlockSpec(memory_space=pltpu.VMEM), pl.BlockSpec(memory_space=pl.ANY)
    whole = pltpu.VMEM((1152, 3072), jnp.bfloat16)
    both = pltpu.VMEM((512, 3072), jnp.bfloat16)
    return pl.pallas_call(
        functools.partial(ffn_body, total_tokens),
        out_shape=[
            jax.ShapeDtypeStruct((256, 1152), jnp.bfloat16),
            jax.ShapeDtypeStruct((256, 1152), jnp.float32),
            jax.ShapeDtypeStruct((8, 1152), jnp.float32),
            jax.ShapeDtypeStruct((576, 3072), jnp.bfloat16),
            jax.ShapeDtypeStruct((576, 3072), jnp.bfloat16),
            jax.ShapeDtypeStruct((1152, 1536), jnp.bfloat16),
        ],
        in_specs=[pl.BlockSpec(memory_space=pltpu.SMEM)] + [vmem] * 3 + [anywhere] * 3,
        out_specs=[vmem] * 3 + [anywhere] * 3,
        scratch_shapes=[whole] * 3
        + [pltpu.VMEM((256, 3072), jnp.float32)] * 2
        + [both] * 3
        + [pltpu.VMEM((1152, 512), jnp.bfloat16)] * 2
        + [pltpu.VMEM((256, 1152), jnp.bfloat16)] * 2
        + [pltpu.VMEM((256, 1152), jnp.float32)] * 2
        + [pltpu.VMEM((256, 128), jnp.float32)]
        + [pltpu.VMEM((576, 3072), jnp.bfloat16)] * 2
        + [
            pltpu.VMEM((1152, 1536), jnp.bfloat16),
            pltpu.SemaphoreType.DMA((3, 4)),
            pltpu.SemaphoreType.DMA((12,)),
            pltpu.SemaphoreType.DMA((12,)),
            pltpu.SemaphoreType.DMA((3, 4)),
        ],
        compiler_params=pltpu.CompilerParams(
            collective_id=5, has_side_effects=True, vmem_limit_bytes=VMEM_MOST
        ),
        name="feed_forward",
    )(lengths, hidden, teacher, notes, gate_w, up_w, down_w)


def backward_body(
    lengths, grad_hidden, cosine, sine, small, x_in, kept_in_t, wcat, keys_values, kept_query, kept_attn, kept_denom,
    grad_gate, grad_up, grad_down,
    own_gate, own_up, own_down, own_query_t, own_key_t, own_value_t, own_out_t, grad_tokens, totals, grad_cat,
    x, attn_in_t, query, attn, denom, own_cat, weights, whole_kv, part_kv, turned, total, own_kv, left, grad_t, note, seq_in, dp_in, row_sum,
    load, store, kv_send, kv_recv, *scratch
):
    place = position()
    d, s = mesh_place(*place)
    greet(place, True)
    sums = dict(zip(FFN_NAMES, (grad_gate, grad_up, grad_down)))
    owned = dict(zip(FFN_NAMES, (own_gate, own_up, own_down)))
    kv_arrived, scratch = scratch[: len(FOLD_KV)], scratch[len(FOLD_KV):]
    note_sems, scratch = scratch[:4], scratch[4:]
    split = len(fold_scratch(FOLD_FFN, False))
    folds = [
        JobFold(place, job, j, sums[job[0]], owned[job[0]], scratch[:split], False) for j, job in enumerate(FOLD_FFN)
    ]
    cat_folds = [JobFold(place, job, j, grad_cat, own_cat, scratch[split:], True) for j, job in enumerate(FOLD_CAT)]
    tiles = Notes(place, lambda peer: note, row_sum, seq_in, dp_in, note_sems)

    def kv_fold(j, slot, row, order):
        def out(value):
            own_kv[row: row + 256, slot * 128: slot * 128 + 128] = value

        spot = kv_spot(part_kv, slot, row)
        return Fold(place, order, lambda who: spot(who), kv_arrived[j], (kv_send, kv_recv), j, out, kv_amount(part_kv))

    kv_folds = [kv_fold(j, *job) for j, job in enumerate(FOLD_KV)]
    steps = [
        [fold.fold.steps() for fold in cat_folds],
        [fold.fold.steps() for fold in folds],
        [fold.steps() for fold in kv_folds],
    ]

    def run(tokens):
        for token in tokens:
            steps[token // 10000][token // 100 % 100][token % 100]()

    for dy in (1, 0):
        for fold in folds:
            fold.begin(dy)

    def block_load(b):
        return pltpu.make_async_copy(wcat.at[:, lanes_at(b, 384)], weights.at[:, lanes_at(b, 384)], load.at[b])

    repeat(8, lambda b: block_load(b).start())
    kept = [
        pltpu.make_async_copy(source, target, load.at[8 + k])
        for k, (source, target) in enumerate(
            ((keys_values, whole_kv), (kept_query, query), (kept_attn, attn), (kept_denom, denom),
             (kept_in_t, attn_in_t), (x_in, x))
        )
    ]
    for copy in kept:
        copy.start()
    run(BACKWARD_PLAN[0][0])
    grad_t[...] = grad_hidden[...].T.astype(jnp.bfloat16)
    total[...] = jnp.zeros_like(total)

    def out_rows(b):
        return jnp.concatenate([jnp.zeros((112, 256), jnp.bfloat16), grad_t[rows_at(b, 144), :]], axis=0)

    def out_back(b):
        block_load(b).wait()
        total[...] += dot(weights[:, lanes_at(b, 384)][:, 128:], out_rows(b))

    repeat(8, out_back)
    run(BACKWARD_PLAN[0][1])
    for copy in kept:
        copy.wait()
    scale = HEAD_DIMENSION ** (-0.5)

    def attend_back(slot, group):
        lanes = lanes_at(slot, 128)
        bound = key_limit(lengths[slot], s)
        wide = heads_wide(query, group, lanes)
        grads, ratios = [], []
        for i in range(3):
            rows = pl.ds(pl.multiple_of(group * 192 + 64 * i, 64), 64)
            grad = total[rows, lanes].astype(jnp.bfloat16).astype(jnp.float32)
            bottom = denom[group, i: i + 1, lanes]
            ratios.append(jnp.sum(grad * attn[rows, lanes], axis=0, keepdims=True) / bottom)
            grads.append((grad / bottom).astype(jnp.bfloat16))
        grads, ratios = jnp.concatenate(grads, axis=1), jnp.concatenate(ratios, axis=1)

        def one_chunk(chunk, sum_query):
            cols = lanes_at(chunk, 256)
            keys = whole_kv[slot, rows_at(group, 64), cols]
            values = whole_kv[slot, rows_at(group, 64, 384), cols]
            expo = probabilities(keys, wide, bound, chunk)
            grad_prob = t_dot(values, grads)
            grad_score = (expo * (grad_prob - ratios)).astype(jnp.bfloat16)
            part_kv[slot, rows_at(group, 64), cols] = (dot_t(wide, grad_score) * scale).astype(jnp.bfloat16)
            part_kv[slot, rows_at(group, 64, 384), cols] = dot_t(grads, expo.astype(jnp.bfloat16)).astype(jnp.bfloat16)
            return sum_query + dot(keys, grad_score)

        sum_query = lax.fori_loop(0, 4, one_chunk, jnp.zeros((64, 384), jnp.float32), unroll=True) * scale
        for i in range(3):
            total[pl.ds(pl.multiple_of(group * 192 + 64 * i, 64), 64), lanes] = sum_query[:, i * 128: i * 128 + 128]

    def unit(k):
        attend_back(k // 6, lax.rem(k, 6))
        for at, tokens in BACKWARD_PLAN[1]:
            pl.when(k == at)(lambda tokens=tokens: run(tokens))

    repeat(12, unit)
    run(BACKWARD_PLAN[2])

    def turn_back(ref, source, count):
        def one(h):
            rows = rows_at(h, 64)
            ref[rows, :] = rotate(source[rows, :], cosine[...], -sine[...]).astype(ref.dtype)

        repeat(count, one)

    turn_back(turned, total, 18)
    turn_back(own_kv, own_kv, 6)
    total[...] = jnp.zeros_like(total)

    def last_block(b):
        rows = jnp.concatenate(
            [
                turned[rows_at(b, 144), :],
                own_kv[rows_at(b, 48), :].astype(jnp.bfloat16),
                own_kv[rows_at(b, 48, 384), :].astype(jnp.bfloat16),
                jnp.zeros((16, 256), jnp.bfloat16),
            ],
            axis=0,
        )
        total[...] += dot(weights[:, lanes_at(b, 384)][:, :256], rows)
        slot = lax.rem(b, 2)
        out = pltpu.make_async_copy(left.at[slot], grad_cat.at[:, lanes_at(b, 384)], store.at[slot])
        pl.when(b >= 2)(lambda: out.wait())
        grad = dot_t(attn_in_t[...], rows)
        out_grad = dot_t(attn[...].astype(jnp.bfloat16), out_rows(b))
        left[slot, :, 0:128] = grad[:, :128].astype(jnp.bfloat16)
        left[slot, :, 128:256] = (grad[:, 128:] + out_grad[:, :128]).astype(jnp.bfloat16)
        left[slot, :, 256:384] = out_grad[:, 128:].astype(jnp.bfloat16)
        out.start()
        for at, tokens in BACKWARD_PLAN[3]:
            pl.when(b == at)(lambda tokens=tokens: run(tokens))

    repeat(8, last_block)
    for slot in range(2):
        pltpu.make_async_copy(left.at[slot], grad_cat.at[:, pl.ds((6 + slot) * 384, 384)], store.at[slot]).wait()
    for dy in (1, 0):
        for fold in cat_folds:
            fold.begin(dy)
    run(BACKWARD_PLAN[4])
    grad_tokens[...] = total[...].T
    note[...] = small[...]

    def finish_rows(k):
        rows = rows_at(k, 32)
        grad = grad_tokens[rows, :]
        normed = x[rows, :].astype(jnp.float32)
        scale_in = lax.rsqrt(jnp.mean(normed * normed, axis=-1, keepdims=True) + norm_eps)
        normed = normed * scale_in
        note[0:1, :] += jnp.sum(grad * normed, axis=0, keepdims=True)
        grad = grad * small[3:4, :]
        inner = grad - normed * jnp.mean(grad * normed, axis=-1, keepdims=True)
        grad_tokens[rows, :] = grad_hidden[rows, :] + scale_in * inner

    repeat(8, finish_rows)
    run(BACKWARD_PLAN[5])
    for k in range(1, 8):
        tiles.along_seq(k).start()
    run(BACKWARD_PLAN[6])
    tiles.wait_seq()
    seq_in[s] = note[...]
    along = seq_in[0]
    for k in range(1, 8):
        along = along + seq_in[k]
    row_sum[...] = along
    run(BACKWARD_PLAN[7])
    for k in range(1, 4):
        tiles.along_dp(k).start()
    run(BACKWARD_PLAN[8])
    tiles.wait_dp()
    dp_in[d] = row_sum[...]
    totals[...] = dp_in[0] + dp_in[1] + dp_in[2] + dp_in[3]
    turned_cat = own_cat[...].T
    row = 0
    for ref in (own_query_t, own_key_t, own_value_t, own_out_t):
        ref[...] = turned_cat[row: row + ref.shape[0], 0:288]
        row += ref.shape[0]
    for fold in folds + kv_folds + cat_folds:
        fold.finish()
    for k in range(1, 8):
        tiles.along_seq(k).wait_send()
    for k in range(1, 4):
        tiles.along_dp(k).wait_send()


def backward_call(
    lengths, grad_hidden, cosine, sine, small, x, attn_in_t, wcat, keys_values, query, attn, denom,
    grad_gate, grad_up, grad_down
):
    vmem, anywhere = pl.BlockSpec(memory_space=pltpu.VMEM), pl.BlockSpec(memory_space=pl.ANY)
    jobs = len(KV_JOBS)
    most = max(fold_slots(order)[1] for _, _, order in FOLD_KV)
    outs = ((288, 384), (288, 384), (144, 768), (144, 288), (48, 288), (48, 288), (144, 288), (256, 1152), (8, 1152))
    return pl.pallas_call(
        backward_body,
        out_shape=[jax.ShapeDtypeStruct(shape, jnp.float32) for shape in outs]
        + [jax.ShapeDtypeStruct((1152, 3072), jnp.bfloat16)],
        in_specs=[pl.BlockSpec(memory_space=pltpu.SMEM)] + [vmem] * 4 + [anywhere] * 10,
        out_specs=[vmem] * len(outs) + [anywhere],
        scratch_shapes=[
            pltpu.VMEM((256, 1152), jnp.bfloat16),
            pltpu.VMEM((1152, 256), jnp.bfloat16),
            pltpu.VMEM((1152, 256), jnp.bfloat16),
            pltpu.VMEM((1152, 256), jnp.float32),
            pltpu.VMEM((6, 8, 256), jnp.float32),
            pltpu.VMEM((384, 384), jnp.float32),
            pltpu.VMEM((1152, 3072), jnp.bfloat16),
            pltpu.VMEM((2, 768, 1024), jnp.bfloat16),
            pltpu.VMEM((2, 768, 1024), jnp.bfloat16),
            pltpu.VMEM((1152, 256), jnp.bfloat16),
            pltpu.VMEM((1152, 256), jnp.float32),
            pltpu.VMEM((768, 256), jnp.float32),
            pltpu.VMEM((2, 1152, 384), jnp.bfloat16),
            pltpu.VMEM((1152, 256), jnp.bfloat16),
            pltpu.VMEM((8, 1152), jnp.float32),
            pltpu.VMEM((8, 8, 1152), jnp.float32),
            pltpu.VMEM((4, 8, 1152), jnp.float32),
            pltpu.VMEM((8, 1152), jnp.float32),
            pltpu.SemaphoreType.DMA((14,)),
            pltpu.SemaphoreType.DMA((2,)),
            pltpu.SemaphoreType.DMA((jobs,)),
            pltpu.SemaphoreType.DMA((jobs, most)),
        ]
        + [pltpu.VMEM((fold_slots(order)[1], 256, 128), jnp.bfloat16) for _, _, order in FOLD_KV]
        + NOTE_SEMS
        + fold_scratch(FOLD_FFN, False)
        + fold_scratch(FOLD_CAT, True),
        compiler_params=pltpu.CompilerParams(
            collective_id=4, has_side_effects=True, vmem_limit_bytes=VMEM_MOST
        ),
        name="attention_backward",
    )(
        lengths, grad_hidden, cosine, sine, small, x, attn_in_t, wcat, keys_values, query, attn, denom,
        grad_gate, grad_up, grad_down,
    )


def hand_over_body(count, *refs):
    sources, (totals, notes) = refs[:count], refs[count: count + 2]
    targets, (loss, gain_a, gain_f) = refs[count + 2: 2 * count + 2], refs[2 * count + 2: 2 * count + 5]
    held, (into, out) = refs[2 * count + 5: 3 * count + 5], refs[-2:]
    reads = [pltpu.make_async_copy(source, there, into.at[k]) for k, (source, there) in enumerate(zip(sources, held))]
    copies = [pltpu.make_async_copy(there, target, out.at[k]) for k, (there, target) in enumerate(zip(held, targets))]
    for read in reads:
        read.start()
    loss[...] = totals[2:3, 0:1] / notes[10:11, 0:1]
    s = lax.axis_index("seq")
    for k in range(8):
        def own(k=k):
            gain_a[...] = totals[0:1, 144 * k: 144 * k + 144]
            gain_f[...] = totals[1:2, 144 * k: 144 * k + 144]

        pl.when(s == k)(own)
    for read, copy in zip(reads, copies):
        read.wait()
        copy.start()
    for copy in copies:
        copy.wait()


def hand_over(results, totals, notes):
    vmem, anywhere = pl.BlockSpec(memory_space=pltpu.VMEM), pl.BlockSpec(memory_space=pl.ANY)
    count = len(results)
    return pl.pallas_call(
        functools.partial(hand_over_body, count),
        out_shape=[jax.ShapeDtypeStruct(r.shape, r.dtype) for r in results]
        + [jax.ShapeDtypeStruct(shape, jnp.float32) for shape in ((1, 1), (1, 144), (1, 144))],
        in_specs=[anywhere] * count + [vmem] * 2,
        out_specs=[anywhere] * count + [vmem] * 3,
        scratch_shapes=[pltpu.VMEM(r.shape, r.dtype) for r in results]
        + [pltpu.SemaphoreType.DMA((count,)), pltpu.SemaphoreType.DMA((count,))],
        compiler_params=pltpu.CompilerParams(vmem_limit_bytes=VMEM_MOST),
        name="hand_over",
    )(*results, totals, notes)


def per_device_fast(
    tokens, teacher, lengths, w_query, key_weight, value_weight, w_out, w_gate, w_up, w_down, gain_attn, gain_ffn
):
    slots, part, width = tokens.shape
    rows = slots * part
    total_tokens = slots * lax.axis_size("dp") * part * lax.axis_size("seq")
    positions = lax.axis_index("seq") * part + jnp.arange(part, dtype=jnp.int32)
    cosine, sine = rope_tables(positions, HEAD_DIMENSION)
    cosine_t = jnp.concatenate([cosine.T] * slots, axis=1)
    sine_t = jnp.concatenate([sine.T] * slots, axis=1)
    x_b = tokens.reshape(rows, width)
    gate_w, up_w, down_t, cat, attn_in_t, query, keys_values, attn, denom, notes, hidden = forward_call(
        lengths, (w_query.T, key_weight.T, value_weight.T, w_out.T),
        gain_attn, gain_ffn, x_b, cosine_t, sine_t,
        w_gate, w_up, w_down.T,
    )
    output, grad_hidden, small, gate_sums, up_sums, down_sums = ffn_call(
        float(total_tokens), lengths, hidden, teacher.reshape(rows, width), notes, gate_w, up_w, down_t
    )
    *results, totals, _ = backward_call(
        lengths, grad_hidden, cosine_t, sine_t, small, x_b, attn_in_t, cat, keys_values, query, attn, denom,
        gate_sums, up_sums, down_sums,
    )
    (
        output, own_gate, own_up, own_down_t, own_query_t, own_key_t, own_value_t, own_out_t, grad_tokens,
        loss, own_gain_a, own_gain_f,
    ) = hand_over([output] + results, totals, notes)
    return (
        output.reshape(tokens.shape),
        loss.reshape(()),
        grad_tokens.reshape(tokens.shape),
        own_query_t.T,
        own_key_t.T,
        own_value_t.T,
        own_out_t.T,
        own_gate,
        own_up,
        own_down_t.T,
        own_gain_a.reshape(-1),
        own_gain_f.reshape(-1),
    )


def solution(mesh):
    placed = (
        P("dp", "seq", None),
        P("dp", "seq", None),
        P("dp"),
        P("dp", "seq"),
        P("dp", "seq"),
        P("dp", "seq"),
        P("dp", "seq"),
        P("dp", "seq"),
        P("dp", "seq"),
        P("dp", "seq"),
        P("seq"),
        P("seq"),
    )
    fits = mesh.shape["dp"] == 4 and mesh.shape["seq"] == 8
    return jax.shard_map(
        per_device_fast if fits else per_device,
        mesh=mesh,
        in_specs=placed,
        out_specs=(
            P("dp", "seq", None),
            P(),
            P("dp", "seq", None),
            P("dp", "seq"),
            P("dp", "seq"),
            P("dp", "seq"),
            P("dp", "seq"),
            P("dp", "seq"),
            P("dp", "seq"),
            P("dp", "seq"),
            P("seq"),
            P("seq"),
        ),
        check_vma=False,
    )
```

```python
import functools
import math

import jax
import jax.numpy as jnp
from jax import lax
from jax.experimental import pallas as pl
from jax.experimental.pallas import tpu as pltpu
from jax.sharding import PartitionSpec as P

QUERY_HEADS = 18
KEY_VALUE_HEADS = 6
HEAD_DIMENSION = 64


norm_eps = 1e-05
rope_base = 10000.0


def rope_tables(positions, head_width):
    half_width = head_width // 2
    exponents = jnp.arange(half_width, dtype=jnp.float32) * (2.0 / head_width)
    angles = positions.astype(jnp.float32)[:, None] * (rope_base ** (-exponents))[None, :]
    return (jnp.cos(angles), jnp.sin(angles))


def apply_rotary(value_rows, cosine_table, sine_table):
    half_width = value_rows.shape[-1] // 2
    front_half = value_rows[..., :half_width]
    back_half = value_rows[..., half_width:]
    cos_wide = cosine_table[:, None, :]
    sin_wide = sine_table[:, None, :]
    return jnp.concatenate(
        [
            front_half * cos_wide - back_half * sin_wide,
            front_half * sin_wide + back_half * cos_wide,
        ],
        axis=-1,
    )


def allowed_mask(query_pos, key_pos, live_len):
    causal = key_pos[None, :] <= query_pos[:, None]
    present = key_pos[None, :] < live_len[:, None]
    return (causal[None, :, :] & present[:, None, :])[:, None, None, :, :]


def over_blocks(piece_len, unit_len, step_fn, running):
    block_length = math.gcd(piece_len, unit_len * max(1, 512 // unit_len))
    number_of_blocks = piece_len // block_length

    def loop_step(block_number, state):
        return step_fn(state, block_number * block_length, block_length)

    return lax.fori_loop(0, number_of_blocks, loop_step, running)


def collect(shards):
    wide = (
        lax.all_gather(shards[0], "seq", axis=1, tiled=True),
        lax.all_gather(shards[1], "seq", axis=1, tiled=True),
        lax.all_gather(shards[2], "seq", axis=1, tiled=True),
        lax.all_gather(shards[3], "seq", axis=1, tiled=True),
        lax.all_gather(shards[4], "seq", axis=1, tiled=True),
        lax.all_gather(shards[5], "seq", axis=1, tiled=True),
        lax.all_gather(shards[6], "seq", axis=1, tiled=True),
        lax.all_gather(shards[7], "seq", axis=0, tiled=True),
        lax.all_gather(shards[8], "seq", axis=0, tiled=True),
    )
    whole = (
        lax.all_gather(wide[0], "dp", axis=0, tiled=True),
        lax.all_gather(wide[1], "dp", axis=0, tiled=True),
        lax.all_gather(wide[2], "dp", axis=0, tiled=True),
        lax.all_gather(wide[3], "dp", axis=0, tiled=True),
        lax.all_gather(wide[4], "dp", axis=0, tiled=True),
        lax.all_gather(wide[5], "dp", axis=0, tiled=True),
        lax.all_gather(wide[6], "dp", axis=0, tiled=True),
    )
    return tuple(whole) + (wide[7], wide[8])


def reduce_grads(grad_sums):
    summed = (
        lax.psum_scatter(grad_sums[0], "seq", scatter_dimension=1, tiled=True),
        lax.psum_scatter(grad_sums[1], "seq", scatter_dimension=1, tiled=True),
        lax.psum_scatter(grad_sums[2], "seq", scatter_dimension=1, tiled=True),
        lax.psum_scatter(grad_sums[3], "seq", scatter_dimension=1, tiled=True),
        lax.psum_scatter(grad_sums[4], "seq", scatter_dimension=1, tiled=True),
        lax.psum_scatter(grad_sums[5], "seq", scatter_dimension=1, tiled=True),
        lax.psum_scatter(grad_sums[6], "seq", scatter_dimension=1, tiled=True),
        lax.psum_scatter(grad_sums[7], "seq", scatter_dimension=0, tiled=True),
        lax.psum_scatter(grad_sums[8], "seq", scatter_dimension=0, tiled=True),
    )
    owned = (
        lax.psum_scatter(summed[0], "dp", scatter_dimension=0, tiled=True),
        lax.psum_scatter(summed[1], "dp", scatter_dimension=0, tiled=True),
        lax.psum_scatter(summed[2], "dp", scatter_dimension=0, tiled=True),
        lax.psum_scatter(summed[3], "dp", scatter_dimension=0, tiled=True),
        lax.psum_scatter(summed[4], "dp", scatter_dimension=0, tiled=True),
        lax.psum_scatter(summed[5], "dp", scatter_dimension=0, tiled=True),
        lax.psum_scatter(summed[6], "dp", scatter_dimension=0, tiled=True),
    )
    return (tuple(owned), summed[7], summed[8])


def forward_slot(weights, tok_part, live_len, query_pos, cosine_table, sine_table):
    (
        full_query,
        full_key,
        full_value,
        full_out,
        full_gate,
        full_up,
        full_down,
        full_gain_attn,
        full_gain_ffn,
    ) = weights
    slot_position, stretched_length, model_width = tok_part.shape
    number_of_rows = slot_position * stretched_length
    query_group = QUERY_HEADS // KEY_VALUE_HEADS
    scale = HEAD_DIMENSION ** (-0.5)
    tok_float = tok_part.astype(jnp.float32).reshape(number_of_rows, model_width)
    inv_first = lax.rsqrt(jnp.mean(tok_float * tok_float, axis=-1, keepdims=True) + norm_eps)
    normed_first = tok_float * inv_first
    attention_input = (normed_first * full_gain_attn.astype(jnp.float32)).astype(jnp.bfloat16)
    unrotated_query = jnp.dot(
        attention_input, full_query, preferred_element_type=jnp.float32
    ).reshape(slot_position, stretched_length, QUERY_HEADS, HEAD_DIMENSION)
    unrotated_key = jnp.dot(attention_input, full_key, preferred_element_type=jnp.float32).reshape(
        slot_position, stretched_length, KEY_VALUE_HEADS, HEAD_DIMENSION
    )
    value_block = (
        jnp.dot(attention_input, full_value, preferred_element_type=jnp.float32)
        .astype(jnp.bfloat16)
        .reshape(slot_position, stretched_length, KEY_VALUE_HEADS * HEAD_DIMENSION)
    )
    query_b = (
        apply_rotary(unrotated_query, cosine_table, sine_table)
        .astype(jnp.bfloat16)
        .reshape(slot_position, stretched_length, KEY_VALUE_HEADS, query_group, HEAD_DIMENSION)
    )
    key_block = (
        apply_rotary(unrotated_key, cosine_table, sine_table)
        .astype(jnp.bfloat16)
        .reshape(slot_position, stretched_length, KEY_VALUE_HEADS * HEAD_DIMENSION)
    )
    empty_denominator = jnp.zeros(
        (slot_position, KEY_VALUE_HEADS, query_group, stretched_length), jnp.float32
    )
    empty_numerator = jnp.zeros(
        (slot_position, KEY_VALUE_HEADS, query_group, stretched_length, HEAD_DIMENSION), jnp.float32
    )
    key_piece = lax.all_gather(key_block, "seq", axis=1, tiled=True)
    value_piece = lax.all_gather(value_block, "seq", axis=1, tiled=True)

    def one_block(partial_value, offset, block_length):
        denominator, numerator = partial_value
        key_blk = lax.dynamic_slice_in_dim(key_piece, offset, block_length, 1).reshape(
            slot_position, block_length, KEY_VALUE_HEADS, HEAD_DIMENSION
        )
        value_blk = lax.dynamic_slice_in_dim(value_piece, offset, block_length, 1).reshape(
            slot_position, block_length, KEY_VALUE_HEADS, HEAD_DIMENSION
        )
        allowed = allowed_mask(
            query_pos, offset + jnp.arange(block_length, dtype=jnp.int32), live_len
        )
        scores = (
            jnp.einsum("schgd,snhd->shgcn", query_b, key_blk, preferred_element_type=jnp.float32)
            * scale
        )
        exp_scores = jnp.where(allowed, jnp.exp(scores), 0.0)
        denominator = denominator + jnp.sum(exp_scores, axis=-1)
        numerator = numerator + jnp.einsum(
            "shgcn,snhd->shgcd",
            exp_scores.astype(jnp.bfloat16),
            value_blk,
            preferred_element_type=jnp.float32,
        )
        return (denominator, numerator)

    denominator, numerator = over_blocks(
        key_piece.shape[1], stretched_length, one_block, (empty_denominator, empty_numerator)
    )
    attn_float = jnp.transpose(numerator / denominator[..., None], (0, 3, 1, 2, 4)).reshape(
        number_of_rows, QUERY_HEADS * HEAD_DIMENSION
    )
    attn_b = attn_float.astype(jnp.bfloat16)
    hidden = tok_float + jnp.dot(attn_b, full_out, preferred_element_type=jnp.float32)
    inv_second = lax.rsqrt(jnp.mean(hidden * hidden, axis=-1, keepdims=True) + norm_eps)
    normed_second = hidden * inv_second
    ffn_in = (normed_second * full_gain_ffn.astype(jnp.float32)).astype(jnp.bfloat16)
    gate_proj = jnp.dot(ffn_in, full_gate, preferred_element_type=jnp.float32)
    up_proj = jnp.dot(ffn_in, full_up, preferred_element_type=jnp.float32)
    hid_b = (jax.nn.silu(gate_proj) * up_proj).astype(jnp.bfloat16)
    valid_rows = (query_pos[None, :] < live_len[:, None]).reshape(number_of_rows, 1)
    out_float = jnp.where(
        valid_rows, hidden + jnp.dot(hid_b, full_down, preferred_element_type=jnp.float32), 0.0
    )
    saved = (
        attention_input,
        inv_first,
        normed_first,
        query_b,
        key_block,
        value_block,
        attn_float,
        attn_b,
        denominator,
        normed_second,
        inv_second,
        ffn_in,
        gate_proj,
        up_proj,
        hid_b,
    )
    return (out_float, valid_rows, saved)


def backward_slot(weights, saved, cotangent, live_len, query_pos, cosine_table, sine_table):
    (
        full_query,
        full_key,
        full_value,
        full_out,
        full_gate,
        full_up,
        full_down,
        full_gain_attn,
        full_gain_ffn,
    ) = weights
    (
        attention_input,
        inv_first,
        normed_first,
        query_b,
        key_block,
        value_block,
        attn_float,
        attn_b,
        denominator,
        normed_second,
        inv_second,
        ffn_in,
        gate_proj,
        up_proj,
        hid_b,
    ) = saved
    slot_position = query_b.shape[0]
    stretched_length = query_b.shape[1]
    number_of_rows = slot_position * stretched_length
    query_group = QUERY_HEADS // KEY_VALUE_HEADS
    scale = HEAD_DIMENSION ** (-0.5)
    cot_b = cotangent.astype(jnp.bfloat16)
    grad_down = jnp.einsum("rf,rd->fd", hid_b, cot_b, preferred_element_type=jnp.float32)
    grad_hid = jnp.einsum("rd,fd->rf", cot_b, full_down, preferred_element_type=jnp.float32)
    sigmoid_gate = jax.nn.sigmoid(gate_proj)
    grad_gate_b = (
        grad_hid * up_proj * sigmoid_gate * (1.0 + gate_proj * (1.0 - sigmoid_gate))
    ).astype(jnp.bfloat16)
    grad_up_b = (grad_hid * gate_proj * sigmoid_gate).astype(jnp.bfloat16)
    grad_gate = jnp.einsum("rd,rf->df", ffn_in, grad_gate_b, preferred_element_type=jnp.float32)
    grad_up = jnp.einsum("rd,rf->df", ffn_in, grad_up_b, preferred_element_type=jnp.float32)
    grad_ffn_in = jnp.einsum(
        "rf,df->rd", grad_gate_b, full_gate, preferred_element_type=jnp.float32
    ) + jnp.einsum("rf,df->rd", grad_up_b, full_up, preferred_element_type=jnp.float32)
    grad_gain_ffn = jnp.sum(grad_ffn_in * normed_second, axis=0)
    grad_normed = grad_ffn_in * full_gain_ffn.astype(jnp.float32)
    grad_hidden = cotangent + inv_second * (
        grad_normed - normed_second * jnp.mean(grad_normed * normed_second, axis=-1, keepdims=True)
    )
    grad_proj_b = grad_hidden.astype(jnp.bfloat16)
    grad_out = jnp.einsum("rq,rd->qd", attn_b, grad_proj_b, preferred_element_type=jnp.float32)
    grad_attn_b = jnp.einsum(
        "rd,qd->rq", grad_proj_b, full_out, preferred_element_type=jnp.float32
    ).astype(jnp.bfloat16)
    den_rows = jnp.transpose(denominator, (0, 3, 1, 2)).reshape(number_of_rows, QUERY_HEADS)
    grad_heads_float = grad_attn_b.astype(jnp.float32).reshape(
        number_of_rows, QUERY_HEADS, HEAD_DIMENSION
    )
    softmax_ratio = (
        jnp.sum(
            grad_heads_float * attn_float.reshape(number_of_rows, QUERY_HEADS, HEAD_DIMENSION),
            axis=-1,
        )
        / den_rows
    ).reshape(slot_position, stretched_length, QUERY_HEADS)
    scaled_gradient = (
        (grad_heads_float / den_rows[..., None])
        .astype(jnp.bfloat16)
        .reshape(slot_position, stretched_length, QUERY_HEADS * HEAD_DIMENSION)
    )
    ratio_all = lax.all_gather(softmax_ratio, "seq", axis=1, tiled=True)
    head_gradient = scaled_gradient.reshape(
        slot_position, stretched_length, KEY_VALUE_HEADS, query_group, HEAD_DIMENSION
    )
    local_softmax_ratio = jnp.transpose(
        softmax_ratio.reshape(slot_position, stretched_length, KEY_VALUE_HEADS, query_group),
        (0, 2, 3, 1),
    )[..., None]
    empty_query = jnp.zeros(
        (slot_position, KEY_VALUE_HEADS, query_group, stretched_length, HEAD_DIMENSION), jnp.float32
    )
    key_piece = lax.all_gather(key_block, "seq", axis=1, tiled=True)
    value_piece = lax.all_gather(value_block, "seq", axis=1, tiled=True)

    def one_block(partial_value, offset, block_length):
        key_blk = lax.dynamic_slice_in_dim(key_piece, offset, block_length, 1).reshape(
            slot_position, block_length, KEY_VALUE_HEADS, HEAD_DIMENSION
        )
        value_blk = lax.dynamic_slice_in_dim(value_piece, offset, block_length, 1).reshape(
            slot_position, block_length, KEY_VALUE_HEADS, HEAD_DIMENSION
        )
        allowed = allowed_mask(
            query_pos, offset + jnp.arange(block_length, dtype=jnp.int32), live_len
        )
        scores = (
            jnp.einsum("schgd,snhd->shgcn", query_b, key_blk, preferred_element_type=jnp.float32)
            * scale
        )
        exp_scores = jnp.where(allowed, jnp.exp(scores), 0.0)
        grad_prob = jnp.einsum(
            "schgd,snhd->shgcn", head_gradient, value_blk, preferred_element_type=jnp.float32
        )
        grad_score = (exp_scores * (grad_prob - local_softmax_ratio)).astype(jnp.bfloat16)
        return (
            partial_value
            + jnp.einsum(
                "shgcn,snhd->shgcd", grad_score, key_blk, preferred_element_type=jnp.float32
            )
            * scale
        )

    grad_query = over_blocks(key_piece.shape[1], stretched_length, one_block, empty_query)
    query_flat = query_b.reshape(slot_position, stretched_length, QUERY_HEADS * HEAD_DIMENSION)
    per_head_keys = key_block.reshape(
        slot_position, stretched_length, KEY_VALUE_HEADS, HEAD_DIMENSION
    )
    per_head_values = value_block.reshape(
        slot_position, stretched_length, KEY_VALUE_HEADS, HEAD_DIMENSION
    )
    empty_key_value = jnp.zeros(
        (slot_position, KEY_VALUE_HEADS, stretched_length, HEAD_DIMENSION), jnp.float32
    )
    query_piece = lax.all_gather(query_flat, "seq", axis=1, tiled=True)
    grad_piece = lax.all_gather(scaled_gradient, "seq", axis=1, tiled=True)

    def one_block(partial_value, offset, block_length):
        grad_key, value_gradient = partial_value
        query_blk = lax.dynamic_slice_in_dim(query_piece, offset, block_length, 1).reshape(
            slot_position, block_length, KEY_VALUE_HEADS, query_group, HEAD_DIMENSION
        )
        grad_blk = lax.dynamic_slice_in_dim(grad_piece, offset, block_length, 1).reshape(
            slot_position, block_length, KEY_VALUE_HEADS, query_group, HEAD_DIMENSION
        )
        ratio_blk = lax.dynamic_slice_in_dim(ratio_all, offset, block_length, 1).reshape(
            slot_position, block_length, KEY_VALUE_HEADS, query_group
        )
        ratio_blk = jnp.transpose(ratio_blk, (0, 2, 3, 1))[..., None]
        remote_pos = offset + jnp.arange(block_length, dtype=jnp.int32)
        allowed = allowed_mask(remote_pos, query_pos, live_len)
        scores = (
            jnp.einsum(
                "snhgd,schd->shgnc", query_blk, per_head_keys, preferred_element_type=jnp.float32
            )
            * scale
        )
        exp_scores = jnp.where(allowed, jnp.exp(scores), 0.0)
        value_gradient = value_gradient + jnp.einsum(
            "shgnc,snhgd->shcd",
            exp_scores.astype(jnp.bfloat16),
            grad_blk,
            preferred_element_type=jnp.float32,
        )
        grad_prob = jnp.einsum(
            "snhgd,schd->shgnc", grad_blk, per_head_values, preferred_element_type=jnp.float32
        )
        grad_score = (exp_scores * (grad_prob - ratio_blk)).astype(jnp.bfloat16)
        grad_key = (
            grad_key
            + jnp.einsum(
                "shgnc,snhgd->shcd", grad_score, query_blk, preferred_element_type=jnp.float32
            )
            * scale
        )
        return (grad_key, value_gradient)

    grad_key, value_gradient = over_blocks(
        query_piece.shape[1], stretched_length, one_block, (empty_key_value, empty_key_value)
    )
    grad_query = jnp.transpose(grad_query, (0, 3, 1, 2, 4)).reshape(
        slot_position, stretched_length, QUERY_HEADS, HEAD_DIMENSION
    )
    grad_query_b = (
        apply_rotary(grad_query, cosine_table, -sine_table)
        .astype(jnp.bfloat16)
        .reshape(number_of_rows, QUERY_HEADS * HEAD_DIMENSION)
    )
    grad_key_b = (
        apply_rotary(jnp.transpose(grad_key, (0, 2, 1, 3)), cosine_table, -sine_table)
        .astype(jnp.bfloat16)
        .reshape(number_of_rows, KEY_VALUE_HEADS * HEAD_DIMENSION)
    )
    grad_value_b = (
        jnp.transpose(value_gradient, (0, 2, 1, 3))
        .astype(jnp.bfloat16)
        .reshape(number_of_rows, KEY_VALUE_HEADS * HEAD_DIMENSION)
    )
    grad_wq = jnp.einsum(
        "rd,rq->dq", attention_input, grad_query_b, preferred_element_type=jnp.float32
    )
    grad_wk = jnp.einsum(
        "rd,rq->dq", attention_input, grad_key_b, preferred_element_type=jnp.float32
    )
    grad_wv = jnp.einsum(
        "rd,rq->dq", attention_input, grad_value_b, preferred_element_type=jnp.float32
    )
    grad_attn_in = jnp.einsum(
        "rq,dq->rd", grad_query_b, full_query, preferred_element_type=jnp.float32
    )
    grad_attn_in = grad_attn_in + jnp.einsum(
        "rq,dq->rd", grad_key_b, full_key, preferred_element_type=jnp.float32
    )
    grad_attn_in = grad_attn_in + jnp.einsum(
        "rq,dq->rd", grad_value_b, full_value, preferred_element_type=jnp.float32
    )
    grad_gain_attn = jnp.sum(grad_attn_in * normed_first, axis=0)
    grad_first = grad_attn_in * full_gain_attn.astype(jnp.float32)
    grad_tokens = grad_hidden + inv_first * (
        grad_first - normed_first * jnp.mean(grad_first * normed_first, axis=-1, keepdims=True)
    )
    return (
        (
            grad_wq,
            grad_wk,
            grad_wv,
            grad_out,
            grad_gate,
            grad_up,
            grad_down,
            grad_gain_attn,
            grad_gain_ffn,
        ),
        grad_tokens,
    )


def per_device(
    tokens,
    teacher,
    lengths,
    w_query,
    key_weight,
    value_weight,
    w_out,
    w_gate,
    w_up,
    w_down,
    gain_attn,
    gain_ffn,
):
    shards = (w_query, key_weight, value_weight, w_out, w_gate, w_up, w_down, gain_attn, gain_ffn)
    slot_count, stretched_length, model_width = tokens.shape
    total_tokens = slot_count * lax.axis_size("dp") * stretched_length * lax.axis_size("seq")
    query_pos = lax.axis_index("seq") * stretched_length + jnp.arange(
        stretched_length, dtype=jnp.int32
    )
    cosine_table, sine_table = rope_tables(query_pos, HEAD_DIMENSION)
    out_rows = []
    stored = []
    differences = []
    squares_local = jnp.zeros((), jnp.float32)
    count_local = jnp.zeros((), jnp.float32)
    for micro in range(slot_count):
        weights = collect(shards)
        live_len = lengths[micro : micro + 1]
        out_float, valid_rows, saved = forward_slot(
            weights, tokens[micro : micro + 1], live_len, query_pos, cosine_table, sine_table
        )
        teach_float = teacher[micro].astype(jnp.float32)
        difference = jnp.where(valid_rows, out_float - teach_float, 0.0)
        squares_local = squares_local + jnp.sum(difference * difference)
        count_local = count_local + jnp.sum(valid_rows.astype(jnp.float32))
        out_rows.append(out_float.astype(jnp.bfloat16).reshape(1, stretched_length, model_width))
        stored.append(saved)
        differences.append(difference)
    loss_sum, count_sum = lax.psum((squares_local, count_local), ("dp", "seq"))
    loss = loss_sum / count_sum
    factor = total_tokens / count_sum
    grad_sums = None
    token_grads = []
    for micro in range(slot_count):
        weights = collect(shards)
        grads, grad_tokens = backward_slot(
            weights,
            stored[micro],
            factor * differences[micro],
            lengths[micro : micro + 1],
            query_pos,
            cosine_table,
            sine_table,
        )
        grad_sums = grads if grad_sums is None else jax.tree.map(jnp.add, grad_sums, grads)
        token_grads.append(grad_tokens.reshape(1, stretched_length, model_width))
    owned, gain_part_attn, gain_part_ffn = reduce_grads(grad_sums)
    gain_totals = lax.psum((gain_part_attn, gain_part_ffn), "dp")
    output = jnp.concatenate(out_rows, axis=0)
    tokens_grad = jnp.concatenate(token_grads, axis=0)
    return (
        output,
        loss,
        tokens_grad,
        owned[0],
        owned[1],
        owned[2],
        owned[3],
        owned[4],
        owned[5],
        owned[6],
        gain_totals[0],
        gain_totals[1],
    )


MESH_ID = pl.DeviceIdType.MESH
VMEM_MOST = 64 * 1024 * 1024 - 128 * 1024


class Place(tuple):
    def with_line(self):
        z = self[2]
        self.line = (0,) + tuple(pick(z, v) for v in ((1, -1, -1, -1), (2, 1, 1, -2), (3, 2, -2, -3)))
        self.sign = (0,) + tuple(jnp.where(offset > 0, 1, -1) for offset in self.line[1:])
        return self


def position():
    row = lax.axis_index("dp")
    column = lax.axis_index("seq")
    return Place((lax.rem(column, 2), row // 2, column // 2, lax.rem(row, 2))).with_line()


def mesh_place(x, y, z, c):
    return (2 * y + c, 2 * z + x)


def step_to(place, axis, sign=1):
    x, y, z, c = place
    if axis == "x":
        return (1 - x, y, z, c)
    if axis == "y":
        return (x, 1 - y, z, c)
    if axis == "z":
        return (x, y, z + sign, c)
    return (x, y, z, 1 - c)


def pick(z, values):
    return sum(jnp.where(z == i, v, 0) for i, v in enumerate(values) if v)


def shifted(place, rel):
    x, y, z, c = place
    dx, dy, rank = rel
    return ((1 - x) if dx else x, (1 - y) if dy else y, z + place.line[rank], c)


def on_line(z):
    return jnp.logical_and(z >= 0, z < 4)


def greet(place, lines):
    x, y, z, c = place
    d, s = mesh_place(*place)
    barrier = pltpu.get_barrier_semaphore()

    def signal(who):
        pl.semaphore_signal(barrier, inc=1, device_id=who, device_id_type=MESH_ID)

    if lines:
        for k in range(1, 8):
            signal((d, lax.rem(s + k, 8)))
        for k in range(1, 4):
            signal((lax.rem(d + k, 4), s))
        pl.semaphore_wait(barrier, 10)
        return
    for axis in "xyc":
        signal(mesh_place(*step_to(place, axis)))
    pl.when(z < 3)(lambda: signal(mesh_place(x, y, z + 1, c)))
    pl.when(z > 0)(lambda: signal(mesh_place(x, y, z - 1, c)))
    pl.semaphore_wait(barrier, 3 + jnp.where(z > 0, 1, 0) + jnp.where(z < 3, 1, 0))


def wait_bytes(region, sem):
    pltpu.make_async_copy(region, region, sem).wait()


def spread_order(order):
    held = [((0, 0, 0), -1)]
    for level, axis in enumerate(order):
        new = []
        if axis == "z":
            new = [((rel[0], rel[1], rank), level) for rank in (1, 2, 3) for rel, _ in held]
        else:
            new = [((1, rel[1], rel[2]) if axis == "x" else (rel[0], 1, rel[2]), level) for rel, _ in held]
        held = held + new
    return held


class Spread:
    def __init__(self, place, order, own, spot, sems, job, pair=None, amount=None):
        self.place, self.order, self.own, self.spot = place, order, own, spot
        self.recv, self.send, self.recv_core, self.send_core = sems
        self.job, self.pair, self.amount = job, pair, amount
        self.pieces = spread_order(order)

    def number(self, who):
        x, y, z, _ = who
        return z * 4 + y * 2 + x

    def go(self, rel, level, target):
        who = shifted(self.place, rel)
        pltpu.make_async_remote_copy(
            src_ref=self.own if level < 0 else self.spot(who),
            dst_ref=self.spot(who),
            send_sem=self.send.at[self.job],
            recv_sem=self.recv.at[self.job, self.number(who)],
            device_id=mesh_place(*target),
            device_id_type=MESH_ID,
        ).start()

    def to_core(self, rel):
        who = shifted(self.place, rel)
        pltpu.make_async_remote_copy(
            src_ref=self.pair(who),
            dst_ref=self.pair(who),
            send_sem=self.send_core.at[self.job],
            recv_sem=self.recv_core.at[self.job],
            device_id=mesh_place(*step_to(self.place, "c")),
            device_id_type=MESH_ID,
        ).start()

    def steps(self):
        out = []
        arrived = set()
        z = self.place[2]
        for rel, level in self.pieces:

            def run(rel=rel, level=level):
                arrived.add(rel)
                who = shifted(self.place, rel)
                if level >= 0:
                    there = self.spot(who)
                    pltpu.make_async_copy(there, there, self.recv.at[self.job, self.number(who)]).wait()
                if level >= 0 and self.order[level] == "z":
                    on = z - self.place.sign[rel[2]]
                    pl.when(on_line(on))(lambda: self.go(rel, level, (self.place[0], self.place[1], on, self.place[3])))
                for axis in self.order[level + 1:]:
                    if axis == "z":
                        pl.when(z < 3)(lambda: self.go(rel, level, step_to(self.place, "z", 1)))
                        pl.when(z > 0)(lambda: self.go(rel, level, step_to(self.place, "z", -1)))
                    else:
                        self.go(rel, level, step_to(self.place, axis))
                if self.pair is not None and (1 - rel[0], rel[1], rel[2]) in arrived:
                    self.to_core(rel)

            out.append(run)
        return out

    def sent(self):
        total = [0, 0]
        for i, z in enumerate((0, 1)):
            for rel, level in self.pieces:
                if level >= 0 and self.order[level] == "z":
                    offset = (0, ((1, -1)[z]), ((2, 1)[z]), ((3, 2)[z]))[rel[2]]
                    on = z - (1 if offset > 0 else -1)
                    total[i] += 0 <= on < 4
                for axis in self.order[level + 1:]:
                    total[i] += (1, 2)[z] if axis == "z" else 1
        return total

    def wait_core(self):
        wait_bytes(self.amount(16), self.recv_core.at[self.job])

    def finish(self):
        ends, inner = self.sent()
        z = self.place[2]
        at_end = jnp.logical_or(z == 0, z == 3)
        pl.when(at_end)(lambda: wait_bytes(self.amount(ends), self.send.at[self.job]))
        pl.when(jnp.logical_not(at_end))(lambda: wait_bytes(self.amount(inner), self.send.at[self.job]))
        if self.pair is not None:
            wait_bytes(self.amount(16), self.send_core.at[self.job])


def fold_pieces(order):
    out = []
    for dx in (0, 1):
        for dy in (0, 1) if "y" in order else (0,):
            for rank in (0, 1, 2, 3):
                differs = {"x": dx, "y": dy, "z": rank}
                stage = next((i for i, axis in enumerate(order) if differs[axis]), len(order))
                out.append(((dx, dy, rank), stage))
    return sorted(out, key=lambda item: (item[1], -item[0][2], -item[0][0] - item[0][1]))


def fold_slots(order):
    base, starts = 0, []
    for level, axis in enumerate(order):
        starts.append(base)
        after = order[level + 1:]
        wide = (4 if "z" in after else 1) * (2 if "x" in after else 1) * (2 if "y" in after else 1)
        base += wide * 5 if axis == "z" else wide
    return starts, base


class Fold:
    def __init__(self, place, order, mine, arrived, sems, job, out, amount, ready=None):
        self.place, self.order, self.mine, self.arrived = place, order, mine, arrived
        self.send, self.recv = sems
        self.job, self.out, self.amount, self.ready = job, out, amount, ready
        self.pieces = fold_pieces(order)
        self.base, self.slots = fold_slots(order)

    def slot(self, level, rel, last):
        index = 0
        at_z = self.place[2] + self.place.line[rel[2]]
        for other in self.order[level + 1:]:
            size = 4 if other == "z" else 2
            index = index * size + (at_z if other == "z" else (rel[0] if other == "x" else rel[1]))
        if self.order[level] == "z":
            index = index * 5 + (4 if last is True else (at_z if last is False else jnp.where(last, 4, at_z)))
        return self.base[level] + index

    def take(self, mine, slot):
        there = self.arrived.at[slot]
        pltpu.make_async_copy(there, there, self.recv.at[self.job, slot]).wait()
        mine[...] = mine[...] + self.arrived[slot]

    def steps(self):
        out = []
        present = set()
        z = self.place[2]
        for rel, stage in self.pieces:

            def run(rel=rel, stage=stage):
                if self.ready is not None and rel[1] not in present:
                    present.add(rel[1])
                    self.ready(rel[1])
                mine = self.mine(shifted(self.place, rel))
                offset, sign = self.place.line[rel[2]], self.place.sign[rel[2]]
                for level in range(min(stage + 1, len(self.order))):
                    if self.order[level] == "z":
                        if level < stage:
                            pl.when(z > 0)(lambda: self.take(mine, self.slot(level, rel, False)))
                            pl.when(z < 3)(lambda: self.take(mine, self.slot(level, rel, True)))
                        else:
                            behind = z - sign
                            pl.when(on_line(behind))(lambda: self.take(mine, self.slot(level, rel, False)))
                    elif level < stage:
                        self.take(mine, self.slot(level, rel, False))
                if stage == len(self.order):
                    self.out(mine[...].astype(jnp.float32))
                    return
                axis = self.order[stage]
                if axis == "z":
                    target = (self.place[0], self.place[1], z + sign, self.place[3])
                else:
                    target = step_to(self.place, axis)
                slot = self.slot(stage, rel, offset == -1 if axis == "z" else False)
                pltpu.make_async_remote_copy(
                    src_ref=mine,
                    dst_ref=self.arrived.at[slot],
                    send_sem=self.send.at[self.job],
                    recv_sem=self.recv.at[self.job, slot],
                    device_id=mesh_place(*target),
                    device_id_type=MESH_ID,
                ).start()

            out.append(run)
        return out

    def finish(self):
        wait_bytes(self.amount(len(self.pieces) - 1), self.send.at[self.job])


CAT_JOBS = (("cat", 0, 96, "xzy"), ("cat", 96, 96, "yzx"), ("cat", 192, 96, "zxy"))
FFN_JOBS = (
    ("gate", 0, 144, "xzy"), ("up", 0, 96, "yzx"), ("down", 0, 384, "zxy"),
    ("gate", 144, 144, "xzy"), ("up", 96, 96, "yzx"), ("down", 384, 384, "zxy"), ("up", 192, 96, "zyx"),
)
KV_JOBS = tuple((slot, 256 * third, "zx") for slot in (0, 1) for third in (0, 1, 2))
FOLD_FFN = tuple(job[:3] + (job[3][::-1],) for job in FFN_JOBS)
FOLD_CAT = tuple(job[:3] + (job[3][::-1],) for job in CAT_JOBS)
FOLD_KV = tuple((slot, row, order[::-1]) for slot, row, order in KV_JOBS)
FFN_NAMES = ("gate", "up", "down")


def job_shape(job):
    return (144, job[2]) if job[0] == "down" else (job[2], 384)


def piece_of(ref, job, paired=False):
    name, first, count, _ = job
    double = 2 if paired else 1

    def spot(who):
        x, y, z, c = who
        d, s = mesh_place(0 if paired else x, y, z, c)
        if name == "down":
            return ref.at[
                pl.ds(pl.multiple_of(s * 144, 16), 144 * double), pl.ds(pl.multiple_of(d * 768 + first, 128), count)
            ]
        return ref.at[
            pl.ds(pl.multiple_of(d * 288 + first, 8), count), pl.ds(pl.multiple_of(s * 384, 128), 384 * double)
        ]

    return spot


def region(ref, elements, rows, columns):
    units = elements // 2048
    wide = max(k for k in range(1, columns // 128 + 1) if units % k == 0 and units // k <= rows // 16)
    return ref.at[pl.ds(0, units // wide * 16), pl.ds(0, wide * 128)]


def amount_of(ref, job):
    rows, columns = job_shape(job)
    return lambda pieces: region(ref, pieces * rows * columns, *ref.shape)


def own_part(ref, job):
    name, first, count, _ = job
    return ref.at[:, pl.ds(first, count)] if name == "down" else ref.at[pl.ds(first, count), :]


def kv_spot(ref, slot, row):
    def spot(who):
        _, s = mesh_place(*who)
        return ref.at[slot, pl.ds(row, 256), pl.ds(pl.multiple_of(s * 128, 128), 128)]

    return spot


def kv_amount(ref):
    return lambda pieces: ref.at[0, pl.ds(0, 32 * pieces), :]


def make_spreads(place, jobs, shards, wholes, sems):
    return [
        Spread(
            place, job[3], own_part(shards[job[0]], job), piece_of(wholes[job[0]], job), sems, j,
            piece_of(wholes[job[0]], job, True), amount_of(wholes[job[0]], job),
        )
        for j, job in enumerate(jobs)
    ]


def make_kv_spreads(place, own, whole, sems):
    return [
        Spread(
            place, order, own.at[pl.ds(row, 256), pl.ds(slot * 128, 128)], kv_spot(whole, slot, row),
            (sems[0], sems[1], None, None), j, None, kv_amount(whole),
        )
        for j, (slot, row, order) in enumerate(KV_JOBS)
    ]


def spread_sems(jobs):
    n = len(jobs)
    return [
        pltpu.SemaphoreType.DMA((n, 16)), pltpu.SemaphoreType.DMA((n,)),
        pltpu.SemaphoreType.DMA((n,)), pltpu.SemaphoreType.DMA((n,)),
    ]


def fold_scratch(jobs, paired):
    n = len(jobs)
    most = max(fold_slots(job[3])[1] for job in jobs)
    scratch = [
        pltpu.SemaphoreType.DMA((n,)), pltpu.SemaphoreType.DMA((n, most)),
        pltpu.SemaphoreType.DMA((n, 2)), pltpu.SemaphoreType.DMA((n, 2)), pltpu.SemaphoreType.DMA((n, 2)),
    ]
    for job in jobs:
        rows, columns = job_shape(job)
        block = (2, 1152, columns) if job[0] == "down" else (2, rows, 3072)
        scratch += [
            pltpu.VMEM(block, jnp.bfloat16), pltpu.VMEM((fold_slots(job[3])[1], rows, columns), jnp.bfloat16)
        ]
        scratch += [pltpu.VMEM(block, jnp.bfloat16)] if paired else []
    return scratch


class JobFold:
    def __init__(self, place, job, j, sums, owned, scratch, paired):
        self.place, self.job, self.j, self.sums, self.paired = place, job, j, sums, paired
        send, recv, self.load_sem, self.core_send, self.core_recv = scratch[:5]
        each = 3 if paired else 2
        self.acc, arrived = scratch[5 + each * j: 7 + each * j]
        self.other = scratch[7 + each * j] if paired else None
        name, first, count, order = job

        def mine(who):
            x, y, z, c = who
            s = 2 * z + x
            if name == "down":
                return self.acc.at[y, pl.ds(pl.multiple_of(s * 144, 16), 144), :]
            return self.acc.at[y, :, pl.ds(pl.multiple_of(s * 384, 128), 384)]

        def out(value):
            if name == "down":
                owned[:, first: first + count] = value
            else:
                owned[first: first + count, :] = value

        self.fold = Fold(place, order, mine, arrived, (send, recv), j, out, amount_of(sums, job), self.ready)

    def block(self, y, c):
        name, first, count, _ = self.job
        d = 2 * y + c if self.paired else y
        if name == "down":
            return self.sums.at[:, pl.ds(pl.multiple_of(d * 768 + first, 128), count)]
        return self.sums.at[pl.ds(pl.multiple_of(d * 288 + first, 8), count), :]

    def local_copy(self, dy):
        x, y, z, c = self.place
        at = (1 - y) if dy else y
        return pltpu.make_async_copy(self.block(at, c), self.acc.at[at], self.load_sem.at[self.j, dy])

    def core_copy(self, dy):
        x, y, z, c = self.place
        at = (1 - y) if dy else y
        return pltpu.make_async_remote_copy(
            src_ref=self.block(at, 1 - c),
            dst_ref=self.other.at[at],
            send_sem=self.core_send.at[self.j, dy],
            recv_sem=self.core_recv.at[self.j, dy],
            device_id=mesh_place(x, y, z, 1 - c),
            device_id_type=MESH_ID,
        )

    def begin(self, dy):
        if self.paired:
            self.core_copy(dy).start()
        self.local_copy(dy).start()

    def ready(self, dy):
        y = self.place[1]
        at = (1 - y) if dy else y
        self.local_copy(dy).wait()
        if not self.paired:
            return
        self.core_copy(dy).wait_recv()

        def add(k, _):
            if self.job[0] == "down":
                part = (at, pl.ds(pl.multiple_of(k * 144, 16), 144), slice(None))
            else:
                part = (at, slice(None), pl.ds(pl.multiple_of(k * 384, 128), 384))
            self.acc[part] = self.acc[part] + self.other[part]
            return _

        lax.fori_loop(0, 8, add, 0)

    def finish(self):
        self.fold.finish()
        for dy in (0, 1) if self.paired else ():
            self.core_copy(dy).wait_send()


class Notes:
    def __init__(self, place, tile_of, own, by_seq, by_dp, sems):
        self.d, self.s = mesh_place(*place)
        self.tile_of, self.own, self.by_seq, self.by_dp = tile_of, own, by_seq, by_dp
        self.seq_send, self.seq_recv, self.dp_send, self.dp_recv = sems

    def along_seq(self, k):
        peer = lax.rem(self.s + k, 8)
        return pltpu.make_async_remote_copy(
            src_ref=self.tile_of(peer), dst_ref=self.by_seq.at[self.s], send_sem=self.seq_send.at[k],
            recv_sem=self.seq_recv.at[self.s], device_id=(self.d, peer), device_id_type=MESH_ID,
        )

    def along_dp(self, k):
        peer = lax.rem(self.d + k, 4)
        return pltpu.make_async_remote_copy(
            src_ref=self.own, dst_ref=self.by_dp.at[self.d], send_sem=self.dp_send.at[k],
            recv_sem=self.dp_recv.at[self.d], device_id=(peer, self.s), device_id_type=MESH_ID,
        )

    def wait_seq(self):
        for k in range(1, 8):
            peer = lax.rem(self.s + k, 8)
            there = self.by_seq.at[peer]
            pltpu.make_async_copy(there, there, self.seq_recv.at[peer]).wait()

    def wait_dp(self):
        for k in range(1, 4):
            peer = lax.rem(self.d + k, 4)
            there = self.by_dp.at[peer]
            pltpu.make_async_copy(there, there, self.dp_recv.at[peer]).wait()


NOTE_SEMS = [
    pltpu.SemaphoreType.DMA((8,)), pltpu.SemaphoreType.DMA((8,)),
    pltpu.SemaphoreType.DMA((4,)), pltpu.SemaphoreType.DMA((4,)),
]


FORWARD_PLAN = (
    (200, 0, 100,),
    (1, 2, 201, 8, 101, 102, 204, 3, 208, 4, 108, 9, 109, 104, 202, 103, 10, 205, 110, 209, 5, 105, 206, 212,
        203, 6, 11, 210, 12, 111, 112, 106, 7, 207,),
    (10500, 107, 211, 10200, 10300, 10400, 10000, 10100, 10600, 213, 113, 13, 114, 214, 215, 115, 14, 15,),
    (20200, 20300, 20500, 20400, 20000, 20100,),
    (20201, 20204, 20301, 20304, 10001, 20001, 20004, 20401, 10504, 10204, 20504, 20002, 20404, 10501, 20501,
        10201, 20101, 20104, 10102, 10101, 10108, 10008, 10002, 10301, 20202, 20005, 20302, 10302, 10508,
        10208, 10408, 10402, 10401, 20102, 10308, 10601, 20205, 20402, 20502, 10604, 20305, 10608, 10004,
        20405, 20505, 10104, 10009, 20105, 10509, 10202, 10502, 10304, 10209, 20003, 10404, 20006, 20203,
        10309, 10602, 20303, 20206, 10205, 10010, 10212, 20103, 10505, 10109, 10605, 10003, 20106, 20306,
        10512, 20403, 20503, 10110, 20406, 10310, 20506, 10103, 10005, 10303, 10609, 10409, 10105, 10410,
        10305, 10012, 10210, 10403, 10405, 10510, 10011, 20007, 10612, 10311, 10312, 10206, 20207, 10606,
        10506, 10513, 20307, 10503, 10112, 10203, 10213, 20107, 10006, 20407, 20507,),
    (
        (0, (10412,)),
        (1, (10111, 10106,)),
        (2, (10610,)),
        (3, (10306, 10511,)),
        (4, (10211,)),
        (5, (10406, 10603,)),
        (6, (10013,)),
        (7, (10613, 10411, 10514,)),
        (8, (10007,)),
        (9, (10107, 10313, 10214,)),
        (10, (10207, 10507,)),
        (11, (10307, 10607,)),
    ),
    (10407, 10113, 10611, 10014, 10413, 10614, 10314, 10114, 10414, 10515, 10215, 10015, 10115, 10615, 10415, 10315,),
)
BACKWARD_PLAN = (
    (
        (10100, 10102, 10101, 10103, 10104, 10106, 10105, 10400, 10200,),
        (10401, 10107, 10108, 10109, 10110, 10201,),
    ),
    (
        (0, (10000, 10402, 10300,)),
        (1, (10301,)),
        (2, (10202,)),
        (3, (10204,)),
        (4, (10403,)),
        (5, (10112,)),
        (6, (20000, 20100, 20200, 20001, 20101, 20201, 20002, 20102, 20202, 20003, 20103, 20203, 10111, 10203,
            10500, 10302, 10002, 20004,)),
        (7, (10113, 20104,)),
        (8, (10404, 20204,)),
        (9, (20005, 20105, 10501, 10303,)),
        (10, (10601, 20006, 20205,)),
        (11, (20106,)),
    ),
    (20500, 20501, 20502, 20503, 20300, 20400, 20401, 20402, 20403, 20301, 20206, 10600, 10602, 10502, 10405,
        10304, 10306, 10004, 10205, 10406, 10407, 10408, 20302, 20303, 10305, 10410, 20007, 10001, 10003,
        10005, 10503, 10006, 10409, 20107, 10604, 20504, 20505, 20207, 20506, 10206, 10207, 10208, 10209,
        10210, 10603, 10504, 10007, 10008, 10307, 10308, 10010, 10505, 20304, 10009, 10310, 20404, 10605,
        10412, 10114, 10506, 10606, 20305, 20306, 20405, 10411, 10507, 10508, 10509, 10309, 20406, 10510,
        10012, 20507, 10607, 10608, 10609, 10011, 10610, 10312, 10211, 20407, 10311, 10413, 20307,),
    (
        (0, (10013,)),
        (5, (10313, 10115,)),
    ),
    (10511, 10414, 10212, 10014, 10611, 10213, 10214, 10314, 200, 201, 202,),
    (203, 205, 204, 206, 0, 1,),
    (10415, 2, 207, 3, 208, 10512, 4, 5, 10612, 10015, 6, 10613, 10614, 10513, 209, 10514, 7,),
    (10315, 10215, 100, 102, 210, 104, 106, 8, 101, 103, 211, 105, 9, 107, 10, 11, 212,),
    (10615, 12, 10515, 13, 213, 214, 108, 109, 110, 14, 112, 215, 111, 113, 114, 15, 115,),
)


def dot(a, b):
    return jnp.dot(a, b, preferred_element_type=jnp.float32)


def dot_t(a, b):
    return lax.dot_general(a, b, (((1,), (1,)), ((), ())), preferred_element_type=jnp.float32)


def t_dot(a, b):
    return lax.dot_general(a, b, (((0,), (0,)), ((), ())), preferred_element_type=jnp.float32)


def repeat(count, body):
    def step(k, nothing):
        body(k)
        return nothing

    lax.fori_loop(0, count, step, 0)


def rows_at(k, size, base=0):
    return pl.ds(pl.multiple_of(base + k * size, 16), size)


def lanes_at(k, size, base=0):
    return pl.ds(pl.multiple_of(base + k * size, 128), size)


def rotate(u, cosine, sine):
    front, back = u[:32], u[32:]
    return jnp.concatenate([front * cosine - back * sine, front * sine + back * cosine], axis=0)


def probabilities(keys, query, limit, chunk):
    scores = t_dot(keys, query) * (HEAD_DIMENSION ** (-0.5))
    key_pos = chunk * 256 + lax.broadcasted_iota(jnp.int32, (256, 384), 0)
    return jnp.where(key_pos <= limit, jnp.exp(scores), 0.0)


def heads_wide(ref, group, lanes):
    return jnp.concatenate(
        [ref[pl.ds(pl.multiple_of(group * 192 + 64 * i, 64), 64), lanes] for i in range(3)], axis=1
    )


def key_limit(length, s):
    query_pos = s * 128 + lax.broadcasted_iota(jnp.int32, (1, 128), 1)
    return jnp.concatenate([jnp.minimum(query_pos, length - 1)] * 3, axis=1)


def forward_body(
    lengths, query_t, key_t, value_t, out_t, gain_a, gain_f, x, cosine, sine, gate, up, down,
    gate_w, up_w, down_w, wcat, kept_in_t, kept_query, kept_kv, kept_attn, kept_denom, notes, hidden,
    tile, cat_t, cat, attn_in_t, query, keys_values, attn, denom,
    attn_in, raw, own_kv, weights, proj, seq_in, dp_in, own_sems, note_a, note_b, note_c, note_d, *sems
):
    place = position()
    d, s = mesh_place(*place)
    row = 0
    for part in (query_t, key_t, value_t, out_t):
        cat_t[row: row + part.shape[0], 0:288] = part[...].astype(jnp.float32)
        row += part.shape[0]
    cat[...] = cat_t[...].T[0:288, :].astype(jnp.bfloat16)
    tile[...] = jnp.zeros_like(tile)
    for k in range(8):
        def own_gains(k=k):
            tile[0:1, 144 * k: 144 * k + 144] = gain_a[...].astype(jnp.float32).reshape(1, 144)
            tile[1:2, 144 * k: 144 * k + 144] = gain_f[...].astype(jnp.float32).reshape(1, 144)

        pl.when(s == k)(own_gains)
    tile[2:3, :] = jnp.broadcast_to((lengths[0] + lengths[1]).astype(jnp.float32), (1, 1152))
    greet(place, True)
    shards = dict(zip(FFN_NAMES, (gate, up, down)))
    wholes = dict(zip(FFN_NAMES, (gate_w, up_w, down_w)))
    cat_spreads = make_spreads(place, CAT_JOBS, {"cat": cat}, {"cat": weights}, sems[:4])
    ffn_spreads = make_spreads(place, FFN_JOBS, shards, wholes, sems[4:8])
    kv_spreads = make_kv_spreads(place, own_kv, keys_values, sems[8:10])
    steps = [[spread.steps() for spread in family] for family in (cat_spreads, ffn_spreads, kv_spreads)]

    def run(tokens):
        for token in tokens:
            steps[token // 10000][token // 100 % 100][token % 100]()

    tiles = Notes(place, lambda peer: tile, tile, seq_in, dp_in, (note_a, note_b, note_c, note_d))
    run(FORWARD_PLAN[0])
    for k in range(1, 8):
        tiles.along_seq(k).start()
    for k in range(1, 4):
        tiles.along_dp(k).start()
    own = [
        pltpu.make_async_copy(
            shards[name], piece_of(wholes[name], (name, 0, 768 if name == "down" else 288, ""))(place), own_sems.at[k]
        )
        for k, name in enumerate(FFN_NAMES)
    ]
    for copy in own:
        copy.start()
    weights[rows_at(d, 288), lanes_at(s, 384)] = cat[...]
    for copy in own:
        copy.wait()
    run(FORWARD_PLAN[1])
    tiles.wait_seq()
    tiles.wait_dp()
    seq_in[s] = tile[...]
    dp_in[d] = tile[...]
    gains = seq_in[0]
    for k in range(1, 8):
        gains = gains + seq_in[k]
    notes[0:8, :] = gains
    notes[8:16, :] = dp_in[0] + dp_in[1] + dp_in[2] + dp_in[3]

    def norm(k):
        rows = rows_at(k, 32)
        part = x[rows, :].astype(jnp.float32)
        scale = lax.rsqrt(jnp.mean(part * part, axis=-1, keepdims=True) + norm_eps)
        attn_in[rows, :] = (part * scale * notes[0:1, :]).astype(jnp.bfloat16)

    repeat(8, norm)
    attn_in_t[...] = attn_in[...].T
    run(FORWARD_PLAN[2])
    for spread in cat_spreads:
        spread.wait_core()

    def project(b):
        block = dot(attn_in[...], weights[:, lanes_at(b, 384)][:, :256]).T
        raw[rows_at(b, 144), :] = block[:144]
        raw[rows_at(b, 48, 1152), :] = block[144:192]
        raw[rows_at(b, 48, 1536), :] = block[192:240]

    repeat(8, project)
    out_copy = pltpu.make_async_copy(weights, wcat, own_sems.at[3])
    out_copy.start()

    def turn(ref, rows_of):
        def one(h):
            ref[rows_at(h, 64), :] = rotate(raw[rows_of(h), :], cosine[...], sine[...]).astype(jnp.bfloat16)

        return one

    repeat(6, turn(own_kv, lambda h: rows_at(h, 64, 1152)))
    own_kv[384:768, :] = raw[1536:1920, :].astype(jnp.bfloat16)
    repeat(18, turn(query, lambda h: rows_at(h, 64)))
    keeps = [
        pltpu.make_async_copy(source, target, own_sems.at[4 + k])
        for k, (source, target) in enumerate(
            ((attn_in_t, kept_in_t), (query, kept_query), (keys_values, kept_kv), (attn, kept_attn), (denom, kept_denom))
        )
    ]
    keeps[0].start()
    keeps[1].start()
    run(FORWARD_PLAN[3])
    here = lanes_at(s, 128)
    for slot in range(2):
        keys_values[slot, :, here] = own_kv[:, slot * 128: slot * 128 + 128]
    run(FORWARD_PLAN[4])
    keeps[2].start()

    def attend(slot, group):
        lanes = lanes_at(slot, 128)
        bound = key_limit(lengths[slot], s)
        wide = heads_wide(query, group, lanes)

        def one_chunk(chunk, carry):
            total, numer = carry
            cols = lanes_at(chunk, 256)
            expo = probabilities(keys_values[slot, rows_at(group, 64), cols], wide, bound, chunk)
            total = total + jnp.sum(expo, axis=0, keepdims=True)
            numer = numer + dot(keys_values[slot, rows_at(group, 64, 384), cols], expo.astype(jnp.bfloat16))
            return (total, numer)

        total, numer = lax.fori_loop(
            0, 4, one_chunk, (jnp.zeros((1, 384), jnp.float32), jnp.zeros((64, 384), jnp.float32)), unroll=True
        )
        mean = numer / total
        for i in range(3):
            attn[pl.ds(pl.multiple_of(group * 192 + 64 * i, 64), 64), lanes] = mean[:, i * 128: i * 128 + 128]
        denom[group, 0:3, lanes] = jnp.concatenate([total[:, i * 128: i * 128 + 128] for i in range(3)], axis=0)

    def unit(k):
        attend(k // 6, lax.rem(k, 6))
        for at, tokens in FORWARD_PLAN[5]:
            pl.when(k == at)(lambda tokens=tokens: run(tokens))

    repeat(12, unit)
    keeps[3].start()
    keeps[4].start()

    def out_project(b):
        block = t_dot(attn[...].astype(jnp.bfloat16), weights[:, lanes_at(b, 384)][:, 128:]).T
        proj[rows_at(b, 144), :] = block[112:256]

    repeat(8, out_project)
    hidden[...] = x[...].astype(jnp.float32) + proj[...].T
    run(FORWARD_PLAN[6])
    for spread in cat_spreads + ffn_spreads + kv_spreads:
        spread.finish()
    for spread in ffn_spreads:
        spread.wait_core()
    for k in range(1, 8):
        tiles.along_seq(k).wait_send()
    for k in range(1, 4):
        tiles.along_dp(k).wait_send()
    for copy in [out_copy] + keeps:
        copy.wait()


def forward_call(lengths, shards_t, gain_a, gain_f, x, cosine, sine, gate, up, down):
    vmem, anywhere = pl.BlockSpec(memory_space=pltpu.VMEM), pl.BlockSpec(memory_space=pl.ANY)
    kept = [
        ((1152, 256), jnp.bfloat16), ((1152, 256), jnp.bfloat16), ((2, 768, 1024), jnp.bfloat16),
        ((1152, 256), jnp.float32), ((6, 8, 256), jnp.float32),
    ]
    return pl.pallas_call(
        forward_body,
        out_shape=[jax.ShapeDtypeStruct((1152, 3072), jnp.bfloat16)] * 4
        + [jax.ShapeDtypeStruct(*item) for item in kept]
        + [jax.ShapeDtypeStruct((16, 1152), jnp.float32), jax.ShapeDtypeStruct((256, 1152), jnp.float32)],
        in_specs=[pl.BlockSpec(memory_space=pltpu.SMEM)] + [vmem] * 12,
        out_specs=[anywhere] * 9 + [vmem] * 2,
        scratch_shapes=[pltpu.VMEM((8, 1152), jnp.float32), pltpu.VMEM((384, 384), jnp.float32), pltpu.VMEM((288, 384), jnp.bfloat16)]
        + [pltpu.VMEM(*item) for item in kept]
        + [
            pltpu.VMEM((256, 1152), jnp.bfloat16),
            pltpu.VMEM((1920, 256), jnp.float32),
            pltpu.VMEM((768, 256), jnp.bfloat16),
            pltpu.VMEM((1152, 3072), jnp.bfloat16),
            pltpu.VMEM((1152, 256), jnp.float32),
            pltpu.VMEM((8, 8, 1152), jnp.float32),
            pltpu.VMEM((4, 8, 1152), jnp.float32),
            pltpu.SemaphoreType.DMA((9,)),
        ]
        + NOTE_SEMS
        + spread_sems(CAT_JOBS)
        + spread_sems(FFN_JOBS)
        + spread_sems(KV_JOBS)[:2],
        compiler_params=pltpu.CompilerParams(
            collective_id=3, has_side_effects=True, vmem_limit_bytes=VMEM_MOST
        ),
        name="attention_forward",
    )(lengths, *shards_t, gain_a, gain_f, x, cosine, sine, gate, up, down)


def ffn_body(
    total_tokens, lengths, hidden, teacher, notes, gate_w, up_w, down_w,
    out, grad_hidden, small, gate_sums, up_sums, down_sums,
    w_gate, w_up, w_down, gate, up, hid, grads_gate, grads_up, inputs_t, cot_t, inputs, cot_b, acc, cot, rate,
    sums_gate, sums_up, sums_down, load, swap_send, swap_recv, store
):
    place = position()
    x, y, z, c = place
    _, s = mesh_place(*place)
    other = mesh_place(x, y, z, 1 - c)
    barrier = pltpu.get_barrier_semaphore()
    pl.semaphore_signal(barrier, inc=1, device_id=other, device_id_type=MESH_ID)
    pl.semaphore_wait(barrier, 1)
    columns = lambda j: lanes_at(j, 768)

    def load_copy(k, source, target, j):
        return pltpu.make_async_copy(source.at[:, columns(j)], target.at[:, columns(j)], load.at[k, j])

    def loads(j):
        return [load_copy(k, *pair, j) for k, pair in enumerate(((gate_w, w_gate), (up_w, w_up), (down_w, w_down)))]

    for j in range(4):
        for copy in loads(j):
            copy.start()

    def swap(source, target, k):
        return pltpu.make_async_remote_copy(
            src_ref=source, dst_ref=target, send_sem=swap_send.at[k], recv_sem=swap_recv.at[k],
            device_id=other, device_id_type=MESH_ID,
        )

    own, theirs = pl.ds(0, 256), pl.ds(256, 256)
    swap_inputs = swap(inputs_t.at[:, own], inputs_t.at[:, theirs], 0)
    swap_cot = swap(cot_t.at[:, own], cot_t.at[:, theirs], 1)

    def swap_hid(i, core):
        at = columns(core + 2 * i)
        return swap(hid.at[own, at], hid.at[theirs, at], 2 + i)

    def swap_grads(ref, j, k):
        return swap(ref.at[own, columns(j)], ref.at[theirs, columns(j)], k + j)

    def norm(k):
        rows = rows_at(k, 32)
        part = hidden[rows, :]
        scale = lax.rsqrt(jnp.mean(part * part, axis=-1, keepdims=True) + norm_eps)
        rate[rows, :] = jnp.broadcast_to(scale, (32, 128))
        inputs[rows, :] = (part * scale * notes[1:2, :]).astype(jnp.bfloat16)

    repeat(8, norm)
    inputs_t[:, 0:256] = inputs[...].T
    acc[...] = jnp.zeros_like(acc)

    def forward(j):
        at = columns(j)
        from_gate, from_up, from_down = loads(j)
        from_gate.wait()
        gate_part = dot(inputs[...], w_gate[:, at])
        from_up.wait()
        up_part = dot(inputs[...], w_up[:, at])
        gate[:, at] = gate_part
        up[:, at] = up_part
        hid[0:256, at] = (gate_part * jax.nn.sigmoid(gate_part) * up_part).astype(jnp.bfloat16)
        from_down.wait()
        acc[...] += dot_t(hid[0:256, at], w_down[:, at])

    repeat(4, forward)
    swap_inputs.start()
    for i in range(2):
        swap_hid(i, 1 - c).start()
    factor = total_tokens / notes[10:11, :]
    small[...] = jnp.zeros_like(small)

    def losses(k):
        rows = rows_at(k, 32)
        first = s * 128 + lax.rem(k, 4) * 32
        live = first + lax.broadcasted_iota(jnp.int32, (32, 1), 0) < lengths[k // 4]
        value = jnp.where(live, hidden[rows, :] + acc[rows, :], 0.0)
        out[rows, :] = value.astype(jnp.bfloat16)
        diff = jnp.where(live, value - teacher[rows, :].astype(jnp.float32), 0.0)
        small[2:3, :] += jnp.sum(diff * diff, axis=0, keepdims=True)
        grad = factor * diff
        cot[rows, :] = grad
        cot_b[rows, :] = grad.astype(jnp.bfloat16)

    repeat(8, losses)
    cot_t[:, 0:256] = cot_b[...].T
    acc[...] = jnp.zeros_like(acc)

    def backward(j):
        at = columns(j)
        grad_hid = dot(cot_b[...], w_down[:, at])
        gate_part = gate[:, at]
        sig = jax.nn.sigmoid(gate_part)
        grads_gate[0:256, at] = (
            grad_hid * up[:, at] * sig * (1.0 + gate_part * (1.0 - sig))
        ).astype(jnp.bfloat16)
        grads_up[0:256, at] = (grad_hid * gate_part * sig).astype(jnp.bfloat16)
        acc[...] += dot_t(grads_gate[0:256, at], w_gate[:, at]) + dot_t(grads_up[0:256, at], w_up[:, at])
        swap_grads(grads_gate, j, 4).start()
        swap_grads(grads_up, j, 8).start()
        pl.when(j == 0)(swap_cot.start)

    repeat(4, backward)

    def finish_rows(k):
        rows = rows_at(k, 32)
        scale = rate[rows, 0:1]
        normed = hidden[rows, :] * scale
        grad = acc[rows, :]
        small[1:2, :] += jnp.sum(grad * normed, axis=0, keepdims=True)
        grad = grad * notes[1:2, :]
        inner = grad - normed * jnp.mean(grad * normed, axis=-1, keepdims=True)
        grad_hidden[rows, :] = cot[rows, :] + scale * inner

    repeat(8, finish_rows)
    small[2:3, :] = jnp.broadcast_to(jnp.sum(small[2:3, :], axis=-1, keepdims=True), (1, 1152))
    small[3:4, :] = notes[0:1, :]
    swap_cot.wait_recv()
    swap_inputs.wait_recv()

    def stored(k, source, target, i):
        at = columns(i)
        return pltpu.make_async_copy(source.at[:, at], target.at[:, at], store.at[k, i])

    def down_grads(i):
        swap_hid(i, c).wait_recv()
        sums_down[:, columns(i)] = dot(cot_t[...], hid[:, columns(c + 2 * i)]).astype(jnp.bfloat16)
        stored(0, sums_down, down_sums, i).start()

    repeat(2, down_grads)

    def wide_grads(j):
        at = columns(j)
        swap_grads(grads_gate, j, 4).wait_recv()
        swap_grads(grads_up, j, 8).wait_recv()
        for half in range(2):
            rows = rows_at(c + 2 * half, 288)
            kept = slice(288 * half, 288 * half + 288)
            sums_gate[kept, at] = dot(inputs_t[rows, :], grads_gate[:, at]).astype(jnp.bfloat16)
            sums_up[kept, at] = dot(inputs_t[rows, :], grads_up[:, at]).astype(jnp.bfloat16)
        stored(1, sums_gate, gate_sums, j).start()
        stored(2, sums_up, up_sums, j).start()

    repeat(4, wide_grads)
    swap_inputs.wait_send()
    swap_cot.wait_send()
    for i in range(2):
        swap_hid(i, 1 - c).wait_send()
        stored(0, sums_down, down_sums, i).wait()
    for j in range(4):
        swap_grads(grads_gate, j, 4).wait_send()
        swap_grads(grads_up, j, 8).wait_send()
        stored(1, sums_gate, gate_sums, j).wait()
        stored(2, sums_up, up_sums, j).wait()


def ffn_call(total_tokens, lengths, hidden, teacher, notes, gate_w, up_w, down_w):
    vmem, anywhere = pl.BlockSpec(memory_space=pltpu.VMEM), pl.BlockSpec(memory_space=pl.ANY)
    whole = pltpu.VMEM((1152, 3072), jnp.bfloat16)
    both = pltpu.VMEM((512, 3072), jnp.bfloat16)
    return pl.pallas_call(
        functools.partial(ffn_body, total_tokens),
        out_shape=[
            jax.ShapeDtypeStruct((256, 1152), jnp.bfloat16),
            jax.ShapeDtypeStruct((256, 1152), jnp.float32),
            jax.ShapeDtypeStruct((8, 1152), jnp.float32),
            jax.ShapeDtypeStruct((576, 3072), jnp.bfloat16),
            jax.ShapeDtypeStruct((576, 3072), jnp.bfloat16),
            jax.ShapeDtypeStruct((1152, 1536), jnp.bfloat16),
        ],
        in_specs=[pl.BlockSpec(memory_space=pltpu.SMEM)] + [vmem] * 3 + [anywhere] * 3,
        out_specs=[vmem] * 3 + [anywhere] * 3,
        scratch_shapes=[whole] * 3
        + [pltpu.VMEM((256, 3072), jnp.float32)] * 2
        + [both] * 3
        + [pltpu.VMEM((1152, 512), jnp.bfloat16)] * 2
        + [pltpu.VMEM((256, 1152), jnp.bfloat16)] * 2
        + [pltpu.VMEM((256, 1152), jnp.float32)] * 2
        + [pltpu.VMEM((256, 128), jnp.float32)]
        + [pltpu.VMEM((576, 3072), jnp.bfloat16)] * 2
        + [
            pltpu.VMEM((1152, 1536), jnp.bfloat16),
            pltpu.SemaphoreType.DMA((3, 4)),
            pltpu.SemaphoreType.DMA((12,)),
            pltpu.SemaphoreType.DMA((12,)),
            pltpu.SemaphoreType.DMA((3, 4)),
        ],
        compiler_params=pltpu.CompilerParams(
            collective_id=5, has_side_effects=True, vmem_limit_bytes=VMEM_MOST
        ),
        name="feed_forward",
    )(lengths, hidden, teacher, notes, gate_w, up_w, down_w)


def backward_body(
    lengths, grad_hidden, cosine, sine, small, x_in, kept_in_t, wcat, keys_values, kept_query, kept_attn, kept_denom,
    grad_gate, grad_up, grad_down,
    own_gate, own_up, own_down, own_query_t, own_key_t, own_value_t, own_out_t, grad_tokens, totals, grad_cat,
    x, attn_in_t, query, attn, denom, own_cat, weights, whole_kv, part_kv, turned, total, own_kv, left, grad_t, note, seq_in, dp_in, row_sum,
    load, store, kv_send, kv_recv, *scratch
):
    place = position()
    d, s = mesh_place(*place)
    greet(place, True)
    sums = dict(zip(FFN_NAMES, (grad_gate, grad_up, grad_down)))
    owned = dict(zip(FFN_NAMES, (own_gate, own_up, own_down)))
    kv_arrived, scratch = scratch[: len(FOLD_KV)], scratch[len(FOLD_KV):]
    note_sems, scratch = scratch[:4], scratch[4:]
    split = len(fold_scratch(FOLD_FFN, False))
    folds = [
        JobFold(place, job, j, sums[job[0]], owned[job[0]], scratch[:split], False) for j, job in enumerate(FOLD_FFN)
    ]
    cat_folds = [JobFold(place, job, j, grad_cat, own_cat, scratch[split:], True) for j, job in enumerate(FOLD_CAT)]
    tiles = Notes(place, lambda peer: note, row_sum, seq_in, dp_in, note_sems)

    def kv_fold(j, slot, row, order):
        def out(value):
            own_kv[row: row + 256, slot * 128: slot * 128 + 128] = value

        spot = kv_spot(part_kv, slot, row)
        return Fold(place, order, lambda who: spot(who), kv_arrived[j], (kv_send, kv_recv), j, out, kv_amount(part_kv))

    kv_folds = [kv_fold(j, *job) for j, job in enumerate(FOLD_KV)]
    steps = [
        [fold.fold.steps() for fold in cat_folds],
        [fold.fold.steps() for fold in folds],
        [fold.steps() for fold in kv_folds],
    ]

    def run(tokens):
        for token in tokens:
            steps[token // 10000][token // 100 % 100][token % 100]()

    for dy in (1, 0):
        for fold in folds:
            fold.begin(dy)

    def block_load(b):
        return pltpu.make_async_copy(wcat.at[:, lanes_at(b, 384)], weights.at[:, lanes_at(b, 384)], load.at[b])

    repeat(8, lambda b: block_load(b).start())
    kept = [
        pltpu.make_async_copy(source, target, load.at[8 + k])
        for k, (source, target) in enumerate(
            ((keys_values, whole_kv), (kept_query, query), (kept_attn, attn), (kept_denom, denom),
             (kept_in_t, attn_in_t), (x_in, x))
        )
    ]
    for copy in kept:
        copy.start()
    run(BACKWARD_PLAN[0][0])
    grad_t[...] = grad_hidden[...].T.astype(jnp.bfloat16)
    total[...] = jnp.zeros_like(total)

    def out_rows(b):
        return jnp.concatenate([jnp.zeros((112, 256), jnp.bfloat16), grad_t[rows_at(b, 144), :]], axis=0)

    def out_back(b):
        block_load(b).wait()
        total[...] += dot(weights[:, lanes_at(b, 384)][:, 128:], out_rows(b))

    repeat(8, out_back)
    run(BACKWARD_PLAN[0][1])
    for copy in kept:
        copy.wait()
    scale = HEAD_DIMENSION ** (-0.5)

    def attend_back(slot, group):
        lanes = lanes_at(slot, 128)
        bound = key_limit(lengths[slot], s)
        wide = heads_wide(query, group, lanes)
        grads, ratios = [], []
        for i in range(3):
            rows = pl.ds(pl.multiple_of(group * 192 + 64 * i, 64), 64)
            grad = total[rows, lanes].astype(jnp.bfloat16).astype(jnp.float32)
            bottom = denom[group, i: i + 1, lanes]
            ratios.append(jnp.sum(grad * attn[rows, lanes], axis=0, keepdims=True) / bottom)
            grads.append((grad / bottom).astype(jnp.bfloat16))
        grads, ratios = jnp.concatenate(grads, axis=1), jnp.concatenate(ratios, axis=1)

        def one_chunk(chunk, sum_query):
            cols = lanes_at(chunk, 256)
            keys = whole_kv[slot, rows_at(group, 64), cols]
            values = whole_kv[slot, rows_at(group, 64, 384), cols]
            expo = probabilities(keys, wide, bound, chunk)
            grad_prob = t_dot(values, grads)
            grad_score = (expo * (grad_prob - ratios)).astype(jnp.bfloat16)
            part_kv[slot, rows_at(group, 64), cols] = (dot_t(wide, grad_score) * scale).astype(jnp.bfloat16)
            part_kv[slot, rows_at(group, 64, 384), cols] = dot_t(grads, expo.astype(jnp.bfloat16)).astype(jnp.bfloat16)
            return sum_query + dot(keys, grad_score)

        sum_query = lax.fori_loop(0, 4, one_chunk, jnp.zeros((64, 384), jnp.float32), unroll=True) * scale
        for i in range(3):
            total[pl.ds(pl.multiple_of(group * 192 + 64 * i, 64), 64), lanes] = sum_query[:, i * 128: i * 128 + 128]

    def unit(k):
        attend_back(k // 6, lax.rem(k, 6))
        for at, tokens in BACKWARD_PLAN[1]:
            pl.when(k == at)(lambda tokens=tokens: run(tokens))

    repeat(12, unit)
    run(BACKWARD_PLAN[2])

    def turn_back(ref, source, count):
        def one(h):
            rows = rows_at(h, 64)
            ref[rows, :] = rotate(source[rows, :], cosine[...], -sine[...]).astype(ref.dtype)

        repeat(count, one)

    turn_back(turned, total, 18)
    turn_back(own_kv, own_kv, 6)
    total[...] = jnp.zeros_like(total)

    def last_block(b):
        rows = jnp.concatenate(
            [
                turned[rows_at(b, 144), :],
                own_kv[rows_at(b, 48), :].astype(jnp.bfloat16),
                own_kv[rows_at(b, 48, 384), :].astype(jnp.bfloat16),
                jnp.zeros((16, 256), jnp.bfloat16),
            ],
            axis=0,
        )
        total[...] += dot(weights[:, lanes_at(b, 384)][:, :256], rows)
        slot = lax.rem(b, 2)
        out = pltpu.make_async_copy(left.at[slot], grad_cat.at[:, lanes_at(b, 384)], store.at[slot])
        pl.when(b >= 2)(lambda: out.wait())
        grad = dot_t(attn_in_t[...], rows)
        out_grad = dot_t(attn[...].astype(jnp.bfloat16), out_rows(b))
        left[slot, :, 0:128] = grad[:, :128].astype(jnp.bfloat16)
        left[slot, :, 128:256] = (grad[:, 128:] + out_grad[:, :128]).astype(jnp.bfloat16)
        left[slot, :, 256:384] = out_grad[:, 128:].astype(jnp.bfloat16)
        out.start()
        for at, tokens in BACKWARD_PLAN[3]:
            pl.when(b == at)(lambda tokens=tokens: run(tokens))

    repeat(8, last_block)
    for slot in range(2):
        pltpu.make_async_copy(left.at[slot], grad_cat.at[:, pl.ds((6 + slot) * 384, 384)], store.at[slot]).wait()
    for dy in (1, 0):
        for fold in cat_folds:
            fold.begin(dy)
    run(BACKWARD_PLAN[4])
    grad_tokens[...] = total[...].T
    note[...] = small[...]

    def finish_rows(k):
        rows = rows_at(k, 32)
        grad = grad_tokens[rows, :]
        normed = x[rows, :].astype(jnp.float32)
        scale_in = lax.rsqrt(jnp.mean(normed * normed, axis=-1, keepdims=True) + norm_eps)
        normed = normed * scale_in
        note[0:1, :] += jnp.sum(grad * normed, axis=0, keepdims=True)
        grad = grad * small[3:4, :]
        inner = grad - normed * jnp.mean(grad * normed, axis=-1, keepdims=True)
        grad_tokens[rows, :] = grad_hidden[rows, :] + scale_in * inner

    repeat(8, finish_rows)
    run(BACKWARD_PLAN[5])
    for k in range(1, 8):
        tiles.along_seq(k).start()
    run(BACKWARD_PLAN[6])
    tiles.wait_seq()
    seq_in[s] = note[...]
    along = seq_in[0]
    for k in range(1, 8):
        along = along + seq_in[k]
    row_sum[...] = along
    run(BACKWARD_PLAN[7])
    for k in range(1, 4):
        tiles.along_dp(k).start()
    run(BACKWARD_PLAN[8])
    tiles.wait_dp()
    dp_in[d] = row_sum[...]
    totals[...] = dp_in[0] + dp_in[1] + dp_in[2] + dp_in[3]
    turned_cat = own_cat[...].T
    row = 0
    for ref in (own_query_t, own_key_t, own_value_t, own_out_t):
        ref[...] = turned_cat[row: row + ref.shape[0], 0:288]
        row += ref.shape[0]
    for fold in folds + kv_folds + cat_folds:
        fold.finish()
    for k in range(1, 8):
        tiles.along_seq(k).wait_send()
    for k in range(1, 4):
        tiles.along_dp(k).wait_send()


def backward_call(
    lengths, grad_hidden, cosine, sine, small, x, attn_in_t, wcat, keys_values, query, attn, denom,
    grad_gate, grad_up, grad_down
):
    vmem, anywhere = pl.BlockSpec(memory_space=pltpu.VMEM), pl.BlockSpec(memory_space=pl.ANY)
    jobs = len(KV_JOBS)
    most = max(fold_slots(order)[1] for _, _, order in FOLD_KV)
    outs = ((288, 384), (288, 384), (144, 768), (144, 288), (48, 288), (48, 288), (144, 288), (256, 1152), (8, 1152))
    return pl.pallas_call(
        backward_body,
        out_shape=[jax.ShapeDtypeStruct(shape, jnp.float32) for shape in outs]
        + [jax.ShapeDtypeStruct((1152, 3072), jnp.bfloat16)],
        in_specs=[pl.BlockSpec(memory_space=pltpu.SMEM)] + [vmem] * 4 + [anywhere] * 10,
        out_specs=[vmem] * len(outs) + [anywhere],
        scratch_shapes=[
            pltpu.VMEM((256, 1152), jnp.bfloat16),
            pltpu.VMEM((1152, 256), jnp.bfloat16),
            pltpu.VMEM((1152, 256), jnp.bfloat16),
            pltpu.VMEM((1152, 256), jnp.float32),
            pltpu.VMEM((6, 8, 256), jnp.float32),
            pltpu.VMEM((384, 384), jnp.float32),
            pltpu.VMEM((1152, 3072), jnp.bfloat16),
            pltpu.VMEM((2, 768, 1024), jnp.bfloat16),
            pltpu.VMEM((2, 768, 1024), jnp.bfloat16),
            pltpu.VMEM((1152, 256), jnp.bfloat16),
            pltpu.VMEM((1152, 256), jnp.float32),
            pltpu.VMEM((768, 256), jnp.float32),
            pltpu.VMEM((2, 1152, 384), jnp.bfloat16),
            pltpu.VMEM((1152, 256), jnp.bfloat16),
            pltpu.VMEM((8, 1152), jnp.float32),
            pltpu.VMEM((8, 8, 1152), jnp.float32),
            pltpu.VMEM((4, 8, 1152), jnp.float32),
            pltpu.VMEM((8, 1152), jnp.float32),
            pltpu.SemaphoreType.DMA((14,)),
            pltpu.SemaphoreType.DMA((2,)),
            pltpu.SemaphoreType.DMA((jobs,)),
            pltpu.SemaphoreType.DMA((jobs, most)),
        ]
        + [pltpu.VMEM((fold_slots(order)[1], 256, 128), jnp.bfloat16) for _, _, order in FOLD_KV]
        + NOTE_SEMS
        + fold_scratch(FOLD_FFN, False)
        + fold_scratch(FOLD_CAT, True),
        compiler_params=pltpu.CompilerParams(
            collective_id=4, has_side_effects=True, vmem_limit_bytes=VMEM_MOST
        ),
        name="attention_backward",
    )(
        lengths, grad_hidden, cosine, sine, small, x, attn_in_t, wcat, keys_values, query, attn, denom,
        grad_gate, grad_up, grad_down,
    )


def hand_over_body(count, *refs):
    sources, (totals, notes) = refs[:count], refs[count: count + 2]
    targets, (loss, gain_a, gain_f) = refs[count + 2: 2 * count + 2], refs[2 * count + 2: 2 * count + 5]
    held, (into, out) = refs[2 * count + 5: 3 * count + 5], refs[-2:]
    reads = [pltpu.make_async_copy(source, there, into.at[k]) for k, (source, there) in enumerate(zip(sources, held))]
    copies = [pltpu.make_async_copy(there, target, out.at[k]) for k, (there, target) in enumerate(zip(held, targets))]
    largest_first = sorted(range(count), key=lambda k: -math.prod(held[k].shape))
    for k in largest_first:
        reads[k].start()
    loss[...] = totals[2:3, 0:1] / notes[10:11, 0:1]
    s = lax.axis_index("seq")
    for k in range(8):
        def own(k=k):
            gain_a[...] = totals[0:1, 144 * k: 144 * k + 144]
            gain_f[...] = totals[1:2, 144 * k: 144 * k + 144]

        pl.when(s == k)(own)
    for k in largest_first:
        reads[k].wait()
        copies[k].start()
    for copy in copies:
        copy.wait()


def hand_over(results, totals, notes):
    vmem, anywhere = pl.BlockSpec(memory_space=pltpu.VMEM), pl.BlockSpec(memory_space=pl.ANY)
    count = len(results)
    return pl.pallas_call(
        functools.partial(hand_over_body, count),
        out_shape=[jax.ShapeDtypeStruct(r.shape, r.dtype) for r in results]
        + [jax.ShapeDtypeStruct(shape, jnp.float32) for shape in ((1, 1), (1, 144), (1, 144))],
        in_specs=[anywhere] * count + [vmem] * 2,
        out_specs=[anywhere] * count + [vmem] * 3,
        scratch_shapes=[pltpu.VMEM(r.shape, r.dtype) for r in results]
        + [pltpu.SemaphoreType.DMA((count,)), pltpu.SemaphoreType.DMA((count,))],
        compiler_params=pltpu.CompilerParams(vmem_limit_bytes=VMEM_MOST),
        name="hand_over",
    )(*results, totals, notes)


def per_device_fast(
    tokens, teacher, lengths, w_query, key_weight, value_weight, w_out, w_gate, w_up, w_down, gain_attn, gain_ffn
):
    slots, part, width = tokens.shape
    rows = slots * part
    total_tokens = slots * lax.axis_size("dp") * part * lax.axis_size("seq")
    positions = lax.axis_index("seq") * part + jnp.arange(part, dtype=jnp.int32)
    cosine, sine = rope_tables(positions, HEAD_DIMENSION)
    cosine_t = jnp.concatenate([cosine.T] * slots, axis=1)
    sine_t = jnp.concatenate([sine.T] * slots, axis=1)
    x_b = tokens.reshape(rows, width)
    gate_w, up_w, down_t, cat, attn_in_t, query, keys_values, attn, denom, notes, hidden = forward_call(
        lengths, (w_query.T, key_weight.T, value_weight.T, w_out.T),
        gain_attn, gain_ffn, x_b, cosine_t, sine_t,
        w_gate, w_up, w_down.T,
    )
    output, grad_hidden, small, gate_sums, up_sums, down_sums = ffn_call(
        float(total_tokens), lengths, hidden, teacher.reshape(rows, width), notes, gate_w, up_w, down_t
    )
    *results, totals, _ = backward_call(
        lengths, grad_hidden, cosine_t, sine_t, small, x_b, attn_in_t, cat, keys_values, query, attn, denom,
        gate_sums, up_sums, down_sums,
    )
    (
        output, own_gate, own_up, own_down_t, own_query_t, own_key_t, own_value_t, own_out_t, grad_tokens,
        loss, own_gain_a, own_gain_f,
    ) = hand_over([output] + results, totals, notes)
    return (
        output.reshape(tokens.shape),
        loss.reshape(()),
        grad_tokens.reshape(tokens.shape),
        own_query_t.T,
        own_key_t.T,
        own_value_t.T,
        own_out_t.T,
        own_gate,
        own_up,
        own_down_t.T,
        own_gain_a.reshape(-1),
        own_gain_f.reshape(-1),
    )


def solution(mesh):
    placed = (
        P("dp", "seq", None),
        P("dp", "seq", None),
        P("dp"),
        P("dp", "seq"),
        P("dp", "seq"),
        P("dp", "seq"),
        P("dp", "seq"),
        P("dp", "seq"),
        P("dp", "seq"),
        P("dp", "seq"),
        P("seq"),
        P("seq"),
    )
    fits = mesh.shape["dp"] == 4 and mesh.shape["seq"] == 8
    return jax.shard_map(
        per_device_fast if fits else per_device,
        mesh=mesh,
        in_specs=placed,
        out_specs=(
            P("dp", "seq", None),
            P(),
            P("dp", "seq", None),
            P("dp", "seq"),
            P("dp", "seq"),
            P("dp", "seq"),
            P("dp", "seq"),
            P("dp", "seq"),
            P("dp", "seq"),
            P("dp", "seq"),
            P("seq"),
            P("seq"),
        ),
        check_vma=False,
    )
```
